32 devices in a mesh: dp: 8 (over z, x), tensor: 4 (over y, core).
Axes of the slice: x: 2, y: 2, z: 4, core: 2. Of those that a mesh axis runs over, the one named last changes fastest.
Arguments:
- tokens: bfloat16 [8192, 2048], P('dp'), may hold values from -6 to 6
- lengths: int32 [8], P('dp'), may hold values from 1 to 1024, 4915 in all
- norm_attn: float32 [2048], P('dp'), may hold values from 0.5 to 1.5
- query_proj: float32 [2048, 1024], P('dp', 'tensor'), may hold values from -0.125 to 0.125
- key_proj: float32 [2048, 1024], P('dp', 'tensor'), may hold values from -0.125 to 0.125
- value_proj: float32 [2048, 2048], P('dp', 'tensor'), may hold values from -0.125 to 0.125
- outgate_proj: float32 [2048, 2048], P('dp', 'tensor'), may hold values from -0.125 to 0.125
- rank_proj: float32 [2048, 16], P('dp'), may hold values from -0.125 to 0.125
- decay_proj: float32 [16, 4, 256], P(None, 'tensor', 'dp'), may hold values from -1.5 to 1.5
- decay_bias: float32 [4, 256], P('tensor', 'dp'), may hold values from -4 to 5
- head_gain: float32 [512], P('dp'), may hold values from 0.5 to 1.5
- out_proj: float32 [2048, 2048], P('tensor', 'dp'), may hold values from -0.25 to 0.25
- norm_ffn: float32 [2048], P('dp'), may hold values from 0.5 to 1.5
- gate_proj: float32 [2048, 5632], P('dp', 'tensor'), may hold values from -0.125 to 0.125
- up_proj: float32 [2048, 5632], P('dp', 'tensor'), may hold values from -0.125 to 0.125
- down_proj: float32 [5632, 2048], P('tensor', 'dp'), may hold values from -0.15625 to 0.15625
- cotangent: bfloat16 [8192, 2048], P('dp'), may hold values from -6 to 6
Outputs:
- output: bfloat16 [8192, 2048], P('dp')
- grad_tokens: bfloat16 [8192, 2048], P('dp')
- grad_norm_attn: float32 [2048], P('dp')
- grad_query_proj: float32 [2048, 1024], P('dp', 'tensor')
- grad_key_proj: float32 [2048, 1024], P('dp', 'tensor')
- grad_value_proj: float32 [2048, 2048], P('dp', 'tensor')
- grad_outgate_proj: float32 [2048, 2048], P('dp', 'tensor')
- grad_rank_proj: float32 [2048, 16], P('dp')
- grad_decay_proj: float32 [16, 4, 256], P(None, 'tensor', 'dp')
- grad_decay_bias: float32 [4, 256], P('tensor', 'dp')
- grad_head_gain: float32 [512], P('dp')
- grad_out_proj: float32 [2048, 2048], P('tensor', 'dp')
- grad_norm_ffn: float32 [2048], P('dp')
- grad_gate_proj: float32 [2048, 5632], P('dp', 'tensor')
- grad_up_proj: float32 [2048, 5632], P('dp', 'tensor')
- grad_down_proj: float32 [5632, 2048], P('tensor', 'dp')
The draws below stay inside these ranges and needn't reach their ends.
Inputs may be any that keep to these rules, and one draw needn't show every extreme that they name: `lengths`: each slot's live positions come first; some slot is full.
All inputs are finite; a program needn't handle non-finite values. No bound on the sum of `lengths` on one device may be relied on, other than what follows from the above.
Results may differ from the reference program's by a relative error of at most 0.04.
Values may be sent and summed in bfloat16 or wider, within the bound.
A program may use at most 256 MiB of HBM per device.

```python
import math
import jax
import jax.numpy as jnp
import numpy as np
from jax import lax

D = 2048
HEADS = 4
DK = 256
DV = 512
RANK = 16
FF = 5632
GROUP = 64
SEQ_LEN = 1024
KALL = 1024
VALL = 2048
SLOTS = 8
TOKENS = 8192


def level_of(stream_key, extent, shards, low, top_value):
    level, own = 1.0, jax.random.fold_in(stream_key, 6)
    for position, parts in shards:
        steps = jnp.exp(jax.random.uniform(jax.random.fold_in(own, position), (parts,), jnp.float32, low / len(shards), top_value / len(shards)))
        level = level * jnp.repeat(steps, extent[position] // parts).reshape([-1 if axis == position else 1 for axis in range(len(extent))])
    return level


def length_profile(count, total, limit, lean):
    weights = [(1 << 20) // math.isqrt(standing ** lean) + 1 for standing in range(2, count + 1)]
    spare, counts = total - limit - (count - 1), [1] * (count - 1)
    while spare > 0:
        free = [i for i in range(count - 1) if counts[i] < limit]
        pool, remaining = sum([weights[i] for i in free]), spare
        for i in free:
            more = min(limit - counts[i], max(1, remaining * weights[i] // pool), spare)
            counts[i] = counts[i] + more
            spare = spare - more
    return np.array([limit] + counts)


def uneven_parts(own_key, number_of, total, limit, lean):
    if number_of == 2:
        one = jax.random.randint(own_key, (), max(1, total - limit), min(limit, total - 1) + 1)
        return jnp.stack([one, total - one])
    sizes = jnp.asarray(length_profile(number_of, total, limit, lean), jnp.int32)
    pairs = (number_of - 1) // 2
    source_of, taker = sizes[1:1 + 2 * pairs:2], sizes[2:2 + 2 * pairs:2]
    margin = jnp.minimum(source_of - 1, limit - taker)
    shifted = jax.random.randint(jax.random.fold_in(own_key, 1), (pairs,), 0, 1 << 20) % (margin + 1)
    sizes = sizes.at[1:1 + 2 * pairs:2].set(source_of - shifted).at[2:2 + 2 * pairs:2].set(taker + shifted)
    return sizes[jax.random.permutation(jax.random.fold_in(own_key, 2), number_of)]


def noise(own_key, extent, scale, bound, cuts=(), held_as=jnp.bfloat16):
    loudness = level_of(own_key, extent, cuts, -0.22, 0.18) if cuts else 1.0
    entries = jax.random.normal(own_key, extent, jnp.float32) * scale * loudness
    return jnp.minimum(jnp.maximum(entries, -bound), bound).astype(held_as)


def setup_inputs(seed: int = 0) -> dict:
    streams_of = jax.random.split(jax.random.key(seed), 18)
    return {
        "tokens": noise(streams_of[0], (TOKENS, D), 1.0, 6.0, ((0, 8),)),
        "lengths": uneven_parts(streams_of[1], SLOTS, SLOTS * SEQ_LEN * 3 // 5, SEQ_LEN, 2).astype(jnp.int32),
        "norm_attn": jnp.clip(1.0 + 0.1 * jax.random.normal(streams_of[2], (D,), jnp.float32), 0.5, 1.5),
        "query_proj": noise(streams_of[3], (D, KALL), D ** -0.5, 0.125, ((0, 8), (1, 4)), jnp.float32),
        "key_proj": noise(streams_of[4], (D, KALL), D ** -0.5, 0.125, ((0, 8), (1, 4)), jnp.float32),
        "value_proj": noise(streams_of[5], (D, VALL), D ** -0.5, 0.125, ((0, 8), (1, 4)), jnp.float32),
        "outgate_proj": noise(streams_of[6], (D, VALL), D ** -0.5, 0.125, ((0, 8), (1, 4)), jnp.float32),
        "rank_proj": noise(streams_of[7], (D, RANK), D ** -0.5, 0.125, ((0, 8),), jnp.float32),
        "decay_proj": noise(streams_of[8], (RANK, HEADS, DK), RANK ** -0.5, 1.5, ((1, 4), (2, 8)), jnp.float32),
        "decay_bias": jnp.clip(-4.0 + 9.0 * jax.random.uniform(streams_of[9], (HEADS, DK), jnp.float32) ** level_of(streams_of[9], (HEADS, DK), ((0, 4), (1, 8)), -0.2, 0.2), -4.0, 5.0),
        "head_gain": jnp.clip(1.0 + 0.1 * jax.random.normal(streams_of[10], (DV,), jnp.float32), 0.5, 1.5),
        "out_proj": noise(streams_of[11], (VALL, D), (VALL // 4) ** -0.5, 0.25, ((0, 4), (1, 8)), jnp.float32),
        "norm_ffn": jnp.clip(1.0 + 0.1 * jax.random.normal(streams_of[12], (D,), jnp.float32), 0.5, 1.5),
        "gate_proj": noise(streams_of[13], (D, FF), D ** -0.5, 0.125, ((0, 8), (1, 4)), jnp.float32),
        "up_proj": noise(streams_of[14], (D, FF), D ** -0.5, 0.125, ((0, 8), (1, 4)), jnp.float32),
        "down_proj": noise(streams_of[15], (FF, D), (FF // 4) ** -0.5, 0.15625, ((0, 4), (1, 8)), jnp.float32),
        "cotangent": noise(streams_of[16], (TOKENS, D), 1.0, 6.0, ((0, 8),)),
    }


@jax.custom_vjp
def low(v):
    return lax.optimization_barrier(v.astype(jnp.bfloat16)).astype(jnp.float32)

@jax.custom_vjp
def low_back(v):
    return v

def low_keep(v):
    return (low(v), None)

def low_pass(kept, grad):
    return (grad,)

def back_keep(v):
    return (v, None)

def back_low(kept, grad):
    return (low(grad),)
low.defvjp(low_keep, low_pass)
low_back.defvjp(back_keep, back_low)
norm_eps = 1e-06
head_eps = 1.0
highest_precision = lax.Precision.HIGHEST

def rms_scale(values, gain):
    return values * lax.rsqrt(lax.optimization_barrier(jnp.mean(values * values, axis=-1, keepdims=True)) + norm_eps) * gain

def product(left, right):
    return jnp.dot(left, right, precision=highest_precision, preferred_element_type=jnp.float32)

def group_step(running_state, block):
    query_matrix, key_matrix, value_matrix, decay = block
    cumulative_decay = jnp.cumsum(decay, axis=1)
    steps = decay.shape[1]
    lower = (jnp.arange(steps)[:, None] >= jnp.arange(steps)[None, :]).astype(jnp.float32)
    spread = jnp.exp(jnp.minimum(cumulative_decay[:, :, None, :] - cumulative_decay[:, None, :, :], 0.0)) * lower[None, :, :, None]
    weighted = query_matrix[:, :, None, :] * spread
    scores = jnp.einsum('hijk,hjk->hij', weighted, key_matrix, precision=highest_precision)
    inner = jnp.einsum('hij,hjv->hiv', scores, value_matrix, precision=highest_precision)
    outer_product = jnp.einsum('muq,mqj->muj', query_matrix * jnp.exp(cumulative_decay), running_state, precision=highest_precision)
    final_decay_row = cumulative_decay[:, -1:, :]
    carried_state = jnp.exp(final_decay_row[:, 0, :])[:, :, None] * running_state
    carried_state = carried_state + jnp.einsum('zbm,zbi->zmi', key_matrix * jnp.exp(final_decay_row - cumulative_decay), value_matrix, precision=highest_precision)
    return (carried_state, inner + outer_product)

def recurrence(query_matrix, key_matrix, value_matrix, decay):
    length = query_matrix.shape[0]
    heads = query_matrix.shape[1]
    count = length // GROUP

    def split(values):
        return jnp.transpose(values.reshape(count, GROUP, heads, values.shape[2]), (0, 2, 1, 3))
    start = jnp.zeros((heads, key_matrix.shape[2], value_matrix.shape[2]), jnp.float32)
    _, blocks = lax.scan(jax.checkpoint(group_step), start, (split(query_matrix), split(key_matrix), split(value_matrix), split(decay)))
    return jnp.transpose(blocks, (0, 2, 1, 3)).reshape(length, heads, value_matrix.shape[2])

def mixer(query_matrix, key_matrix, value_matrix, outgate_rows, rank_rows, decay_weight, bias_weight, gain_weight):
    heads = bias_weight.shape[0]
    length = query_matrix.shape[0]
    seqs = length // SEQ_LEN
    before = product(rank_rows, decay_weight.reshape(decay_weight.shape[0], -1)) + bias_weight.reshape(-1)
    decay = jax.nn.log_sigmoid(before) / 16.0

    def arrange(values, width):
        return values.reshape(seqs, SEQ_LEN, heads, width)
    scale = DK ** (-0.5)
    mixed = jax.vmap(recurrence)(arrange(query_matrix * scale, DK), arrange(key_matrix, DK), arrange(value_matrix, DV), arrange(decay, DK))
    mixed = mixed.reshape(length, heads, DV)
    normed = mixed * lax.rsqrt(lax.optimization_barrier(jnp.mean(mixed * mixed, axis=-1, keepdims=True)) + head_eps) * gain_weight
    return (normed * jax.nn.silu(outgate_rows.reshape(length, heads, DV))).reshape(length, heads * DV)

def layer(inputs, weights, mask):
    norm_attn, query_proj, key_proj, value_proj, outgate_proj, rank_proj, decay_proj, decay_bias, head_gain, out_proj, norm_ffn, gate_proj, up_proj, down_proj = weights
    normed = low(rms_scale(inputs, low(norm_attn)))
    query_matrix = low_back(product(normed, low(query_proj)))
    key_matrix = low_back(product(normed, low(key_proj)))
    value_matrix = low_back(product(normed, low(value_proj)))
    outgate_rows = low_back(product(normed, low(outgate_proj)))
    rank_rows = low_back(product(normed, low(rank_proj)))
    gated = low(mixer(query_matrix, key_matrix, value_matrix, outgate_rows, rank_rows, low(decay_proj), low(decay_bias), low(head_gain)))
    attn = low_back(product(gated, low(out_proj)))
    middle = inputs + attn
    normed_ffn = low(rms_scale(middle, low(norm_ffn)))
    gate_rows = low_back(product(normed_ffn, low(gate_proj)))
    up_rows = low_back(product(normed_ffn, low(up_proj)))
    hidden = low(jax.nn.silu(gate_rows) * up_rows)
    ffn = low_back(product(hidden, low(down_proj)))
    return mask[:, None] * (middle + ffn)

def reference(tokens, lengths, norm_attn, query_proj, key_proj, value_proj, outgate_proj, rank_proj, decay_proj, decay_bias, head_gain, out_proj, norm_ffn, gate_proj, up_proj, down_proj, cotangent):
    weights = (norm_attn, query_proj, key_proj, value_proj, outgate_proj, rank_proj, decay_proj, decay_bias, head_gain, out_proj, norm_ffn, gate_proj, up_proj, down_proj)
    inputs_all = tokens.astype(jnp.float32).reshape(SLOTS, SEQ_LEN, D)
    cotangent_all = cotangent.astype(jnp.float32).reshape(SLOTS, SEQ_LEN, D)
    positions = jnp.arange(SEQ_LEN, dtype=jnp.int32)

    def one_slot(totals, item):
        inputs_slot, cotangent_slot, live = item
        mask = (positions < live).astype(jnp.float32)

        def apply(inputs_in, weights_in):
            return layer(inputs_in, weights_in, mask)
        result, pull = jax.vjp(apply, inputs_slot, weights)
        grad_inputs, grad_weights = pull(cotangent_slot)
        totals = jax.tree.map(jnp.add, totals, grad_weights)
        return (totals, (result.astype(jnp.bfloat16), grad_inputs.astype(jnp.bfloat16)))
    start = jax.tree.map(jnp.zeros_like, weights)
    totals, (results, grad_inputs) = lax.scan(one_slot, start, (inputs_all, cotangent_all, lengths))
    return (results.reshape(TOKENS, D), grad_inputs.reshape(TOKENS, D), totals[0], totals[1], totals[2], totals[3], totals[4], totals[5], totals[6], totals[7], totals[8], totals[9], totals[10], totals[11], totals[12], totals[13])
```

```python
import jax
import jax.numpy as jnp
from jax import lax
from jax.experimental import pallas as pl
from jax.experimental.pallas import tpu as pltpu
from jax.sharding import PartitionSpec as P

SEQ_LEN = 1024
LINE = 4

norm_eps = 1e-06
head_eps = 1.0
highest_precision = lax.Precision.HIGHEST
half = jnp.bfloat16
f32 = jnp.float32
CHUNK = 128


def level_count():
    return CHUNK.bit_length() - 1


def span_matrix():
    rows = lax.broadcasted_iota(jnp.int32, (CHUNK, CHUNK), 0)
    cols = lax.broadcasted_iota(jnp.int32, (CHUNK, CHUNK), 1)
    parts = []
    for level in range(level_count()):
        size = 1 << level
        middle = (rows // (2 * size)) * (2 * size) + size
        right = rows >= middle
        parts.append(
            jnp.where(right, (cols >= middle) & (cols <= rows), (cols > rows) & (cols < middle))
        )
    parts.append(cols <= rows)
    parts.append(cols > rows)
    stacked = jnp.concatenate(parts, axis=0).astype(half)
    return jnp.concatenate([stacked, stacked], axis=1)


def dot(left, right, dims):
    return lax.dot_general(left, right, (dims, ((), ())), preferred_element_type=f32)


NN = ((1,), (0,))
NT = ((1,), (1,))
TN = ((0,), (0,))


def log_decay(pre):
    return (jnp.minimum(pre, 0.0) - jnp.log1p(jnp.exp(-jnp.abs(pre)))) * (1.0 / 16.0)


def split_two(values):
    high = values.astype(half)
    low = (values - high.astype(f32)).astype(half)
    return jnp.concatenate([high, low], axis=0)


def level_parts(level):
    rows = lax.broadcasted_iota(jnp.int32, (CHUNK, CHUNK), 0)
    cols = lax.broadcasted_iota(jnp.int32, (CHUNK, CHUNK), 1)
    return rows, cols, (lax.shift_right_logical(rows ^ cols, level) == 1)


def forward_body(pre_ref, q_ref, k_ref, v_ref, span_ref, mixed_ref, score_ref, state_ref, state):
    @pl.when(pl.program_id(0) == 0)
    def _():
        state[...] = jnp.zeros_like(state)

    decay = log_decay(pre_ref[...])
    sums = dot(span_ref[...], split_two(decay), NN)
    q = q_ref[...]
    k = k_ref[...]
    v = v_ref[...]
    q32 = q.astype(f32)
    k32 = k.astype(f32)
    rows, cols, _ = level_parts(0)
    scores = jnp.where(rows == cols, dot(q, k, NT), 0.0)
    row_ids = lax.broadcasted_iota(jnp.int32, q.shape, 0)
    for level in range(level_count()):
        right = (lax.shift_right_logical(row_ids, level) & 1) == 1
        grow = jnp.exp(sums[level * CHUNK : (level + 1) * CHUNK])
        mixed_rows = (jnp.where(right, q32, k32) * grow).astype(half)
        pair = level_parts(level)[2] & (rows > cols)
        scores = jnp.where(pair, dot(mixed_rows, mixed_rows, NT), scores)
    levels = level_count()
    head_sum = sums[levels * CHUNK : (levels + 1) * CHUNK]
    tail_sum = sums[(levels + 1) * CHUNK :]
    q_in = (q32 * jnp.exp(head_sum)).astype(half)
    k_out = (k32 * jnp.exp(tail_sum)).astype(half)
    score_half = scores.astype(half)
    state_now = state[...]
    state_half = state_now.astype(half)
    mixed_ref[...] = (dot(score_half, v, NN) + dot(q_in, state_half, NN)).astype(mixed_ref.dtype)
    score_ref[...] = score_half
    state_ref[0] = state_half
    whole = jnp.exp(jnp.transpose(head_sum[CHUNK - 8 :, :]))[:, 7:8]
    state[...] = whole * state_now + dot(k_out, v, TN)


def backward_body(
    pre_ref, q_ref, k_ref, v_ref, d_ref, score_ref, state_ref, span_ref,
    dqkv_ref, dpre_ref, carry,
):
    @pl.when(pl.program_id(0) == 0)
    def _():
        carry[...] = jnp.zeros_like(carry)

    levels = level_count()
    pre = pre_ref[...]
    decay = log_decay(pre)
    sums = dot(span_ref[...], split_two(decay), NN)
    q = q_ref[...]
    k = k_ref[...]
    v = v_ref[...]
    d_mixed = d_ref[...]
    q32 = q.astype(f32)
    k32 = k.astype(f32)
    scores = score_ref[...]
    state_half = state_ref[0]
    carry_now = carry[...]
    carry_half = carry_now.astype(half)
    rows, cols, _ = level_parts(0)
    row_ids = lax.broadcasted_iota(jnp.int32, q.shape, 0)
    d_scores = dot(d_mixed, v, NT)
    diagonal = jnp.where(rows == cols, d_scores, 0.0)
    sym = jnp.where(rows > cols, d_scores, jnp.transpose(d_scores))
    diag_col = jnp.sum(diagonal, axis=1, keepdims=True)
    dq = diag_col * k32
    dk = diag_col * q32
    pieces = []
    for level in range(levels):
        right = (lax.shift_right_logical(row_ids, level) & 1) == 1
        grow = jnp.exp(sums[level * CHUNK : (level + 1) * CHUNK])
        scaled = jnp.where(right, q32, k32) * grow
        block = jnp.where(level_parts(level)[2], sym, 0.0).astype(half)
        back = dot(block, scaled.astype(half), NN)
        pieces.append((scaled * back).astype(half))
        grown = grow * back
        dq = dq + jnp.where(right, grown, 0.0)
        dk = dk + jnp.where(right, 0.0, grown)
    head_sum = sums[levels * CHUNK : (levels + 1) * CHUNK]
    tail_sum = sums[(levels + 1) * CHUNK :]
    head_grow = jnp.exp(head_sum)
    tail_grow = jnp.exp(tail_sum)
    q_in = q32 * head_grow
    k_out = k32 * tail_grow
    k_out_half = k_out.astype(half)
    back_q = dot(d_mixed, state_half, NT)
    back_k = dot(v, carry_half, NT)
    pieces.append((q_in * back_q).astype(half))
    pieces.append((k_out * back_k).astype(half))
    dq = dq + head_grow * back_q
    dk = dk + tail_grow * back_k
    wide = q.shape[1]
    dqkv_ref[:, :wide] = dq.astype(half)
    dqkv_ref[:, wide : 2 * wide] = dk.astype(half)
    dqkv_ref[:, 2 * wide :] = (
        dot(scores, d_mixed, TN) + dot(k_out_half, carry_half, NN)
    ).astype(half)
    whole = jnp.exp(jnp.transpose(head_sum[CHUNK - 8 :, :]))[:, 7:8]
    end_col = whole * jnp.sum(state_half.astype(f32) * carry_now, axis=1, keepdims=True)
    end_row = jnp.transpose(jnp.broadcast_to(end_col, (end_col.shape[0], 128)))[0:1, :]
    d_decay = dot(span_ref[:, :CHUNK], jnp.concatenate(pieces, axis=0), TN) + end_row
    dpre_ref[...] = d_decay * (jax.nn.sigmoid(-pre) * (1.0 / 16.0))
    carry[...] = whole * carry_now + dot(q_in.astype(half), d_mixed, TN)


def recur_forward(pre, qkv, span, dk, dv):
    length = qkv.shape[0]
    count = length // CHUNK

    def row(wide, place=0):
        return pl.BlockSpec((CHUNK, wide), lambda i: (i, place))

    return pl.pallas_call(
        forward_body,
        grid=(count,),
        in_specs=[
            row(dk), row(dk, 0), row(dk, 1), row(dv, 2 * dk // dv),
            pl.BlockSpec(span.shape, lambda i: (0, 0)),
        ],
        out_specs=[row(dv), row(CHUNK), pl.BlockSpec((1, dk, dv), lambda i: (i, 0, 0))],
        out_shape=[
            jax.ShapeDtypeStruct((length, dv), half),
            jax.ShapeDtypeStruct((length, CHUNK), half),
            jax.ShapeDtypeStruct((count, dk, dv), half),
        ],
        scratch_shapes=[pltpu.VMEM((dk, dv), f32)],
        compiler_params=pltpu.CompilerParams(dimension_semantics=("arbitrary",)),
        cost_estimate=pl.CostEstimate(
            flops=6 * 10**9, bytes_accessed=8 * 2**20, transcendentals=2 * 2**20
        ),
        name="recur_forward",
    )(pre, qkv, qkv, qkv, span)


def recur_backward(pre, qkv, d_mixed, scores, states, span, dk, dv):
    length = qkv.shape[0]
    count = length // CHUNK

    def row(wide, place=0):
        return pl.BlockSpec((CHUNK, wide), lambda i: (count - 1 - i, place))

    return pl.pallas_call(
        backward_body,
        grid=(count,),
        in_specs=[
            row(dk), row(dk, 0), row(dk, 1), row(dv, 2 * dk // dv), row(dv), row(CHUNK),
            pl.BlockSpec((1, dk, dv), lambda i: (count - 1 - i, 0, 0)),
            pl.BlockSpec(span.shape, lambda i: (0, 0)),
        ],
        out_specs=[row(2 * dk + dv), row(dk)],
        out_shape=[
            jax.ShapeDtypeStruct((length, 2 * dk + dv), half),
            jax.ShapeDtypeStruct((length, dk), f32),
        ],
        scratch_shapes=[pltpu.VMEM((dk, dv), f32)],
        compiler_params=pltpu.CompilerParams(dimension_semantics=("arbitrary",)),
        cost_estimate=pl.CostEstimate(
            flops=8 * 10**9, bytes_accessed=10 * 2**20, transcendentals=2 * 2**20
        ),
        name="recur_backward",
    )(pre, qkv, qkv, qkv, d_mixed, scores, states, span)

MESH = pl.DeviceIdType.MESH
BULK = 13
PIECES = 4


class Links:
    def __init__(self, send, recv, local):
        place = lax.axis_index("dp")
        self.z = place // 2
        self.x = place % 2
        self.t = lax.axis_index("tensor")
        self.core = self.t % 2
        self.send, self.recv, self.local = send, recv, local
        self.count = 0
        self.local_count = 0

    def take(self, number=1):
        first = self.count
        self.count += number
        return first

    def take_local(self, number=1):
        first = self.local_count
        self.local_count += number
        return first

    def beside(self):
        return {"dp": self.z * 2 + 1 - self.x}

    def up(self):
        return {"dp": self.z * 2 + 2 + self.x}

    def down(self):
        return {"dp": self.z * 2 - 2 + self.x}

    def partner(self):
        return {"tensor": self.t + 1 - 2 * self.core}

    def across(self):
        return {"tensor": (self.t + 2) % 4}

    def greet(self):
        barrier = pltpu.get_barrier_semaphore()
        around = [{"dp": ((self.z + step) % LINE) * 2 + self.x} for step in (1, 3)]
        for other in (*around, self.beside(), self.partner(), self.across()):
            pl.semaphore_signal(barrier, inc=1, device_id=other, device_id_type=MESH)
        pl.semaphore_wait(barrier, 5)

    def copy(self, index, src, dst, target):
        return pltpu.make_async_remote_copy(
            src_ref=src,
            dst_ref=dst,
            send_sem=self.send.at[index],
            recv_sem=self.recv.at[index],
            device_id=target,
            device_id_type=MESH,
        )

    def arrived(self, index, dst):
        self.copy(index, dst, dst, self.beside()).wait_recv()

    def sent(self, index, src):
        self.copy(index, src, src, self.beside()).wait_send()


class Gather:
    SEMS = 26

    def __init__(self, links, shard, full):
        self.links, self.shard, self.full = links, shard, full
        self.rows = shard.shape[0]
        self.bulk = self.rows * BULK // 16
        self.base = links.take(self.SEMS)
        self.own_sem = links.take_local()
        self.pending = []

    def at(self, z, x, rest):
        first = (z * 2 + x) * self.rows + (self.bulk if rest else 0)
        return self.full.at[pl.ds(first, self.rows - self.bulk if rest else self.bulk), :]

    def mine(self, rest):
        if rest:
            return self.shard.at[pl.ds(self.bulk, self.rows - self.bulk), :]
        return self.shard.at[pl.ds(0, self.bulk), :]

    def go(self, index, src, dst, target, when=None):
        links = self.links

        def start():
            links.copy(self.base + index, src, dst, target).start()

        if when is None:
            start()
        else:
            pl.when(when)(start)
        self.pending.append((index, src, when))

    def start(self):
        links = self.links
        z, x = links.z, links.x
        keep = self.full.at[pl.ds((z * 2 + x) * self.rows, self.rows), :]
        self.keep = pltpu.make_async_copy(self.shard, keep, links.local.at[self.own_sem])
        self.keep.start()
        self.go(0, self.mine(False), self.at(z, x, False), links.up(), z < 3)
        self.go(3, self.mine(False), self.at(z, x, False), links.down(), z > 0)
        self.go(13, self.mine(True), self.at(z, x, True), links.beside())
        self.go(6, self.mine(False), self.at(z, x, False), links.beside())

    def bulk_step(self, k):
        links = self.links
        z, x = links.z, links.x
        for side, base, cross, target, more in (
            (-k, 0, 7, links.up(), z < 3),
            (k, 3, 10, links.down(), z > 0),
        ):
            there = z + side
            valid = there >= 0 if side < 0 else there <= 3
            piece = self.at(there, x, False)

            @pl.when(valid)
            def _():
                links.arrived(self.base + base + k - 1, piece)

            if k < 3:
                self.go(base + k, piece, piece, target, valid & more)
            self.go(cross + k - 1, piece, piece, links.beside(), valid)

    def rest_start(self):
        links = self.links
        z, x = links.z, links.x
        other = self.at(z, 1 - x, True)
        links.arrived(self.base + 13, other)
        mine = self.mine(True)
        for index, src, dst in ((14, mine, self.at(z, x, True)), (15, other, other)):
            self.go(index, src, dst, links.up(), z < 3)
            self.go(index + 6, src, dst, links.down(), z > 0)

    def rest_step(self, k):
        links = self.links
        z, x = links.z, links.x
        for side, base, target, more in (
            (-k, 14, links.up(), z < 3),
            (k, 20, links.down(), z > 0),
        ):
            there = z + side
            valid = there >= 0 if side < 0 else there <= 3
            for which in range(2):
                piece = self.at(there, x if which == 0 else 1 - x, True)

                @pl.when(valid)
                def _():
                    links.arrived(self.base + base + 2 * (k - 1) + which, piece)

                if k < 3:
                    self.go(base + 2 * k + which, piece, piece, target, valid & more)

    def finish(self):
        links = self.links
        z, x = links.z, links.x
        links.arrived(self.base + 6, self.at(z, 1 - x, False))
        for k in (1, 2, 3):
            for side, cross in ((-k, 7), (k, 10)):
                there = z + side
                valid = there >= 0 if side < 0 else there <= 3

                @pl.when(valid)
                def _():
                    links.arrived(self.base + cross + k - 1, self.at(there, 1 - x, False))

        for index, src, when in self.pending:

            def done():
                links.sent(self.base + index, src)

            if when is None:
                done()
            else:
                pl.when(when)(done)
        self.keep.wait()


def add_rows(out, outs_at, terms, rows):
    def body(i, carry):
        tile = pl.ds(pl.multiple_of(i * 16, 16), 16)
        value = terms[0][tile, :].astype(f32)
        for term in terms[1:]:
            value = value + term[tile, :].astype(f32)
        out[pl.ds(pl.multiple_of(outs_at + i * 16, 16), 16), :] = value.astype(out.dtype)
        return carry

    lax.fori_loop(0, rows // 16, body, 0)


ORDER = ((3, 3, 0, 0), (2, 0, 3, 1), (1, 2, 1, 2), (0, 1, 2, 3))


class Scatter:
    SEMS = 15

    def __init__(self, links, total, own, buffers):
        self.links, self.total, self.own = links, total, own
        self.beside, self.kept, self.passed, self.kept2, self.passed2, self.last = buffers
        self.rows = total.shape[0] // (2 * LINE)
        self.bulk = self.rows * BULK // 16
        self.rest = self.rows - self.bulk
        self.base = links.take(self.SEMS)
        self.loads = links.take_local(12)
        low, high = links.z % 2, links.z // 2
        self.order = []
        for c in ORDER:
            self.order.append(
                c[0] + (c[1] - c[0]) * low + (c[2] - c[0]) * high
                + (c[3] - c[1] - c[2] + c[0]) * low * high
            )

    @staticmethod
    def scratch(rows, n):
        bulk = rows * BULK // 16
        rest = rows - bulk
        return [
            pltpu.VMEM((LINE, bulk, n), half),
            pltpu.VMEM((LINE, bulk, n), half),
            pltpu.VMEM((LINE + 1, bulk, n), half),
            pltpu.VMEM((LINE, 2 * rest, n), half),
            pltpu.VMEM((LINE + 1, 2 * rest, n), half),
            pltpu.VMEM((rest, n), half),
        ]

    def block(self, z, x, rest):
        first = (z * 2 + x) * self.rows + (self.bulk if rest else 0)
        return self.total.at[pl.ds(first, self.rest if rest else self.bulk), :]

    def load(self, k, part):
        links = self.links
        d = self.order[k]
        if part == 2:
            src, dst = self.block(d, links.x, False), self.kept.at[k]
        else:
            src = self.block(d, part, True)
            dst = self.kept2.at[k, pl.ds(part * self.rest, self.rest), :]
        return pltpu.make_async_copy(src, dst, links.local.at[self.loads + 3 * k + part])

    def start(self):
        links = self.links
        for k in range(LINE):
            for part in range(3):
                self.load(k, part).start()
        for k in range(LINE):
            src = self.block(self.order[k], 1 - links.x, False)
            links.copy(self.base + k, src, self.beside.at[k], links.beside()).start()

    def step(self, k, rest):
        links = self.links
        z = links.z
        d = self.order[k]
        if rest:
            kept, passed, rows, first = self.kept2.at[k], self.passed2, 2 * self.rest, self.base + 9
            self.load(k, 0).wait()
            self.load(k, 1).wait()
            terms = [kept]
        else:
            kept, passed, rows, first = self.kept.at[k], self.passed, self.bulk, self.base + 4
            self.load(k, 2).wait()
            links.arrived(self.base + k, self.beside.at[k])
            terms = [kept, self.beside.at[k]]
        upward = d > z
        carried = (upward & (z > 0)) | ((d < z) & (z < 3))

        @pl.when(carried)
        def _():
            links.arrived(first + d, passed.at[d])
            add_rows(kept, 0, terms + [passed.at[d]], rows)

        if not rest:

            @pl.when(jnp.logical_not(carried))
            def _():
                add_rows(kept, 0, terms, rows)

        @pl.when(upward)
        def _():
            links.copy(first + d, kept, passed.at[d], links.up()).start()

        @pl.when((d < z) & (d < z - 1))
        def _():
            links.copy(first + d, kept, passed.at[d], links.down()).start()

        @pl.when((d < z) & (d == z - 1))
        def _():
            links.copy(first + LINE, kept, passed.at[LINE], links.down()).start()

    def close(self, rest):
        links = self.links
        z, x = links.z, links.x
        k = LINE - 1
        if rest:
            kept, passed, rows, first = self.kept2.at[k], self.passed2, 2 * self.rest, self.base + 9
            self.load(k, 0).wait()
            self.load(k, 1).wait()
            terms, out = [kept], kept
        else:
            kept, passed, rows, first = self.kept.at[k], self.passed, self.bulk, self.base + 4
            self.load(k, 2).wait()
            links.arrived(self.base + k, self.beside.at[k])
            terms, out = [kept, self.beside.at[k]], self.own

        @pl.when(z > 0)
        def _():
            links.arrived(first + z, passed.at[z])

        @pl.when(z < 3)
        def _():
            links.arrived(first + LINE, passed.at[LINE])

        @pl.when(z == 0)
        def _():
            add_rows(out, 0, terms + [passed.at[LINE]], rows)

        @pl.when(z == 3)
        def _():
            add_rows(out, 0, terms + [passed.at[z]], rows)

        @pl.when((z > 0) & (z < 3))
        def _():
            add_rows(out, 0, terms + [passed.at[z], passed.at[LINE]], rows)

        if rest:
            away = kept.at[pl.ds((1 - x) * self.rest, self.rest), :]
            links.copy(self.base + 14, away, self.last, links.beside()).start()

    def finish(self):
        links = self.links
        z, x = links.z, links.x
        links.arrived(self.base + 14, self.last)
        mine = self.kept2.at[LINE - 1, pl.ds(x * self.rest, self.rest), :]
        add_rows(self.own, self.bulk, [mine, self.last], self.rest)
        links.sent(self.base + 14, self.last)
        for k in range(LINE):
            links.sent(self.base + k, self.beside.at[k])
        for k in range(LINE - 1):
            d = self.order[k]
            for kept, first in ((self.kept.at[k], self.base + 4), (self.kept2.at[k], self.base + 9)):

                @pl.when((d > z) | (d < z - 1))
                def _():
                    links.sent(first + d, kept)

                @pl.when(d == z - 1)
                def _():
                    links.sent(first + LINE, kept)


class Total:
    SEMS = 3 * PIECES

    def __init__(self, links, part, out, buffers):
        self.links, self.part, self.out = links, part, out
        self.mine, self.first, self.second = buffers
        self.rows = part.shape[0] // 2 // PIECES
        self.base = links.take(self.SEMS)
        self.loads = links.take_local(2 * PIECES)

    @staticmethod
    def scratch(rows, n):
        return [pltpu.VMEM((PIECES, rows // 2 // PIECES, n), half) for _ in range(3)]

    def at(self, ref, core, j):
        return ref.at[pl.ds((core * PIECES + j) * self.rows, self.rows), :]

    def load(self, j):
        src = self.at(self.part, self.links.core, j)
        return pltpu.make_async_copy(src, self.mine.at[j], self.links.local.at[self.loads + j])

    def store(self, j):
        dst = self.at(self.out, self.links.core, j)
        sem = self.links.local.at[self.loads + PIECES + j]
        return pltpu.make_async_copy(self.first.at[j], dst, sem)

    def start(self):
        links = self.links
        for j in range(PIECES):
            self.load(j).start()
            src = self.at(self.part, 1 - links.core, j)
            links.copy(self.base + j, src, self.first.at[j], links.partner()).start()

    def middle(self):
        links = self.links
        for j in range(PIECES):
            self.load(j).wait()
            links.arrived(self.base + j, self.first.at[j])
            add_rows(self.mine.at[j], 0, [self.mine.at[j], self.first.at[j]], self.rows)
            index = self.base + PIECES + j
            links.copy(index, self.mine.at[j], self.second.at[j], links.across()).start()

    def spread(self):
        links = self.links
        for j in range(PIECES):
            links.arrived(self.base + PIECES + j, self.second.at[j])
            add_rows(self.first.at[j], 0, [self.mine.at[j], self.second.at[j]], self.rows)
            index = self.base + 2 * PIECES + j
            dst = self.at(self.out, links.core, j)
            links.copy(index, self.first.at[j], dst, links.partner()).start()
            self.store(j).start()

    def finish(self):
        links = self.links
        for j in range(PIECES):
            links.arrived(self.base + 2 * PIECES + j, self.at(self.out, 1 - links.core, j))
            self.store(j).wait()
            for stage in range(3):
                links.sent(self.base + stage * PIECES + j, self.mine.at[j])


def exchange(number, shards=(), totals=(), parts=()):
    gathers, scatters, sums = len(shards), len(totals), len(parts)
    scratch = []
    for total in totals:
        scratch += Scatter.scratch(total.shape[0] // (2 * LINE), total.shape[1])
    for part in parts:
        scratch += Total.scratch(part.shape[0], part.shape[1])
    remote = Gather.SEMS * gathers + Scatter.SEMS * scatters + Total.SEMS * sums
    near = gathers + 12 * scatters + 2 * PIECES * sums
    scratch += [
        pltpu.SemaphoreType.DMA((remote,)),
        pltpu.SemaphoreType.DMA((remote,)),
        pltpu.SemaphoreType.DMA((near,)),
    ]

    def kernel(*refs):
        refs = list(refs)

        def pop(count):
            taken, refs[:count] = refs[:count], []
            return taken

        shard_refs, total_refs, part_refs = pop(gathers), pop(scatters), pop(sums)
        full_refs, own_refs, sum_refs = pop(gathers), pop(scatters), pop(sums)
        buffers = [pop(6) for _ in range(scatters)]
        sum_buffers = [pop(3) for _ in range(sums)]
        links = Links(*refs)
        gather = [Gather(links, s, f) for s, f in zip(shard_refs, full_refs)]
        scatter = [Scatter(links, *a) for a in zip(total_refs, own_refs, buffers)]
        total = [Total(links, *a) for a in zip(part_refs, sum_refs, sum_buffers)]
        links.greet()
        for item in gather + scatter + total:
            item.start()
        for item in total:
            item.middle()
        for k in range(LINE - 1):
            for item in scatter:
                item.step(k, True)
        for item in scatter:
            item.close(True)
        for item in gather:
            item.bulk_step(1)
        for item in gather:
            item.rest_start()
        for item in scatter:
            item.step(0, False)
        for item in gather:
            item.bulk_step(2)
        for item in gather:
            item.rest_step(1)
        for item in scatter:
            item.step(1, False)
        for item in gather:
            item.bulk_step(3)
        for item in scatter:
            item.step(2, False)
        for item in total:
            item.spread()
        for item in gather:
            item.rest_step(2)
        for item in scatter:
            item.close(False)
        for item in gather:
            item.rest_step(3)
        for item in gather + scatter + total:
            item.finish()

    whole = pl.BlockSpec(memory_space=pl.ANY)
    near_spec = pl.BlockSpec(memory_space=pltpu.VMEM)
    outs = pl.pallas_call(
        kernel,
        in_specs=[near_spec] * gathers + [whole] * (scatters + sums),
        out_specs=[whole] * gathers + [near_spec] * scatters + [whole] * sums,
        out_shape=[
            jax.ShapeDtypeStruct((s.shape[0] * 2 * LINE, s.shape[1]), half) for s in shards
        ]
        + [jax.ShapeDtypeStruct((t.shape[0] // (2 * LINE), t.shape[1]), f32) for t in totals]
        + [jax.ShapeDtypeStruct(p.shape, half) for p in parts],
        scratch_shapes=scratch,
        compiler_params=pltpu.CompilerParams(
            collective_id=number, has_side_effects=True, vmem_limit_bytes=60 * 2**20
        ),
        name=f"exchange_{number}",
    )(*shards, *totals, *parts)
    return outs[:gathers], outs[gathers : gathers + scatters], outs[gathers + scatters :]


class Ring:
    def __init__(self, size):
        self.size = size
        self.wide = size // LINE
        place = lax.axis_index("dp")
        self.z = place // self.wide
        self.x = place % self.wide

    def z_pairs(self, step):
        wide = self.wide
        return [
            (z * wide + x, ((z + step) % LINE) * wide + x) for z in range(LINE) for x in range(wide)
        ]

    def x_pairs(self, step):
        wide = self.wide
        return [(z * wide + x, z * wide + (x + step) % wide) for z in range(LINE) for x in range(wide)]


def gather(ring, shard):
    rows = shard.shape[0]
    pieces = [(ring.z, shard)]
    for step in (1, 3, 2):
        pieces.append(((ring.z - step) % LINE, lax.ppermute(shard, "dp", ring.z_pairs(step))))
    out = jnp.zeros((ring.size * rows, shard.shape[1]), shard.dtype)
    for z, piece in pieces:
        for step in range(ring.wide):
            moved = lax.ppermute(piece, "dp", ring.x_pairs(step)) if step else piece
            place = z * ring.wide + (ring.x - step) % ring.wide
            out = lax.dynamic_update_slice(out, moved, (place * rows, 0))
    return out


def scatter(ring, total):
    rows = total.shape[0] // ring.size

    def block(z, x):
        place = (z % LINE) * ring.wide + x % ring.wide
        return lax.dynamic_slice(total, (place * rows, 0), (rows, total.shape[1]))

    result = None
    for step in (2, 1, 3, 0):
        z = ring.z + step
        kept = block(z, ring.x).astype(f32)
        for side in range(1, ring.wide):
            away = lax.ppermute(block(z, ring.x + side), "dp", ring.x_pairs(side))
            kept = kept + away.astype(f32)
        if step:
            kept = lax.ppermute(kept.astype(half), "dp", ring.z_pairs(step)).astype(f32)
        result = kept if result is None else result + kept
    return result


CORE = [(i, i ^ 1) for i in range(4)]
ACROSS = [(i, i ^ 2) for i in range(4)]


def tensor_sum(part):
    rows = part.shape[0] // 2
    second = (lax.axis_index("tensor") & 1) == 1
    upper, lower = part[:rows], part[rows:]
    mine = jnp.where(second, lower, upper)
    away = jnp.where(second, upper, lower)
    mine = (mine.astype(f32) + lax.ppermute(away, "tensor", CORE).astype(f32)).astype(half)
    mine = (mine.astype(f32) + lax.ppermute(mine, "tensor", ACROSS).astype(f32)).astype(half)
    theirs = lax.ppermute(mine, "tensor", CORE)
    return jnp.concatenate(
        [jnp.where(second, theirs, mine), jnp.where(second, mine, theirs)], axis=0
    )


def rms_parts(values):
    scale = lax.rsqrt(jnp.mean(values * values, axis=-1, keepdims=True) + norm_eps)
    return values * scale, scale


def rms_back(unit, scale, gain, cot):
    weighted = cot * gain
    inner = jnp.mean(weighted * unit, axis=-1, keepdims=True)
    return scale * (weighted - unit * inner), jnp.sum(cot * unit, axis=0)


def gated_rows(mixed, outgate, gain):
    scale = lax.rsqrt(jnp.mean(mixed * mixed, axis=-1, keepdims=True) + head_eps)
    return mixed * scale * gain * jax.nn.silu(outgate)


def local(
    tokens, lengths, norm_attn, query_proj, key_proj, value_proj, outgate_proj, rank_proj,
    decay_proj, decay_bias, head_gain, out_proj, norm_ffn, gate_proj, up_proj, down_proj, cotangent,
    *, size,
):
    ring = Ring(size)
    rows_total = tokens.shape[0]
    width = norm_attn.shape[0]
    rank = rank_proj.shape[1]
    dk = query_proj.shape[1]
    dv = value_proj.shape[1]
    ff = gate_proj.shape[1]
    bits = decay_proj.shape[2]
    gains = head_gain.shape[0]

    def as_column(values):
        flat = values.reshape(-1, 1)
        return jnp.pad(flat, ((0, width - flat.shape[0]), (0, 0)))

    decay_cols = rank * bits // width
    small = jnp.concatenate(
        [
            rank_proj,
            norm_attn[:, None],
            norm_ffn[:, None],
            as_column(head_gain),
            as_column(decay_bias),
            decay_proj.reshape(decay_cols, width).T,
        ],
        axis=1,
    )
    small = jnp.pad(small, ((0, 0), (0, 128 - small.shape[1]))).astype(half)
    qkv = jnp.concatenate([query_proj * 0.0625, key_proj, value_proj], axis=1).astype(half)
    first = (qkv, small, outgate_proj.astype(half), out_proj.T.astype(half))
    second = (gate_proj.astype(half), up_proj.astype(half), down_proj.T.astype(half))
    fast = size == 2 * LINE

    def collect(number, shards, parts):
        if fast:
            fulls, _, sums = exchange(number, shards, (), parts)
            return fulls, sums
        return [gather(ring, s) for s in shards], [tensor_sum(p) for p in parts]

    def deliver(number, totals, parts):
        if fast:
            _, owns, sums = exchange(number, (), totals, parts)
            return owns, sums
        return [scatter(ring, t) for t in totals], [tensor_sum(p) for p in parts]

    (qkv_full, small_full, outgate_full, out_full), _ = collect(0, first, ())
    rank_full = small_full[:, :rank]
    small32 = small_full.astype(f32)
    gain_attn = small32[:, rank]
    gain_ffn = small32[:, rank + 1]
    by_place = small32.reshape(size, width, 128)
    gain_head = by_place[:, :gains, rank + 2].reshape(-1)
    bias = by_place[:, :bits, rank + 3].reshape(-1)
    decay_weight = jnp.transpose(
        jnp.transpose(by_place[:, :, rank + 4 : rank + 4 + decay_cols], (0, 2, 1)).reshape(
            size, rank, bits
        ),
        (1, 0, 2),
    ).reshape(rank, -1)

    positions = jnp.arange(SEQ_LEN, dtype=jnp.int32)
    mask = (positions[None, :] < lengths[:, None]).astype(f32).reshape(rows_total, 1)
    tokens32 = tokens.astype(f32)
    unit, scale = rms_parts(tokens32)
    normed = (unit * gain_attn).astype(half)
    qkv = dot(normed, qkv_full, NN).astype(half)
    rank_rows = dot(normed, rank_full, NN)
    pre = (
        jnp.dot(rank_rows, decay_weight, precision=highest_precision, preferred_element_type=f32)
        + bias
    )
    span = span_matrix()
    mixed, scores, states = recur_forward(pre, qkv, span, dk, dv)
    outgate = dot(normed, outgate_full, NN).astype(half)
    gated, pull_gated = jax.vjp(gated_rows, mixed.astype(f32), outgate.astype(f32), gain_head)
    gated = gated.astype(half)
    (gate_full, up_full, down_full), (attn,) = collect(
        1, second, (dot(gated, out_full, NT).astype(half),)
    )
    middle = tokens32 + attn.astype(f32)
    unit_ffn, scale_ffn = rms_parts(middle)
    normed_ffn = (unit_ffn * gain_ffn).astype(half)
    gate_rows = dot(normed_ffn, gate_full, NN)
    up_rows = dot(normed_ffn, up_full, NN)
    hidden, pull_glu = jax.vjp(lambda g, u: jax.nn.silu(g) * u, gate_rows, up_rows)
    hidden = hidden.astype(half)
    d_out = cotangent.astype(f32) * mask
    d_out_half = d_out.astype(half)
    grad_down = dot(d_out_half, hidden, TN).astype(half)
    d_gate, d_up = pull_glu(dot(d_out_half, down_full, NN))
    d_gate = d_gate.astype(half)
    d_up = d_up.astype(half)
    d_normed_ffn = (dot(d_gate, gate_full, NT) + dot(d_up, up_full, NT)).astype(half)
    grad_gate = dot(normed_ffn, d_gate, TN).astype(half)
    grad_up = dot(normed_ffn, d_up, TN).astype(half)
    ffn = dot(hidden, down_full, NT).astype(half)
    (down_own, gate_own, up_own), (d_normed_ffn, ffn) = deliver(
        2, (grad_down, grad_gate, grad_up), (d_normed_ffn, ffn)
    )
    output = (mask * (middle + ffn.astype(f32))).astype(half)
    d_back, grad_gain_ffn = rms_back(unit_ffn, scale_ffn, gain_ffn, d_normed_ffn.astype(f32))
    d_middle = d_out + d_back
    d_attn = d_middle.astype(half)
    grad_out = dot(d_attn, gated, TN).astype(half)
    d_mixed, d_outgate, grad_head = pull_gated(dot(d_attn, out_full, NN))
    d_outgate = d_outgate.astype(half)
    grad_outgate = dot(normed, d_outgate, TN).astype(half)
    d_qkv, d_pre = recur_backward(pre, qkv, d_mixed.astype(half), scores, states, span, dk, dv)
    d_rank = dot(d_pre.astype(half), decay_weight.astype(half), NT).astype(half)
    d_normed = (
        dot(d_qkv, qkv_full, NT) + dot(d_outgate, outgate_full, NT) + dot(d_rank, rank_full, NT)
    )
    grad_gain_attn = jnp.sum(d_normed * unit, axis=0)
    d_normed = d_normed.astype(half)
    grad_qkv = dot(normed, d_qkv, TN).astype(half)
    grad_rank = dot(normed, d_rank, TN)
    grad_decay = jnp.transpose(
        dot(rank_rows.astype(half), d_pre.astype(half), TN).reshape(rank, size, bits), (1, 0, 2)
    ).reshape(size, decay_cols, width)

    def spread(values):
        blocks = values.reshape(size, -1, 1)
        return jnp.pad(blocks, ((0, 0), (0, width - blocks.shape[1]), (0, 0)))

    grad_small = jnp.concatenate(
        [
            grad_rank.reshape(size, width, rank),
            grad_gain_attn.reshape(size, width, 1),
            grad_gain_ffn.reshape(size, width, 1),
            spread(grad_head),
            spread(jnp.sum(d_pre, axis=0)),
            jnp.transpose(grad_decay, (0, 2, 1)),
        ],
        axis=2,
    )
    grad_small = jnp.pad(grad_small, ((0, 0), (0, 0), (0, 128 - grad_small.shape[2])))
    grad_small = grad_small.reshape(size * width, 128).astype(half)

    (out_own, outgate_own, qkv_own, small_own), (d_normed,) = deliver(
        3, (grad_out, grad_outgate, grad_qkv, grad_small), (d_normed,)
    )
    d_back, _ = rms_back(unit, scale, gain_attn, d_normed.astype(f32))
    grad_tokens = (d_middle + d_back).astype(half)
    heads_own = small_own.astype(half)
    heads_own = heads_own.astype(f32) + lax.ppermute(heads_own, "tensor", CORE).astype(f32)
    heads_own = heads_own.astype(half)
    heads_own = heads_own.astype(f32) + lax.ppermute(heads_own, "tensor", ACROSS).astype(f32)
    return (
        output,
        grad_tokens,
        heads_own[:, rank],
        qkv_own[:, :dk] * 0.0625,
        qkv_own[:, dk : 2 * dk],
        qkv_own[:, 2 * dk : 2 * dk + dv],
        outgate_own,
        heads_own[:, :rank],
        small_own[:, rank + 4 : rank + 4 + decay_cols].T.reshape(decay_proj.shape),
        small_own[:bits, rank + 3].reshape(decay_bias.shape),
        heads_own[:gains, rank + 2],
        out_own.T,
        heads_own[:, rank + 1] * 0.25,
        gate_own,
        up_own,
        down_own.T,
    )


def solution(mesh):
    size = mesh.shape["dp"]

    def run(*args):
        return local(*args, size=size)

    weight = P("dp", "tensor")
    cross = P("tensor", "dp")
    return jax.shard_map(
        run,
        mesh=mesh,
        in_specs=(
            P("dp", None), P("dp"), P("dp"), weight, weight, weight, weight, P("dp", None),
            P(None, "tensor", "dp"), cross, P("dp"), cross, P("dp"), weight, weight, cross,
            P("dp", None),
        ),
        out_specs=(
            P("dp", None), P("dp", None), P("dp"), weight, weight, weight, weight, P("dp", None),
            P(None, "tensor", "dp"), cross, P("dp"), cross, P("dp"), weight, weight, cross,
        ),
        check_vma=False,
    )
```

```python
import jax
import jax.numpy as jnp
from jax import lax
from jax.experimental import pallas as pl
from jax.experimental.pallas import tpu as pltpu
from jax.sharding import PartitionSpec as P

SEQ_LEN = 1024
LINE = 4

norm_eps = 1e-06
head_eps = 1.0
highest_precision = lax.Precision.HIGHEST
half = jnp.bfloat16
f32 = jnp.float32
CHUNK = 128


def level_count():
    return CHUNK.bit_length() - 1


def span_matrix():
    rows = lax.broadcasted_iota(jnp.int32, (CHUNK, CHUNK), 0)
    cols = lax.broadcasted_iota(jnp.int32, (CHUNK, CHUNK), 1)
    parts = []
    for level in range(level_count()):
        size = 1 << level
        middle = (rows // (2 * size)) * (2 * size) + size
        right = rows >= middle
        parts.append(
            jnp.where(right, (cols >= middle) & (cols <= rows), (cols > rows) & (cols < middle))
        )
    parts.append(cols <= rows)
    parts.append(cols > rows)
    stacked = jnp.concatenate(parts, axis=0).astype(half)
    return jnp.concatenate([stacked, stacked], axis=1)


def dot(left, right, dims):
    return lax.dot_general(left, right, (dims, ((), ())), preferred_element_type=f32)


NN = ((1,), (0,))
NT = ((1,), (1,))
TN = ((0,), (0,))


def log_decay(pre):
    return (jnp.minimum(pre, 0.0) - jnp.log1p(jnp.exp(-jnp.abs(pre)))) * (1.0 / 16.0)


def split_two(values):
    high = values.astype(half)
    low = (values - high.astype(f32)).astype(half)
    return jnp.concatenate([high, low], axis=0)


def level_parts(level):
    rows = lax.broadcasted_iota(jnp.int32, (CHUNK, CHUNK), 0)
    cols = lax.broadcasted_iota(jnp.int32, (CHUNK, CHUNK), 1)
    return rows, cols, (lax.shift_right_logical(rows ^ cols, level) == 1)


def forward_body(pre_ref, q_ref, k_ref, v_ref, span_ref, mixed_ref, score_ref, state_ref, state):
    @pl.when(pl.program_id(0) == 0)
    def _():
        state[...] = jnp.zeros_like(state)

    decay = log_decay(pre_ref[...])
    sums = dot(span_ref[...], split_two(decay), NN)
    q = q_ref[...]
    k = k_ref[...]
    v = v_ref[...]
    q32 = q.astype(f32)
    k32 = k.astype(f32)
    rows, cols, _ = level_parts(0)
    scores = jnp.where(rows == cols, dot(q, k, NT), 0.0)
    row_ids = lax.broadcasted_iota(jnp.int32, q.shape, 0)
    for level in range(level_count()):
        right = (lax.shift_right_logical(row_ids, level) & 1) == 1
        grow = jnp.exp(sums[level * CHUNK : (level + 1) * CHUNK])
        mixed_rows = (jnp.where(right, q32, k32) * grow).astype(half)
        pair = level_parts(level)[2] & (rows > cols)
        scores = jnp.where(pair, dot(mixed_rows, mixed_rows, NT), scores)
    levels = level_count()
    head_sum = sums[levels * CHUNK : (levels + 1) * CHUNK]
    tail_sum = sums[(levels + 1) * CHUNK :]
    q_in = (q32 * jnp.exp(head_sum)).astype(half)
    k_out = (k32 * jnp.exp(tail_sum)).astype(half)
    score_half = scores.astype(half)
    state_now = state[...]
    state_half = state_now.astype(half)
    mixed_ref[...] = (dot(score_half, v, NN) + dot(q_in, state_half, NN)).astype(mixed_ref.dtype)
    score_ref[...] = score_half
    state_ref[0] = state_half
    whole = jnp.exp(jnp.transpose(head_sum[CHUNK - 8 :, :]))[:, 7:8]
    state[...] = whole * state_now + dot(k_out, v, TN)


def backward_math(pre, q, k, v, d_mixed, scores, state_half, span_ref, carry):
    levels = level_count()
    decay = log_decay(pre)
    sums = dot(span_ref[...], split_two(decay), NN)
    q32 = q.astype(f32)
    k32 = k.astype(f32)
    carry_now = carry[...]
    carry_half = carry_now.astype(half)
    rows, cols, _ = level_parts(0)
    row_ids = lax.broadcasted_iota(jnp.int32, q.shape, 0)
    d_scores = dot(d_mixed, v, NT)
    diagonal = jnp.where(rows == cols, d_scores, 0.0)
    sym = jnp.where(rows > cols, d_scores, jnp.transpose(d_scores))
    diag_col = jnp.sum(diagonal, axis=1, keepdims=True)
    dq = diag_col * k32
    dk = diag_col * q32
    pieces = []
    for level in range(levels):
        right = (lax.shift_right_logical(row_ids, level) & 1) == 1
        grow = jnp.exp(sums[level * CHUNK : (level + 1) * CHUNK])
        scaled = jnp.where(right, q32, k32) * grow
        block = jnp.where(level_parts(level)[2], sym, 0.0).astype(half)
        back = dot(block, scaled.astype(half), NN)
        pieces.append((scaled * back).astype(half))
        grown = grow * back
        dq = dq + jnp.where(right, grown, 0.0)
        dk = dk + jnp.where(right, 0.0, grown)
    head_sum = sums[levels * CHUNK : (levels + 1) * CHUNK]
    tail_sum = sums[(levels + 1) * CHUNK :]
    head_grow = jnp.exp(head_sum)
    tail_grow = jnp.exp(tail_sum)
    q_in = q32 * head_grow
    k_out = k32 * tail_grow
    k_out_half = k_out.astype(half)
    back_q = dot(d_mixed, state_half, NT)
    back_k = dot(v, carry_half, NT)
    pieces.append((q_in * back_q).astype(half))
    pieces.append((k_out * back_k).astype(half))
    dq = dq + head_grow * back_q
    dk = dk + tail_grow * back_k
    dv = dot(scores, d_mixed, TN) + dot(k_out_half, carry_half, NN)
    d_qkv = jnp.concatenate([dq.astype(half), dk.astype(half), dv.astype(half)], axis=1)
    whole = jnp.exp(jnp.transpose(head_sum[CHUNK - 8 :, :]))[:, 7:8]
    end_col = whole * jnp.sum(state_half.astype(f32) * carry_now, axis=1, keepdims=True)
    end_row = jnp.transpose(jnp.broadcast_to(end_col, (end_col.shape[0], 128)))[0:1, :]
    d_decay = dot(span_ref[:, :CHUNK], jnp.concatenate(pieces, axis=0), TN) + end_row
    carry[...] = whole * carry_now + dot(q_in.astype(half), d_mixed, TN)
    return d_qkv, d_decay * (jax.nn.sigmoid(-pre) * (1.0 / 16.0))


def backward_body(
    pre_ref, q_ref, k_ref, v_ref, d_ref, score_ref, state_ref, span_ref,
    dqkv_ref, dpre_ref, carry,
):
    @pl.when(pl.program_id(0) == 0)
    def _():
        carry[...] = jnp.zeros_like(carry)

    dqkv_ref[...], dpre_ref[...] = backward_math(
        pre_ref[...], q_ref[...], k_ref[...], v_ref[...], d_ref[...], score_ref[...],
        state_ref[0], span_ref, carry,
    )


def recur_forward(pre, qkv, span, dk, dv):
    length = qkv.shape[0]
    count = length // CHUNK

    def row(wide, place=0):
        return pl.BlockSpec((CHUNK, wide), lambda i: (i, place))

    return pl.pallas_call(
        forward_body,
        grid=(count,),
        in_specs=[
            row(dk), row(dk, 0), row(dk, 1), row(dv, 2 * dk // dv),
            pl.BlockSpec(span.shape, lambda i: (0, 0)),
        ],
        out_specs=[row(dv), row(CHUNK), pl.BlockSpec((1, dk, dv), lambda i: (i, 0, 0))],
        out_shape=[
            jax.ShapeDtypeStruct((length, dv), half),
            jax.ShapeDtypeStruct((length, CHUNK), half),
            jax.ShapeDtypeStruct((count, dk, dv), half),
        ],
        scratch_shapes=[pltpu.VMEM((dk, dv), f32)],
        compiler_params=pltpu.CompilerParams(dimension_semantics=("arbitrary",)),
        cost_estimate=pl.CostEstimate(
            flops=6 * 10**9, bytes_accessed=8 * 2**20, transcendentals=2 * 2**20
        ),
        name="recur_forward",
    )(pre, qkv, qkv, qkv, span)


def recur_backward(pre, qkv, d_mixed, scores, states, span, dk, dv):
    length = qkv.shape[0]
    count = length // CHUNK

    def row(wide, place=0):
        return pl.BlockSpec((CHUNK, wide), lambda i: (count - 1 - i, place))

    return pl.pallas_call(
        backward_body,
        grid=(count,),
        in_specs=[
            row(dk), row(dk, 0), row(dk, 1), row(dv, 2 * dk // dv), row(dv), row(CHUNK),
            pl.BlockSpec((1, dk, dv), lambda i: (count - 1 - i, 0, 0)),
            pl.BlockSpec(span.shape, lambda i: (0, 0)),
        ],
        out_specs=[row(2 * dk + dv), row(dk)],
        out_shape=[
            jax.ShapeDtypeStruct((length, 2 * dk + dv), half),
            jax.ShapeDtypeStruct((length, dk), f32),
        ],
        scratch_shapes=[pltpu.VMEM((dk, dv), f32)],
        compiler_params=pltpu.CompilerParams(dimension_semantics=("arbitrary",)),
        cost_estimate=pl.CostEstimate(
            flops=8 * 10**9, bytes_accessed=10 * 2**20, transcendentals=2 * 2**20
        ),
        name="recur_backward",
    )(pre, qkv, qkv, qkv, d_mixed, scores, states, span)

MESH = pl.DeviceIdType.MESH
BULK = 13
PIECES = 4


class Links:
    def __init__(self, send, recv, local):
        place = lax.axis_index("dp")
        self.z = place // 2
        self.x = place % 2
        self.t = lax.axis_index("tensor")
        self.core = self.t % 2
        self.send, self.recv, self.local = send, recv, local
        self.count = 0
        self.local_count = 0

    def take(self, number=1):
        first = self.count
        self.count += number
        return first

    def take_local(self, number=1):
        first = self.local_count
        self.local_count += number
        return first

    def beside(self):
        return {"dp": self.z * 2 + 1 - self.x}

    def up(self):
        return {"dp": self.z * 2 + 2 + self.x}

    def down(self):
        return {"dp": self.z * 2 - 2 + self.x}

    def partner(self):
        return {"tensor": self.t + 1 - 2 * self.core}

    def across(self):
        return {"tensor": (self.t + 2) % 4}

    def greet(self):
        barrier = pltpu.get_barrier_semaphore()
        around = [{"dp": ((self.z + step) % LINE) * 2 + self.x} for step in (1, 3)]
        for other in (*around, self.beside(), self.partner(), self.across()):
            pl.semaphore_signal(barrier, inc=1, device_id=other, device_id_type=MESH)
        pl.semaphore_wait(barrier, 5)

    def copy(self, index, src, dst, target):
        return pltpu.make_async_remote_copy(
            src_ref=src,
            dst_ref=dst,
            send_sem=self.send.at[index],
            recv_sem=self.recv.at[index],
            device_id=target,
            device_id_type=MESH,
        )

    def arrived(self, index, dst):
        self.copy(index, dst, dst, self.beside()).wait_recv()

    def sent(self, index, src):
        self.copy(index, src, src, self.beside()).wait_send()


class Gather:
    SEMS = 26

    def __init__(self, links, shard, full):
        self.links, self.shard, self.full = links, shard, full
        self.rows = shard.shape[0]
        self.bulk = self.rows * BULK // 16
        self.base = links.take(self.SEMS)
        self.own_sem = links.take_local()
        self.pending = []

    def at(self, z, x, rest):
        first = (z * 2 + x) * self.rows + (self.bulk if rest else 0)
        return self.full.at[pl.ds(first, self.rows - self.bulk if rest else self.bulk), :]

    def mine(self, rest):
        if rest:
            return self.shard.at[pl.ds(self.bulk, self.rows - self.bulk), :]
        return self.shard.at[pl.ds(0, self.bulk), :]

    def go(self, index, src, dst, target, when=None):
        links = self.links

        def start():
            links.copy(self.base + index, src, dst, target).start()

        if when is None:
            start()
        else:
            pl.when(when)(start)
        self.pending.append((index, src, when))

    def start(self):
        links = self.links
        z, x = links.z, links.x
        keep = self.full.at[pl.ds((z * 2 + x) * self.rows, self.rows), :]
        self.keep = pltpu.make_async_copy(self.shard, keep, links.local.at[self.own_sem])
        self.keep.start()
        self.go(0, self.mine(False), self.at(z, x, False), links.up(), z < 3)
        self.go(3, self.mine(False), self.at(z, x, False), links.down(), z > 0)
        self.go(13, self.mine(True), self.at(z, x, True), links.beside())
        self.go(6, self.mine(False), self.at(z, x, False), links.beside())

    def bulk_step(self, k):
        links = self.links
        z, x = links.z, links.x
        for side, base, cross, target, more in (
            (-k, 0, 7, links.up(), z < 3),
            (k, 3, 10, links.down(), z > 0),
        ):
            there = z + side
            valid = there >= 0 if side < 0 else there <= 3
            piece = self.at(there, x, False)

            @pl.when(valid)
            def _():
                links.arrived(self.base + base + k - 1, piece)

            if k < 3:
                self.go(base + k, piece, piece, target, valid & more)
            self.go(cross + k - 1, piece, piece, links.beside(), valid)

    def rest_start(self):
        links = self.links
        z, x = links.z, links.x
        other = self.at(z, 1 - x, True)
        links.arrived(self.base + 13, other)
        mine = self.mine(True)
        for index, src, dst in ((14, mine, self.at(z, x, True)), (15, other, other)):
            self.go(index, src, dst, links.up(), z < 3)
            self.go(index + 6, src, dst, links.down(), z > 0)

    def rest_step(self, k):
        links = self.links
        z, x = links.z, links.x
        for side, base, target, more in (
            (-k, 14, links.up(), z < 3),
            (k, 20, links.down(), z > 0),
        ):
            there = z + side
            valid = there >= 0 if side < 0 else there <= 3
            for which in range(2):
                piece = self.at(there, x if which == 0 else 1 - x, True)

                @pl.when(valid)
                def _():
                    links.arrived(self.base + base + 2 * (k - 1) + which, piece)

                if k < 3:
                    self.go(base + 2 * k + which, piece, piece, target, valid & more)

    def finish(self):
        links = self.links
        z, x = links.z, links.x
        links.arrived(self.base + 6, self.at(z, 1 - x, False))
        for k in (1, 2, 3):
            for side, cross in ((-k, 7), (k, 10)):
                there = z + side
                valid = there >= 0 if side < 0 else there <= 3

                @pl.when(valid)
                def _():
                    links.arrived(self.base + cross + k - 1, self.at(there, 1 - x, False))

        for index, src, when in self.pending:

            def done():
                links.sent(self.base + index, src)

            if when is None:
                done()
            else:
                pl.when(when)(done)
        self.keep.wait()


def add_rows(out, outs_at, terms, rows):
    def body(i, carry):
        tile = pl.ds(pl.multiple_of(i * 16, 16), 16)
        value = terms[0][tile, :].astype(f32)
        for term in terms[1:]:
            value = value + term[tile, :].astype(f32)
        out[pl.ds(pl.multiple_of(outs_at + i * 16, 16), 16), :] = value.astype(out.dtype)
        return carry

    lax.fori_loop(0, rows // 16, body, 0)


ORDER = ((3, 3, 0, 0), (2, 0, 3, 1), (1, 2, 1, 2), (0, 1, 2, 3))


class Scatter:
    SEMS = 15

    def __init__(self, links, total, own, buffers):
        self.links, self.total, self.own = links, total, own
        self.beside, self.kept, self.passed, self.kept2, self.passed2, self.last = buffers
        self.rows = total.shape[0] // (2 * LINE)
        self.bulk = self.rows * BULK // 16
        self.rest = self.rows - self.bulk
        self.base = links.take(self.SEMS)
        self.loads = links.take_local(12)
        low, high = links.z % 2, links.z // 2
        self.order = []
        for c in ORDER:
            self.order.append(
                c[0] + (c[1] - c[0]) * low + (c[2] - c[0]) * high
                + (c[3] - c[1] - c[2] + c[0]) * low * high
            )

    @staticmethod
    def scratch(rows, n):
        bulk = rows * BULK // 16
        rest = rows - bulk
        return [
            pltpu.VMEM((LINE, bulk, n), half),
            pltpu.VMEM((LINE, bulk, n), half),
            pltpu.VMEM((LINE + 1, bulk, n), half),
            pltpu.VMEM((LINE, 2 * rest, n), half),
            pltpu.VMEM((LINE + 1, 2 * rest, n), half),
            pltpu.VMEM((rest, n), half),
        ]

    def block(self, z, x, rest):
        first = (z * 2 + x) * self.rows + (self.bulk if rest else 0)
        return self.total.at[pl.ds(first, self.rest if rest else self.bulk), :]

    def load(self, k, part):
        links = self.links
        d = self.order[k]
        if part == 2:
            src, dst = self.block(d, links.x, False), self.kept.at[k]
        else:
            src = self.block(d, part, True)
            dst = self.kept2.at[k, pl.ds(part * self.rest, self.rest), :]
        return pltpu.make_async_copy(src, dst, links.local.at[self.loads + 3 * k + part])

    def start(self):
        links = self.links
        for k in range(LINE):
            for part in range(3):
                self.load(k, part).start()
        for k in range(LINE):
            src = self.block(self.order[k], 1 - links.x, False)
            links.copy(self.base + k, src, self.beside.at[k], links.beside()).start()

    def step(self, k, rest):
        links = self.links
        z = links.z
        d = self.order[k]
        if rest:
            kept, passed, rows, first = self.kept2.at[k], self.passed2, 2 * self.rest, self.base + 9
            self.load(k, 0).wait()
            self.load(k, 1).wait()
            terms = [kept]
        else:
            kept, passed, rows, first = self.kept.at[k], self.passed, self.bulk, self.base + 4
            self.load(k, 2).wait()
            links.arrived(self.base + k, self.beside.at[k])
            terms = [kept, self.beside.at[k]]
        upward = d > z
        carried = (upward & (z > 0)) | ((d < z) & (z < 3))

        @pl.when(carried)
        def _():
            links.arrived(first + d, passed.at[d])
            add_rows(kept, 0, terms + [passed.at[d]], rows)

        if not rest:

            @pl.when(jnp.logical_not(carried))
            def _():
                add_rows(kept, 0, terms, rows)

        @pl.when(upward)
        def _():
            links.copy(first + d, kept, passed.at[d], links.up()).start()

        @pl.when((d < z) & (d < z - 1))
        def _():
            links.copy(first + d, kept, passed.at[d], links.down()).start()

        @pl.when((d < z) & (d == z - 1))
        def _():
            links.copy(first + LINE, kept, passed.at[LINE], links.down()).start()

    def close(self, rest):
        links = self.links
        z, x = links.z, links.x
        k = LINE - 1
        if rest:
            kept, passed, rows, first = self.kept2.at[k], self.passed2, 2 * self.rest, self.base + 9
            self.load(k, 0).wait()
            self.load(k, 1).wait()
            terms, out = [kept], kept
        else:
            kept, passed, rows, first = self.kept.at[k], self.passed, self.bulk, self.base + 4
            self.load(k, 2).wait()
            links.arrived(self.base + k, self.beside.at[k])
            terms, out = [kept, self.beside.at[k]], self.own

        @pl.when(z > 0)
        def _():
            links.arrived(first + z, passed.at[z])

        @pl.when(z < 3)
        def _():
            links.arrived(first + LINE, passed.at[LINE])

        @pl.when(z == 0)
        def _():
            add_rows(out, 0, terms + [passed.at[LINE]], rows)

        @pl.when(z == 3)
        def _():
            add_rows(out, 0, terms + [passed.at[z]], rows)

        @pl.when((z > 0) & (z < 3))
        def _():
            add_rows(out, 0, terms + [passed.at[z], passed.at[LINE]], rows)

        if rest:
            away = kept.at[pl.ds((1 - x) * self.rest, self.rest), :]
            links.copy(self.base + 14, away, self.last, links.beside()).start()

    def finish(self):
        links = self.links
        z, x = links.z, links.x
        links.arrived(self.base + 14, self.last)
        mine = self.kept2.at[LINE - 1, pl.ds(x * self.rest, self.rest), :]
        add_rows(self.own, self.bulk, [mine, self.last], self.rest)
        links.sent(self.base + 14, self.last)
        for k in range(LINE):
            links.sent(self.base + k, self.beside.at[k])
        for k in range(LINE - 1):
            d = self.order[k]
            for kept, first in ((self.kept.at[k], self.base + 4), (self.kept2.at[k], self.base + 9)):

                @pl.when((d > z) | (d < z - 1))
                def _():
                    links.sent(first + d, kept)

                @pl.when(d == z - 1)
                def _():
                    links.sent(first + LINE, kept)


class Total:
    SEMS = 3 * PIECES

    def __init__(self, links, part, out, buffers):
        self.links, self.part, self.out = links, part, out
        self.mine, self.first, self.second = buffers
        self.rows = part.shape[0] // 2 // PIECES
        self.base = links.take(self.SEMS)
        self.loads = links.take_local(2 * PIECES)

    @staticmethod
    def scratch(rows, n):
        return [pltpu.VMEM((PIECES, rows // 2 // PIECES, n), half) for _ in range(3)]

    def at(self, ref, core, j):
        return ref.at[pl.ds((core * PIECES + j) * self.rows, self.rows), :]

    def load(self, j):
        src = self.at(self.part, self.links.core, j)
        return pltpu.make_async_copy(src, self.mine.at[j], self.links.local.at[self.loads + j])

    def store(self, j):
        dst = self.at(self.out, self.links.core, j)
        sem = self.links.local.at[self.loads + PIECES + j]
        return pltpu.make_async_copy(self.first.at[j], dst, sem)

    def start(self):
        links = self.links
        for j in range(PIECES):
            self.load(j).start()
            src = self.at(self.part, 1 - links.core, j)
            links.copy(self.base + j, src, self.first.at[j], links.partner()).start()

    def middle(self):
        links = self.links
        for j in range(PIECES):
            self.load(j).wait()
            links.arrived(self.base + j, self.first.at[j])
            add_rows(self.mine.at[j], 0, [self.mine.at[j], self.first.at[j]], self.rows)
            index = self.base + PIECES + j
            links.copy(index, self.mine.at[j], self.second.at[j], links.across()).start()

    def spread(self):
        links = self.links
        for j in range(PIECES):
            links.arrived(self.base + PIECES + j, self.second.at[j])
            add_rows(self.first.at[j], 0, [self.mine.at[j], self.second.at[j]], self.rows)
            index = self.base + 2 * PIECES + j
            dst = self.at(self.out, links.core, j)
            links.copy(index, self.first.at[j], dst, links.partner()).start()
            self.store(j).start()

    def landed(self):
        links = self.links
        for j in range(PIECES):
            links.arrived(self.base + 2 * PIECES + j, self.at(self.out, 1 - links.core, j))
            self.store(j).wait()

    def finish(self):
        links = self.links
        for j in range(PIECES):
            for stage in range(3):
                links.sent(self.base + stage * PIECES + j, self.mine.at[j])


def exchange(number, shards=(), totals=(), parts=()):
    gathers, scatters, sums = len(shards), len(totals), len(parts)
    scratch = []
    for total in totals:
        scratch += Scatter.scratch(total.shape[0] // (2 * LINE), total.shape[1])
    for part in parts:
        scratch += Total.scratch(part.shape[0], part.shape[1])
    remote = Gather.SEMS * gathers + Scatter.SEMS * scatters + Total.SEMS * sums
    near = gathers + 12 * scatters + 2 * PIECES * sums
    scratch += [
        pltpu.SemaphoreType.DMA((remote,)),
        pltpu.SemaphoreType.DMA((remote,)),
        pltpu.SemaphoreType.DMA((near,)),
    ]

    def kernel(*refs):
        refs = list(refs)

        def pop(count):
            taken, refs[:count] = refs[:count], []
            return taken

        shard_refs, total_refs, part_refs = pop(gathers), pop(scatters), pop(sums)
        full_refs, own_refs, sum_refs = pop(gathers), pop(scatters), pop(sums)
        buffers = [pop(6) for _ in range(scatters)]
        sum_buffers = [pop(3) for _ in range(sums)]
        links = Links(*refs)
        gather = [Gather(links, s, f) for s, f in zip(shard_refs, full_refs)]
        scatter = [Scatter(links, *a) for a in zip(total_refs, own_refs, buffers)]
        total = [Total(links, *a) for a in zip(part_refs, sum_refs, sum_buffers)]
        links.greet()
        for item in gather + scatter + total:
            item.start()
        for item in total:
            item.middle()
        for k in range(LINE - 1):
            for item in scatter:
                item.step(k, True)
        for item in scatter:
            item.close(True)
        for item in gather:
            item.bulk_step(1)
        for item in gather:
            item.rest_start()
        for item in scatter:
            item.step(0, False)
        for item in gather:
            item.bulk_step(2)
        for item in gather:
            item.rest_step(1)
        for item in scatter:
            item.step(1, False)
        for item in gather:
            item.bulk_step(3)
        for item in scatter:
            item.step(2, False)
        for item in total:
            item.spread()
        for item in gather:
            item.rest_step(2)
        for item in scatter:
            item.close(False)
        for item in gather:
            item.rest_step(3)
        for item in total:
            item.landed()
        for item in gather + scatter + total:
            item.finish()

    whole = pl.BlockSpec(memory_space=pl.ANY)
    near_spec = pl.BlockSpec(memory_space=pltpu.VMEM)
    outs = pl.pallas_call(
        kernel,
        in_specs=[near_spec] * gathers + [whole] * (scatters + sums),
        out_specs=[whole] * gathers + [near_spec] * scatters + [whole] * sums,
        out_shape=[
            jax.ShapeDtypeStruct((s.shape[0] * 2 * LINE, s.shape[1]), half) for s in shards
        ]
        + [jax.ShapeDtypeStruct((t.shape[0] // (2 * LINE), t.shape[1]), f32) for t in totals]
        + [jax.ShapeDtypeStruct(p.shape, half) for p in parts],
        scratch_shapes=scratch,
        compiler_params=pltpu.CompilerParams(
            collective_id=number, has_side_effects=True, vmem_limit_bytes=60 * 2**20
        ),
        name=f"exchange_{number}",
    )(*shards, *totals, *parts)
    return outs[:gathers], outs[gathers : gathers + scatters], outs[gathers + scatters :]


class Stream:
    def __init__(self, sems, base, arrays, buffers, index):
        self.sems, self.base, self.arrays, self.buffers, self.index = (
            sems, base, arrays, buffers, index,
        )

    def copies(self, i, inward):
        slot = i % 2
        for n, (array, buffer) in enumerate(zip(self.arrays, self.buffers)):
            rows = buffer.shape[1]
            first = pl.multiple_of(self.index(i) * rows, rows)
            far, near = array.at[pl.ds(first, rows), :], buffer.at[slot]
            sem = self.sems.at[self.base + 2 * n + slot]
            src, dst = (far, near) if inward else (near, far)
            yield pltpu.make_async_copy(src, dst, sem)

    def start(self, i, inward):
        for copy in self.copies(i, inward):
            copy.start()

    def wait(self, i, inward):
        for copy in self.copies(i, inward):
            copy.wait()


def row_sum(values):
    return jnp.sum(values, axis=0, keepdims=True)


def attention_back(tile, weights, gains, sums, carry):
    (cot, middle, d_out, tokens, qkv, mixed, outgate, pre, scores, state) = tile
    (w_out, w_qkv, w_gate, w_small, w_decay, span) = weights
    gain_ffn, gain_head = gains
    sum_ffn, sum_head, sum_bias, sum_attn = sums
    unit, scale = rms_parts(middle[...].astype(f32))
    cot = cot[...].astype(f32)
    sum_ffn[...] += row_sum(cot * unit)
    weighted = cot * gain_ffn[...]
    inner = jnp.mean(weighted * unit, axis=-1, keepdims=True)
    d_attn = (d_out[...].astype(f32) + scale * (weighted - unit * inner)).astype(half)
    d_gated = dot(d_attn, w_out[...], NN)
    rows = mixed[...].astype(f32)
    gate = outgate[...].astype(f32)
    head_scale = lax.rsqrt(jnp.mean(rows * rows, axis=-1, keepdims=True) + head_eps)
    head_unit = rows * head_scale
    sig = jax.nn.sigmoid(gate)
    d_outgate = (
        d_gated * head_unit * gain_head[...] * sig * (1.0 + gate * (1.0 - sig))
    ).astype(half)
    d_normed_head = d_gated * gate * sig
    sum_head[...] += row_sum(d_normed_head * head_unit)
    weighted = d_normed_head * gain_head[...]
    inner = jnp.mean(weighted * head_unit, axis=-1, keepdims=True)
    d_mixed = (head_scale * (weighted - head_unit * inner)).astype(half)
    dk = w_decay.shape[1]
    d_qkv, d_pre = backward_math(
        pre[...], qkv[:, :dk], qkv[:, dk : 2 * dk], qkv[:, 2 * dk :], d_mixed,
        scores[...], state[...], span, carry,
    )
    sum_bias[...] += row_sum(d_pre)
    d_pre = d_pre.astype(half)
    d_rank = dot(d_pre, w_decay[...], NT).astype(half)
    d_normed = (
        dot(d_qkv, w_qkv[...], NT) + dot(d_outgate, w_gate[...], NT) + dot(d_rank, w_small[...], NT)
    )
    unit, _ = rms_parts(tokens[...].astype(f32))
    sum_attn[...] += row_sum(d_normed * unit)
    return d_attn, d_outgate, d_qkv, d_pre, d_rank, d_normed.astype(half)


def backward_exchange(number, totals, part, rows_in, weights, gains):
    scatters = len(totals)
    length, width = part.shape
    count = length // CHUNK
    dk = weights[4].shape[1]
    dv = weights[0].shape[1]
    outs_wide = (width, dv, 2 * dk + dv, dk, 128, width)
    in_shapes = [(CHUNK, width)] + [(a.shape[0] // count, a.shape[1]) for a in rows_in]
    in_types = [half] + [a.dtype for a in rows_in]
    streams = len(in_shapes)
    sum_wide = (width, dv, dk, width)
    scratch = []
    for total in totals:
        scratch += Scatter.scratch(total.shape[0] // (2 * LINE), total.shape[1])
    scratch += Total.scratch(length, width)
    scratch += [pltpu.VMEM((2,) + s, t) for s, t in zip(in_shapes, in_types)]
    scratch += [pltpu.VMEM((2, CHUNK, w), half) for w in outs_wide]
    scratch += [pltpu.VMEM(w.shape, half) for w in weights]
    scratch += [pltpu.VMEM((dk, dv), f32)]
    remote = Scatter.SEMS * scatters + Total.SEMS
    near = 12 * scatters + 2 * PIECES
    extra = 2 * streams + 2 * len(outs_wide) + len(weights)
    scratch += [
        pltpu.SemaphoreType.DMA((remote,)),
        pltpu.SemaphoreType.DMA((remote,)),
        pltpu.SemaphoreType.DMA((near,)),
        pltpu.SemaphoreType.DMA((extra,)),
    ]

    def kernel(*refs):
        refs = list(refs)

        def pop(count):
            taken, refs[:count] = refs[:count], []
            return taken

        total_refs, (part_ref,), row_refs = pop(scatters), pop(1), pop(streams - 1)
        weight_refs, gain_refs = pop(len(weights)), pop(2)
        own_refs, (sum_ref,), out_refs, gain_sums = pop(scatters), pop(1), pop(6), pop(4)
        buffers = [pop(6) for _ in range(scatters)]
        sum_buffers = pop(3)
        in_buffers, out_buffers, near_weights = pop(streams), pop(6), pop(len(weights))
        (carry,) = pop(1)
        sems = refs.pop()
        links = Links(*refs)
        scatter = [Scatter(links, *a) for a in zip(total_refs, own_refs, buffers)]
        total = Total(links, part_ref, sum_ref, sum_buffers)
        inputs = Stream(sems, 0, [sum_ref] + row_refs, in_buffers, lambda i: count - 1 - i)
        outputs = Stream(sems, 2 * streams, out_refs, out_buffers, lambda i: count - 1 - i)
        loads = [
            pltpu.make_async_copy(far, close, sems.at[2 * streams + 12 + n])
            for n, (far, close) in enumerate(zip(weight_refs, near_weights))
        ]
        links.greet()
        for item in scatter:
            item.start()
        total.start()
        for load in loads:
            load.start()
        total.middle()
        for k in range(LINE - 1):
            for item in scatter:
                item.step(k, True)
        for item in scatter:
            item.close(True)
        for k in range(2):
            for item in scatter:
                item.step(k, False)
        total.spread()
        total.landed()
        for load in loads:
            load.wait()
        for ref in (*gain_sums, carry):
            ref[...] = jnp.zeros_like(ref)
        inputs.start(0, True)

        def body(i, state):
            @pl.when(i + 1 < count)
            def _():
                inputs.start(i + 1, True)

            inputs.wait(i, True)
            slot = i % 2
            results = attention_back(
                [b.at[slot] for b in in_buffers], near_weights, gain_refs, gain_sums, carry
            )

            @pl.when(i >= 2)
            def _():
                outputs.wait(i - 2, False)

            for buffer, value in zip(out_buffers, results):
                buffer[slot] = value
            outputs.start(i, False)

            @pl.when(i == 2)
            def _():
                for item in scatter:
                    item.step(2, False)

            @pl.when(i == 5)
            def _():
                for item in scatter:
                    item.close(False)

            return state

        lax.fori_loop(0, count, body, 0)
        outputs.wait(count - 2, False)
        outputs.wait(count - 1, False)
        for item in scatter:
            item.finish()
        total.finish()

    whole = pl.BlockSpec(memory_space=pl.ANY)
    near_spec = pl.BlockSpec(memory_space=pltpu.VMEM)
    outs = pl.pallas_call(
        kernel,
        in_specs=[whole] * (scatters + 1 + len(rows_in) + len(weights)) + [near_spec] * 2,
        out_specs=[near_spec] * scatters + [whole] * 7 + [near_spec] * 4,
        out_shape=[jax.ShapeDtypeStruct((t.shape[0] // (2 * LINE), t.shape[1]), f32) for t in totals]
        + [jax.ShapeDtypeStruct(part.shape, half)]
        + [jax.ShapeDtypeStruct((length, w), half) for w in outs_wide]
        + [jax.ShapeDtypeStruct((1, w), f32) for w in sum_wide],
        scratch_shapes=scratch,
        compiler_params=pltpu.CompilerParams(
            collective_id=number, has_side_effects=True, vmem_limit_bytes=62 * 2**20
        ),
        name=f"backward_exchange_{number}",
    )(*totals, part, *rows_in, *weights, *gains)
    return outs[:scatters], outs[scatters + 1 : scatters + 7], outs[scatters + 7 :]


class Ring:
    def __init__(self, size):
        self.size = size
        self.wide = size // LINE
        place = lax.axis_index("dp")
        self.z = place // self.wide
        self.x = place % self.wide

    def z_pairs(self, step):
        wide = self.wide
        return [
            (z * wide + x, ((z + step) % LINE) * wide + x) for z in range(LINE) for x in range(wide)
        ]

    def x_pairs(self, step):
        wide = self.wide
        return [(z * wide + x, z * wide + (x + step) % wide) for z in range(LINE) for x in range(wide)]


def gather(ring, shard):
    rows = shard.shape[0]
    pieces = [(ring.z, shard)]
    for step in (1, 3, 2):
        pieces.append(((ring.z - step) % LINE, lax.ppermute(shard, "dp", ring.z_pairs(step))))
    out = jnp.zeros((ring.size * rows, shard.shape[1]), shard.dtype)
    for z, piece in pieces:
        for step in range(ring.wide):
            moved = lax.ppermute(piece, "dp", ring.x_pairs(step)) if step else piece
            place = z * ring.wide + (ring.x - step) % ring.wide
            out = lax.dynamic_update_slice(out, moved, (place * rows, 0))
    return out


def scatter(ring, total):
    rows = total.shape[0] // ring.size

    def block(z, x):
        place = (z % LINE) * ring.wide + x % ring.wide
        return lax.dynamic_slice(total, (place * rows, 0), (rows, total.shape[1]))

    result = None
    for step in (2, 1, 3, 0):
        z = ring.z + step
        kept = block(z, ring.x).astype(f32)
        for side in range(1, ring.wide):
            away = lax.ppermute(block(z, ring.x + side), "dp", ring.x_pairs(side))
            kept = kept + away.astype(f32)
        if step:
            kept = lax.ppermute(kept.astype(half), "dp", ring.z_pairs(step)).astype(f32)
        result = kept if result is None else result + kept
    return result


CORE = [(i, i ^ 1) for i in range(4)]
ACROSS = [(i, i ^ 2) for i in range(4)]


def tensor_sum(part):
    rows = part.shape[0] // 2
    second = (lax.axis_index("tensor") & 1) == 1
    upper, lower = part[:rows], part[rows:]
    mine = jnp.where(second, lower, upper)
    away = jnp.where(second, upper, lower)
    mine = (mine.astype(f32) + lax.ppermute(away, "tensor", CORE).astype(f32)).astype(half)
    mine = (mine.astype(f32) + lax.ppermute(mine, "tensor", ACROSS).astype(f32)).astype(half)
    theirs = lax.ppermute(mine, "tensor", CORE)
    return jnp.concatenate(
        [jnp.where(second, theirs, mine), jnp.where(second, mine, theirs)], axis=0
    )


def rms_parts(values):
    scale = lax.rsqrt(jnp.mean(values * values, axis=-1, keepdims=True) + norm_eps)
    return values * scale, scale


def rms_back(unit, scale, gain, cot):
    weighted = cot * gain
    inner = jnp.mean(weighted * unit, axis=-1, keepdims=True)
    return scale * (weighted - unit * inner), jnp.sum(cot * unit, axis=0)


def gated_rows(mixed, outgate, gain):
    scale = lax.rsqrt(jnp.mean(mixed * mixed, axis=-1, keepdims=True) + head_eps)
    return mixed * scale * gain * jax.nn.silu(outgate)


def local(
    tokens, lengths, norm_attn, query_proj, key_proj, value_proj, outgate_proj, rank_proj,
    decay_proj, decay_bias, head_gain, out_proj, norm_ffn, gate_proj, up_proj, down_proj, cotangent,
    *, size,
):
    ring = Ring(size)
    rows_total = tokens.shape[0]
    width = norm_attn.shape[0]
    rank = rank_proj.shape[1]
    dk = query_proj.shape[1]
    dv = value_proj.shape[1]
    ff = gate_proj.shape[1]
    bits = decay_proj.shape[2]
    gains = head_gain.shape[0]

    def as_column(values):
        flat = values.reshape(-1, 1)
        return jnp.pad(flat, ((0, width - flat.shape[0]), (0, 0)))

    decay_cols = rank * bits // width
    small = jnp.concatenate(
        [
            rank_proj,
            norm_attn[:, None],
            norm_ffn[:, None],
            as_column(head_gain),
            as_column(decay_bias),
            decay_proj.reshape(decay_cols, width).T,
        ],
        axis=1,
    )
    small = jnp.pad(small, ((0, 0), (0, 128 - small.shape[1]))).astype(half)
    qkv = jnp.concatenate([query_proj * 0.0625, key_proj, value_proj], axis=1).astype(half)
    first = (qkv, small, outgate_proj.astype(half), out_proj.T.astype(half))
    second = (gate_proj.astype(half), up_proj.astype(half), down_proj.T.astype(half))
    fast = size == 2 * LINE

    def collect(number, shards, parts):
        if fast:
            fulls, _, sums = exchange(number, shards, (), parts)
            return fulls, sums
        return [gather(ring, s) for s in shards], [tensor_sum(p) for p in parts]

    def deliver(number, totals, parts):
        if fast:
            _, owns, sums = exchange(number, (), totals, parts)
            return owns, sums
        return [scatter(ring, t) for t in totals], [tensor_sum(p) for p in parts]

    (qkv_full, small_full, outgate_full, out_full), _ = collect(0, first, ())
    rank_full = small_full[:, :rank]
    small32 = small_full.astype(f32)
    gain_attn = small32[:, rank]
    gain_ffn = small32[:, rank + 1]
    by_place = small32.reshape(size, width, 128)
    gain_head = by_place[:, :gains, rank + 2].reshape(-1)
    bias = by_place[:, :bits, rank + 3].reshape(-1)
    decay_weight = jnp.transpose(
        jnp.transpose(by_place[:, :, rank + 4 : rank + 4 + decay_cols], (0, 2, 1)).reshape(
            size, rank, bits
        ),
        (1, 0, 2),
    ).reshape(rank, -1)

    positions = jnp.arange(SEQ_LEN, dtype=jnp.int32)
    mask = (positions[None, :] < lengths[:, None]).astype(f32).reshape(rows_total, 1)
    tokens32 = tokens.astype(f32)
    unit, scale = rms_parts(tokens32)
    normed = (unit * gain_attn).astype(half)
    qkv = dot(normed, qkv_full, NN).astype(half)
    rank_rows = dot(normed, rank_full, NN)
    pre = (
        jnp.dot(rank_rows, decay_weight, precision=highest_precision, preferred_element_type=f32)
        + bias
    )
    span = span_matrix()
    mixed, scores, states = recur_forward(pre, qkv, span, dk, dv)
    outgate = dot(normed, outgate_full, NN).astype(half)
    gated, pull_gated = jax.vjp(gated_rows, mixed.astype(f32), outgate.astype(f32), gain_head)
    gated = gated.astype(half)
    (gate_full, up_full, down_full), (attn,) = collect(
        1, second, (dot(gated, out_full, NT).astype(half),)
    )
    middle = tokens32 + attn.astype(f32)
    unit_ffn, scale_ffn = rms_parts(middle)
    normed_ffn = (unit_ffn * gain_ffn).astype(half)
    gate_rows = dot(normed_ffn, gate_full, NN)
    up_rows = dot(normed_ffn, up_full, NN)
    hidden, pull_glu = jax.vjp(lambda g, u: jax.nn.silu(g) * u, gate_rows, up_rows)
    hidden = hidden.astype(half)
    d_out = cotangent.astype(f32) * mask
    d_out_half = d_out.astype(half)
    grad_down = dot(d_out_half, hidden, TN).astype(half)
    d_gate, d_up = pull_glu(dot(d_out_half, down_full, NN))
    d_gate = d_gate.astype(half)
    d_up = d_up.astype(half)
    d_normed_ffn = (dot(d_gate, gate_full, NT) + dot(d_up, up_full, NT)).astype(half)
    grad_gate = dot(normed_ffn, d_gate, TN).astype(half)
    grad_up = dot(normed_ffn, d_up, TN).astype(half)
    ffn = dot(hidden, down_full, NT).astype(half)
    if fast:
        w_decay = jnp.pad(decay_weight, ((0, 128 - rank), (0, 0))).astype(half)
        (down_own, gate_own), outs, sums = backward_exchange(
            2,
            (grad_down, grad_gate),
            d_normed_ffn,
            (
                middle.astype(half), d_out_half, tokens, qkv, mixed, outgate, pre, scores,
                states.reshape(-1, dv),
            ),
            (out_full, qkv_full, outgate_full, small_full, w_decay, span),
            (gain_ffn[None, :], gain_head[None, :]),
        )
        d_attn, d_outgate, d_qkv, d_pre_half, d_rank, d_normed = outs
        grad_gain_ffn, grad_head, grad_bias, grad_gain_attn = sums
        d_middle = d_attn.astype(f32)
        d_rank = d_rank[:, :rank]
    else:
        d_normed_ffn = tensor_sum(d_normed_ffn)
        d_back, grad_gain_ffn = rms_back(unit_ffn, scale_ffn, gain_ffn, d_normed_ffn.astype(f32))
        d_middle = d_out + d_back
        d_attn = d_middle.astype(half)
        d_mixed, d_outgate, grad_head = pull_gated(dot(d_attn, out_full, NN))
        d_outgate = d_outgate.astype(half)
        d_qkv, d_pre = recur_backward(pre, qkv, d_mixed.astype(half), scores, states, span, dk, dv)
        d_rank = dot(d_pre.astype(half), decay_weight.astype(half), NT).astype(half)
        d_normed = (
            dot(d_qkv, qkv_full, NT) + dot(d_outgate, outgate_full, NT) + dot(d_rank, rank_full, NT)
        )
        grad_gain_attn = jnp.sum(d_normed * unit, axis=0)
        d_normed = d_normed.astype(half)
        d_pre_half = d_pre.astype(half)
        grad_bias = jnp.sum(d_pre, axis=0)
    grad_out = dot(d_attn, gated, TN).astype(half)
    grad_outgate = dot(normed, d_outgate, TN).astype(half)
    grad_qkv = dot(normed, d_qkv, TN).astype(half)
    grad_rank = dot(normed, d_rank, TN)
    grad_decay = jnp.transpose(
        dot(rank_rows.astype(half), d_pre_half, TN).reshape(rank, size, bits), (1, 0, 2)
    ).reshape(size, decay_cols, width)

    def spread(values):
        blocks = values.reshape(size, -1, 1)
        return jnp.pad(blocks, ((0, 0), (0, width - blocks.shape[1]), (0, 0)))

    grad_small = jnp.concatenate(
        [
            grad_rank.reshape(size, width, rank),
            grad_gain_attn.reshape(size, width, 1),
            grad_gain_ffn.reshape(size, width, 1),
            spread(grad_head),
            spread(grad_bias),
            jnp.transpose(grad_decay, (0, 2, 1)),
        ],
        axis=2,
    )
    grad_small = jnp.pad(grad_small, ((0, 0), (0, 0), (0, 128 - grad_small.shape[2])))
    grad_small = grad_small.reshape(size * width, 128).astype(half)

    if fast:
        waiting = (grad_up, grad_out, grad_outgate, grad_qkv, grad_small)
        (up_own, out_own, outgate_own, qkv_own, small_own), (d_normed, ffn) = deliver(
            3, waiting, (d_normed, ffn)
        )
    else:
        waiting = (
            grad_down, grad_gate, grad_up, grad_out, grad_outgate, grad_qkv, grad_small,
        )
        (down_own, gate_own, up_own, out_own, outgate_own, qkv_own, small_own), (
            d_normed, ffn,
        ) = deliver(3, waiting, (d_normed, ffn))
    output = (mask * (middle + ffn.astype(f32))).astype(half)
    d_back, _ = rms_back(unit, scale, gain_attn, d_normed.astype(f32))
    grad_tokens = (d_middle + d_back).astype(half)
    heads_own = small_own.astype(half)
    heads_own = heads_own.astype(f32) + lax.ppermute(heads_own, "tensor", CORE).astype(f32)
    heads_own = heads_own.astype(half)
    heads_own = heads_own.astype(f32) + lax.ppermute(heads_own, "tensor", ACROSS).astype(f32)
    return (
        output,
        grad_tokens,
        heads_own[:, rank],
        qkv_own[:, :dk] * 0.0625,
        qkv_own[:, dk : 2 * dk],
        qkv_own[:, 2 * dk : 2 * dk + dv],
        outgate_own,
        heads_own[:, :rank],
        small_own[:, rank + 4 : rank + 4 + decay_cols].T.reshape(decay_proj.shape),
        small_own[:bits, rank + 3].reshape(decay_bias.shape),
        heads_own[:gains, rank + 2],
        out_own.T,
        heads_own[:, rank + 1] * 0.25,
        gate_own,
        up_own,
        down_own.T,
    )


def solution(mesh):
    size = mesh.shape["dp"]

    def run(*args):
        return local(*args, size=size)

    weight = P("dp", "tensor")
    cross = P("tensor", "dp")
    return jax.shard_map(
        run,
        mesh=mesh,
        in_specs=(
            P("dp", None), P("dp"), P("dp"), weight, weight, weight, weight, P("dp", None),
            P(None, "tensor", "dp"), cross, P("dp"), cross, P("dp"), weight, weight, cross,
            P("dp", None),
        ),
        out_specs=(
            P("dp", None), P("dp", None), P("dp"), weight, weight, weight, weight, P("dp", None),
            P(None, "tensor", "dp"), cross, P("dp"), cross, P("dp"), weight, weight, cross,
        ),
        check_vma=False,
    )
```

```python
import jax
import jax.numpy as jnp
from jax import lax
from jax.experimental import pallas as pl
from jax.experimental.pallas import tpu as pltpu
from jax.sharding import PartitionSpec as P

SEQ_LEN = 1024
LINE = 4

norm_eps = 1e-06
head_eps = 1.0
highest_precision = lax.Precision.HIGHEST
half = jnp.bfloat16
f32 = jnp.float32
CHUNK = 128


def level_count():
    return CHUNK.bit_length() - 1


def span_matrix():
    rows = lax.broadcasted_iota(jnp.int32, (CHUNK, CHUNK), 0)
    cols = lax.broadcasted_iota(jnp.int32, (CHUNK, CHUNK), 1)
    parts = []
    for level in range(level_count()):
        size = 1 << level
        middle = (rows // (2 * size)) * (2 * size) + size
        right = rows >= middle
        parts.append(
            jnp.where(right, (cols >= middle) & (cols <= rows), (cols > rows) & (cols < middle))
        )
    parts.append(cols <= rows)
    parts.append(cols > rows)
    stacked = jnp.concatenate(parts, axis=0).astype(half)
    return jnp.concatenate([stacked, stacked], axis=1)


def dot(left, right, dims):
    return lax.dot_general(left, right, (dims, ((), ())), preferred_element_type=f32)


NN = ((1,), (0,))
NT = ((1,), (1,))
TN = ((0,), (0,))


def log_decay(pre):
    return (jnp.minimum(pre, 0.0) - jnp.log1p(jnp.exp(-jnp.abs(pre)))) * (1.0 / 16.0)


def split_two(values):
    high = values.astype(half)
    low = (values - high.astype(f32)).astype(half)
    return jnp.concatenate([high, low], axis=0)


def level_parts(level):
    rows = lax.broadcasted_iota(jnp.int32, (CHUNK, CHUNK), 0)
    cols = lax.broadcasted_iota(jnp.int32, (CHUNK, CHUNK), 1)
    return rows, cols, (lax.shift_right_logical(rows ^ cols, level) == 1)


def forward_body(pre_ref, q_ref, k_ref, v_ref, span_ref, mixed_ref, score_ref, state_ref, state):
    @pl.when(pl.program_id(0) == 0)
    def _():
        state[...] = jnp.zeros_like(state)

    decay = log_decay(pre_ref[...])
    sums = dot(span_ref[...], split_two(decay), NN)
    q = q_ref[...]
    k = k_ref[...]
    v = v_ref[...]
    q32 = q.astype(f32)
    k32 = k.astype(f32)
    rows, cols, _ = level_parts(0)
    scores = jnp.where(rows == cols, dot(q, k, NT), 0.0)
    row_ids = lax.broadcasted_iota(jnp.int32, q.shape, 0)
    for level in range(level_count()):
        right = (lax.shift_right_logical(row_ids, level) & 1) == 1
        grow = jnp.exp(sums[level * CHUNK : (level + 1) * CHUNK])
        mixed_rows = (jnp.where(right, q32, k32) * grow).astype(half)
        pair = level_parts(level)[2] & (rows > cols)
        scores = jnp.where(pair, dot(mixed_rows, mixed_rows, NT), scores)
    levels = level_count()
    head_sum = sums[levels * CHUNK : (levels + 1) * CHUNK]
    tail_sum = sums[(levels + 1) * CHUNK :]
    q_in = (q32 * jnp.exp(head_sum)).astype(half)
    k_out = (k32 * jnp.exp(tail_sum)).astype(half)
    score_half = scores.astype(half)
    state_now = state[...]
    state_half = state_now.astype(half)
    mixed_ref[...] = (dot(score_half, v, NN) + dot(q_in, state_half, NN)).astype(mixed_ref.dtype)
    score_ref[...] = score_half
    state_ref[0] = state_half
    whole = jnp.exp(jnp.transpose(head_sum[CHUNK - 8 :, :]))[:, 7:8]
    state[...] = whole * state_now + dot(k_out, v, TN)


def backward_math(pre, q, k, v, d_mixed, scores, state_half, span_ref, carry):
    levels = level_count()
    decay = log_decay(pre)
    sums = dot(span_ref[...], split_two(decay), NN)
    q32 = q.astype(f32)
    k32 = k.astype(f32)
    carry_now = carry[...]
    carry_half = carry_now.astype(half)
    rows, cols, _ = level_parts(0)
    row_ids = lax.broadcasted_iota(jnp.int32, q.shape, 0)
    d_scores = dot(d_mixed, v, NT)
    diagonal = jnp.where(rows == cols, d_scores, 0.0)
    sym = jnp.where(rows > cols, d_scores, jnp.transpose(d_scores))
    diag_col = jnp.sum(diagonal, axis=1, keepdims=True)
    dq = diag_col * k32
    dk = diag_col * q32
    pieces = []
    for level in range(levels):
        right = (lax.shift_right_logical(row_ids, level) & 1) == 1
        grow = jnp.exp(sums[level * CHUNK : (level + 1) * CHUNK])
        scaled = jnp.where(right, q32, k32) * grow
        block = jnp.where(level_parts(level)[2], sym, 0.0).astype(half)
        back = dot(block, scaled.astype(half), NN)
        pieces.append((scaled * back).astype(half))
        grown = grow * back
        dq = dq + jnp.where(right, grown, 0.0)
        dk = dk + jnp.where(right, 0.0, grown)
    head_sum = sums[levels * CHUNK : (levels + 1) * CHUNK]
    tail_sum = sums[(levels + 1) * CHUNK :]
    head_grow = jnp.exp(head_sum)
    tail_grow = jnp.exp(tail_sum)
    q_in = q32 * head_grow
    k_out = k32 * tail_grow
    k_out_half = k_out.astype(half)
    back_q = dot(d_mixed, state_half, NT)
    back_k = dot(v, carry_half, NT)
    pieces.append((q_in * back_q).astype(half))
    pieces.append((k_out * back_k).astype(half))
    dq = dq + head_grow * back_q
    dk = dk + tail_grow * back_k
    dv = dot(scores, d_mixed, TN) + dot(k_out_half, carry_half, NN)
    d_qkv = jnp.concatenate([dq.astype(half), dk.astype(half), dv.astype(half)], axis=1)
    whole = jnp.exp(jnp.transpose(head_sum[CHUNK - 8 :, :]))[:, 7:8]
    end_col = whole * jnp.sum(state_half.astype(f32) * carry_now, axis=1, keepdims=True)
    end_row = jnp.transpose(jnp.broadcast_to(end_col, (end_col.shape[0], 128)))[0:1, :]
    d_decay = dot(span_ref[:, :CHUNK], jnp.concatenate(pieces, axis=0), TN) + end_row
    carry[...] = whole * carry_now + dot(q_in.astype(half), d_mixed, TN)
    return d_qkv, d_decay * (jax.nn.sigmoid(-pre) * (1.0 / 16.0))


def backward_body(
    pre_ref, q_ref, k_ref, v_ref, d_ref, score_ref, state_ref, span_ref,
    dqkv_ref, dpre_ref, carry,
):
    @pl.when(pl.program_id(0) == 0)
    def _():
        carry[...] = jnp.zeros_like(carry)

    dqkv_ref[...], dpre_ref[...] = backward_math(
        pre_ref[...], q_ref[...], k_ref[...], v_ref[...], d_ref[...], score_ref[...],
        state_ref[0], span_ref, carry,
    )


def recur_forward(pre, qkv, span, dk, dv):
    length = qkv.shape[0]
    count = length // CHUNK

    def row(wide, place=0):
        return pl.BlockSpec((CHUNK, wide), lambda i: (i, place))

    return pl.pallas_call(
        forward_body,
        grid=(count,),
        in_specs=[
            row(dk), row(dk, 0), row(dk, 1), row(dv, 2 * dk // dv),
            pl.BlockSpec(span.shape, lambda i: (0, 0)),
        ],
        out_specs=[row(dv), row(CHUNK), pl.BlockSpec((1, dk, dv), lambda i: (i, 0, 0))],
        out_shape=[
            jax.ShapeDtypeStruct((length, dv), half),
            jax.ShapeDtypeStruct((length, CHUNK), half),
            jax.ShapeDtypeStruct((count, dk, dv), half),
        ],
        scratch_shapes=[pltpu.VMEM((dk, dv), f32)],
        compiler_params=pltpu.CompilerParams(dimension_semantics=("arbitrary",)),
        cost_estimate=pl.CostEstimate(
            flops=6 * 10**9, bytes_accessed=8 * 2**20, transcendentals=2 * 2**20
        ),
        name="recur_forward",
    )(pre, qkv, qkv, qkv, span)


def recur_backward(pre, qkv, d_mixed, scores, states, span, dk, dv):
    length = qkv.shape[0]
    count = length // CHUNK

    def row(wide, place=0):
        return pl.BlockSpec((CHUNK, wide), lambda i: (count - 1 - i, place))

    return pl.pallas_call(
        backward_body,
        grid=(count,),
        in_specs=[
            row(dk), row(dk, 0), row(dk, 1), row(dv, 2 * dk // dv), row(dv), row(CHUNK),
            pl.BlockSpec((1, dk, dv), lambda i: (count - 1 - i, 0, 0)),
            pl.BlockSpec(span.shape, lambda i: (0, 0)),
        ],
        out_specs=[row(2 * dk + dv), row(dk)],
        out_shape=[
            jax.ShapeDtypeStruct((length, 2 * dk + dv), half),
            jax.ShapeDtypeStruct((length, dk), f32),
        ],
        scratch_shapes=[pltpu.VMEM((dk, dv), f32)],
        compiler_params=pltpu.CompilerParams(dimension_semantics=("arbitrary",)),
        cost_estimate=pl.CostEstimate(
            flops=8 * 10**9, bytes_accessed=10 * 2**20, transcendentals=2 * 2**20
        ),
        name="recur_backward",
    )(pre, qkv, qkv, qkv, d_mixed, scores, states, span)

MESH = pl.DeviceIdType.MESH
BULK = 13
PIECES = 4


class Links:
    def __init__(self, send, recv, local):
        place = lax.axis_index("dp")
        self.z = place // 2
        self.x = place % 2
        self.t = lax.axis_index("tensor")
        self.core = self.t % 2
        self.send, self.recv, self.local = send, recv, local
        self.count = 0
        self.local_count = 0

    def take(self, number=1):
        first = self.count
        self.count += number
        return first

    def take_local(self, number=1):
        first = self.local_count
        self.local_count += number
        return first

    def beside(self):
        return {"dp": self.z * 2 + 1 - self.x}

    def up(self):
        return {"dp": self.z * 2 + 2 + self.x}

    def down(self):
        return {"dp": self.z * 2 - 2 + self.x}

    def partner(self):
        return {"tensor": self.t + 1 - 2 * self.core}

    def across(self):
        return {"tensor": (self.t + 2) % 4}

    def greet(self):
        barrier = pltpu.get_barrier_semaphore()
        around = [{"dp": ((self.z + step) % LINE) * 2 + self.x} for step in (1, 3)]
        for other in (*around, self.beside(), self.partner(), self.across()):
            pl.semaphore_signal(barrier, inc=1, device_id=other, device_id_type=MESH)
        pl.semaphore_wait(barrier, 5)

    def copy(self, index, src, dst, target):
        return pltpu.make_async_remote_copy(
            src_ref=src,
            dst_ref=dst,
            send_sem=self.send.at[index],
            recv_sem=self.recv.at[index],
            device_id=target,
            device_id_type=MESH,
        )

    def arrived(self, index, dst):
        self.copy(index, dst, dst, self.beside()).wait_recv()

    def sent(self, index, src):
        self.copy(index, src, src, self.beside()).wait_send()


class Gather:
    SEMS = 26

    def __init__(self, links, shard, full):
        self.links, self.shard, self.full = links, shard, full
        self.rows = shard.shape[0]
        self.bulk = self.rows * BULK // 16
        self.base = links.take(self.SEMS)
        self.own_sem = links.take_local()
        self.pending = []

    def at(self, z, x, rest):
        first = (z * 2 + x) * self.rows + (self.bulk if rest else 0)
        return self.full.at[pl.ds(first, self.rows - self.bulk if rest else self.bulk), :]

    def mine(self, rest):
        if rest:
            return self.shard.at[pl.ds(self.bulk, self.rows - self.bulk), :]
        return self.shard.at[pl.ds(0, self.bulk), :]

    def go(self, index, src, dst, target, when=None):
        links = self.links

        def start():
            links.copy(self.base + index, src, dst, target).start()

        if when is None:
            start()
        else:
            pl.when(when)(start)
        self.pending.append((index, src, when))

    def start(self):
        links = self.links
        z, x = links.z, links.x
        keep = self.full.at[pl.ds((z * 2 + x) * self.rows, self.rows), :]
        self.keep = pltpu.make_async_copy(self.shard, keep, links.local.at[self.own_sem])
        self.keep.start()
        self.go(0, self.mine(False), self.at(z, x, False), links.up(), z < 3)
        self.go(3, self.mine(False), self.at(z, x, False), links.down(), z > 0)
        self.go(13, self.mine(True), self.at(z, x, True), links.beside())
        self.go(6, self.mine(False), self.at(z, x, False), links.beside())

    def bulk_step(self, k):
        links = self.links
        z, x = links.z, links.x
        for side, base, cross, target, more in (
            (-k, 0, 7, links.up(), z < 3),
            (k, 3, 10, links.down(), z > 0),
        ):
            there = z + side
            valid = there >= 0 if side < 0 else there <= 3
            piece = self.at(there, x, False)

            @pl.when(valid)
            def _():
                links.arrived(self.base + base + k - 1, piece)

            if k < 3:
                self.go(base + k, piece, piece, target, valid & more)
            self.go(cross + k - 1, piece, piece, links.beside(), valid)

    def rest_start(self):
        links = self.links
        z, x = links.z, links.x
        other = self.at(z, 1 - x, True)
        links.arrived(self.base + 13, other)
        mine = self.mine(True)
        for index, src, dst in ((14, mine, self.at(z, x, True)), (15, other, other)):
            self.go(index, src, dst, links.up(), z < 3)
            self.go(index + 6, src, dst, links.down(), z > 0)

    def rest_step(self, k):
        links = self.links
        z, x = links.z, links.x
        for side, base, target, more in (
            (-k, 14, links.up(), z < 3),
            (k, 20, links.down(), z > 0),
        ):
            there = z + side
            valid = there >= 0 if side < 0 else there <= 3
            for which in range(2):
                piece = self.at(there, x if which == 0 else 1 - x, True)

                @pl.when(valid)
                def _():
                    links.arrived(self.base + base + 2 * (k - 1) + which, piece)

                if k < 3:
                    self.go(base + 2 * k + which, piece, piece, target, valid & more)

    def finish(self):
        links = self.links
        z, x = links.z, links.x
        links.arrived(self.base + 6, self.at(z, 1 - x, False))
        for k in (1, 2, 3):
            for side, cross in ((-k, 7), (k, 10)):
                there = z + side
                valid = there >= 0 if side < 0 else there <= 3

                @pl.when(valid)
                def _():
                    links.arrived(self.base + cross + k - 1, self.at(there, 1 - x, False))

        for index, src, when in self.pending:

            def done():
                links.sent(self.base + index, src)

            if when is None:
                done()
            else:
                pl.when(when)(done)
        self.keep.wait()


def add_rows(out, outs_at, terms, rows):
    def body(i, carry):
        tile = pl.ds(pl.multiple_of(i * 16, 16), 16)
        value = terms[0][tile, :].astype(f32)
        for term in terms[1:]:
            value = value + term[tile, :].astype(f32)
        out[pl.ds(pl.multiple_of(outs_at + i * 16, 16), 16), :] = value.astype(out.dtype)
        return carry

    lax.fori_loop(0, rows // 16, body, 0)


ORDER = ((3, 3, 0, 0), (2, 0, 3, 1), (1, 2, 1, 2), (0, 1, 2, 3))


class Scatter:
    SEMS = 15

    def __init__(self, links, total, own, buffers):
        self.links, self.total, self.own = links, total, own
        self.beside, self.kept, self.passed, self.kept2, self.passed2, self.last = buffers
        self.rows = total.shape[0] // (2 * LINE)
        self.bulk = self.rows * BULK // 16
        self.rest = self.rows - self.bulk
        self.base = links.take(self.SEMS)
        self.loads = links.take_local(12)
        low, high = links.z % 2, links.z // 2
        self.order = []
        for c in ORDER:
            self.order.append(
                c[0] + (c[1] - c[0]) * low + (c[2] - c[0]) * high
                + (c[3] - c[1] - c[2] + c[0]) * low * high
            )

    @staticmethod
    def scratch(rows, n):
        bulk = rows * BULK // 16
        rest = rows - bulk
        return [
            pltpu.VMEM((LINE, bulk, n), half),
            pltpu.VMEM((LINE, bulk, n), half),
            pltpu.VMEM((LINE + 1, bulk, n), half),
            pltpu.VMEM((LINE, 2 * rest, n), half),
            pltpu.VMEM((LINE + 1, 2 * rest, n), half),
            pltpu.VMEM((rest, n), half),
        ]

    def block(self, z, x, rest):
        first = (z * 2 + x) * self.rows + (self.bulk if rest else 0)
        return self.total.at[pl.ds(first, self.rest if rest else self.bulk), :]

    def load(self, k, part):
        links = self.links
        d = self.order[k]
        if part == 2:
            src, dst = self.block(d, links.x, False), self.kept.at[k]
        else:
            src = self.block(d, part, True)
            dst = self.kept2.at[k, pl.ds(part * self.rest, self.rest), :]
        return pltpu.make_async_copy(src, dst, links.local.at[self.loads + 3 * k + part])

    def start(self):
        for k in range(LINE):
            for part in range(3):
                self.load(k, part).start()

    def aside(self, k):
        links = self.links
        src = self.block(self.order[k], 1 - links.x, False)
        links.copy(self.base + k, src, self.beside.at[k], links.beside()).start()

    def step(self, k, rest):
        links = self.links
        z = links.z
        d = self.order[k]
        if rest:
            kept, passed, rows, first = self.kept2.at[k], self.passed2, 2 * self.rest, self.base + 9
            self.load(k, 0).wait()
            self.load(k, 1).wait()
            terms = [kept]
        else:
            kept, passed, rows, first = self.kept.at[k], self.passed, self.bulk, self.base + 4
            self.load(k, 2).wait()
            links.arrived(self.base + k, self.beside.at[k])
            terms = [kept, self.beside.at[k]]
        upward = d > z
        carried = (upward & (z > 0)) | ((d < z) & (z < 3))

        @pl.when(carried)
        def _():
            links.arrived(first + d, passed.at[d])
            add_rows(kept, 0, terms + [passed.at[d]], rows)

        if not rest:

            @pl.when(jnp.logical_not(carried))
            def _():
                add_rows(kept, 0, terms, rows)

        @pl.when(upward)
        def _():
            links.copy(first + d, kept, passed.at[d], links.up()).start()

        @pl.when((d < z) & (d < z - 1))
        def _():
            links.copy(first + d, kept, passed.at[d], links.down()).start()

        @pl.when((d < z) & (d == z - 1))
        def _():
            links.copy(first + LINE, kept, passed.at[LINE], links.down()).start()

    def close(self, rest):
        links = self.links
        z, x = links.z, links.x
        k = LINE - 1
        if rest:
            kept, passed, rows, first = self.kept2.at[k], self.passed2, 2 * self.rest, self.base + 9
            self.load(k, 0).wait()
            self.load(k, 1).wait()
            terms, out = [kept], kept
        else:
            kept, passed, rows, first = self.kept.at[k], self.passed, self.bulk, self.base + 4
            self.load(k, 2).wait()
            links.arrived(self.base + k, self.beside.at[k])
            terms, out = [kept, self.beside.at[k]], self.own

        @pl.when(z > 0)
        def _():
            links.arrived(first + z, passed.at[z])

        @pl.when(z < 3)
        def _():
            links.arrived(first + LINE, passed.at[LINE])

        @pl.when(z == 0)
        def _():
            add_rows(out, 0, terms + [passed.at[LINE]], rows)

        @pl.when(z == 3)
        def _():
            add_rows(out, 0, terms + [passed.at[z]], rows)

        @pl.when((z > 0) & (z < 3))
        def _():
            add_rows(out, 0, terms + [passed.at[z], passed.at[LINE]], rows)

        if rest:
            away = kept.at[pl.ds((1 - x) * self.rest, self.rest), :]
            links.copy(self.base + 14, away, self.last, links.beside()).start()

    def finish(self):
        links = self.links
        z, x = links.z, links.x
        links.arrived(self.base + 14, self.last)
        mine = self.kept2.at[LINE - 1, pl.ds(x * self.rest, self.rest), :]
        add_rows(self.own, self.bulk, [mine, self.last], self.rest)
        links.sent(self.base + 14, self.last)
        for k in range(LINE):
            links.sent(self.base + k, self.beside.at[k])
        for k in range(LINE - 1):
            d = self.order[k]
            for kept, first in ((self.kept.at[k], self.base + 4), (self.kept2.at[k], self.base + 9)):

                @pl.when((d > z) | (d < z - 1))
                def _():
                    links.sent(first + d, kept)

                @pl.when(d == z - 1)
                def _():
                    links.sent(first + LINE, kept)


class Total:
    SEMS = 3 * PIECES

    def __init__(self, links, part, out, buffers):
        self.links, self.part, self.out = links, part, out
        self.mine, self.first, self.second = buffers
        self.rows = part.shape[0] // 2 // PIECES
        self.base = links.take(self.SEMS)
        self.loads = links.take_local(2 * PIECES)

    @staticmethod
    def scratch(rows, n):
        return [pltpu.VMEM((PIECES, rows // 2 // PIECES, n), half) for _ in range(3)]

    def at(self, ref, core, j):
        return ref.at[pl.ds((core * PIECES + j) * self.rows, self.rows), :]

    def load(self, j):
        src = self.at(self.part, self.links.core, j)
        return pltpu.make_async_copy(src, self.mine.at[j], self.links.local.at[self.loads + j])

    def store(self, j):
        dst = self.at(self.out, self.links.core, j)
        sem = self.links.local.at[self.loads + PIECES + j]
        return pltpu.make_async_copy(self.first.at[j], dst, sem)

    def start(self):
        links = self.links
        for j in range(PIECES):
            self.load(j).start()
            src = self.at(self.part, 1 - links.core, j)
            links.copy(self.base + j, src, self.first.at[j], links.partner()).start()

    def middle(self):
        links = self.links
        for j in range(PIECES):
            self.load(j).wait()
            links.arrived(self.base + j, self.first.at[j])
            add_rows(self.mine.at[j], 0, [self.mine.at[j], self.first.at[j]], self.rows)
            index = self.base + PIECES + j
            links.copy(index, self.mine.at[j], self.second.at[j], links.across()).start()

    def spread(self):
        links = self.links
        for j in range(PIECES):
            links.arrived(self.base + PIECES + j, self.second.at[j])
            add_rows(self.first.at[j], 0, [self.mine.at[j], self.second.at[j]], self.rows)
            index = self.base + 2 * PIECES + j
            dst = self.at(self.out, links.core, j)
            links.copy(index, self.first.at[j], dst, links.partner()).start()
            self.store(j).start()

    def landed(self):
        links = self.links
        for j in range(PIECES):
            links.arrived(self.base + 2 * PIECES + j, self.at(self.out, 1 - links.core, j))
            self.store(j).wait()

    def finish(self):
        links = self.links
        for j in range(PIECES):
            for stage in range(3):
                links.sent(self.base + stage * PIECES + j, self.mine.at[j])


def exchange(number, shards=(), totals=(), parts=()):
    gathers, scatters, sums = len(shards), len(totals), len(parts)
    scratch = []
    for total in totals:
        scratch += Scatter.scratch(total.shape[0] // (2 * LINE), total.shape[1])
    for part in parts:
        scratch += Total.scratch(part.shape[0], part.shape[1])
    remote = Gather.SEMS * gathers + Scatter.SEMS * scatters + Total.SEMS * sums
    near = gathers + 12 * scatters + 2 * PIECES * sums
    scratch += [
        pltpu.SemaphoreType.DMA((remote,)),
        pltpu.SemaphoreType.DMA((remote,)),
        pltpu.SemaphoreType.DMA((near,)),
    ]

    def kernel(*refs):
        refs = list(refs)

        def pop(count):
            taken, refs[:count] = refs[:count], []
            return taken

        shard_refs, total_refs, part_refs = pop(gathers), pop(scatters), pop(sums)
        full_refs, own_refs, sum_refs = pop(gathers), pop(scatters), pop(sums)
        buffers = [pop(6) for _ in range(scatters)]
        sum_buffers = [pop(3) for _ in range(sums)]
        links = Links(*refs)
        gather = [Gather(links, s, f) for s, f in zip(shard_refs, full_refs)]
        scatter = [Scatter(links, *a) for a in zip(total_refs, own_refs, buffers)]
        total = [Total(links, *a) for a in zip(part_refs, sum_refs, sum_buffers)]
        links.greet()
        for item in gather + scatter + total:
            item.start()
        for k in range(LINE):
            for item in scatter:
                item.aside(k)
        for item in total:
            item.middle()
        for k in range(LINE - 1):
            for item in scatter:
                item.step(k, True)
        for item in scatter:
            item.close(True)
        for item in gather:
            item.bulk_step(1)
        for item in gather:
            item.rest_start()
        for item in scatter:
            item.step(0, False)
        for item in gather:
            item.bulk_step(2)
        for item in gather:
            item.rest_step(1)
        for item in scatter:
            item.step(1, False)
        for item in gather:
            item.bulk_step(3)
        for item in scatter:
            item.step(2, False)
        for item in total:
            item.spread()
        for item in gather:
            item.rest_step(2)
        for item in scatter:
            item.close(False)
        for item in gather:
            item.rest_step(3)
        for item in total:
            item.landed()
        for item in gather + scatter + total:
            item.finish()

    whole = pl.BlockSpec(memory_space=pl.ANY)
    near_spec = pl.BlockSpec(memory_space=pltpu.VMEM)
    outs = pl.pallas_call(
        kernel,
        in_specs=[near_spec] * gathers + [whole] * (scatters + sums),
        out_specs=[whole] * gathers + [near_spec] * scatters + [whole] * sums,
        out_shape=[
            jax.ShapeDtypeStruct((s.shape[0] * 2 * LINE, s.shape[1]), half) for s in shards
        ]
        + [jax.ShapeDtypeStruct((t.shape[0] // (2 * LINE), t.shape[1]), f32) for t in totals]
        + [jax.ShapeDtypeStruct(p.shape, half) for p in parts],
        scratch_shapes=scratch,
        compiler_params=pltpu.CompilerParams(
            collective_id=number, has_side_effects=True, vmem_limit_bytes=60 * 2**20
        ),
        name=f"exchange_{number}",
    )(*shards, *totals, *parts)
    return outs[:gathers], outs[gathers : gathers + scatters], outs[gathers + scatters :]


class Stream:
    def __init__(self, sems, base, arrays, buffers, index):
        self.sems, self.base, self.arrays, self.buffers, self.index = (
            sems, base, arrays, buffers, index,
        )

    def copies(self, i, inward):
        slot = i % 2
        for n, (array, buffer) in enumerate(zip(self.arrays, self.buffers)):
            rows = buffer.shape[1]
            first = pl.multiple_of(self.index(i) * rows, rows)
            far, near = array.at[pl.ds(first, rows), :], buffer.at[slot]
            sem = self.sems.at[self.base + 2 * n + slot]
            src, dst = (far, near) if inward else (near, far)
            yield pltpu.make_async_copy(src, dst, sem)

    def start(self, i, inward):
        for copy in self.copies(i, inward):
            copy.start()

    def wait(self, i, inward):
        for copy in self.copies(i, inward):
            copy.wait()


def row_sum(values):
    return jnp.sum(values, axis=0, keepdims=True)


def attention_back(tile, weights, gains, sums, carry):
    (cot, middle, d_out, tokens, qkv, mixed, outgate, pre, scores, state) = tile
    (w_out, w_qkv, w_gate, w_small, w_decay, span) = weights
    gain_ffn, gain_head = gains
    sum_ffn, sum_head, sum_bias, sum_attn = sums
    unit, scale = rms_parts(middle[...].astype(f32))
    cot = cot[...].astype(f32)
    sum_ffn[...] += row_sum(cot * unit)
    weighted = cot * gain_ffn[...]
    inner = jnp.mean(weighted * unit, axis=-1, keepdims=True)
    d_attn = (d_out[...].astype(f32) + scale * (weighted - unit * inner)).astype(half)
    d_gated = dot(d_attn, w_out[...], NN)
    rows = mixed[...].astype(f32)
    gate = outgate[...].astype(f32)
    head_scale = lax.rsqrt(jnp.mean(rows * rows, axis=-1, keepdims=True) + head_eps)
    head_unit = rows * head_scale
    sig = jax.nn.sigmoid(gate)
    d_outgate = (
        d_gated * head_unit * gain_head[...] * sig * (1.0 + gate * (1.0 - sig))
    ).astype(half)
    d_normed_head = d_gated * gate * sig
    sum_head[...] += row_sum(d_normed_head * head_unit)
    weighted = d_normed_head * gain_head[...]
    inner = jnp.mean(weighted * head_unit, axis=-1, keepdims=True)
    d_mixed = (head_scale * (weighted - head_unit * inner)).astype(half)
    dk = w_decay.shape[1]
    d_qkv, d_pre = backward_math(
        pre[...], qkv[:, :dk], qkv[:, dk : 2 * dk], qkv[:, 2 * dk :], d_mixed,
        scores[...], state[...], span, carry,
    )
    sum_bias[...] += row_sum(d_pre)
    d_pre = d_pre.astype(half)
    d_rank = dot(d_pre, w_decay[...], NT).astype(half)
    d_normed = (
        dot(d_qkv, w_qkv[...], NT) + dot(d_outgate, w_gate[...], NT) + dot(d_rank, w_small[...], NT)
    )
    unit, _ = rms_parts(tokens[...].astype(f32))
    sum_attn[...] += row_sum(d_normed * unit)
    return d_attn, d_outgate, d_qkv, d_pre, d_rank, d_normed.astype(half)


def backward_exchange(number, totals, part, rows_in, weights, gains):
    scatters = len(totals)
    length, width = part.shape
    count = length // CHUNK
    dk = weights[4].shape[1]
    dv = weights[0].shape[1]
    outs_wide = (width, dv, 2 * dk + dv, dk, 128, width)
    in_shapes = [(CHUNK, width)] + [(a.shape[0] // count, a.shape[1]) for a in rows_in]
    in_types = [half] + [a.dtype for a in rows_in]
    streams = len(in_shapes)
    sum_wide = (width, dv, dk, width)
    scratch = []
    for total in totals:
        scratch += Scatter.scratch(total.shape[0] // (2 * LINE), total.shape[1])
    scratch += Total.scratch(length, width)
    scratch += [pltpu.VMEM((2,) + s, t) for s, t in zip(in_shapes, in_types)]
    scratch += [pltpu.VMEM((2, CHUNK, w), half) for w in outs_wide]
    scratch += [pltpu.VMEM(w.shape, half) for w in weights]
    scratch += [pltpu.VMEM((dk, dv), f32)]
    remote = Scatter.SEMS * scatters + Total.SEMS
    near = 12 * scatters + 2 * PIECES
    extra = 2 * streams + 2 * len(outs_wide) + len(weights)
    scratch += [
        pltpu.SemaphoreType.DMA((remote,)),
        pltpu.SemaphoreType.DMA((remote,)),
        pltpu.SemaphoreType.DMA((near,)),
        pltpu.SemaphoreType.DMA((extra,)),
    ]

    def kernel(*refs):
        refs = list(refs)

        def pop(count):
            taken, refs[:count] = refs[:count], []
            return taken

        total_refs, (part_ref,), row_refs = pop(scatters), pop(1), pop(streams - 1)
        weight_refs, gain_refs = pop(len(weights)), pop(2)
        own_refs, (sum_ref,), out_refs, gain_sums = pop(scatters), pop(1), pop(6), pop(4)
        buffers = [pop(6) for _ in range(scatters)]
        sum_buffers = pop(3)
        in_buffers, out_buffers, near_weights = pop(streams), pop(6), pop(len(weights))
        (carry,) = pop(1)
        sems = refs.pop()
        links = Links(*refs)
        scatter = [Scatter(links, *a) for a in zip(total_refs, own_refs, buffers)]
        total = Total(links, part_ref, sum_ref, sum_buffers)
        inputs = Stream(sems, 0, [sum_ref] + row_refs, in_buffers, lambda i: count - 1 - i)
        outputs = Stream(sems, 2 * streams, out_refs, out_buffers, lambda i: count - 1 - i)
        loads = [
            pltpu.make_async_copy(far, close, sems.at[2 * streams + 12 + n])
            for n, (far, close) in enumerate(zip(weight_refs, near_weights))
        ]
        links.greet()
        for item in scatter:
            item.start()
        total.start()
        for k in range(LINE):
            for item in scatter:
                item.aside(k)
        for load in loads:
            load.start()
        total.middle()
        for k in range(LINE - 1):
            for item in scatter:
                item.step(k, True)
        for item in scatter:
            item.close(True)
        for k in range(2):
            for item in scatter:
                item.step(k, False)
        total.spread()
        total.landed()
        for load in loads:
            load.wait()
        for ref in (*gain_sums, carry):
            ref[...] = jnp.zeros_like(ref)
        inputs.start(0, True)

        def body(i, state):
            @pl.when(i + 1 < count)
            def _():
                inputs.start(i + 1, True)

            inputs.wait(i, True)
            slot = i % 2
            results = attention_back(
                [b.at[slot] for b in in_buffers], near_weights, gain_refs, gain_sums, carry
            )

            @pl.when(i >= 2)
            def _():
                outputs.wait(i - 2, False)

            for buffer, value in zip(out_buffers, results):
                buffer[slot] = value
            outputs.start(i, False)

            @pl.when(i == 2)
            def _():
                for item in scatter:
                    item.step(2, False)

            @pl.when(i == 5)
            def _():
                for item in scatter:
                    item.close(False)

            return state

        lax.fori_loop(0, count, body, 0)
        outputs.wait(count - 2, False)
        outputs.wait(count - 1, False)
        for item in scatter:
            item.finish()
        total.finish()

    whole = pl.BlockSpec(memory_space=pl.ANY)
    near_spec = pl.BlockSpec(memory_space=pltpu.VMEM)
    outs = pl.pallas_call(
        kernel,
        in_specs=[whole] * (scatters + 1 + len(rows_in) + len(weights)) + [near_spec] * 2,
        out_specs=[near_spec] * scatters + [whole] * 7 + [near_spec] * 4,
        out_shape=[jax.ShapeDtypeStruct((t.shape[0] // (2 * LINE), t.shape[1]), f32) for t in totals]
        + [jax.ShapeDtypeStruct(part.shape, half)]
        + [jax.ShapeDtypeStruct((length, w), half) for w in outs_wide]
        + [jax.ShapeDtypeStruct((1, w), f32) for w in sum_wide],
        scratch_shapes=scratch,
        compiler_params=pltpu.CompilerParams(
            collective_id=number, has_side_effects=True, vmem_limit_bytes=62 * 2**20
        ),
        name=f"backward_exchange_{number}",
    )(*totals, part, *rows_in, *weights, *gains)
    return outs[:scatters], outs[scatters + 1 : scatters + 7], outs[scatters + 7 :]


class Ring:
    def __init__(self, size):
        self.size = size
        self.wide = size // LINE
        place = lax.axis_index("dp")
        self.z = place // self.wide
        self.x = place % self.wide

    def z_pairs(self, step):
        wide = self.wide
        return [
            (z * wide + x, ((z + step) % LINE) * wide + x) for z in range(LINE) for x in range(wide)
        ]

    def x_pairs(self, step):
        wide = self.wide
        return [(z * wide + x, z * wide + (x + step) % wide) for z in range(LINE) for x in range(wide)]


def gather(ring, shard):
    rows = shard.shape[0]
    pieces = [(ring.z, shard)]
    for step in (1, 3, 2):
        pieces.append(((ring.z - step) % LINE, lax.ppermute(shard, "dp", ring.z_pairs(step))))
    out = jnp.zeros((ring.size * rows, shard.shape[1]), shard.dtype)
    for z, piece in pieces:
        for step in range(ring.wide):
            moved = lax.ppermute(piece, "dp", ring.x_pairs(step)) if step else piece
            place = z * ring.wide + (ring.x - step) % ring.wide
            out = lax.dynamic_update_slice(out, moved, (place * rows, 0))
    return out


def scatter(ring, total):
    rows = total.shape[0] // ring.size

    def block(z, x):
        place = (z % LINE) * ring.wide + x % ring.wide
        return lax.dynamic_slice(total, (place * rows, 0), (rows, total.shape[1]))

    result = None
    for step in (2, 1, 3, 0):
        z = ring.z + step
        kept = block(z, ring.x).astype(f32)
        for side in range(1, ring.wide):
            away = lax.ppermute(block(z, ring.x + side), "dp", ring.x_pairs(side))
            kept = kept + away.astype(f32)
        if step:
            kept = lax.ppermute(kept.astype(half), "dp", ring.z_pairs(step)).astype(f32)
        result = kept if result is None else result + kept
    return result


CORE = [(i, i ^ 1) for i in range(4)]
ACROSS = [(i, i ^ 2) for i in range(4)]


def tensor_sum(part):
    rows = part.shape[0] // 2
    second = (lax.axis_index("tensor") & 1) == 1
    upper, lower = part[:rows], part[rows:]
    mine = jnp.where(second, lower, upper)
    away = jnp.where(second, upper, lower)
    mine = (mine.astype(f32) + lax.ppermute(away, "tensor", CORE).astype(f32)).astype(half)
    mine = (mine.astype(f32) + lax.ppermute(mine, "tensor", ACROSS).astype(f32)).astype(half)
    theirs = lax.ppermute(mine, "tensor", CORE)
    return jnp.concatenate(
        [jnp.where(second, theirs, mine), jnp.where(second, mine, theirs)], axis=0
    )


def rms_parts(values):
    scale = lax.rsqrt(jnp.mean(values * values, axis=-1, keepdims=True) + norm_eps)
    return values * scale, scale


def rms_back(unit, scale, gain, cot):
    weighted = cot * gain
    inner = jnp.mean(weighted * unit, axis=-1, keepdims=True)
    return scale * (weighted - unit * inner), jnp.sum(cot * unit, axis=0)


def gated_rows(mixed, outgate, gain):
    scale = lax.rsqrt(jnp.mean(mixed * mixed, axis=-1, keepdims=True) + head_eps)
    return mixed * scale * gain * jax.nn.silu(outgate)


def local(
    tokens, lengths, norm_attn, query_proj, key_proj, value_proj, outgate_proj, rank_proj,
    decay_proj, decay_bias, head_gain, out_proj, norm_ffn, gate_proj, up_proj, down_proj, cotangent,
    *, size,
):
    ring = Ring(size)
    rows_total = tokens.shape[0]
    width = norm_attn.shape[0]
    rank = rank_proj.shape[1]
    dk = query_proj.shape[1]
    dv = value_proj.shape[1]
    ff = gate_proj.shape[1]
    bits = decay_proj.shape[2]
    gains = head_gain.shape[0]

    def as_column(values):
        flat = values.reshape(-1, 1)
        return jnp.pad(flat, ((0, width - flat.shape[0]), (0, 0)))

    decay_cols = rank * bits // width
    small = jnp.concatenate(
        [
            rank_proj,
            norm_attn[:, None],
            norm_ffn[:, None],
            as_column(head_gain),
            as_column(decay_bias),
            decay_proj.reshape(decay_cols, width).T,
        ],
        axis=1,
    )
    small = jnp.pad(small, ((0, 0), (0, 128 - small.shape[1]))).astype(half)
    qkv = jnp.concatenate([query_proj * 0.0625, key_proj, value_proj], axis=1).astype(half)
    first = (qkv, small, outgate_proj.astype(half), out_proj.T.astype(half))
    second = (gate_proj.astype(half), up_proj.astype(half), down_proj.T.astype(half))
    fast = size == 2 * LINE

    def collect(number, shards, parts):
        if fast:
            fulls, _, sums = exchange(number, shards, (), parts)
            return fulls, sums
        return [gather(ring, s) for s in shards], [tensor_sum(p) for p in parts]

    def deliver(number, totals, parts):
        if fast:
            _, owns, sums = exchange(number, (), totals, parts)
            return owns, sums
        return [scatter(ring, t) for t in totals], [tensor_sum(p) for p in parts]

    (qkv_full, small_full, outgate_full, out_full), _ = collect(0, first, ())
    rank_full = small_full[:, :rank]
    small32 = small_full.astype(f32)
    gain_attn = small32[:, rank]
    gain_ffn = small32[:, rank + 1]
    by_place = small32.reshape(size, width, 128)
    gain_head = by_place[:, :gains, rank + 2].reshape(-1)
    bias = by_place[:, :bits, rank + 3].reshape(-1)
    decay_weight = jnp.transpose(
        jnp.transpose(by_place[:, :, rank + 4 : rank + 4 + decay_cols], (0, 2, 1)).reshape(
            size, rank, bits
        ),
        (1, 0, 2),
    ).reshape(rank, -1)

    positions = jnp.arange(SEQ_LEN, dtype=jnp.int32)
    mask = (positions[None, :] < lengths[:, None]).astype(f32).reshape(rows_total, 1)
    tokens32 = tokens.astype(f32)
    unit, scale = rms_parts(tokens32)
    normed = (unit * gain_attn).astype(half)
    qkv = dot(normed, qkv_full, NN).astype(half)
    rank_rows = dot(normed, rank_full, NN)
    pre = (
        jnp.dot(rank_rows, decay_weight, precision=highest_precision, preferred_element_type=f32)
        + bias
    )
    span = span_matrix()
    mixed, scores, states = recur_forward(pre, qkv, span, dk, dv)
    outgate = dot(normed, outgate_full, NN).astype(half)
    gated, pull_gated = jax.vjp(gated_rows, mixed.astype(f32), outgate.astype(f32), gain_head)
    gated = gated.astype(half)
    (gate_full, up_full, down_full), (attn,) = collect(
        1, second, (dot(gated, out_full, NT).astype(half),)
    )
    middle = tokens32 + attn.astype(f32)
    unit_ffn, scale_ffn = rms_parts(middle)
    normed_ffn = (unit_ffn * gain_ffn).astype(half)
    gate_rows = dot(normed_ffn, gate_full, NN)
    up_rows = dot(normed_ffn, up_full, NN)
    hidden, pull_glu = jax.vjp(lambda g, u: jax.nn.silu(g) * u, gate_rows, up_rows)
    hidden = hidden.astype(half)
    d_out = cotangent.astype(f32) * mask
    d_out_half = d_out.astype(half)
    grad_down = dot(d_out_half, hidden, TN).astype(half)
    d_gate, d_up = pull_glu(dot(d_out_half, down_full, NN))
    d_gate = d_gate.astype(half)
    d_up = d_up.astype(half)
    d_normed_ffn = (dot(d_gate, gate_full, NT) + dot(d_up, up_full, NT)).astype(half)
    grad_gate = dot(normed_ffn, d_gate, TN).astype(half)
    grad_up = dot(normed_ffn, d_up, TN).astype(half)
    ffn = dot(hidden, down_full, NT).astype(half)
    if fast:
        w_decay = jnp.pad(decay_weight, ((0, 128 - rank), (0, 0))).astype(half)
        (down_own, gate_own), outs, sums = backward_exchange(
            2,
            (grad_down, grad_gate),
            d_normed_ffn,
            (
                middle.astype(half), d_out_half, tokens, qkv, mixed, outgate, pre, scores,
                states.reshape(-1, dv),
            ),
            (out_full, qkv_full, outgate_full, small_full, w_decay, span),
            (gain_ffn[None, :], gain_head[None, :]),
        )
        d_attn, d_outgate, d_qkv, d_pre_half, d_rank, d_normed = outs
        grad_gain_ffn, grad_head, grad_bias, grad_gain_attn = sums
        d_middle = d_attn.astype(f32)
        d_rank = d_rank[:, :rank]
    else:
        d_normed_ffn = tensor_sum(d_normed_ffn)
        d_back, grad_gain_ffn = rms_back(unit_ffn, scale_ffn, gain_ffn, d_normed_ffn.astype(f32))
        d_middle = d_out + d_back
        d_attn = d_middle.astype(half)
        d_mixed, d_outgate, grad_head = pull_gated(dot(d_attn, out_full, NN))
        d_outgate = d_outgate.astype(half)
        d_qkv, d_pre = recur_backward(pre, qkv, d_mixed.astype(half), scores, states, span, dk, dv)
        d_rank = dot(d_pre.astype(half), decay_weight.astype(half), NT).astype(half)
        d_normed = (
            dot(d_qkv, qkv_full, NT) + dot(d_outgate, outgate_full, NT) + dot(d_rank, rank_full, NT)
        )
        grad_gain_attn = jnp.sum(d_normed * unit, axis=0)
        d_normed = d_normed.astype(half)
        d_pre_half = d_pre.astype(half)
        grad_bias = jnp.sum(d_pre, axis=0)
    grad_out = dot(d_attn, gated, TN).astype(half)
    grad_outgate = dot(normed, d_outgate, TN).astype(half)
    grad_qkv = dot(normed, d_qkv, TN).astype(half)
    grad_rank = dot(normed, d_rank, TN)
    grad_decay = jnp.transpose(
        dot(rank_rows.astype(half), d_pre_half, TN).reshape(rank, size, bits), (1, 0, 2)
    ).reshape(size, decay_cols, width)

    def spread(values):
        blocks = values.reshape(size, -1, 1)
        return jnp.pad(blocks, ((0, 0), (0, width - blocks.shape[1]), (0, 0)))

    grad_small = jnp.concatenate(
        [
            grad_rank.reshape(size, width, rank),
            grad_gain_attn.reshape(size, width, 1),
            grad_gain_ffn.reshape(size, width, 1),
            spread(grad_head),
            spread(grad_bias),
            jnp.transpose(grad_decay, (0, 2, 1)),
        ],
        axis=2,
    )
    grad_small = jnp.pad(grad_small, ((0, 0), (0, 0), (0, 128 - grad_small.shape[2])))
    grad_small = grad_small.reshape(size * width, 128).astype(half)

    if fast:
        waiting = (grad_up, grad_out, grad_outgate, grad_qkv, grad_small)
        (up_own, out_own, outgate_own, qkv_own, small_own), (d_normed, ffn) = deliver(
            3, waiting, (d_normed, ffn)
        )
    else:
        waiting = (
            grad_down, grad_gate, grad_up, grad_out, grad_outgate, grad_qkv, grad_small,
        )
        (down_own, gate_own, up_own, out_own, outgate_own, qkv_own, small_own), (
            d_normed, ffn,
        ) = deliver(3, waiting, (d_normed, ffn))
    output = (mask * (middle + ffn.astype(f32))).astype(half)
    d_back, _ = rms_back(unit, scale, gain_attn, d_normed.astype(f32))
    grad_tokens = (d_middle + d_back).astype(half)
    heads_own = small_own.astype(half)
    heads_own = heads_own.astype(f32) + lax.ppermute(heads_own, "tensor", CORE).astype(f32)
    heads_own = heads_own.astype(half)
    heads_own = heads_own.astype(f32) + lax.ppermute(heads_own, "tensor", ACROSS).astype(f32)
    return (
        output,
        grad_tokens,
        heads_own[:, rank],
        qkv_own[:, :dk] * 0.0625,
        qkv_own[:, dk : 2 * dk],
        qkv_own[:, 2 * dk : 2 * dk + dv],
        outgate_own,
        heads_own[:, :rank],
        small_own[:, rank + 4 : rank + 4 + decay_cols].T.reshape(decay_proj.shape),
        small_own[:bits, rank + 3].reshape(decay_bias.shape),
        heads_own[:gains, rank + 2],
        out_own.T,
        heads_own[:, rank + 1] * 0.25,
        gate_own,
        up_own,
        down_own.T,
    )


def solution(mesh):
    size = mesh.shape["dp"]

    def run(*args):
        return local(*args, size=size)

    weight = P("dp", "tensor")
    cross = P("tensor", "dp")
    return jax.shard_map(
        run,
        mesh=mesh,
        in_specs=(
            P("dp", None), P("dp"), P("dp"), weight, weight, weight, weight, P("dp", None),
            P(None, "tensor", "dp"), cross, P("dp"), cross, P("dp"), weight, weight, cross,
            P("dp", None),
        ),
        out_specs=(
            P("dp", None), P("dp", None), P("dp"), weight, weight, weight, weight, P("dp", None),
            P(None, "tensor", "dp"), cross, P("dp"), cross, P("dp"), weight, weight, cross,
        ),
        check_vma=False,
    )
```

```python
import jax
import jax.numpy as jnp
from jax import lax
from jax.experimental import pallas as pl
from jax.experimental.pallas import tpu as pltpu
from jax.sharding import PartitionSpec as P

SEQ_LEN = 1024
LINE = 4

norm_eps = 1e-06
head_eps = 1.0
highest_precision = lax.Precision.HIGHEST
half = jnp.bfloat16
f32 = jnp.float32
CHUNK = 128


def level_count():
    return CHUNK.bit_length() - 1


def span_matrix():
    rows = lax.broadcasted_iota(jnp.int32, (CHUNK, CHUNK), 0)
    cols = lax.broadcasted_iota(jnp.int32, (CHUNK, CHUNK), 1)
    parts = []
    for level in range(level_count()):
        size = 1 << level
        middle = (rows // (2 * size)) * (2 * size) + size
        right = rows >= middle
        parts.append(
            jnp.where(right, (cols >= middle) & (cols <= rows), (cols > rows) & (cols < middle))
        )
    parts.append(cols <= rows)
    parts.append(cols > rows)
    stacked = jnp.concatenate(parts, axis=0).astype(half)
    return jnp.concatenate([stacked, stacked], axis=1)


def dot(left, right, dims):
    return lax.dot_general(left, right, (dims, ((), ())), preferred_element_type=f32)


NN = ((1,), (0,))
NT = ((1,), (1,))
TN = ((0,), (0,))


def log_decay(pre):
    return (jnp.minimum(pre, 0.0) - jnp.log1p(jnp.exp(-jnp.abs(pre)))) * (1.0 / 16.0)


def split_two(values):
    high = values.astype(half)
    low = (values - high.astype(f32)).astype(half)
    return jnp.concatenate([high, low], axis=0)


def level_parts(level):
    rows = lax.broadcasted_iota(jnp.int32, (CHUNK, CHUNK), 0)
    cols = lax.broadcasted_iota(jnp.int32, (CHUNK, CHUNK), 1)
    return rows, cols, (lax.shift_right_logical(rows ^ cols, level) == 1)


def forward_body(pre_ref, q_ref, k_ref, v_ref, span_ref, mixed_ref, score_ref, state_ref, state):
    @pl.when(pl.program_id(0) == 0)
    def _():
        state[...] = jnp.zeros_like(state)

    decay = log_decay(pre_ref[...])
    sums = dot(span_ref[...], split_two(decay), NN)
    q = q_ref[...]
    k = k_ref[...]
    v = v_ref[...]
    q32 = q.astype(f32)
    k32 = k.astype(f32)
    rows, cols, _ = level_parts(0)
    scores = jnp.where(rows == cols, dot(q, k, NT), 0.0)
    row_ids = lax.broadcasted_iota(jnp.int32, q.shape, 0)
    for level in range(level_count()):
        right = (lax.shift_right_logical(row_ids, level) & 1) == 1
        grow = jnp.exp(sums[level * CHUNK : (level + 1) * CHUNK])
        mixed_rows = (jnp.where(right, q32, k32) * grow).astype(half)
        pair = level_parts(level)[2] & (rows > cols)
        scores = jnp.where(pair, dot(mixed_rows, mixed_rows, NT), scores)
    levels = level_count()
    head_sum = sums[levels * CHUNK : (levels + 1) * CHUNK]
    tail_sum = sums[(levels + 1) * CHUNK :]
    q_in = (q32 * jnp.exp(head_sum)).astype(half)
    k_out = (k32 * jnp.exp(tail_sum)).astype(half)
    score_half = scores.astype(half)
    state_now = state[...]
    state_half = state_now.astype(half)
    mixed_ref[...] = (dot(score_half, v, NN) + dot(q_in, state_half, NN)).astype(mixed_ref.dtype)
    score_ref[...] = score_half
    state_ref[0] = state_half
    whole = jnp.exp(jnp.transpose(head_sum[CHUNK - 8 :, :]))[:, 7:8]
    state[...] = whole * state_now + dot(k_out, v, TN)


def backward_math(pre, q, k, v, d_mixed, scores, state_half, span_ref, carry):
    levels = level_count()
    decay = log_decay(pre)
    sums = dot(span_ref[...], split_two(decay), NN)
    q32 = q.astype(f32)
    k32 = k.astype(f32)
    carry_now = carry[...]
    carry_half = carry_now.astype(half)
    rows, cols, _ = level_parts(0)
    row_ids = lax.broadcasted_iota(jnp.int32, q.shape, 0)
    d_scores = dot(d_mixed, v, NT)
    diagonal = jnp.where(rows == cols, d_scores, 0.0)
    sym = jnp.where(rows > cols, d_scores, jnp.transpose(d_scores))
    diag_col = jnp.sum(diagonal, axis=1, keepdims=True)
    dq = diag_col * k32
    dk = diag_col * q32
    pieces = []
    for level in range(levels):
        right = (lax.shift_right_logical(row_ids, level) & 1) == 1
        grow = jnp.exp(sums[level * CHUNK : (level + 1) * CHUNK])
        scaled = jnp.where(right, q32, k32) * grow
        block = jnp.where(level_parts(level)[2], sym, 0.0).astype(half)
        back = dot(block, scaled.astype(half), NN)
        pieces.append((scaled * back).astype(half))
        grown = grow * back
        dq = dq + jnp.where(right, grown, 0.0)
        dk = dk + jnp.where(right, 0.0, grown)
    head_sum = sums[levels * CHUNK : (levels + 1) * CHUNK]
    tail_sum = sums[(levels + 1) * CHUNK :]
    head_grow = jnp.exp(head_sum)
    tail_grow = jnp.exp(tail_sum)
    q_in = q32 * head_grow
    k_out = k32 * tail_grow
    k_out_half = k_out.astype(half)
    back_q = dot(d_mixed, state_half, NT)
    back_k = dot(v, carry_half, NT)
    pieces.append((q_in * back_q).astype(half))
    pieces.append((k_out * back_k).astype(half))
    dq = dq + head_grow * back_q
    dk = dk + tail_grow * back_k
    dv = dot(scores, d_mixed, TN) + dot(k_out_half, carry_half, NN)
    d_qkv = jnp.concatenate([dq.astype(half), dk.astype(half), dv.astype(half)], axis=1)
    whole = jnp.exp(jnp.transpose(head_sum[CHUNK - 8 :, :]))[:, 7:8]
    end_col = whole * jnp.sum(state_half.astype(f32) * carry_now, axis=1, keepdims=True)
    end_row = jnp.transpose(jnp.broadcast_to(end_col, (end_col.shape[0], 128)))[0:1, :]
    d_decay = dot(span_ref[:, :CHUNK], jnp.concatenate(pieces, axis=0), TN) + end_row
    carry[...] = whole * carry_now + dot(q_in.astype(half), d_mixed, TN)
    return d_qkv, d_decay * (jax.nn.sigmoid(-pre) * (1.0 / 16.0))


def backward_body(
    pre_ref, q_ref, k_ref, v_ref, d_ref, score_ref, state_ref, span_ref,
    dqkv_ref, dpre_ref, carry,
):
    @pl.when(pl.program_id(0) == 0)
    def _():
        carry[...] = jnp.zeros_like(carry)

    dqkv_ref[...], dpre_ref[...] = backward_math(
        pre_ref[...], q_ref[...], k_ref[...], v_ref[...], d_ref[...], score_ref[...],
        state_ref[0], span_ref, carry,
    )


def recur_forward(pre, qkv, span, dk, dv):
    length = qkv.shape[0]
    count = length // CHUNK

    def row(wide, place=0):
        return pl.BlockSpec((CHUNK, wide), lambda i: (i, place))

    return pl.pallas_call(
        forward_body,
        grid=(count,),
        in_specs=[
            row(dk), row(dk, 0), row(dk, 1), row(dv, 2 * dk // dv),
            pl.BlockSpec(span.shape, lambda i: (0, 0)),
        ],
        out_specs=[row(dv), row(CHUNK), pl.BlockSpec((1, dk, dv), lambda i: (i, 0, 0))],
        out_shape=[
            jax.ShapeDtypeStruct((length, dv), half),
            jax.ShapeDtypeStruct((length, CHUNK), half),
            jax.ShapeDtypeStruct((count, dk, dv), half),
        ],
        scratch_shapes=[pltpu.VMEM((dk, dv), f32)],
        compiler_params=pltpu.CompilerParams(dimension_semantics=("arbitrary",)),
        cost_estimate=pl.CostEstimate(
            flops=6 * 10**9, bytes_accessed=8 * 2**20, transcendentals=2 * 2**20
        ),
        name="recur_forward",
    )(pre, qkv, qkv, qkv, span)


def recur_backward(pre, qkv, d_mixed, scores, states, span, dk, dv):
    length = qkv.shape[0]
    count = length // CHUNK

    def row(wide, place=0):
        return pl.BlockSpec((CHUNK, wide), lambda i: (count - 1 - i, place))

    return pl.pallas_call(
        backward_body,
        grid=(count,),
        in_specs=[
            row(dk), row(dk, 0), row(dk, 1), row(dv, 2 * dk // dv), row(dv), row(CHUNK),
            pl.BlockSpec((1, dk, dv), lambda i: (count - 1 - i, 0, 0)),
            pl.BlockSpec(span.shape, lambda i: (0, 0)),
        ],
        out_specs=[row(2 * dk + dv), row(dk)],
        out_shape=[
            jax.ShapeDtypeStruct((length, 2 * dk + dv), half),
            jax.ShapeDtypeStruct((length, dk), f32),
        ],
        scratch_shapes=[pltpu.VMEM((dk, dv), f32)],
        compiler_params=pltpu.CompilerParams(dimension_semantics=("arbitrary",)),
        cost_estimate=pl.CostEstimate(
            flops=8 * 10**9, bytes_accessed=10 * 2**20, transcendentals=2 * 2**20
        ),
        name="recur_backward",
    )(pre, qkv, qkv, qkv, d_mixed, scores, states, span)

MESH = pl.DeviceIdType.MESH
BULK = 13
PIECES = 4
VMEM_LIMIT = 63 * 2**20


class Links:
    def __init__(self, send, recv, local):
        place = lax.axis_index("dp")
        self.z = place // 2
        self.x = place % 2
        self.t = lax.axis_index("tensor")
        self.core = self.t % 2
        self.send, self.recv, self.local = send, recv, local
        self.count = 0
        self.local_count = 0

    def take(self, number=1):
        first = self.count
        self.count += number
        return first

    def take_local(self, number=1):
        first = self.local_count
        self.local_count += number
        return first

    def beside(self):
        return {"dp": self.z * 2 + 1 - self.x}

    def up(self):
        return {"dp": self.z * 2 + 2 + self.x}

    def down(self):
        return {"dp": self.z * 2 - 2 + self.x}

    def partner(self):
        return {"tensor": self.t + 1 - 2 * self.core}

    def across(self):
        return {"tensor": (self.t + 2) % 4}

    def greet(self):
        barrier = pltpu.get_barrier_semaphore()
        around = [{"dp": ((self.z + step) % LINE) * 2 + self.x} for step in (1, 3)]
        for other in (*around, self.beside(), self.partner(), self.across()):
            pl.semaphore_signal(barrier, inc=1, device_id=other, device_id_type=MESH)
        pl.semaphore_wait(barrier, 5)

    def copy(self, index, src, dst, target):
        return pltpu.make_async_remote_copy(
            src_ref=src,
            dst_ref=dst,
            send_sem=self.send.at[index],
            recv_sem=self.recv.at[index],
            device_id=target,
            device_id_type=MESH,
        )

    def arrived(self, index, dst):
        self.copy(index, dst, dst, self.beside()).wait_recv()

    def sent(self, index, src):
        self.copy(index, src, src, self.beside()).wait_send()


class Gather:
    SEMS = 26

    def __init__(self, links, shard, full):
        self.links, self.shard, self.full = links, shard, full
        self.rows = shard.shape[0]
        self.bulk = self.rows * BULK // 16
        self.base = links.take(self.SEMS)
        self.own_sem = links.take_local()
        self.pending = []

    def at(self, z, x, rest):
        first = (z * 2 + x) * self.rows + (self.bulk if rest else 0)
        return self.full.at[pl.ds(first, self.rows - self.bulk if rest else self.bulk), :]

    def mine(self, rest):
        if rest:
            return self.shard.at[pl.ds(self.bulk, self.rows - self.bulk), :]
        return self.shard.at[pl.ds(0, self.bulk), :]

    def go(self, index, src, dst, target, when=None):
        links = self.links

        def start():
            links.copy(self.base + index, src, dst, target).start()

        if when is None:
            start()
        else:
            pl.when(when)(start)
        self.pending.append((index, src, when))

    def start(self):
        links = self.links
        z, x = links.z, links.x
        keep = self.full.at[pl.ds((z * 2 + x) * self.rows, self.rows), :]
        self.keep = pltpu.make_async_copy(self.shard, keep, links.local.at[self.own_sem])
        self.keep.start()
        self.go(0, self.mine(False), self.at(z, x, False), links.up(), z < 3)
        self.go(3, self.mine(False), self.at(z, x, False), links.down(), z > 0)
        self.go(13, self.mine(True), self.at(z, x, True), links.beside())
        self.go(6, self.mine(False), self.at(z, x, False), links.beside())

    def bulk_step(self, k):
        links = self.links
        z, x = links.z, links.x
        for side, base, cross, target, more in (
            (-k, 0, 7, links.up(), z < 3),
            (k, 3, 10, links.down(), z > 0),
        ):
            there = z + side
            valid = there >= 0 if side < 0 else there <= 3
            piece = self.at(there, x, False)

            @pl.when(valid)
            def _():
                links.arrived(self.base + base + k - 1, piece)

            if k < 3:
                self.go(base + k, piece, piece, target, valid & more)
            self.go(cross + k - 1, piece, piece, links.beside(), valid)

    def rest_start(self):
        links = self.links
        z, x = links.z, links.x
        other = self.at(z, 1 - x, True)
        links.arrived(self.base + 13, other)
        mine = self.mine(True)
        for index, src, dst in ((14, mine, self.at(z, x, True)), (15, other, other)):
            self.go(index, src, dst, links.up(), z < 3)
            self.go(index + 6, src, dst, links.down(), z > 0)

    def rest_step(self, k):
        links = self.links
        z, x = links.z, links.x
        for side, base, target, more in (
            (-k, 14, links.up(), z < 3),
            (k, 20, links.down(), z > 0),
        ):
            there = z + side
            valid = there >= 0 if side < 0 else there <= 3
            for which in range(2):
                piece = self.at(there, x if which == 0 else 1 - x, True)

                @pl.when(valid)
                def _():
                    links.arrived(self.base + base + 2 * (k - 1) + which, piece)

                if k < 3:
                    self.go(base + 2 * k + which, piece, piece, target, valid & more)

    def finish(self):
        links = self.links
        z, x = links.z, links.x
        links.arrived(self.base + 6, self.at(z, 1 - x, False))
        for k in (1, 2, 3):
            for side, cross in ((-k, 7), (k, 10)):
                there = z + side
                valid = there >= 0 if side < 0 else there <= 3

                @pl.when(valid)
                def _():
                    links.arrived(self.base + cross + k - 1, self.at(there, 1 - x, False))

        for index, src, when in self.pending:

            def done():
                links.sent(self.base + index, src)

            if when is None:
                done()
            else:
                pl.when(when)(done)
        self.keep.wait()


def add_rows(out, outs_at, terms, rows):
    def body(i, carry):
        tile = pl.ds(pl.multiple_of(i * 16, 16), 16)
        value = terms[0][tile, :].astype(f32)
        for term in terms[1:]:
            value = value + term[tile, :].astype(f32)
        out[pl.ds(pl.multiple_of(outs_at + i * 16, 16), 16), :] = value.astype(out.dtype)
        return carry

    lax.fori_loop(0, rows // 16, body, 0)


ORDER = ((3, 3, 0, 0), (2, 0, 3, 1), (1, 2, 1, 2), (0, 1, 2, 3))


def turn(order, k):
    return (
        (1 - k) * (2 - k) * (3 - k) // 6 * order[0]
        + k * (2 - k) * (3 - k) // 2 * order[1]
        + k * (k - 1) * (3 - k) // 2 * order[2]
        + k * (k - 1) * (k - 2) // 6 * order[3]
    )


class Scatter:
    SEMS = 15

    def __init__(self, links, total, own, buffers):
        self.links, self.total, self.own = links, total, own
        self.beside, self.kept, self.passed, self.kept2, self.passed2, self.last = buffers
        self.rows = total.shape[0] // (2 * LINE)
        self.bulk = self.rows * BULK // 16
        self.rest = self.rows - self.bulk
        self.base = links.take(self.SEMS)
        self.loads = links.take_local(12)
        low, high = links.z % 2, links.z // 2
        self.order = []
        for c in ORDER:
            self.order.append(
                c[0] + (c[1] - c[0]) * low + (c[2] - c[0]) * high
                + (c[3] - c[1] - c[2] + c[0]) * low * high
            )

    @staticmethod
    def scratch(rows, n):
        bulk = rows * BULK // 16
        rest = rows - bulk
        return [
            pltpu.VMEM((LINE, bulk, n), half),
            pltpu.VMEM((LINE, bulk, n), half),
            pltpu.VMEM((LINE + 1, bulk, n), half),
            pltpu.VMEM((LINE, 2 * rest, n), half),
            pltpu.VMEM((LINE + 1, 2 * rest, n), half),
            pltpu.VMEM((rest, n), half),
        ]

    def block(self, z, x, rest):
        first = (z * 2 + x) * self.rows + (self.bulk if rest else 0)
        return self.total.at[pl.ds(first, self.rest if rest else self.bulk), :]

    def turn(self, k):
        if isinstance(k, int):
            return self.order[k]
        return turn(self.order, k)

    def load(self, k, part):
        links = self.links
        d = self.turn(k)
        if part == 2:
            src, dst = self.block(d, links.x, False), self.kept.at[k]
        else:
            src = self.block(d, part, True)
            dst = self.kept2.at[k, pl.ds(part * self.rest, self.rest), :]
        return pltpu.make_async_copy(src, dst, links.local.at[self.loads + 3 * k + part])

    def start(self):
        for k in range(LINE):
            self.fetch(k)

    def fetch(self, k):
        for part in range(3):
            self.load(k, part).start()

    def aside(self, k):
        links = self.links
        src = self.block(self.turn(k), 1 - links.x, False)
        links.copy(self.base + k, src, self.beside.at[k], links.beside()).start()

    def step(self, k, rest):
        links = self.links
        z = links.z
        d = self.order[k]
        if rest:
            kept, passed, rows, first = self.kept2.at[k], self.passed2, 2 * self.rest, self.base + 9
            self.load(k, 0).wait()
            self.load(k, 1).wait()
            terms = [kept]
        else:
            kept, passed, rows, first = self.kept.at[k], self.passed, self.bulk, self.base + 4
            self.load(k, 2).wait()
            links.arrived(self.base + k, self.beside.at[k])
            terms = [kept, self.beside.at[k]]
        upward = d > z
        carried = (upward & (z > 0)) | ((d < z) & (z < 3))

        @pl.when(carried)
        def _():
            links.arrived(first + d, passed.at[d])
            add_rows(kept, 0, terms + [passed.at[d]], rows)

        if not rest:

            @pl.when(jnp.logical_not(carried))
            def _():
                add_rows(kept, 0, terms, rows)

        @pl.when(upward)
        def _():
            links.copy(first + d, kept, passed.at[d], links.up()).start()

        @pl.when((d < z) & (d < z - 1))
        def _():
            links.copy(first + d, kept, passed.at[d], links.down()).start()

        @pl.when((d < z) & (d == z - 1))
        def _():
            links.copy(first + LINE, kept, passed.at[LINE], links.down()).start()

    def close(self, rest):
        links = self.links
        z, x = links.z, links.x
        k = LINE - 1
        if rest:
            kept, passed, rows, first = self.kept2.at[k], self.passed2, 2 * self.rest, self.base + 9
            self.load(k, 0).wait()
            self.load(k, 1).wait()
            terms, out = [kept], kept
        else:
            kept, passed, rows, first = self.kept.at[k], self.passed, self.bulk, self.base + 4
            self.load(k, 2).wait()
            links.arrived(self.base + k, self.beside.at[k])
            terms, out = [kept, self.beside.at[k]], self.own

        @pl.when(z > 0)
        def _():
            links.arrived(first + z, passed.at[z])

        @pl.when(z < 3)
        def _():
            links.arrived(first + LINE, passed.at[LINE])

        @pl.when(z == 0)
        def _():
            add_rows(out, 0, terms + [passed.at[LINE]], rows)

        @pl.when(z == 3)
        def _():
            add_rows(out, 0, terms + [passed.at[z]], rows)

        @pl.when((z > 0) & (z < 3))
        def _():
            add_rows(out, 0, terms + [passed.at[z], passed.at[LINE]], rows)

        if rest:
            away = kept.at[pl.ds((1 - x) * self.rest, self.rest), :]
            links.copy(self.base + 14, away, self.last, links.beside()).start()

    def finish(self):
        links = self.links
        z, x = links.z, links.x
        links.arrived(self.base + 14, self.last)
        mine = self.kept2.at[LINE - 1, pl.ds(x * self.rest, self.rest), :]
        add_rows(self.own, self.bulk, [mine, self.last], self.rest)
        links.sent(self.base + 14, self.last)
        for k in range(LINE):
            links.sent(self.base + k, self.beside.at[k])
        for k in range(LINE - 1):
            d = self.order[k]
            for kept, first in ((self.kept.at[k], self.base + 4), (self.kept2.at[k], self.base + 9)):

                @pl.when((d > z) | (d < z - 1))
                def _():
                    links.sent(first + d, kept)

                @pl.when(d == z - 1)
                def _():
                    links.sent(first + LINE, kept)


class Total:
    SEMS = 3 * PIECES

    def __init__(self, links, part, out, buffers):
        self.links, self.part, self.out = links, part, out
        self.mine, self.first, self.second = buffers
        self.rows = part.shape[0] // 2 // PIECES
        self.base = links.take(self.SEMS)
        self.loads = links.take_local(2 * PIECES)

    @staticmethod
    def scratch(rows, n):
        return [pltpu.VMEM((PIECES, rows // 2 // PIECES, n), half) for _ in range(3)]

    def at(self, ref, core, j):
        return ref.at[pl.ds((core * PIECES + j) * self.rows, self.rows), :]

    def load(self, j):
        src = self.at(self.part, self.links.core, j)
        return pltpu.make_async_copy(src, self.mine.at[j], self.links.local.at[self.loads + j])

    def store(self, j):
        dst = self.at(self.out, self.links.core, j)
        sem = self.links.local.at[self.loads + PIECES + j]
        return pltpu.make_async_copy(self.first.at[j], dst, sem)

    def start(self):
        links = self.links
        for j in range(PIECES):
            self.load(j).start()
            src = self.at(self.part, 1 - links.core, j)
            links.copy(self.base + j, src, self.first.at[j], links.partner()).start()

    def middle(self):
        links = self.links
        for j in range(PIECES):
            self.load(j).wait()
            links.arrived(self.base + j, self.first.at[j])
            add_rows(self.mine.at[j], 0, [self.mine.at[j], self.first.at[j]], self.rows)
            index = self.base + PIECES + j
            links.copy(index, self.mine.at[j], self.second.at[j], links.across()).start()

    def spread(self):
        links = self.links
        for j in range(PIECES):
            links.arrived(self.base + PIECES + j, self.second.at[j])
            add_rows(self.first.at[j], 0, [self.mine.at[j], self.second.at[j]], self.rows)
            index = self.base + 2 * PIECES + j
            dst = self.at(self.out, links.core, j)
            links.copy(index, self.first.at[j], dst, links.partner()).start()
            self.store(j).start()

    def landed(self):
        links = self.links
        for j in range(PIECES):
            links.arrived(self.base + 2 * PIECES + j, self.at(self.out, 1 - links.core, j))
            self.store(j).wait()

    def finish(self):
        links = self.links
        for j in range(PIECES):
            for stage in range(3):
                links.sent(self.base + stage * PIECES + j, self.mine.at[j])


def exchange(number, shards=(), totals=(), parts=()):
    gathers, scatters, sums = len(shards), len(totals), len(parts)
    scratch = []
    for total in totals:
        scratch += Scatter.scratch(total.shape[0] // (2 * LINE), total.shape[1])
    for part in parts:
        scratch += Total.scratch(part.shape[0], part.shape[1])
    remote = Gather.SEMS * gathers + Scatter.SEMS * scatters + Total.SEMS * sums
    near = gathers + 12 * scatters + 2 * PIECES * sums
    scratch += [
        pltpu.SemaphoreType.DMA((remote,)),
        pltpu.SemaphoreType.DMA((remote,)),
        pltpu.SemaphoreType.DMA((near,)),
    ]

    def kernel(*refs):
        refs = list(refs)

        def pop(count):
            taken, refs[:count] = refs[:count], []
            return taken

        shard_refs, total_refs, part_refs = pop(gathers), pop(scatters), pop(sums)
        full_refs, own_refs, sum_refs = pop(gathers), pop(scatters), pop(sums)
        buffers = [pop(6) for _ in range(scatters)]
        sum_buffers = [pop(3) for _ in range(sums)]
        links = Links(*refs)
        gather = [Gather(links, s, f) for s, f in zip(shard_refs, full_refs)]
        scatter = [Scatter(links, *a) for a in zip(total_refs, own_refs, buffers)]
        total = [Total(links, *a) for a in zip(part_refs, sum_refs, sum_buffers)]
        links.greet()
        for item in gather + scatter + total:
            item.start()
        for k in range(LINE):
            for item in scatter:
                item.aside(k)
        for item in total:
            item.middle()
        for k in range(LINE - 1):
            for item in scatter:
                item.step(k, True)
        for item in scatter:
            item.close(True)
        for item in gather:
            item.bulk_step(1)
        for item in gather:
            item.rest_start()
        for item in scatter:
            item.step(0, False)
        for item in gather:
            item.bulk_step(2)
        for item in gather:
            item.rest_step(1)
        for item in scatter:
            item.step(1, False)
        for item in gather:
            item.bulk_step(3)
        for item in scatter:
            item.step(2, False)
        for item in total:
            item.spread()
        for item in gather:
            item.rest_step(2)
        for item in scatter:
            item.close(False)
        for item in gather:
            item.rest_step(3)
        for item in total:
            item.landed()
        for item in gather + scatter + total:
            item.finish()

    whole = pl.BlockSpec(memory_space=pl.ANY)
    near_spec = pl.BlockSpec(memory_space=pltpu.VMEM)
    outs = pl.pallas_call(
        kernel,
        in_specs=[near_spec] * gathers + [whole] * (scatters + sums),
        out_specs=[whole] * gathers + [near_spec] * scatters + [whole] * sums,
        out_shape=[
            jax.ShapeDtypeStruct((s.shape[0] * 2 * LINE, s.shape[1]), half) for s in shards
        ]
        + [jax.ShapeDtypeStruct((t.shape[0] // (2 * LINE), t.shape[1]), f32) for t in totals]
        + [jax.ShapeDtypeStruct(p.shape, half) for p in parts],
        scratch_shapes=scratch,
        compiler_params=pltpu.CompilerParams(
            collective_id=number, has_side_effects=True, vmem_limit_bytes=60 * 2**20
        ),
        name=f"exchange_{number}",
    )(*shards, *totals, *parts)
    return outs[:gathers], outs[gathers : gathers + scatters], outs[gathers + scatters :]


class Stream:
    def __init__(self, sems, base, arrays, buffers, index):
        self.sems, self.base, self.arrays, self.buffers, self.index = (
            sems, base, arrays, buffers, index,
        )

    def copies(self, i, inward):
        slot = i % 2
        for n, (array, buffer) in enumerate(zip(self.arrays, self.buffers)):
            rows = buffer.shape[1]
            first = pl.multiple_of(self.index(i) * rows, rows)
            far, near = array.at[pl.ds(first, rows), :], buffer.at[slot]
            sem = self.sems.at[self.base + 2 * n + slot]
            src, dst = (far, near) if inward else (near, far)
            yield pltpu.make_async_copy(src, dst, sem)

    def start(self, i, inward):
        for copy in self.copies(i, inward):
            copy.start()

    def wait(self, i, inward):
        for copy in self.copies(i, inward):
            copy.wait()


class Maker:
    STEPS = 2 * LINE

    def __init__(self, links, sems, base, lefts, left_buffers, pairs):
        self.links, self.sems, self.base = links, sems, base
        self.lefts, self.left_buffers, self.pairs = lefts, left_buffers, pairs
        self.rows = left_buffers[0].shape[2]

    @staticmethod
    def sem_count(lefts, pairs):
        return 2 * (lefts + pairs)

    def place(self, j):
        order = self.pairs[0][4].order
        x = self.links.x
        column = 1 - x + (j % 2) * (2 * x - 1)
        return (turn(order, j // 2) * 2 + column) * self.rows

    def moves(self, j):
        first = pl.multiple_of(self.place(j), self.rows)
        slot = j % 2
        for n, (left, buffer) in enumerate(zip(self.lefts, self.left_buffers)):
            yield pltpu.make_async_copy(
                left.at[:, pl.ds(first, self.rows)], buffer.at[slot],
                self.sems.at[self.base + 2 * n + slot],
            )

    def stores(self, j):
        first = pl.multiple_of(self.place(j), self.rows)
        slot = j % 2
        base = self.base + 2 * len(self.lefts)
        for n, (_, _, buffer, total, _) in enumerate(self.pairs):
            yield pltpu.make_async_copy(
                buffer.at[slot], total.at[pl.ds(first, self.rows), :],
                self.sems.at[base + 2 * n + slot],
            )

    def start(self):
        for move in self.moves(0):
            move.start()

    def run(self, between):
        def body(j, state):
            @pl.when(j + 1 < self.STEPS)
            def _():
                for move in self.moves(j + 1):
                    move.start()

            for move in self.moves(j):
                move.wait()
            slot = j % 2
            for which, b, buffer, _, _ in self.pairs:
                left = self.left_buffers[which][slot]
                buffer[slot] = dot(left, b[...], TN).astype(half)
            for store in self.stores(j):
                store.start()

            @pl.when(j >= 1)
            def _():
                for store in self.stores(j - 1):
                    store.wait()

            @pl.when(j % 2 == 1)
            def _():
                for pair in self.pairs:
                    pair[4].aside(j // 2)

            @pl.when((j % 2 == 0) & (j >= 2))
            def _():
                for pair in self.pairs:
                    pair[4].fetch(j // 2 - 1)

            between(j)
            return state

        lax.fori_loop(0, self.STEPS, body, 0)
        for store in self.stores(self.STEPS - 1):
            store.wait()
        for pair in self.pairs:
            pair[4].fetch(LINE - 1)


def row_sum(values):
    return jnp.sum(values, axis=0, keepdims=True)


def attention_back(tile, weights, gains, sums, carry):
    (cot, middle, d_out, tokens, qkv, mixed, outgate, pre, scores, state) = tile
    (w_out, w_qkv, w_gate, w_small, w_decay, span) = weights
    gain_ffn, gain_head = gains
    sum_ffn, sum_head, sum_bias, sum_attn = sums
    unit, scale = rms_parts(middle[...].astype(f32))
    cot = cot[...].astype(f32)
    sum_ffn[...] += row_sum(cot * unit)
    weighted = cot * gain_ffn[...]
    inner = jnp.mean(weighted * unit, axis=-1, keepdims=True)
    d_attn = (d_out[...].astype(f32) + scale * (weighted - unit * inner)).astype(half)
    d_gated = dot(d_attn, w_out[...], NN)
    rows = mixed[...].astype(f32)
    gate = outgate[...].astype(f32)
    head_scale = lax.rsqrt(jnp.mean(rows * rows, axis=-1, keepdims=True) + head_eps)
    head_unit = rows * head_scale
    sig = jax.nn.sigmoid(gate)
    d_outgate = (
        d_gated * head_unit * gain_head[...] * sig * (1.0 + gate * (1.0 - sig))
    ).astype(half)
    d_normed_head = d_gated * gate * sig
    sum_head[...] += row_sum(d_normed_head * head_unit)
    weighted = d_normed_head * gain_head[...]
    inner = jnp.mean(weighted * head_unit, axis=-1, keepdims=True)
    d_mixed = (head_scale * (weighted - head_unit * inner)).astype(half)
    dk = w_decay.shape[1]
    d_qkv, d_pre = backward_math(
        pre[...], qkv[:, :dk], qkv[:, dk : 2 * dk], qkv[:, 2 * dk :], d_mixed,
        scores[...], state[...], span, carry,
    )
    sum_bias[...] += row_sum(d_pre)
    d_pre = d_pre.astype(half)
    d_rank = dot(d_pre, w_decay[...], NT).astype(half)
    d_normed = (
        dot(d_qkv, w_qkv[...], NT) + dot(d_outgate, w_gate[...], NT) + dot(d_rank, w_small[...], NT)
    )
    unit, _ = rms_parts(tokens[...].astype(f32))
    sum_attn[...] += row_sum(d_normed * unit)
    return d_attn, d_outgate, d_qkv, d_pre, d_rank, d_normed.astype(half)


def backward_exchange(number, totals, part, rows_in, weights, gains, left, right):
    scatters = len(totals) + 1
    length, width = part.shape
    count = length // CHUNK
    dk = weights[4].shape[1]
    dv = weights[0].shape[1]
    outs_wide = (width, dv, 2 * dk + dv, dk, 128, width)
    in_shapes = [(CHUNK, width)] + [(a.shape[0] // count, a.shape[1]) for a in rows_in]
    in_types = [half] + [a.dtype for a in rows_in]
    streams = len(in_shapes)
    sum_wide = (width, dv, dk, width)
    made = jax.ShapeDtypeStruct((left.shape[1], right.shape[1]), half)
    rows = made.shape[0] // (2 * LINE)
    scratch = []
    for total in (*totals, made):
        scratch += Scatter.scratch(total.shape[0] // (2 * LINE), total.shape[1])
    scratch += Total.scratch(length, width)
    scratch += [pltpu.VMEM((2,) + s, t) for s, t in zip(in_shapes, in_types)]
    scratch += [pltpu.VMEM((2, CHUNK, w), half) for w in outs_wide]
    scratch += [pltpu.VMEM(w.shape, half) for w in (*weights, right)]
    scratch += [pltpu.VMEM((2, length, rows), half), pltpu.VMEM((2, rows, made.shape[1]), half)]
    scratch += [pltpu.VMEM((dk, dv), f32)]
    remote = Scatter.SEMS * scatters + Total.SEMS
    near = 12 * scatters + 2 * PIECES
    maker_base = 2 * streams + 2 * len(outs_wide) + len(weights) + 1
    extra = maker_base + Maker.sem_count(1, 1)
    scratch += [
        pltpu.SemaphoreType.DMA((remote,)),
        pltpu.SemaphoreType.DMA((remote,)),
        pltpu.SemaphoreType.DMA((near,)),
        pltpu.SemaphoreType.DMA((extra,)),
    ]

    def kernel(*refs):
        refs = list(refs)

        def pop(count):
            taken, refs[:count] = refs[:count], []
            return taken

        total_refs, (part_ref,), row_refs = pop(scatters - 1), pop(1), pop(streams - 1)
        weight_refs, (left_ref, right_ref), gain_refs = pop(len(weights)), pop(2), pop(2)
        own_refs, (sum_ref, made_ref), out_refs, gain_sums = pop(scatters), pop(2), pop(6), pop(4)
        buffers = [pop(6) for _ in range(scatters)]
        sum_buffers = pop(3)
        in_buffers, out_buffers, near_weights = pop(streams), pop(6), pop(len(weights) + 1)
        (left_buffer, made_buffer, carry) = pop(3)
        sems = refs.pop()
        links = Links(*refs)
        scatter = [
            Scatter(links, *a) for a in zip((*total_refs, made_ref), own_refs, buffers)
        ]
        ready, late = scatter[:-1], scatter[-1:]
        total = Total(links, part_ref, sum_ref, sum_buffers)
        inputs = Stream(sems, 0, [sum_ref] + row_refs, in_buffers, lambda i: count - 1 - i)
        outputs = Stream(sems, 2 * streams, out_refs, out_buffers, lambda i: count - 1 - i)
        right_near = near_weights.pop()
        loads = [
            pltpu.make_async_copy(far, close, sems.at[2 * streams + 12 + n])
            for n, (far, close) in enumerate(
                zip((right_ref, *weight_refs), (right_near, *near_weights))
            )
        ]
        maker = Maker(
            links, sems, maker_base, [left_ref], [left_buffer],
            [(0, right_near, made_buffer, made_ref, late[0])],
        )
        links.greet()
        maker.start()
        total.start()
        for k in range(LINE):
            for item in ready:
                item.aside(k)
        for load in loads:
            load.start()
        for item in ready:
            item.start()
        loads[0].wait()

        def between(j):
            @pl.when(j == 1)
            def _():
                total.middle()

            @pl.when(j == 3)
            def _():
                for item in ready:
                    item.step(0, True)

            @pl.when(j == 5)
            def _():
                for item in ready:
                    item.step(1, True)
                    item.step(0, False)

            @pl.when(j == 7)
            def _():
                for item in ready:
                    item.step(2, True)

        maker.run(between)
        for item in ready:
            item.close(True)
            item.step(1, False)
        for k in range(LINE - 1):
            for item in late:
                item.step(k, True)
        for item in ready:
            item.step(2, False)
        for item in late:
            item.close(True)
        total.spread()
        total.landed()
        for load in loads[1:]:
            load.wait()
        for ref in (*gain_sums, carry):
            ref[...] = jnp.zeros_like(ref)
        inputs.start(0, True)

        def body(i, state):
            @pl.when(i + 1 < count)
            def _():
                inputs.start(i + 1, True)

            inputs.wait(i, True)
            slot = i % 2
            results = attention_back(
                [b.at[slot] for b in in_buffers], near_weights, gain_refs, gain_sums, carry
            )

            @pl.when(i >= 2)
            def _():
                outputs.wait(i - 2, False)

            for buffer, value in zip(out_buffers, results):
                buffer[slot] = value
            outputs.start(i, False)

            @pl.when(i == 0)
            def _():
                for item in ready:
                    item.close(False)
                for item in late:
                    item.step(0, False)

            @pl.when(i == 2)
            def _():
                for item in late:
                    item.step(1, False)

            @pl.when(i == 4)
            def _():
                for item in late:
                    item.step(2, False)

            @pl.when(i == 6)
            def _():
                for item in late:
                    item.close(False)

            return state

        lax.fori_loop(0, count, body, 0)
        outputs.wait(count - 2, False)
        outputs.wait(count - 1, False)
        for item in scatter:
            item.finish()
        total.finish()

    whole = pl.BlockSpec(memory_space=pl.ANY)
    near_spec = pl.BlockSpec(memory_space=pltpu.VMEM)
    outs = pl.pallas_call(
        kernel,
        in_specs=[whole] * (scatters + len(rows_in) + len(weights) + 2) + [near_spec] * 2,
        out_specs=[near_spec] * scatters + [whole] * 8 + [near_spec] * 4,
        out_shape=[
            jax.ShapeDtypeStruct((t.shape[0] // (2 * LINE), t.shape[1]), f32)
            for t in (*totals, made)
        ]
        + [jax.ShapeDtypeStruct(part.shape, half), made]
        + [jax.ShapeDtypeStruct((length, w), half) for w in outs_wide]
        + [jax.ShapeDtypeStruct((1, w), f32) for w in sum_wide],
        scratch_shapes=scratch,
        compiler_params=pltpu.CompilerParams(
            collective_id=number, has_side_effects=True, vmem_limit_bytes=VMEM_LIMIT
        ),
        name=f"backward_exchange_{number}",
    )(*totals, part, *rows_in, *weights, left, right, *gains)
    return outs[:scatters], outs[scatters + 2 : scatters + 8], outs[scatters + 8 :]


def last_exchange(number, total, parts, left_up, right_up, left_norm, right_norms, left_out, right_out):
    ups = jax.ShapeDtypeStruct((left_up.shape[1], right_up.shape[1]), half)
    rest = [jax.ShapeDtypeStruct((left_out.shape[1], right_out.shape[1]), half)]
    rest += [jax.ShapeDtypeStruct((left_norm.shape[1], r.shape[1]), half) for r in right_norms]
    made = [ups, *rest]
    rights = [right_up, right_out, *right_norms]
    lefts = [left_up, left_out, left_norm]
    length = left_up.shape[0]
    rows = ups.shape[0] // (2 * LINE)
    scatters, sums = len(made) + 1, len(parts)
    scratch = []
    for item in (*made, total):
        scratch += Scatter.scratch(item.shape[0] // (2 * LINE), item.shape[1])
    for part in parts:
        scratch += Total.scratch(part.shape[0], part.shape[1])
    scratch += [pltpu.VMEM(r.shape, half) for r in rights]
    scratch += [pltpu.VMEM((2, length, rows), half)] * 2
    scratch += [pltpu.VMEM((2, rows, m.shape[1]), half) for m in made]
    remote = Scatter.SEMS * scatters + Total.SEMS * sums
    near = 12 * scatters + 2 * PIECES * sums
    first_count, second_count = Maker.sem_count(1, 1), Maker.sem_count(2, len(rest))
    scratch += [
        pltpu.SemaphoreType.DMA((remote,)),
        pltpu.SemaphoreType.DMA((remote,)),
        pltpu.SemaphoreType.DMA((near,)),
        pltpu.SemaphoreType.DMA((first_count + second_count + len(rights),)),
    ]

    def kernel(*refs):
        refs = list(refs)

        def pop(count):
            taken, refs[:count] = refs[:count], []
            return taken

        (total_ref,), part_refs = pop(1), pop(sums)
        left_refs, right_refs = pop(3), pop(len(rights))
        own_refs, made_refs, sum_refs = pop(scatters), pop(len(made)), pop(sums)
        buffers = [pop(6) for _ in range(scatters)]
        sum_buffers = [pop(3) for _ in range(sums)]
        near_rights, left_buffers, made_buffers = pop(len(rights)), pop(2), pop(len(made))
        sems = refs.pop()
        links = Links(*refs)
        scatter = [Scatter(links, *a) for a in zip((*made_refs, total_ref), own_refs, buffers)]
        up, late, small = scatter[0], scatter[1:], scatter[-1]
        totals = [Total(links, *a) for a in zip(part_refs, sum_refs, sum_buffers)]
        loads = [
            pltpu.make_async_copy(far, close, sems.at[first_count + second_count + n])
            for n, (far, close) in enumerate(zip(right_refs, near_rights))
        ]
        first = Maker(
            links, sems, 0, left_refs[:1], left_buffers[:1],
            [(0, near_rights[0], made_buffers[0], made_refs[0], up)],
        )
        second = Maker(
            links, sems, first_count, left_refs[1:], left_buffers,
            [
                (min(n, 1), near_rights[n + 1], made_buffers[n + 1], made_refs[n + 1], scatter[n + 1])
                for n in range(len(rest))
            ],
        )
        links.greet()
        loads[0].start()
        first.start()
        for item in totals:
            item.start()
        for load in loads[1:]:
            load.start()
        small.start()
        loads[0].wait()

        def between_first(j):
            @pl.when(j == 5)
            def _():
                for item in totals:
                    item.middle()

        first.run(between_first)
        second.start()
        for k in range(LINE):
            small.aside(k)
        up.step(0, True)
        for load in loads[1:]:
            load.wait()

        def between_second(j):
            @pl.when(j == 1)
            def _():
                up.step(1, True)
                up.step(0, False)

            @pl.when(j == 3)
            def _():
                up.step(2, True)

            @pl.when(j == 5)
            def _():
                up.close(True)
                up.step(1, False)

        second.run(between_second)
        for item in late:
            item.step(0, True)
        up.step(2, False)
        for item in late:
            item.step(1, True)
        up.close(False)
        for item in late:
            item.step(2, True)
        for item in late:
            item.step(0, False)
        for item in late:
            item.close(True)
        for item in late:
            item.step(1, False)
        totals[0].spread()
        for item in late:
            item.step(2, False)
        for item in totals[1:]:
            item.spread()
        for item in late:
            item.close(False)
        for item in totals:
            item.landed()
        for item in scatter + totals:
            item.finish()

    whole = pl.BlockSpec(memory_space=pl.ANY)
    near_spec = pl.BlockSpec(memory_space=pltpu.VMEM)
    outs = pl.pallas_call(
        kernel,
        in_specs=[whole] * (1 + sums + 3 + len(rights)),
        out_specs=[near_spec] * scatters + [whole] * (len(made) + sums),
        out_shape=[
            jax.ShapeDtypeStruct((t.shape[0] // (2 * LINE), t.shape[1]), f32)
            for t in (*made, total)
        ]
        + made
        + [jax.ShapeDtypeStruct(p.shape, half) for p in parts],
        scratch_shapes=scratch,
        compiler_params=pltpu.CompilerParams(
            collective_id=number, has_side_effects=True, vmem_limit_bytes=VMEM_LIMIT
        ),
        name=f"last_exchange_{number}",
    )(total, *parts, *lefts, *rights)
    return outs[:scatters], outs[scatters + len(made) :]


class Ring:
    def __init__(self, size):
        self.size = size
        self.wide = size // LINE
        place = lax.axis_index("dp")
        self.z = place // self.wide
        self.x = place % self.wide

    def z_pairs(self, step):
        wide = self.wide
        return [
            (z * wide + x, ((z + step) % LINE) * wide + x) for z in range(LINE) for x in range(wide)
        ]

    def x_pairs(self, step):
        wide = self.wide
        return [(z * wide + x, z * wide + (x + step) % wide) for z in range(LINE) for x in range(wide)]


def gather(ring, shard):
    rows = shard.shape[0]
    pieces = [(ring.z, shard)]
    for step in (1, 3, 2):
        pieces.append(((ring.z - step) % LINE, lax.ppermute(shard, "dp", ring.z_pairs(step))))
    out = jnp.zeros((ring.size * rows, shard.shape[1]), shard.dtype)
    for z, piece in pieces:
        for step in range(ring.wide):
            moved = lax.ppermute(piece, "dp", ring.x_pairs(step)) if step else piece
            place = z * ring.wide + (ring.x - step) % ring.wide
            out = lax.dynamic_update_slice(out, moved, (place * rows, 0))
    return out


def scatter(ring, total):
    rows = total.shape[0] // ring.size

    def block(z, x):
        place = (z % LINE) * ring.wide + x % ring.wide
        return lax.dynamic_slice(total, (place * rows, 0), (rows, total.shape[1]))

    result = None
    for step in (2, 1, 3, 0):
        z = ring.z + step
        kept = block(z, ring.x).astype(f32)
        for side in range(1, ring.wide):
            away = lax.ppermute(block(z, ring.x + side), "dp", ring.x_pairs(side))
            kept = kept + away.astype(f32)
        if step:
            kept = lax.ppermute(kept.astype(half), "dp", ring.z_pairs(step)).astype(f32)
        result = kept if result is None else result + kept
    return result


CORE = [(i, i ^ 1) for i in range(4)]
ACROSS = [(i, i ^ 2) for i in range(4)]


def tensor_sum(part):
    rows = part.shape[0] // 2
    second = (lax.axis_index("tensor") & 1) == 1
    upper, lower = part[:rows], part[rows:]
    mine = jnp.where(second, lower, upper)
    away = jnp.where(second, upper, lower)
    mine = (mine.astype(f32) + lax.ppermute(away, "tensor", CORE).astype(f32)).astype(half)
    mine = (mine.astype(f32) + lax.ppermute(mine, "tensor", ACROSS).astype(f32)).astype(half)
    theirs = lax.ppermute(mine, "tensor", CORE)
    return jnp.concatenate(
        [jnp.where(second, theirs, mine), jnp.where(second, mine, theirs)], axis=0
    )


def rms_parts(values):
    scale = lax.rsqrt(jnp.mean(values * values, axis=-1, keepdims=True) + norm_eps)
    return values * scale, scale


def rms_back(unit, scale, gain, cot):
    weighted = cot * gain
    inner = jnp.mean(weighted * unit, axis=-1, keepdims=True)
    return scale * (weighted - unit * inner), jnp.sum(cot * unit, axis=0)


def gated_rows(mixed, outgate, gain):
    scale = lax.rsqrt(jnp.mean(mixed * mixed, axis=-1, keepdims=True) + head_eps)
    return mixed * scale * gain * jax.nn.silu(outgate)


def local(
    tokens, lengths, norm_attn, query_proj, key_proj, value_proj, outgate_proj, rank_proj,
    decay_proj, decay_bias, head_gain, out_proj, norm_ffn, gate_proj, up_proj, down_proj, cotangent,
    *, size,
):
    ring = Ring(size)
    rows_total = tokens.shape[0]
    width = norm_attn.shape[0]
    rank = rank_proj.shape[1]
    dk = query_proj.shape[1]
    dv = value_proj.shape[1]
    ff = gate_proj.shape[1]
    bits = decay_proj.shape[2]
    gains = head_gain.shape[0]

    def as_column(values):
        flat = values.reshape(-1, 1)
        return jnp.pad(flat, ((0, width - flat.shape[0]), (0, 0)))

    decay_cols = rank * bits // width
    small = jnp.concatenate(
        [
            rank_proj,
            norm_attn[:, None],
            norm_ffn[:, None],
            as_column(head_gain),
            as_column(decay_bias),
            decay_proj.reshape(decay_cols, width).T,
        ],
        axis=1,
    )
    small = jnp.pad(small, ((0, 0), (0, 128 - small.shape[1]))).astype(half)
    qkv = jnp.concatenate([query_proj * 0.0625, key_proj, value_proj], axis=1).astype(half)
    first = (qkv, small, outgate_proj.astype(half), out_proj.T.astype(half))
    second = (gate_proj.astype(half), up_proj.astype(half), down_proj.T.astype(half))
    fast = size == 2 * LINE

    def collect(number, shards, parts):
        if fast:
            fulls, _, sums = exchange(number, shards, (), parts)
            return fulls, sums
        return [gather(ring, s) for s in shards], [tensor_sum(p) for p in parts]

    def deliver(number, totals, parts):
        if fast:
            _, owns, sums = exchange(number, (), totals, parts)
            return owns, sums
        return [scatter(ring, t) for t in totals], [tensor_sum(p) for p in parts]

    (qkv_full, small_full, outgate_full, out_full), _ = collect(0, first, ())
    rank_full = small_full[:, :rank]
    small32 = small_full.astype(f32)
    gain_attn = small32[:, rank]
    gain_ffn = small32[:, rank + 1]
    by_place = small32.reshape(size, width, 128)
    gain_head = by_place[:, :gains, rank + 2].reshape(-1)
    bias = by_place[:, :bits, rank + 3].reshape(-1)
    decay_weight = jnp.transpose(
        jnp.transpose(by_place[:, :, rank + 4 : rank + 4 + decay_cols], (0, 2, 1)).reshape(
            size, rank, bits
        ),
        (1, 0, 2),
    ).reshape(rank, -1)

    positions = jnp.arange(SEQ_LEN, dtype=jnp.int32)
    mask = (positions[None, :] < lengths[:, None]).astype(f32).reshape(rows_total, 1)
    tokens32 = tokens.astype(f32)
    unit, scale = rms_parts(tokens32)
    normed = (unit * gain_attn).astype(half)
    qkv = dot(normed, qkv_full, NN).astype(half)
    rank_rows = dot(normed, rank_full, NN)
    pre = (
        jnp.dot(rank_rows, decay_weight, precision=highest_precision, preferred_element_type=f32)
        + bias
    )
    span = span_matrix()
    mixed, scores, states = recur_forward(pre, qkv, span, dk, dv)
    outgate = dot(normed, outgate_full, NN).astype(half)
    gated, pull_gated = jax.vjp(gated_rows, mixed.astype(f32), outgate.astype(f32), gain_head)
    gated = gated.astype(half)
    (gate_full, up_full, down_full), (attn,) = collect(
        1, second, (dot(gated, out_full, NT).astype(half),)
    )
    middle = tokens32 + attn.astype(f32)
    unit_ffn, scale_ffn = rms_parts(middle)
    normed_ffn = (unit_ffn * gain_ffn).astype(half)
    gate_rows = dot(normed_ffn, gate_full, NN)
    up_rows = dot(normed_ffn, up_full, NN)
    hidden, pull_glu = jax.vjp(lambda g, u: jax.nn.silu(g) * u, gate_rows, up_rows)
    hidden = hidden.astype(half)
    d_out = cotangent.astype(f32) * mask
    d_out_half = d_out.astype(half)
    grad_down = dot(d_out_half, hidden, TN).astype(half)
    d_gate, d_up = pull_glu(dot(d_out_half, down_full, NN))
    d_gate = d_gate.astype(half)
    d_up = d_up.astype(half)
    d_normed_ffn = (dot(d_gate, gate_full, NT) + dot(d_up, up_full, NT)).astype(half)
    ffn = dot(hidden, down_full, NT).astype(half)
    if fast:
        w_decay = jnp.pad(decay_weight, ((0, 128 - rank), (0, 0))).astype(half)
        (down_own, gate_own), outs, sums = backward_exchange(
            2,
            (grad_down,),
            d_normed_ffn,
            (
                middle.astype(half), d_out_half, tokens, qkv, mixed, outgate, pre, scores,
                states.reshape(-1, dv),
            ),
            (out_full, qkv_full, outgate_full, small_full, w_decay, span),
            (gain_ffn[None, :], gain_head[None, :]),
            normed_ffn,
            d_gate,
        )
        d_attn, d_outgate, d_qkv, d_pre_half, d_rank, d_normed = outs
        grad_gain_ffn, grad_head, grad_bias, grad_gain_attn = sums
        d_middle = d_attn.astype(f32)
        d_rank = d_rank[:, :rank]
    else:
        d_normed_ffn = tensor_sum(d_normed_ffn)
        d_back, grad_gain_ffn = rms_back(unit_ffn, scale_ffn, gain_ffn, d_normed_ffn.astype(f32))
        d_middle = d_out + d_back
        d_attn = d_middle.astype(half)
        d_mixed, d_outgate, grad_head = pull_gated(dot(d_attn, out_full, NN))
        d_outgate = d_outgate.astype(half)
        d_qkv, d_pre = recur_backward(pre, qkv, d_mixed.astype(half), scores, states, span, dk, dv)
        d_rank = dot(d_pre.astype(half), decay_weight.astype(half), NT).astype(half)
        d_normed = (
            dot(d_qkv, qkv_full, NT) + dot(d_outgate, outgate_full, NT) + dot(d_rank, rank_full, NT)
        )
        grad_gain_attn = jnp.sum(d_normed * unit, axis=0)
        d_normed = d_normed.astype(half)
        d_pre_half = d_pre.astype(half)
        grad_bias = jnp.sum(d_pre, axis=0)
    grad_rank = dot(normed, d_rank, TN)
    grad_decay = jnp.transpose(
        dot(rank_rows.astype(half), d_pre_half, TN).reshape(rank, size, bits), (1, 0, 2)
    ).reshape(size, decay_cols, width)

    def spread(values):
        blocks = values.reshape(size, -1, 1)
        return jnp.pad(blocks, ((0, 0), (0, width - blocks.shape[1]), (0, 0)))

    grad_small = jnp.concatenate(
        [
            grad_rank.reshape(size, width, rank),
            grad_gain_attn.reshape(size, width, 1),
            grad_gain_ffn.reshape(size, width, 1),
            spread(grad_head),
            spread(grad_bias),
            jnp.transpose(grad_decay, (0, 2, 1)),
        ],
        axis=2,
    )
    grad_small = jnp.pad(grad_small, ((0, 0), (0, 0), (0, 128 - grad_small.shape[2])))
    grad_small = grad_small.reshape(size * width, 128).astype(half)

    if fast:
        (up_own, out_own, outgate_own, qkv_own, small_own), (d_normed, ffn) = last_exchange(
            3, grad_small, (d_normed, ffn), normed_ffn, d_up, normed, (d_outgate, d_qkv), d_attn, gated
        )
    else:
        waiting = (
            grad_down,
            dot(normed_ffn, d_gate, TN).astype(half),
            dot(normed_ffn, d_up, TN).astype(half),
            dot(d_attn, gated, TN).astype(half),
            dot(normed, d_outgate, TN).astype(half),
            dot(normed, d_qkv, TN).astype(half),
            grad_small,
        )
        (down_own, gate_own, up_own, out_own, outgate_own, qkv_own, small_own), (
            d_normed, ffn,
        ) = deliver(3, waiting, (d_normed, ffn))
    output = (mask * (middle + ffn.astype(f32))).astype(half)
    d_back, _ = rms_back(unit, scale, gain_attn, d_normed.astype(f32))
    grad_tokens = (d_middle + d_back).astype(half)
    heads_own = small_own.astype(half)
    heads_own = heads_own.astype(f32) + lax.ppermute(heads_own, "tensor", CORE).astype(f32)
    heads_own = heads_own.astype(half)
    heads_own = heads_own.astype(f32) + lax.ppermute(heads_own, "tensor", ACROSS).astype(f32)
    return (
        output,
        grad_tokens,
        heads_own[:, rank],
        qkv_own[:, :dk] * 0.0625,
        qkv_own[:, dk : 2 * dk],
        qkv_own[:, 2 * dk : 2 * dk + dv],
        outgate_own,
        heads_own[:, :rank],
        small_own[:, rank + 4 : rank + 4 + decay_cols].T.reshape(decay_proj.shape),
        small_own[:bits, rank + 3].reshape(decay_bias.shape),
        heads_own[:gains, rank + 2],
        out_own.T,
        heads_own[:, rank + 1] * 0.25,
        gate_own,
        up_own,
        down_own.T,
    )


def solution(mesh):
    size = mesh.shape["dp"]

    def run(*args):
        return local(*args, size=size)

    weight = P("dp", "tensor")
    cross = P("tensor", "dp")
    return jax.shard_map(
        run,
        mesh=mesh,
        in_specs=(
            P("dp", None), P("dp"), P("dp"), weight, weight, weight, weight, P("dp", None),
            P(None, "tensor", "dp"), cross, P("dp"), cross, P("dp"), weight, weight, cross,
            P("dp", None),
        ),
        out_specs=(
            P("dp", None), P("dp", None), P("dp"), weight, weight, weight, weight, P("dp", None),
            P(None, "tensor", "dp"), cross, P("dp"), cross, P("dp"), weight, weight, cross,
        ),
        check_vma=False,
    )
```

```python
import jax
import jax.numpy as jnp
from jax import lax
from jax.experimental import pallas as pl
from jax.experimental.pallas import tpu as pltpu
from jax.sharding import PartitionSpec as P

SEQ_LEN = 1024
LINE = 4

norm_eps = 1e-06
head_eps = 1.0
highest_precision = lax.Precision.HIGHEST
half = jnp.bfloat16
f32 = jnp.float32
CHUNK = 128


def level_count():
    return CHUNK.bit_length() - 1


def span_matrix():
    rows = lax.broadcasted_iota(jnp.int32, (CHUNK, CHUNK), 0)
    cols = lax.broadcasted_iota(jnp.int32, (CHUNK, CHUNK), 1)
    parts = []
    for level in range(level_count()):
        size = 1 << level
        middle = (rows // (2 * size)) * (2 * size) + size
        right = rows >= middle
        parts.append(
            jnp.where(right, (cols >= middle) & (cols <= rows), (cols > rows) & (cols < middle))
        )
    parts.append(cols <= rows)
    parts.append(cols > rows)
    stacked = jnp.concatenate(parts, axis=0).astype(half)
    return jnp.concatenate([stacked, stacked], axis=1)


def dot(left, right, dims):
    return lax.dot_general(left, right, (dims, ((), ())), preferred_element_type=f32)


NN = ((1,), (0,))
NT = ((1,), (1,))
TN = ((0,), (0,))


def log_decay(pre):
    return (jnp.minimum(pre, 0.0) - jnp.log1p(jnp.exp(-jnp.abs(pre)))) * (1.0 / 16.0)


def split_two(values):
    high = values.astype(half)
    low = (values - high.astype(f32)).astype(half)
    return jnp.concatenate([high, low], axis=0)


def level_parts(level):
    rows = lax.broadcasted_iota(jnp.int32, (CHUNK, CHUNK), 0)
    cols = lax.broadcasted_iota(jnp.int32, (CHUNK, CHUNK), 1)
    return rows, cols, (lax.shift_right_logical(rows ^ cols, level) == 1)


def forward_math(pre, q, k, v, span_ref, state):
    decay = log_decay(pre)
    sums = dot(span_ref[...], split_two(decay), NN)
    q32 = q.astype(f32)
    k32 = k.astype(f32)
    rows, cols, _ = level_parts(0)
    scores = jnp.where(rows == cols, dot(q, k, NT), 0.0)
    row_ids = lax.broadcasted_iota(jnp.int32, q.shape, 0)
    for level in range(level_count()):
        right = (lax.shift_right_logical(row_ids, level) & 1) == 1
        grow = jnp.exp(sums[level * CHUNK : (level + 1) * CHUNK])
        mixed_rows = (jnp.where(right, q32, k32) * grow).astype(half)
        pair = level_parts(level)[2] & (rows > cols)
        scores = jnp.where(pair, dot(mixed_rows, mixed_rows, NT), scores)
    levels = level_count()
    head_sum = sums[levels * CHUNK : (levels + 1) * CHUNK]
    tail_sum = sums[(levels + 1) * CHUNK :]
    q_in = (q32 * jnp.exp(head_sum)).astype(half)
    k_out = (k32 * jnp.exp(tail_sum)).astype(half)
    score_half = scores.astype(half)
    state_now = state[...]
    state_half = state_now.astype(half)
    mixed = dot(score_half, v, NN) + dot(q_in, state_half, NN)
    whole = jnp.exp(jnp.transpose(head_sum[CHUNK - 8 :, :]))[:, 7:8]
    state[...] = whole * state_now + dot(k_out, v, TN)
    return mixed.astype(half), score_half, state_half


def forward_body(pre_ref, q_ref, k_ref, v_ref, span_ref, mixed_ref, score_ref, state_ref, state):
    @pl.when(pl.program_id(0) == 0)
    def _():
        state[...] = jnp.zeros_like(state)

    mixed_ref[...], score_ref[...], state_ref[0] = forward_math(
        pre_ref[...], q_ref[...], k_ref[...], v_ref[...], span_ref, state
    )


def backward_math(pre, q, k, v, d_mixed, scores, state_half, span_ref, carry):
    levels = level_count()
    decay = log_decay(pre)
    sums = dot(span_ref[...], split_two(decay), NN)
    q32 = q.astype(f32)
    k32 = k.astype(f32)
    carry_now = carry[...]
    carry_half = carry_now.astype(half)
    rows, cols, _ = level_parts(0)
    row_ids = lax.broadcasted_iota(jnp.int32, q.shape, 0)
    d_scores = dot(d_mixed, v, NT)
    diagonal = jnp.where(rows == cols, d_scores, 0.0)
    sym = jnp.where(rows > cols, d_scores, jnp.transpose(d_scores))
    diag_col = jnp.sum(diagonal, axis=1, keepdims=True)
    dq = diag_col * k32
    dk = diag_col * q32
    pieces = []
    for level in range(levels):
        right = (lax.shift_right_logical(row_ids, level) & 1) == 1
        grow = jnp.exp(sums[level * CHUNK : (level + 1) * CHUNK])
        scaled = jnp.where(right, q32, k32) * grow
        block = jnp.where(level_parts(level)[2], sym, 0.0).astype(half)
        back = dot(block, scaled.astype(half), NN)
        pieces.append((scaled * back).astype(half))
        grown = grow * back
        dq = dq + jnp.where(right, grown, 0.0)
        dk = dk + jnp.where(right, 0.0, grown)
    head_sum = sums[levels * CHUNK : (levels + 1) * CHUNK]
    tail_sum = sums[(levels + 1) * CHUNK :]
    head_grow = jnp.exp(head_sum)
    tail_grow = jnp.exp(tail_sum)
    q_in = q32 * head_grow
    k_out = k32 * tail_grow
    k_out_half = k_out.astype(half)
    back_q = dot(d_mixed, state_half, NT)
    back_k = dot(v, carry_half, NT)
    pieces.append((q_in * back_q).astype(half))
    pieces.append((k_out * back_k).astype(half))
    dq = dq + head_grow * back_q
    dk = dk + tail_grow * back_k
    dv = dot(scores, d_mixed, TN) + dot(k_out_half, carry_half, NN)
    d_qkv = jnp.concatenate([dq.astype(half), dk.astype(half), dv.astype(half)], axis=1)
    whole = jnp.exp(jnp.transpose(head_sum[CHUNK - 8 :, :]))[:, 7:8]
    end_col = whole * jnp.sum(state_half.astype(f32) * carry_now, axis=1, keepdims=True)
    end_row = jnp.transpose(jnp.broadcast_to(end_col, (end_col.shape[0], 128)))[0:1, :]
    d_decay = dot(span_ref[:, :CHUNK], jnp.concatenate(pieces, axis=0), TN) + end_row
    carry[...] = whole * carry_now + dot(q_in.astype(half), d_mixed, TN)
    return d_qkv, d_decay * (jax.nn.sigmoid(-pre) * (1.0 / 16.0))


def backward_body(
    pre_ref, q_ref, k_ref, v_ref, d_ref, score_ref, state_ref, span_ref,
    dqkv_ref, dpre_ref, carry,
):
    @pl.when(pl.program_id(0) == 0)
    def _():
        carry[...] = jnp.zeros_like(carry)

    dqkv_ref[...], dpre_ref[...] = backward_math(
        pre_ref[...], q_ref[...], k_ref[...], v_ref[...], d_ref[...], score_ref[...],
        state_ref[0], span_ref, carry,
    )


def recur_forward(pre, qkv, span, dk, dv):
    length = qkv.shape[0]
    count = length // CHUNK

    def row(wide, place=0):
        return pl.BlockSpec((CHUNK, wide), lambda i: (i, place))

    return pl.pallas_call(
        forward_body,
        grid=(count,),
        in_specs=[
            row(dk), row(dk, 0), row(dk, 1), row(dv, 2 * dk // dv),
            pl.BlockSpec(span.shape, lambda i: (0, 0)),
        ],
        out_specs=[row(dv), row(CHUNK), pl.BlockSpec((1, dk, dv), lambda i: (i, 0, 0))],
        out_shape=[
            jax.ShapeDtypeStruct((length, dv), half),
            jax.ShapeDtypeStruct((length, CHUNK), half),
            jax.ShapeDtypeStruct((count, dk, dv), half),
        ],
        scratch_shapes=[pltpu.VMEM((dk, dv), f32)],
        compiler_params=pltpu.CompilerParams(dimension_semantics=("arbitrary",)),
        cost_estimate=pl.CostEstimate(
            flops=6 * 10**9, bytes_accessed=8 * 2**20, transcendentals=2 * 2**20
        ),
        name="recur_forward",
    )(pre, qkv, qkv, qkv, span)


def recur_backward(pre, qkv, d_mixed, scores, states, span, dk, dv):
    length = qkv.shape[0]
    count = length // CHUNK

    def row(wide, place=0):
        return pl.BlockSpec((CHUNK, wide), lambda i: (count - 1 - i, place))

    return pl.pallas_call(
        backward_body,
        grid=(count,),
        in_specs=[
            row(dk), row(dk, 0), row(dk, 1), row(dv, 2 * dk // dv), row(dv), row(CHUNK),
            pl.BlockSpec((1, dk, dv), lambda i: (count - 1 - i, 0, 0)),
            pl.BlockSpec(span.shape, lambda i: (0, 0)),
        ],
        out_specs=[row(2 * dk + dv), row(dk)],
        out_shape=[
            jax.ShapeDtypeStruct((length, 2 * dk + dv), half),
            jax.ShapeDtypeStruct((length, dk), f32),
        ],
        scratch_shapes=[pltpu.VMEM((dk, dv), f32)],
        compiler_params=pltpu.CompilerParams(dimension_semantics=("arbitrary",)),
        cost_estimate=pl.CostEstimate(
            flops=8 * 10**9, bytes_accessed=10 * 2**20, transcendentals=2 * 2**20
        ),
        name="recur_backward",
    )(pre, qkv, qkv, qkv, d_mixed, scores, states, span)

MESH = pl.DeviceIdType.MESH
BULK = 13
PIECES = 4
VMEM_LIMIT = 63 * 2**20


class Links:
    def __init__(self, send, recv, local):
        place = lax.axis_index("dp")
        self.z = place // 2
        self.x = place % 2
        self.t = lax.axis_index("tensor")
        self.core = self.t % 2
        self.send, self.recv, self.local = send, recv, local
        self.count = 0
        self.local_count = 0

    def take(self, number=1):
        first = self.count
        self.count += number
        return first

    def take_local(self, number=1):
        first = self.local_count
        self.local_count += number
        return first

    def beside(self):
        return {"dp": self.z * 2 + 1 - self.x}

    def up(self):
        return {"dp": self.z * 2 + 2 + self.x}

    def down(self):
        return {"dp": self.z * 2 - 2 + self.x}

    def partner(self):
        return {"tensor": self.t + 1 - 2 * self.core}

    def across(self):
        return {"tensor": (self.t + 2) % 4}

    def greet(self):
        barrier = pltpu.get_barrier_semaphore()
        around = [{"dp": ((self.z + step) % LINE) * 2 + self.x} for step in (1, 3)]
        for other in (*around, self.beside(), self.partner(), self.across()):
            pl.semaphore_signal(barrier, inc=1, device_id=other, device_id_type=MESH)
        pl.semaphore_wait(barrier, 5)

    def copy(self, index, src, dst, target):
        return pltpu.make_async_remote_copy(
            src_ref=src,
            dst_ref=dst,
            send_sem=self.send.at[index],
            recv_sem=self.recv.at[index],
            device_id=target,
            device_id_type=MESH,
        )

    def arrived(self, index, dst):
        self.copy(index, dst, dst, self.beside()).wait_recv()

    def sent(self, index, src):
        self.copy(index, src, src, self.beside()).wait_send()


class Gather:
    SEMS = 26

    def __init__(self, links, shard, full):
        self.links, self.shard, self.full = links, shard, full
        self.rows = shard.shape[0]
        self.bulk = self.rows * BULK // 16
        self.base = links.take(self.SEMS)
        self.own_sem = links.take_local()
        self.pending = []

    def at(self, z, x, rest):
        first = (z * 2 + x) * self.rows + (self.bulk if rest else 0)
        return self.full.at[pl.ds(first, self.rows - self.bulk if rest else self.bulk), :]

    def mine(self, rest):
        if rest:
            return self.shard.at[pl.ds(self.bulk, self.rows - self.bulk), :]
        return self.shard.at[pl.ds(0, self.bulk), :]

    def go(self, index, rest, src, dst, target, when=None):
        links = self.links

        def start():
            links.copy(self.base + index, src, dst, target).start()

        if when is None:
            start()
        else:
            pl.when(when())(start)
        self.pending.append((index, rest, when))

    def keep(self):
        links = self.links
        own = self.full.at[pl.ds((links.z * 2 + links.x) * self.rows, self.rows), :]
        return pltpu.make_async_copy(self.shard, own, links.local.at[self.own_sem])

    def there(self, side):
        place = self.links.z + side
        return place >= 0 if side < 0 else place <= LINE - 1

    def onward(self, side):
        z = self.links.z
        more = z < LINE - 1 if side <= 0 else z > 0
        return self.there(side) & more

    def start(self):
        links = self.links
        z, x = links.z, links.x
        self.keep().start()
        own, rest = self.mine(False), self.mine(True)
        self.go(0, False, own, self.at(z, x, False), links.up(), lambda: z < LINE - 1)
        self.go(3, False, own, self.at(z, x, False), links.down(), lambda: z > 0)
        self.go(13, True, rest, self.at(z, x, True), links.beside())
        self.go(6, False, own, self.at(z, x, False), links.beside())

    def bulk_step(self, k):
        links = self.links
        z, x = links.z, links.x
        for side, base, cross, target in ((-k, 0, 7, links.up()), (k, 3, 10, links.down())):
            piece = self.at(z + side, x, False)

            @pl.when(self.there(side))
            def _():
                links.arrived(self.base + base + k - 1, piece)

            if k < 3:
                self.go(base + k, False, piece, piece, target, lambda side=side: self.onward(side))
            self.go(
                cross + k - 1, False, piece, piece, links.beside(), lambda side=side: self.there(side)
            )

    def rest_start(self):
        links = self.links
        z, x = links.z, links.x
        other = self.at(z, 1 - x, True)
        links.arrived(self.base + 13, other)
        mine = self.mine(True)
        for index, src, dst in ((14, mine, self.at(z, x, True)), (15, other, other)):
            self.go(index, True, src, dst, links.up(), lambda: z < LINE - 1)
            self.go(index + 6, True, src, dst, links.down(), lambda: z > 0)

    def rest_step(self, k):
        links = self.links
        z, x = links.z, links.x
        for side, base, target in ((-k, 14, links.up()), (k, 20, links.down())):
            for which in range(2):
                piece = self.at(z + side, x if which == 0 else 1 - x, True)

                @pl.when(self.there(side))
                def _():
                    links.arrived(self.base + base + 2 * (k - 1) + which, piece)

                if k < 3:
                    self.go(
                        base + 2 * k + which, True, piece, piece, target,
                        lambda side=side: self.onward(side),
                    )

    def finish(self):
        self.landed()
        self.drain()

    def landed(self):
        links = self.links
        z, x = links.z, links.x
        links.arrived(self.base + 6, self.at(z, 1 - x, False))
        for k in (1, 2, 3):
            for side, cross in ((-k, 7), (k, 10)):
                there = z + side
                valid = there >= 0 if side < 0 else there <= 3

                @pl.when(valid)
                def _():
                    links.arrived(self.base + cross + k - 1, self.at(there, 1 - x, False))

        self.keep().wait()

    def drain(self):
        links = self.links
        for index, rest, when in self.pending:

            def done():
                links.sent(self.base + index, self.mine(rest))

            if when is None:
                done()
            else:
                pl.when(when())(done)


def add_rows(out, outs_at, terms, rows):
    def body(i, carry):
        tile = pl.ds(pl.multiple_of(i * 16, 16), 16)
        value = terms[0][tile, :].astype(f32)
        for term in terms[1:]:
            value = value + term[tile, :].astype(f32)
        out[pl.ds(pl.multiple_of(outs_at + i * 16, 16), 16), :] = value.astype(out.dtype)
        return carry

    lax.fori_loop(0, rows // 16, body, 0)


ORDER = ((3, 3, 0, 0), (2, 0, 3, 1), (1, 2, 1, 2), (0, 1, 2, 3))


def turn(order, k):
    return (
        (1 - k) * (2 - k) * (3 - k) // 6 * order[0]
        + k * (2 - k) * (3 - k) // 2 * order[1]
        + k * (k - 1) * (3 - k) // 2 * order[2]
        + k * (k - 1) * (k - 2) // 6 * order[3]
    )


class Scatter:
    SEMS = 15

    def __init__(self, links, total, own, buffers):
        self.links, self.total, self.own = links, total, own
        self.beside, self.kept, self.passed, self.kept2, self.passed2, self.last = buffers
        self.rows = total.shape[0] // (2 * LINE)
        self.bulk = self.rows * BULK // 16
        self.rest = self.rows - self.bulk
        self.base = links.take(self.SEMS)
        self.loads = links.take_local(12)
        low, high = links.z % 2, links.z // 2
        self.order = []
        for c in ORDER:
            self.order.append(
                c[0] + (c[1] - c[0]) * low + (c[2] - c[0]) * high
                + (c[3] - c[1] - c[2] + c[0]) * low * high
            )

    @staticmethod
    def scratch(rows, n):
        bulk = rows * BULK // 16
        rest = rows - bulk
        return [
            pltpu.VMEM((LINE, bulk, n), half),
            pltpu.VMEM((LINE, bulk, n), half),
            pltpu.VMEM((LINE + 1, bulk, n), half),
            pltpu.VMEM((LINE, 2 * rest, n), half),
            pltpu.VMEM((LINE + 1, 2 * rest, n), half),
            pltpu.VMEM((rest, n), half),
        ]

    def block(self, z, x, rest):
        first = (z * 2 + x) * self.rows + (self.bulk if rest else 0)
        return self.total.at[pl.ds(first, self.rest if rest else self.bulk), :]

    def turn(self, k):
        if isinstance(k, int):
            return self.order[k]
        return turn(self.order, k)

    def load(self, k, part):
        links = self.links
        d = self.turn(k)
        if part == 2:
            src, dst = self.block(d, links.x, False), self.kept.at[k]
        else:
            src = self.block(d, part, True)
            dst = self.kept2.at[k, pl.ds(part * self.rest, self.rest), :]
        return pltpu.make_async_copy(src, dst, links.local.at[self.loads + 3 * k + part])

    def start(self):
        for k in range(LINE):
            self.fetch(k)

    def fetch(self, k):
        for part in range(3):
            self.load(k, part).start()

    def aside(self, k):
        links = self.links
        src = self.block(self.turn(k), 1 - links.x, False)
        links.copy(self.base + k, src, self.beside.at[k], links.beside()).start()

    def step(self, k, rest):
        links = self.links
        z = links.z
        d = self.order[k]
        if rest:
            kept, passed, rows, first = self.kept2.at[k], self.passed2, 2 * self.rest, self.base + 9
            self.load(k, 0).wait()
            self.load(k, 1).wait()
            terms = [kept]
        else:
            kept, passed, rows, first = self.kept.at[k], self.passed, self.bulk, self.base + 4
            self.load(k, 2).wait()
            links.arrived(self.base + k, self.beside.at[k])
            terms = [kept, self.beside.at[k]]
        upward = d > z
        carried = (upward & (z > 0)) | ((d < z) & (z < 3))

        @pl.when(carried)
        def _():
            links.arrived(first + d, passed.at[d])
            add_rows(kept, 0, terms + [passed.at[d]], rows)

        if not rest:

            @pl.when(jnp.logical_not(carried))
            def _():
                add_rows(kept, 0, terms, rows)

        @pl.when(upward)
        def _():
            links.copy(first + d, kept, passed.at[d], links.up()).start()

        @pl.when((d < z) & (d < z - 1))
        def _():
            links.copy(first + d, kept, passed.at[d], links.down()).start()

        @pl.when((d < z) & (d == z - 1))
        def _():
            links.copy(first + LINE, kept, passed.at[LINE], links.down()).start()

    def close(self, rest):
        links = self.links
        z, x = links.z, links.x
        k = LINE - 1
        if rest:
            kept, passed, rows, first = self.kept2.at[k], self.passed2, 2 * self.rest, self.base + 9
            self.load(k, 0).wait()
            self.load(k, 1).wait()
            terms, out = [kept], kept
        else:
            kept, passed, rows, first = self.kept.at[k], self.passed, self.bulk, self.base + 4
            self.load(k, 2).wait()
            links.arrived(self.base + k, self.beside.at[k])
            terms, out = [kept, self.beside.at[k]], self.own

        @pl.when(z > 0)
        def _():
            links.arrived(first + z, passed.at[z])

        @pl.when(z < 3)
        def _():
            links.arrived(first + LINE, passed.at[LINE])

        @pl.when(z == 0)
        def _():
            add_rows(out, 0, terms + [passed.at[LINE]], rows)

        @pl.when(z == 3)
        def _():
            add_rows(out, 0, terms + [passed.at[z]], rows)

        @pl.when((z > 0) & (z < 3))
        def _():
            add_rows(out, 0, terms + [passed.at[z], passed.at[LINE]], rows)

        if rest:
            away = kept.at[pl.ds((1 - x) * self.rest, self.rest), :]
            links.copy(self.base + 14, away, self.last, links.beside()).start()

    def finish(self):
        links = self.links
        z, x = links.z, links.x
        links.arrived(self.base + 14, self.last)
        mine = self.kept2.at[LINE - 1, pl.ds(x * self.rest, self.rest), :]
        add_rows(self.own, self.bulk, [mine, self.last], self.rest)
        links.sent(self.base + 14, self.last)
        for k in range(LINE):
            links.sent(self.base + k, self.beside.at[k])
        for k in range(LINE - 1):
            d = self.order[k]
            for kept, first in ((self.kept.at[k], self.base + 4), (self.kept2.at[k], self.base + 9)):

                @pl.when((d > z) | (d < z - 1))
                def _():
                    links.sent(first + d, kept)

                @pl.when(d == z - 1)
                def _():
                    links.sent(first + LINE, kept)


class Total:
    SEMS = 3 * PIECES

    def __init__(self, links, part, out, buffers):
        self.links, self.part, self.out = links, part, out
        self.mine, self.first, self.second = buffers
        self.rows = part.shape[0] // 2 // PIECES
        self.base = links.take(self.SEMS)
        self.loads = links.take_local(2 * PIECES)

    @staticmethod
    def scratch(rows, n):
        return [pltpu.VMEM((PIECES, rows // 2 // PIECES, n), half) for _ in range(3)]

    def at(self, ref, core, j):
        return ref.at[pl.ds((core * PIECES + j) * self.rows, self.rows), :]

    def load(self, j):
        src = self.at(self.part, self.links.core, j)
        return pltpu.make_async_copy(src, self.mine.at[j], self.links.local.at[self.loads + j])

    def store(self, j):
        dst = self.at(self.out, self.links.core, j)
        sem = self.links.local.at[self.loads + PIECES + j]
        return pltpu.make_async_copy(self.first.at[j], dst, sem)

    def start(self):
        links = self.links
        for j in range(PIECES):
            self.load(j).start()
            src = self.at(self.part, 1 - links.core, j)
            links.copy(self.base + j, src, self.first.at[j], links.partner()).start()

    def middle(self):
        links = self.links
        for j in range(PIECES):
            self.load(j).wait()
            links.arrived(self.base + j, self.first.at[j])
            add_rows(self.mine.at[j], 0, [self.mine.at[j], self.first.at[j]], self.rows)
            index = self.base + PIECES + j
            links.copy(index, self.mine.at[j], self.second.at[j], links.across()).start()

    def spread(self):
        links = self.links
        for j in range(PIECES):
            links.arrived(self.base + PIECES + j, self.second.at[j])
            add_rows(self.first.at[j], 0, [self.mine.at[j], self.second.at[j]], self.rows)
            index = self.base + 2 * PIECES + j
            dst = self.at(self.out, links.core, j)
            links.copy(index, self.first.at[j], dst, links.partner()).start()
            self.store(j).start()

    def landed(self):
        links = self.links
        for j in range(PIECES):
            links.arrived(self.base + 2 * PIECES + j, self.at(self.out, 1 - links.core, j))
            self.store(j).wait()

    def finish(self):
        links = self.links
        for j in range(PIECES):
            for stage in range(3):
                links.sent(self.base + stage * PIECES + j, self.mine.at[j])


def exchange(number, shards=(), totals=(), parts=()):
    gathers, scatters, sums = len(shards), len(totals), len(parts)
    scratch = []
    for total in totals:
        scratch += Scatter.scratch(total.shape[0] // (2 * LINE), total.shape[1])
    for part in parts:
        scratch += Total.scratch(part.shape[0], part.shape[1])
    remote = Gather.SEMS * gathers + Scatter.SEMS * scatters + Total.SEMS * sums
    near = gathers + 12 * scatters + 2 * PIECES * sums
    scratch += [
        pltpu.SemaphoreType.DMA((remote,)),
        pltpu.SemaphoreType.DMA((remote,)),
        pltpu.SemaphoreType.DMA((near,)),
    ]

    def kernel(*refs):
        refs = list(refs)

        def pop(count):
            taken, refs[:count] = refs[:count], []
            return taken

        shard_refs, total_refs, part_refs = pop(gathers), pop(scatters), pop(sums)
        full_refs, own_refs, sum_refs = pop(gathers), pop(scatters), pop(sums)
        buffers = [pop(6) for _ in range(scatters)]
        sum_buffers = [pop(3) for _ in range(sums)]
        links = Links(*refs)
        gather = [Gather(links, s, f) for s, f in zip(shard_refs, full_refs)]
        scatter = [Scatter(links, *a) for a in zip(total_refs, own_refs, buffers)]
        total = [Total(links, *a) for a in zip(part_refs, sum_refs, sum_buffers)]
        links.greet()
        for item in gather + scatter + total:
            item.start()
        for k in range(LINE):
            for item in scatter:
                item.aside(k)
        for item in total:
            item.middle()
        for k in range(LINE - 1):
            for item in scatter:
                item.step(k, True)
        for item in scatter:
            item.close(True)
        for item in gather:
            item.bulk_step(1)
        for item in gather:
            item.rest_start()
        for item in scatter:
            item.step(0, False)
        for item in gather:
            item.bulk_step(2)
        for item in gather:
            item.rest_step(1)
        for item in scatter:
            item.step(1, False)
        for item in gather:
            item.bulk_step(3)
        for item in scatter:
            item.step(2, False)
        for item in total:
            item.spread()
        for item in gather:
            item.rest_step(2)
        for item in scatter:
            item.close(False)
        for item in gather:
            item.rest_step(3)
        for item in total:
            item.landed()
        for item in gather + scatter + total:
            item.finish()

    whole = pl.BlockSpec(memory_space=pl.ANY)
    near_spec = pl.BlockSpec(memory_space=pltpu.VMEM)
    outs = pl.pallas_call(
        kernel,
        in_specs=[near_spec] * gathers + [whole] * (scatters + sums),
        out_specs=[whole] * gathers + [near_spec] * scatters + [whole] * sums,
        out_shape=[
            jax.ShapeDtypeStruct((s.shape[0] * 2 * LINE, s.shape[1]), half) for s in shards
        ]
        + [jax.ShapeDtypeStruct((t.shape[0] // (2 * LINE), t.shape[1]), f32) for t in totals]
        + [jax.ShapeDtypeStruct(p.shape, half) for p in parts],
        scratch_shapes=scratch,
        compiler_params=pltpu.CompilerParams(
            collective_id=number, has_side_effects=True, vmem_limit_bytes=60 * 2**20
        ),
        name=f"exchange_{number}",
    )(*shards, *totals, *parts)
    return outs[:gathers], outs[gathers : gathers + scatters], outs[gathers + scatters :]


class Stream:
    def __init__(self, sems, base, arrays, buffers, index):
        self.sems, self.base, self.arrays, self.buffers, self.index = (
            sems, base, arrays, buffers, index,
        )

    def copies(self, i, inward):
        slot = i % 2
        for n, (array, buffer) in enumerate(zip(self.arrays, self.buffers)):
            rows = buffer.shape[1]
            first = pl.multiple_of(self.index(i) * rows, rows)
            far, near = array.at[pl.ds(first, rows), :], buffer.at[slot]
            sem = self.sems.at[self.base + 2 * n + slot]
            src, dst = (far, near) if inward else (near, far)
            yield pltpu.make_async_copy(src, dst, sem)

    def start(self, i, inward):
        for copy in self.copies(i, inward):
            copy.start()

    def wait(self, i, inward):
        for copy in self.copies(i, inward):
            copy.wait()


class Maker:
    STEPS = 2 * LINE

    def __init__(self, links, sems, base, lefts, left_buffers, pairs):
        self.links, self.sems, self.base = links, sems, base
        self.lefts, self.left_buffers, self.pairs = lefts, left_buffers, pairs
        self.rows = left_buffers[0].shape[2]

    @staticmethod
    def sem_count(lefts, pairs):
        return 2 * (lefts + pairs)

    def place(self, j):
        order = self.pairs[0][4].order
        x = self.links.x
        column = 1 - x + (j % 2) * (2 * x - 1)
        return (turn(order, j // 2) * 2 + column) * self.rows

    def moves(self, j):
        first = pl.multiple_of(self.place(j), self.rows)
        slot = j % 2
        for n, (left, buffer) in enumerate(zip(self.lefts, self.left_buffers)):
            yield pltpu.make_async_copy(
                left.at[:, pl.ds(first, self.rows)], buffer.at[slot],
                self.sems.at[self.base + 2 * n + slot],
            )

    def stores(self, j):
        first = pl.multiple_of(self.place(j), self.rows)
        slot = j % 2
        base = self.base + 2 * len(self.lefts)
        for n, (_, _, buffer, total, _) in enumerate(self.pairs):
            yield pltpu.make_async_copy(
                buffer.at[slot], total.at[pl.ds(first, self.rows), :],
                self.sems.at[base + 2 * n + slot],
            )

    def start(self):
        for move in self.moves(0):
            move.start()

    def run(self, between):
        def body(j, state):
            @pl.when(j + 1 < self.STEPS)
            def _():
                for move in self.moves(j + 1):
                    move.start()

            for move in self.moves(j):
                move.wait()
            slot = j % 2
            for which, b, buffer, _, _ in self.pairs:
                left = self.left_buffers[which][slot]
                buffer[slot] = dot(left, b[...], TN).astype(half)
            for store in self.stores(j):
                store.start()

            @pl.when(j >= 1)
            def _():
                for store in self.stores(j - 1):
                    store.wait()

            @pl.when(j % 2 == 1)
            def _():
                for pair in self.pairs:
                    pair[4].aside(j // 2)

            @pl.when((j % 2 == 0) & (j >= 2))
            def _():
                for pair in self.pairs:
                    pair[4].fetch(j // 2 - 1)

            between(j)
            return state

        lax.fori_loop(0, self.STEPS, body, 0)
        for store in self.stores(self.STEPS - 1):
            store.wait()
        for pair in self.pairs:
            pair[4].fetch(LINE - 1)


def row_sum(values):
    return jnp.sum(values, axis=0, keepdims=True)


def attention_back(tile, weights, gains, sums, carry):
    (cot, middle, d_out, tokens, qkv, mixed, outgate, pre, scores, state) = tile
    (w_out, w_qkv, w_gate, w_small, w_decay, span) = weights
    gain_ffn, gain_head = gains
    sum_ffn, sum_head, sum_bias, sum_attn = sums
    unit, scale = rms_parts(middle[...].astype(f32))
    cot = cot[...].astype(f32)
    sum_ffn[...] += row_sum(cot * unit)
    weighted = cot * gain_ffn[...]
    inner = jnp.mean(weighted * unit, axis=-1, keepdims=True)
    d_attn = (d_out[...].astype(f32) + scale * (weighted - unit * inner)).astype(half)
    d_gated = dot(d_attn, w_out[...], NN)
    rows = mixed[...].astype(f32)
    gate = outgate[...].astype(f32)
    head_scale = lax.rsqrt(jnp.mean(rows * rows, axis=-1, keepdims=True) + head_eps)
    head_unit = rows * head_scale
    sig = jax.nn.sigmoid(gate)
    d_outgate = (
        d_gated * head_unit * gain_head[...] * sig * (1.0 + gate * (1.0 - sig))
    ).astype(half)
    d_normed_head = d_gated * gate * sig
    sum_head[...] += row_sum(d_normed_head * head_unit)
    weighted = d_normed_head * gain_head[...]
    inner = jnp.mean(weighted * head_unit, axis=-1, keepdims=True)
    d_mixed = (head_scale * (weighted - head_unit * inner)).astype(half)
    dk = w_decay.shape[1]
    d_qkv, d_pre = backward_math(
        pre[...], qkv[:, :dk], qkv[:, dk : 2 * dk], qkv[:, 2 * dk :], d_mixed,
        scores[...], state[...], span, carry,
    )
    sum_bias[...] += row_sum(d_pre)
    d_pre = d_pre.astype(half)
    d_rank = dot(d_pre, w_decay[...], NT).astype(half)
    d_normed = (
        dot(d_qkv, w_qkv[...], NT) + dot(d_outgate, w_gate[...], NT) + dot(d_rank, w_small[...], NT)
    )
    unit, _ = rms_parts(tokens[...].astype(f32))
    sum_attn[...] += row_sum(d_normed * unit)
    return d_attn, d_outgate, d_qkv, d_pre, d_rank, d_normed.astype(half)


def backward_exchange(number, totals, part, rows_in, weights, gains, left, right):
    scatters = len(totals) + 1
    length, width = part.shape
    count = length // CHUNK
    dk = weights[4].shape[1]
    dv = weights[0].shape[1]
    outs_wide = (width, dv, 2 * dk + dv, dk, 128, width)
    in_shapes = [(CHUNK, width)] + [(a.shape[0] // count, a.shape[1]) for a in rows_in]
    in_types = [half] + [a.dtype for a in rows_in]
    streams = len(in_shapes)
    sum_wide = (width, dv, dk, width)
    made = jax.ShapeDtypeStruct((left.shape[1], right.shape[1]), half)
    rows = made.shape[0] // (2 * LINE)
    scratch = []
    for total in (*totals, made):
        scratch += Scatter.scratch(total.shape[0] // (2 * LINE), total.shape[1])
    scratch += Total.scratch(length, width)
    scratch += [pltpu.VMEM((2,) + s, t) for s, t in zip(in_shapes, in_types)]
    scratch += [pltpu.VMEM((2, CHUNK, w), half) for w in outs_wide]
    scratch += [pltpu.VMEM(w.shape, half) for w in (*weights, right)]
    scratch += [pltpu.VMEM((2, length, rows), half), pltpu.VMEM((2, rows, made.shape[1]), half)]
    scratch += [pltpu.VMEM((dk, dv), f32)]
    remote = Scatter.SEMS * scatters + Total.SEMS
    near = 12 * scatters + 2 * PIECES
    maker_base = 2 * streams + 2 * len(outs_wide) + len(weights) + 1
    extra = maker_base + Maker.sem_count(1, 1)
    scratch += [
        pltpu.SemaphoreType.DMA((remote,)),
        pltpu.SemaphoreType.DMA((remote,)),
        pltpu.SemaphoreType.DMA((near,)),
        pltpu.SemaphoreType.DMA((extra,)),
    ]

    def kernel(*refs):
        refs = list(refs)

        def pop(count):
            taken, refs[:count] = refs[:count], []
            return taken

        total_refs, (part_ref,), row_refs = pop(scatters - 1), pop(1), pop(streams - 1)
        weight_refs, (left_ref, right_ref), gain_refs = pop(len(weights)), pop(2), pop(2)
        own_refs, (sum_ref, made_ref), out_refs, gain_sums = pop(scatters), pop(2), pop(6), pop(4)
        buffers = [pop(6) for _ in range(scatters)]
        sum_buffers = pop(3)
        in_buffers, out_buffers, near_weights = pop(streams), pop(6), pop(len(weights) + 1)
        (left_buffer, made_buffer, carry) = pop(3)
        sems = refs.pop()
        links = Links(*refs)
        scatter = [
            Scatter(links, *a) for a in zip((*total_refs, made_ref), own_refs, buffers)
        ]
        ready, late = scatter[:-1], scatter[-1:]
        total = Total(links, part_ref, sum_ref, sum_buffers)
        inputs = Stream(sems, 0, [sum_ref] + row_refs, in_buffers, lambda i: count - 1 - i)
        outputs = Stream(sems, 2 * streams, out_refs, out_buffers, lambda i: count - 1 - i)
        right_near = near_weights.pop()
        loads = [
            pltpu.make_async_copy(far, close, sems.at[2 * streams + 12 + n])
            for n, (far, close) in enumerate(
                zip((right_ref, *weight_refs), (right_near, *near_weights))
            )
        ]
        maker = Maker(
            links, sems, maker_base, [left_ref], [left_buffer],
            [(0, right_near, made_buffer, made_ref, late[0])],
        )
        links.greet()
        maker.start()
        total.start()
        for k in range(LINE):
            for item in ready:
                item.aside(k)
        for load in loads:
            load.start()
        for item in ready:
            item.start()
        loads[0].wait()

        def between(j):
            @pl.when(j == 1)
            def _():
                total.middle()

            @pl.when(j == 3)
            def _():
                for item in ready:
                    item.step(0, True)

            @pl.when(j == 5)
            def _():
                for item in ready:
                    item.step(1, True)
                    item.step(0, False)

            @pl.when(j == 7)
            def _():
                for item in ready:
                    item.step(2, True)

        maker.run(between)
        for item in ready:
            item.close(True)
            item.step(1, False)
        for k in range(LINE - 1):
            for item in late:
                item.step(k, True)
        for item in ready:
            item.step(2, False)
        for item in late:
            item.close(True)
        total.spread()
        total.landed()
        for load in loads[1:]:
            load.wait()
        for ref in (*gain_sums, carry):
            ref[...] = jnp.zeros_like(ref)
        inputs.start(0, True)

        def body(i, state):
            @pl.when(i + 1 < count)
            def _():
                inputs.start(i + 1, True)

            inputs.wait(i, True)
            slot = i % 2
            results = attention_back(
                [b.at[slot] for b in in_buffers], near_weights, gain_refs, gain_sums, carry
            )

            @pl.when(i >= 2)
            def _():
                outputs.wait(i - 2, False)

            for buffer, value in zip(out_buffers, results):
                buffer[slot] = value
            outputs.start(i, False)

            @pl.when(i == 0)
            def _():
                for item in ready:
                    item.close(False)
                for item in late:
                    item.step(0, False)

            @pl.when(i == 2)
            def _():
                for item in late:
                    item.step(1, False)

            @pl.when(i == 4)
            def _():
                for item in late:
                    item.step(2, False)

            @pl.when(i == 6)
            def _():
                for item in late:
                    item.close(False)

            return state

        lax.fori_loop(0, count, body, 0)
        outputs.wait(count - 2, False)
        outputs.wait(count - 1, False)
        for item in scatter:
            item.finish()
        total.finish()

    whole = pl.BlockSpec(memory_space=pl.ANY)
    near_spec = pl.BlockSpec(memory_space=pltpu.VMEM)
    outs = pl.pallas_call(
        kernel,
        in_specs=[whole] * (scatters + len(rows_in) + len(weights) + 2) + [near_spec] * 2,
        out_specs=[near_spec] * scatters + [whole] * 8 + [near_spec] * 4,
        out_shape=[
            jax.ShapeDtypeStruct((t.shape[0] // (2 * LINE), t.shape[1]), f32)
            for t in (*totals, made)
        ]
        + [jax.ShapeDtypeStruct(part.shape, half), made]
        + [jax.ShapeDtypeStruct((length, w), half) for w in outs_wide]
        + [jax.ShapeDtypeStruct((1, w), f32) for w in sum_wide],
        scratch_shapes=scratch,
        compiler_params=pltpu.CompilerParams(
            collective_id=number, has_side_effects=True, vmem_limit_bytes=VMEM_LIMIT
        ),
        name=f"backward_exchange_{number}",
    )(*totals, part, *rows_in, *weights, left, right, *gains)
    return outs[:scatters], outs[scatters + 2 : scatters + 8], outs[scatters + 8 :]


def last_exchange(number, total, parts, left_up, right_up, left_norm, right_norms, left_out, right_out):
    ups = jax.ShapeDtypeStruct((left_up.shape[1], right_up.shape[1]), half)
    rest = [jax.ShapeDtypeStruct((left_out.shape[1], right_out.shape[1]), half)]
    rest += [jax.ShapeDtypeStruct((left_norm.shape[1], r.shape[1]), half) for r in right_norms]
    made = [ups, *rest]
    rights = [right_up, right_out, *right_norms]
    lefts = [left_up, left_out, left_norm]
    length = left_up.shape[0]
    rows = ups.shape[0] // (2 * LINE)
    scatters, sums = len(made) + 1, len(parts)
    scratch = []
    for item in (*made, total):
        scratch += Scatter.scratch(item.shape[0] // (2 * LINE), item.shape[1])
    for part in parts:
        scratch += Total.scratch(part.shape[0], part.shape[1])
    scratch += [pltpu.VMEM(r.shape, half) for r in rights]
    scratch += [pltpu.VMEM((2, length, rows), half)] * 2
    scratch += [pltpu.VMEM((2, rows, m.shape[1]), half) for m in made]
    remote = Scatter.SEMS * scatters + Total.SEMS * sums
    near = 12 * scatters + 2 * PIECES * sums
    first_count, second_count = Maker.sem_count(1, 1), Maker.sem_count(2, len(rest))
    scratch += [
        pltpu.SemaphoreType.DMA((remote,)),
        pltpu.SemaphoreType.DMA((remote,)),
        pltpu.SemaphoreType.DMA((near,)),
        pltpu.SemaphoreType.DMA((first_count + second_count + len(rights),)),
    ]

    def kernel(*refs):
        refs = list(refs)

        def pop(count):
            taken, refs[:count] = refs[:count], []
            return taken

        (total_ref,), part_refs = pop(1), pop(sums)
        left_refs, right_refs = pop(3), pop(len(rights))
        own_refs, made_refs, sum_refs = pop(scatters), pop(len(made)), pop(sums)
        buffers = [pop(6) for _ in range(scatters)]
        sum_buffers = [pop(3) for _ in range(sums)]
        near_rights, left_buffers, made_buffers = pop(len(rights)), pop(2), pop(len(made))
        sems = refs.pop()
        links = Links(*refs)
        scatter = [Scatter(links, *a) for a in zip((*made_refs, total_ref), own_refs, buffers)]
        up, late, small = scatter[0], scatter[1:], scatter[-1]
        totals = [Total(links, *a) for a in zip(part_refs, sum_refs, sum_buffers)]
        loads = [
            pltpu.make_async_copy(far, close, sems.at[first_count + second_count + n])
            for n, (far, close) in enumerate(zip(right_refs, near_rights))
        ]
        first = Maker(
            links, sems, 0, left_refs[:1], left_buffers[:1],
            [(0, near_rights[0], made_buffers[0], made_refs[0], up)],
        )
        second = Maker(
            links, sems, first_count, left_refs[1:], left_buffers,
            [
                (min(n, 1), near_rights[n + 1], made_buffers[n + 1], made_refs[n + 1], scatter[n + 1])
                for n in range(len(rest))
            ],
        )
        links.greet()
        loads[0].start()
        first.start()
        for item in totals:
            item.start()
        for load in loads[1:]:
            load.start()
        small.start()
        loads[0].wait()

        def between_first(j):
            @pl.when(j == 5)
            def _():
                for item in totals:
                    item.middle()

        first.run(between_first)
        second.start()
        for k in range(LINE):
            small.aside(k)
        up.step(0, True)
        for load in loads[1:]:
            load.wait()

        def between_second(j):
            @pl.when(j == 1)
            def _():
                up.step(1, True)
                up.step(0, False)

            @pl.when(j == 3)
            def _():
                up.step(2, True)

            @pl.when(j == 5)
            def _():
                up.close(True)
                up.step(1, False)

        second.run(between_second)
        for item in late:
            item.step(0, True)
        up.step(2, False)
        for item in late:
            item.step(1, True)
        up.close(False)
        for item in late:
            item.step(2, True)
        for item in late:
            item.step(0, False)
        for item in late:
            item.close(True)
        for item in late:
            item.step(1, False)
        totals[0].spread()
        for item in late:
            item.step(2, False)
        for item in totals[1:]:
            item.spread()
        for item in late:
            item.close(False)
        for item in totals:
            item.landed()
        for item in scatter + totals:
            item.finish()

    whole = pl.BlockSpec(memory_space=pl.ANY)
    near_spec = pl.BlockSpec(memory_space=pltpu.VMEM)
    outs = pl.pallas_call(
        kernel,
        in_specs=[whole] * (1 + sums + 3 + len(rights)),
        out_specs=[near_spec] * scatters + [whole] * (len(made) + sums),
        out_shape=[
            jax.ShapeDtypeStruct((t.shape[0] // (2 * LINE), t.shape[1]), f32)
            for t in (*made, total)
        ]
        + made
        + [jax.ShapeDtypeStruct(p.shape, half) for p in parts],
        scratch_shapes=scratch,
        compiler_params=pltpu.CompilerParams(
            collective_id=number, has_side_effects=True, vmem_limit_bytes=VMEM_LIMIT
        ),
        name=f"last_exchange_{number}",
    )(total, *parts, *lefts, *rights)
    return outs[:scatters], outs[scatters + len(made) :]


def tile_loop(count, inputs, outputs, compute, between):
    inputs.start(0, True)

    def body(i, state):
        @pl.when(i + 1 < count)
        def _():
            inputs.start(i + 1, True)

        inputs.wait(i, True)
        slot = i % 2
        results = compute([b.at[slot] for b in inputs.buffers])

        @pl.when(i >= 2)
        def _():
            outputs.wait(i - 2, False)

        for buffer, value in zip(outputs.buffers, results):
            buffer[slot] = value
        outputs.start(i, False)
        between(i)
        return state

    lax.fori_loop(0, count, body, 0)
    outputs.wait(count - 2, False)
    outputs.wait(count - 1, False)


def front_exchange(number, tokens, nears, rows_near, shards, flips):
    length, width = tokens.shape
    count = length // CHUNK
    w_qkv, w_small, w_decay, span = nears
    dk = w_decay.shape[1]
    dv = w_qkv.shape[1] - 2 * dk
    shapes = [s.shape[::-1] if flip else s.shape for s, flip in zip(shards, flips)]
    ff = shapes[2][1]
    number_of = len(shards)
    first_out = [
        ((CHUNK, width), half), ((CHUNK, 2 * dk + dv), half), ((CHUNK, 128), f32),
        ((CHUNK, dk), f32), ((CHUNK, dv), half), ((CHUNK, CHUNK), half), ((dk, dv), half),
    ]
    second_in = [((CHUNK, width), half), ((CHUNK, dv), half)]
    second_out = [((CHUNK, dv), half), ((CHUNK, dv), half), ((CHUNK, width), half)]
    third_in = [((CHUNK, width), half), ((CHUNK, width), half)]
    third_out = [((CHUNK, width), half), ((CHUNK, width), half), ((CHUNK, ff), half), ((CHUNK, ff), half)]
    first_in = [((CHUNK, width), half)]
    groups = [first_in, first_out, second_in, second_out, third_in, third_out]
    fulls = [jax.ShapeDtypeStruct((s[0] * 2 * LINE, s[1]), half) for s in shapes]
    scratch = [pltpu.VMEM(s.shape, f32) for s in shards]
    scratch += [pltpu.VMEM(s, half) for s in shapes]
    scratch += Total.scratch(length, width)
    for group in groups:
        scratch += [pltpu.VMEM((2,) + s, t) for s, t in group]
    scratch += [pltpu.VMEM(w.shape, w.dtype) for w in nears]
    scratch += [pltpu.VMEM(f.shape, half) for f in fulls[:4]]
    scratch += [pltpu.VMEM((dk, dv), f32)]
    remote = Gather.SEMS * number_of + Total.SEMS
    near = number_of + 2 * PIECES
    bases = [2 * sum(len(g) for g in groups[:n]) for n in range(len(groups) + 1)]
    extra = bases[-1] + number_of + len(nears) + 4
    scratch += [
        pltpu.SemaphoreType.DMA((remote,)),
        pltpu.SemaphoreType.DMA((remote,)),
        pltpu.SemaphoreType.DMA((near,)),
        pltpu.SemaphoreType.DMA((extra,)),
    ]
    outs_first = [((length // CHUNK) * s[0], s[1], t) for s, t in first_out]
    outs_second = [(length, s[1], t) for s, t in second_out]
    outs_third = [(length, s[1], t) for s, t in third_out]

    def kernel(*refs):
        refs = list(refs)

        def pop(count):
            taken, refs[:count] = refs[:count], []
            return taken

        (tokens_ref,), near_refs, shard_refs = pop(1), pop(len(nears)), pop(number_of)
        gain_attn, bias, gain_head, gain_ffn = pop(4)
        full_refs, (sum_ref,) = pop(number_of), pop(1)
        first_refs, second_refs, third_refs = pop(7), pop(3), pop(4)
        staged, cast = pop(number_of), pop(number_of)
        sum_buffers = pop(3)
        buffers = [pop(len(g)) for g in groups]
        close, full_near, (state,) = pop(len(nears)), pop(4), pop(1)
        sems = refs.pop()
        links = Links(*refs)
        gathers = [Gather(links, c, f) for c, f in zip(cast, full_refs)]
        early, (gate, up, down) = gathers[:2], gathers[2:]
        total = Total(links, second_refs[2], sum_ref, sum_buffers)
        sources = [
            [tokens_ref], first_refs, [first_refs[0], first_refs[4]], second_refs,
            [sum_ref, tokens_ref], third_refs,
        ]
        streams = [
            Stream(sems, b, arrays, near_by, lambda i: i)
            for b, arrays, near_by in zip(bases, sources, buffers)
        ]
        at = bases[-1]
        arrive = [
            pltpu.make_async_copy(far, by, sems.at[at + n])
            for n, (far, by) in enumerate(zip(shard_refs, staged))
        ]
        at += number_of
        loads = [
            pltpu.make_async_copy(far, by, sems.at[at + n])
            for n, (far, by) in enumerate(zip(near_refs, close))
        ]
        at += len(nears)
        weights = [
            pltpu.make_async_copy(far, by, sems.at[at + n])
            for n, (far, by) in enumerate(zip(full_refs, full_near))
        ]

        def prepare(n):
            arrive[n].wait()
            values = staged[n][...]
            cast[n][...] = (jnp.transpose(values) if flips[n] else values).astype(half)

        for copy in arrive:
            copy.start()
        for copy in loads:
            copy.start()
        links.greet()
        for n in range(3):
            prepare(n)
        for item in gathers[:3]:
            item.start()
        for n in range(3, number_of):
            prepare(n)
        for copy in loads:
            copy.wait()
        state[...] = jnp.zeros_like(state)

        def first(tile):
            unit, _ = rms_parts(tile[0][...].astype(f32))
            normed = (unit * gain_attn[...]).astype(half)
            qkv = dot(normed, close[0][...], NN).astype(half)
            rank = dot(normed, close[1][...], NN)
            pre = bias[...] + lax.dot_general(
                rank, close[2][...], (NN, ((), ())),
                precision=highest_precision, preferred_element_type=f32,
            )
            results = forward_math(
                pre, qkv[:, :dk], qkv[:, dk : 2 * dk], qkv[:, 2 * dk :], close[3], state
            )
            return normed, qkv, rank, pre, *results

        def first_between(i):
            @pl.when(i == 1)
            def _():
                for item in early:
                    item.bulk_step(1)
                for item in early:
                    item.rest_start()
                up.start()

            @pl.when(i == 4)
            def _():
                for item in early:
                    item.bulk_step(2)
                for item in early:
                    item.rest_step(1)

            @pl.when(i == 6)
            def _():
                gate.bulk_step(1)
                gate.rest_start()

        tile_loop(count, streams[0], streams[1], first, first_between)
        up.bulk_step(1)
        up.rest_start()
        for item in early:
            item.bulk_step(3)
        for k in (2, 3):
            for item in early:
                item.rest_step(k)
        for item in early:
            item.landed()
        for copy in weights[:2]:
            copy.start()
        for copy in weights[:2]:
            copy.wait()

        def second(tile):
            normed, mixed = tile
            outgate = dot(normed[...], full_near[0][...], NN).astype(half)
            gated = gated_rows(mixed[...].astype(f32), outgate.astype(f32), gain_head[...]).astype(half)
            return outgate, gated, dot(gated, full_near[1][...], NT).astype(half)

        def second_between(i):
            @pl.when(i == 3)
            def _():
                gate.bulk_step(2)
                gate.rest_step(1)

            @pl.when(i == 6)
            def _():
                up.bulk_step(2)
                up.rest_step(1)
                down.start()

        tile_loop(count, streams[2], streams[3], second, second_between)
        total.start()
        total.middle()
        gate.bulk_step(3)
        gate.rest_step(2)
        up.bulk_step(3)
        up.rest_step(2)
        down.bulk_step(1)
        down.rest_start()
        gate.rest_step(3)
        up.rest_step(3)
        total.spread()
        gate.landed()
        weights[2].start()
        up.landed()
        weights[3].start()
        total.landed()
        for copy in weights[2:]:
            copy.wait()

        def third(tile):
            middle = tile[1][...].astype(f32) + tile[0][...].astype(f32)
            unit, _ = rms_parts(middle)
            normed = (unit * gain_ffn[...]).astype(half)
            gate_rows = dot(normed, full_near[2][...], NN).astype(half)
            return middle.astype(half), normed, gate_rows, dot(normed, full_near[3][...], NN).astype(half)

        def third_between(i):
            @pl.when(i == 0)
            def _():
                down.bulk_step(2)
                down.rest_step(1)

            @pl.when(i == 3)
            def _():
                down.bulk_step(3)
                down.rest_step(2)

        tile_loop(count, streams[4], streams[5], third, third_between)
        down.rest_step(3)
        down.landed()
        for item in gathers:
            item.drain()
        total.finish()

    whole = pl.BlockSpec(memory_space=pl.ANY)
    near_spec = pl.BlockSpec(memory_space=pltpu.VMEM)
    outs = pl.pallas_call(
        kernel,
        in_specs=[whole] * (1 + len(nears) + number_of) + [near_spec] * 4,
        out_specs=[whole] * (number_of + 1 + 14),
        out_shape=fulls
        + [jax.ShapeDtypeStruct(tokens.shape, half)]
        + [
            jax.ShapeDtypeStruct((r, c), t) for r, c, t in (*outs_first, *outs_second, *outs_third)
        ],
        scratch_shapes=scratch,
        compiler_params=pltpu.CompilerParams(
            collective_id=number, has_side_effects=True, vmem_limit_bytes=VMEM_LIMIT
        ),
        name=f"front_exchange_{number}",
    )(tokens, *nears, *shards, *rows_near)
    return outs[2:number_of], outs[number_of + 1 :], outs[:2]


class Ring:
    def __init__(self, size):
        self.size = size
        self.wide = size // LINE
        place = lax.axis_index("dp")
        self.z = place // self.wide
        self.x = place % self.wide

    def z_pairs(self, step):
        wide = self.wide
        return [
            (z * wide + x, ((z + step) % LINE) * wide + x) for z in range(LINE) for x in range(wide)
        ]

    def x_pairs(self, step):
        wide = self.wide
        return [(z * wide + x, z * wide + (x + step) % wide) for z in range(LINE) for x in range(wide)]


def gather(ring, shard):
    rows = shard.shape[0]
    pieces = [(ring.z, shard)]
    for step in (1, 3, 2):
        pieces.append(((ring.z - step) % LINE, lax.ppermute(shard, "dp", ring.z_pairs(step))))
    out = jnp.zeros((ring.size * rows, shard.shape[1]), shard.dtype)
    for z, piece in pieces:
        for step in range(ring.wide):
            moved = lax.ppermute(piece, "dp", ring.x_pairs(step)) if step else piece
            place = z * ring.wide + (ring.x - step) % ring.wide
            out = lax.dynamic_update_slice(out, moved, (place * rows, 0))
    return out


def scatter(ring, total):
    rows = total.shape[0] // ring.size

    def block(z, x):
        place = (z % LINE) * ring.wide + x % ring.wide
        return lax.dynamic_slice(total, (place * rows, 0), (rows, total.shape[1]))

    result = None
    for step in (2, 1, 3, 0):
        z = ring.z + step
        kept = block(z, ring.x).astype(f32)
        for side in range(1, ring.wide):
            away = lax.ppermute(block(z, ring.x + side), "dp", ring.x_pairs(side))
            kept = kept + away.astype(f32)
        if step:
            kept = lax.ppermute(kept.astype(half), "dp", ring.z_pairs(step)).astype(f32)
        result = kept if result is None else result + kept
    return result


CORE = [(i, i ^ 1) for i in range(4)]
ACROSS = [(i, i ^ 2) for i in range(4)]


def tensor_sum(part):
    rows = part.shape[0] // 2
    second = (lax.axis_index("tensor") & 1) == 1
    upper, lower = part[:rows], part[rows:]
    mine = jnp.where(second, lower, upper)
    away = jnp.where(second, upper, lower)
    mine = (mine.astype(f32) + lax.ppermute(away, "tensor", CORE).astype(f32)).astype(half)
    mine = (mine.astype(f32) + lax.ppermute(mine, "tensor", ACROSS).astype(f32)).astype(half)
    theirs = lax.ppermute(mine, "tensor", CORE)
    return jnp.concatenate(
        [jnp.where(second, theirs, mine), jnp.where(second, mine, theirs)], axis=0
    )


def rms_parts(values):
    scale = lax.rsqrt(jnp.mean(values * values, axis=-1, keepdims=True) + norm_eps)
    return values * scale, scale


def rms_back(unit, scale, gain, cot):
    weighted = cot * gain
    inner = jnp.mean(weighted * unit, axis=-1, keepdims=True)
    return scale * (weighted - unit * inner), jnp.sum(cot * unit, axis=0)


def gated_rows(mixed, outgate, gain):
    scale = lax.rsqrt(jnp.mean(mixed * mixed, axis=-1, keepdims=True) + head_eps)
    return mixed * scale * gain * jax.nn.silu(outgate)


def local(
    tokens, lengths, norm_attn, query_proj, key_proj, value_proj, outgate_proj, rank_proj,
    decay_proj, decay_bias, head_gain, out_proj, norm_ffn, gate_proj, up_proj, down_proj, cotangent,
    *, size,
):
    ring = Ring(size)
    rows_total = tokens.shape[0]
    width = norm_attn.shape[0]
    rank = rank_proj.shape[1]
    dk = query_proj.shape[1]
    dv = value_proj.shape[1]
    ff = gate_proj.shape[1]
    bits = decay_proj.shape[2]
    gains = head_gain.shape[0]

    def as_column(values):
        flat = values.reshape(-1, 1)
        return jnp.pad(flat, ((0, width - flat.shape[0]), (0, 0)))

    decay_cols = rank * bits // width
    small = jnp.concatenate(
        [
            rank_proj,
            norm_attn[:, None],
            norm_ffn[:, None],
            as_column(head_gain),
            as_column(decay_bias),
            decay_proj.reshape(decay_cols, width).T,
        ],
        axis=1,
    )
    small = jnp.pad(small, ((0, 0), (0, 128 - small.shape[1]))).astype(half)
    qkv = jnp.concatenate([query_proj * 0.0625, key_proj, value_proj], axis=1).astype(half)
    fast = size == 2 * LINE

    def collect(number, shards, parts):
        if fast:
            fulls, _, sums = exchange(number, shards, (), parts)
            return fulls, sums
        return [gather(ring, s) for s in shards], [tensor_sum(p) for p in parts]

    def deliver(number, totals, parts):
        if fast:
            _, owns, sums = exchange(number, (), totals, parts)
            return owns, sums
        return [scatter(ring, t) for t in totals], [tensor_sum(p) for p in parts]

    if fast:
        (qkv_full, small_full), _ = collect(0, (qkv, small), ())
    else:
        late = (outgate_proj.astype(half), out_proj.T.astype(half))
        (qkv_full, small_full, outgate_full, out_full), _ = collect(0, (qkv, small, *late), ())
    rank_full = small_full[:, :rank]
    small32 = small_full.astype(f32)
    gain_attn = small32[:, rank]
    gain_ffn = small32[:, rank + 1]
    by_place = small32.reshape(size, width, 128)
    gain_head = by_place[:, :gains, rank + 2].reshape(-1)
    bias = by_place[:, :bits, rank + 3].reshape(-1)
    decay_weight = jnp.transpose(
        jnp.transpose(by_place[:, :, rank + 4 : rank + 4 + decay_cols], (0, 2, 1)).reshape(
            size, rank, bits
        ),
        (1, 0, 2),
    ).reshape(rank, -1)

    positions = jnp.arange(SEQ_LEN, dtype=jnp.int32)
    mask = (positions[None, :] < lengths[:, None]).astype(f32).reshape(rows_total, 1)
    tokens32 = tokens.astype(f32)
    unit, scale = rms_parts(tokens32)
    span = span_matrix()
    if fast:
        w_decay = jnp.pad(decay_weight, ((0, 128 - rank), (0, 0)))
        (gate_full, up_full, down_full), outs, (outgate_full, out_full) = front_exchange(
            1,
            tokens,
            (qkv_full, small_full, w_decay, span),
            (gain_attn[None, :], bias[None, :], gain_head[None, :], gain_ffn[None, :]),
            (outgate_proj, out_proj, gate_proj, up_proj, down_proj),
            (False, True, False, False, True),
        )
        (
            normed, qkv, rank_rows, pre, mixed, scores, states, outgate, gated, _,
            middle_half, normed_ffn, gate_rows, up_rows,
        ) = outs
        rank_rows = rank_rows[:, :rank]
        middle = middle_half.astype(f32)
        gate_rows = gate_rows.astype(f32)
        up_rows = up_rows.astype(f32)
    else:
        normed = (unit * gain_attn).astype(half)
        qkv = dot(normed, qkv_full, NN).astype(half)
        rank_rows = dot(normed, rank_full, NN)
        pre = (
            jnp.dot(
                rank_rows, decay_weight, precision=highest_precision, preferred_element_type=f32
            )
            + bias
        )
        mixed, scores, states = recur_forward(pre, qkv, span, dk, dv)
        outgate = dot(normed, outgate_full, NN).astype(half)
        gated, pull_gated = jax.vjp(gated_rows, mixed.astype(f32), outgate.astype(f32), gain_head)
        gated = gated.astype(half)
        second = (gate_proj.astype(half), up_proj.astype(half), down_proj.T.astype(half))
        (gate_full, up_full, down_full), (attn,) = collect(
            1, second, (dot(gated, out_full, NT).astype(half),)
        )
        middle = tokens32 + attn.astype(f32)
        unit_ffn, scale_ffn = rms_parts(middle)
        normed_ffn = (unit_ffn * gain_ffn).astype(half)
        gate_rows = dot(normed_ffn, gate_full, NN)
        up_rows = dot(normed_ffn, up_full, NN)
    hidden, pull_glu = jax.vjp(lambda g, u: jax.nn.silu(g) * u, gate_rows, up_rows)
    hidden = hidden.astype(half)
    d_out = cotangent.astype(f32) * mask
    d_out_half = d_out.astype(half)
    grad_down = dot(d_out_half, hidden, TN).astype(half)
    d_gate, d_up = pull_glu(dot(d_out_half, down_full, NN))
    d_gate = d_gate.astype(half)
    d_up = d_up.astype(half)
    d_normed_ffn = (dot(d_gate, gate_full, NT) + dot(d_up, up_full, NT)).astype(half)
    ffn = dot(hidden, down_full, NT).astype(half)
    if fast:
        (down_own, gate_own), outs, sums = backward_exchange(
            2,
            (grad_down,),
            d_normed_ffn,
            (
                middle_half, d_out_half, tokens, qkv, mixed, outgate, pre, scores, states,
            ),
            (out_full, qkv_full, outgate_full, small_full, w_decay.astype(half), span),
            (gain_ffn[None, :], gain_head[None, :]),
            normed_ffn,
            d_gate,
        )
        d_attn, d_outgate, d_qkv, d_pre_half, d_rank, d_normed = outs
        grad_gain_ffn, grad_head, grad_bias, grad_gain_attn = sums
        d_middle = d_attn.astype(f32)
        d_rank = d_rank[:, :rank]
    else:
        d_normed_ffn = tensor_sum(d_normed_ffn)
        d_back, grad_gain_ffn = rms_back(unit_ffn, scale_ffn, gain_ffn, d_normed_ffn.astype(f32))
        d_middle = d_out + d_back
        d_attn = d_middle.astype(half)
        d_mixed, d_outgate, grad_head = pull_gated(dot(d_attn, out_full, NN))
        d_outgate = d_outgate.astype(half)
        d_qkv, d_pre = recur_backward(pre, qkv, d_mixed.astype(half), scores, states, span, dk, dv)
        d_rank = dot(d_pre.astype(half), decay_weight.astype(half), NT).astype(half)
        d_normed = (
            dot(d_qkv, qkv_full, NT) + dot(d_outgate, outgate_full, NT) + dot(d_rank, rank_full, NT)
        )
        grad_gain_attn = jnp.sum(d_normed * unit, axis=0)
        d_normed = d_normed.astype(half)
        d_pre_half = d_pre.astype(half)
        grad_bias = jnp.sum(d_pre, axis=0)
    grad_rank = dot(normed, d_rank, TN)
    grad_decay = jnp.transpose(
        dot(rank_rows.astype(half), d_pre_half, TN).reshape(rank, size, bits), (1, 0, 2)
    ).reshape(size, decay_cols, width)

    def spread(values):
        blocks = values.reshape(size, -1, 1)
        return jnp.pad(blocks, ((0, 0), (0, width - blocks.shape[1]), (0, 0)))

    grad_small = jnp.concatenate(
        [
            grad_rank.reshape(size, width, rank),
            grad_gain_attn.reshape(size, width, 1),
            grad_gain_ffn.reshape(size, width, 1),
            spread(grad_head),
            spread(grad_bias),
            jnp.transpose(grad_decay, (0, 2, 1)),
        ],
        axis=2,
    )
    grad_small = jnp.pad(grad_small, ((0, 0), (0, 0), (0, 128 - grad_small.shape[2])))
    grad_small = grad_small.reshape(size * width, 128).astype(half)

    if fast:
        (up_own, out_own, outgate_own, qkv_own, small_own), (d_normed, ffn) = last_exchange(
            3, grad_small, (d_normed, ffn), normed_ffn, d_up, normed, (d_outgate, d_qkv), d_attn, gated
        )
    else:
        waiting = (
            grad_down,
            dot(normed_ffn, d_gate, TN).astype(half),
            dot(normed_ffn, d_up, TN).astype(half),
            dot(d_attn, gated, TN).astype(half),
            dot(normed, d_outgate, TN).astype(half),
            dot(normed, d_qkv, TN).astype(half),
            grad_small,
        )
        (down_own, gate_own, up_own, out_own, outgate_own, qkv_own, small_own), (
            d_normed, ffn,
        ) = deliver(3, waiting, (d_normed, ffn))
    output = (mask * (middle + ffn.astype(f32))).astype(half)
    d_back, _ = rms_back(unit, scale, gain_attn, d_normed.astype(f32))
    grad_tokens = (d_middle + d_back).astype(half)
    heads_own = small_own.astype(half)
    heads_own = heads_own.astype(f32) + lax.ppermute(heads_own, "tensor", CORE).astype(f32)
    heads_own = heads_own.astype(half)
    heads_own = heads_own.astype(f32) + lax.ppermute(heads_own, "tensor", ACROSS).astype(f32)
    return (
        output,
        grad_tokens,
        heads_own[:, rank],
        qkv_own[:, :dk] * 0.0625,
        qkv_own[:, dk : 2 * dk],
        qkv_own[:, 2 * dk : 2 * dk + dv],
        outgate_own,
        heads_own[:, :rank],
        small_own[:, rank + 4 : rank + 4 + decay_cols].T.reshape(decay_proj.shape),
        small_own[:bits, rank + 3].reshape(decay_bias.shape),
        heads_own[:gains, rank + 2],
        out_own.T,
        heads_own[:, rank + 1] * 0.25,
        gate_own,
        up_own,
        down_own.T,
    )


def solution(mesh):
    size = mesh.shape["dp"]

    def run(*args):
        return local(*args, size=size)

    weight = P("dp", "tensor")
    cross = P("tensor", "dp")
    return jax.shard_map(
        run,
        mesh=mesh,
        in_specs=(
            P("dp", None), P("dp"), P("dp"), weight, weight, weight, weight, P("dp", None),
            P(None, "tensor", "dp"), cross, P("dp"), cross, P("dp"), weight, weight, cross,
            P("dp", None),
        ),
        out_specs=(
            P("dp", None), P("dp", None), P("dp"), weight, weight, weight, weight, P("dp", None),
            P(None, "tensor", "dp"), cross, P("dp"), cross, P("dp"), weight, weight, cross,
        ),
        check_vma=False,
    )
```

```python
import jax
import jax.numpy as jnp
from jax import lax
from jax.experimental import pallas as pl
from jax.experimental.pallas import tpu as pltpu
from jax.sharding import PartitionSpec as P

SEQ_LEN = 1024
LINE = 4

norm_eps = 1e-06
head_eps = 1.0
highest_precision = lax.Precision.HIGHEST
half = jnp.bfloat16
f32 = jnp.float32
CHUNK = 128


def level_count():
    return CHUNK.bit_length() - 1


def span_matrix():
    rows = lax.broadcasted_iota(jnp.int32, (CHUNK, CHUNK), 0)
    cols = lax.broadcasted_iota(jnp.int32, (CHUNK, CHUNK), 1)
    parts = []
    for level in range(level_count()):
        size = 1 << level
        middle = (rows // (2 * size)) * (2 * size) + size
        right = rows >= middle
        parts.append(
            jnp.where(right, (cols >= middle) & (cols <= rows), (cols > rows) & (cols < middle))
        )
    parts.append(cols <= rows)
    parts.append(cols > rows)
    stacked = jnp.concatenate(parts, axis=0).astype(half)
    return jnp.concatenate([stacked, stacked], axis=1)


def dot(left, right, dims):
    return lax.dot_general(left, right, (dims, ((), ())), preferred_element_type=f32)


NN = ((1,), (0,))
NT = ((1,), (1,))
TN = ((0,), (0,))


def log_decay(pre):
    return (jnp.minimum(pre, 0.0) - jnp.log1p(jnp.exp(-jnp.abs(pre)))) * (1.0 / 16.0)


def split_two(values):
    high = values.astype(half)
    low = (values - high.astype(f32)).astype(half)
    return jnp.concatenate([high, low], axis=0)


def level_parts(level):
    rows = lax.broadcasted_iota(jnp.int32, (CHUNK, CHUNK), 0)
    cols = lax.broadcasted_iota(jnp.int32, (CHUNK, CHUNK), 1)
    return rows, cols, (lax.shift_right_logical(rows ^ cols, level) == 1)


def forward_math(pre, q, k, v, span_ref, state):
    decay = log_decay(pre)
    sums = dot(span_ref[...], split_two(decay), NN)
    q32 = q.astype(f32)
    k32 = k.astype(f32)
    rows, cols, _ = level_parts(0)
    scores = jnp.where(rows == cols, dot(q, k, NT), 0.0)
    row_ids = lax.broadcasted_iota(jnp.int32, q.shape, 0)
    for level in range(level_count()):
        right = (lax.shift_right_logical(row_ids, level) & 1) == 1
        grow = jnp.exp(sums[level * CHUNK : (level + 1) * CHUNK])
        mixed_rows = (jnp.where(right, q32, k32) * grow).astype(half)
        pair = level_parts(level)[2] & (rows > cols)
        scores = jnp.where(pair, dot(mixed_rows, mixed_rows, NT), scores)
    levels = level_count()
    head_sum = sums[levels * CHUNK : (levels + 1) * CHUNK]
    tail_sum = sums[(levels + 1) * CHUNK :]
    q_in = (q32 * jnp.exp(head_sum)).astype(half)
    k_out = (k32 * jnp.exp(tail_sum)).astype(half)
    score_half = scores.astype(half)
    state_now = state[...]
    state_half = state_now.astype(half)
    mixed = dot(score_half, v, NN) + dot(q_in, state_half, NN)
    whole = jnp.exp(jnp.transpose(head_sum[CHUNK - 8 :, :]))[:, 7:8]
    state[...] = whole * state_now + dot(k_out, v, TN)
    return mixed.astype(half), score_half, state_half


def forward_body(pre_ref, q_ref, k_ref, v_ref, span_ref, mixed_ref, score_ref, state_ref, state):
    @pl.when(pl.program_id(0) == 0)
    def _():
        state[...] = jnp.zeros_like(state)

    mixed_ref[...], score_ref[...], state_ref[0] = forward_math(
        pre_ref[...], q_ref[...], k_ref[...], v_ref[...], span_ref, state
    )


def backward_math(pre, q, k, v, d_mixed, scores, state_half, span_ref, carry):
    levels = level_count()
    decay = log_decay(pre)
    sums = dot(span_ref[...], split_two(decay), NN)
    q32 = q.astype(f32)
    k32 = k.astype(f32)
    carry_now = carry[...]
    carry_half = carry_now.astype(half)
    rows, cols, _ = level_parts(0)
    row_ids = lax.broadcasted_iota(jnp.int32, q.shape, 0)
    d_scores = dot(d_mixed, v, NT)
    diagonal = jnp.where(rows == cols, d_scores, 0.0)
    sym = jnp.where(rows > cols, d_scores, jnp.transpose(d_scores))
    diag_col = jnp.sum(diagonal, axis=1, keepdims=True)
    dq = diag_col * k32
    dk = diag_col * q32
    pieces = []
    for level in range(levels):
        right = (lax.shift_right_logical(row_ids, level) & 1) == 1
        grow = jnp.exp(sums[level * CHUNK : (level + 1) * CHUNK])
        scaled = jnp.where(right, q32, k32) * grow
        block = jnp.where(level_parts(level)[2], sym, 0.0).astype(half)
        back = dot(block, scaled.astype(half), NN)
        pieces.append((scaled * back).astype(half))
        grown = grow * back
        dq = dq + jnp.where(right, grown, 0.0)
        dk = dk + jnp.where(right, 0.0, grown)
    head_sum = sums[levels * CHUNK : (levels + 1) * CHUNK]
    tail_sum = sums[(levels + 1) * CHUNK :]
    head_grow = jnp.exp(head_sum)
    tail_grow = jnp.exp(tail_sum)
    q_in = q32 * head_grow
    k_out = k32 * tail_grow
    k_out_half = k_out.astype(half)
    back_q = dot(d_mixed, state_half, NT)
    back_k = dot(v, carry_half, NT)
    pieces.append((q_in * back_q).astype(half))
    pieces.append((k_out * back_k).astype(half))
    dq = dq + head_grow * back_q
    dk = dk + tail_grow * back_k
    dv = dot(scores, d_mixed, TN) + dot(k_out_half, carry_half, NN)
    d_qkv = jnp.concatenate([dq.astype(half), dk.astype(half), dv.astype(half)], axis=1)
    whole = jnp.exp(jnp.transpose(head_sum[CHUNK - 8 :, :]))[:, 7:8]
    end_col = whole * jnp.sum(state_half.astype(f32) * carry_now, axis=1, keepdims=True)
    end_row = jnp.transpose(jnp.broadcast_to(end_col, (end_col.shape[0], 128)))[0:1, :]
    d_decay = dot(span_ref[:, :CHUNK], jnp.concatenate(pieces, axis=0), TN) + end_row
    carry[...] = whole * carry_now + dot(q_in.astype(half), d_mixed, TN)
    return d_qkv, d_decay * (jax.nn.sigmoid(-pre) * (1.0 / 16.0))


def backward_body(
    pre_ref, q_ref, k_ref, v_ref, d_ref, score_ref, state_ref, span_ref,
    dqkv_ref, dpre_ref, carry,
):
    @pl.when(pl.program_id(0) == 0)
    def _():
        carry[...] = jnp.zeros_like(carry)

    dqkv_ref[...], dpre_ref[...] = backward_math(
        pre_ref[...], q_ref[...], k_ref[...], v_ref[...], d_ref[...], score_ref[...],
        state_ref[0], span_ref, carry,
    )


def recur_forward(pre, qkv, span, dk, dv):
    length = qkv.shape[0]
    count = length // CHUNK

    def row(wide, place=0):
        return pl.BlockSpec((CHUNK, wide), lambda i: (i, place))

    return pl.pallas_call(
        forward_body,
        grid=(count,),
        in_specs=[
            row(dk), row(dk, 0), row(dk, 1), row(dv, 2 * dk // dv),
            pl.BlockSpec(span.shape, lambda i: (0, 0)),
        ],
        out_specs=[row(dv), row(CHUNK), pl.BlockSpec((1, dk, dv), lambda i: (i, 0, 0))],
        out_shape=[
            jax.ShapeDtypeStruct((length, dv), half),
            jax.ShapeDtypeStruct((length, CHUNK), half),
            jax.ShapeDtypeStruct((count, dk, dv), half),
        ],
        scratch_shapes=[pltpu.VMEM((dk, dv), f32)],
        compiler_params=pltpu.CompilerParams(dimension_semantics=("arbitrary",)),
        cost_estimate=pl.CostEstimate(
            flops=6 * 10**9, bytes_accessed=8 * 2**20, transcendentals=2 * 2**20
        ),
        name="recur_forward",
    )(pre, qkv, qkv, qkv, span)


def recur_backward(pre, qkv, d_mixed, scores, states, span, dk, dv):
    length = qkv.shape[0]
    count = length // CHUNK

    def row(wide, place=0):
        return pl.BlockSpec((CHUNK, wide), lambda i: (count - 1 - i, place))

    return pl.pallas_call(
        backward_body,
        grid=(count,),
        in_specs=[
            row(dk), row(dk, 0), row(dk, 1), row(dv, 2 * dk // dv), row(dv), row(CHUNK),
            pl.BlockSpec((1, dk, dv), lambda i: (count - 1 - i, 0, 0)),
            pl.BlockSpec(span.shape, lambda i: (0, 0)),
        ],
        out_specs=[row(2 * dk + dv), row(dk)],
        out_shape=[
            jax.ShapeDtypeStruct((length, 2 * dk + dv), half),
            jax.ShapeDtypeStruct((length, dk), f32),
        ],
        scratch_shapes=[pltpu.VMEM((dk, dv), f32)],
        compiler_params=pltpu.CompilerParams(dimension_semantics=("arbitrary",)),
        cost_estimate=pl.CostEstimate(
            flops=8 * 10**9, bytes_accessed=10 * 2**20, transcendentals=2 * 2**20
        ),
        name="recur_backward",
    )(pre, qkv, qkv, qkv, d_mixed, scores, states, span)

MESH = pl.DeviceIdType.MESH
BULK = 13
PIECES = 4
VMEM_LIMIT = 67043328


class Links:
    def __init__(self, send, recv, local):
        place = lax.axis_index("dp")
        self.z = place // 2
        self.x = place % 2
        self.t = lax.axis_index("tensor")
        self.core = self.t % 2
        self.send, self.recv, self.local = send, recv, local
        self.count = 0
        self.local_count = 0

    def take(self, number=1):
        first = self.count
        self.count += number
        return first

    def take_local(self, number=1):
        first = self.local_count
        self.local_count += number
        return first

    def beside(self):
        return {"dp": self.z * 2 + 1 - self.x}

    def up(self):
        return {"dp": self.z * 2 + 2 + self.x}

    def down(self):
        return {"dp": self.z * 2 - 2 + self.x}

    def partner(self):
        return {"tensor": self.t + 1 - 2 * self.core}

    def across(self):
        return {"tensor": (self.t + 2) % 4}

    def greet(self):
        barrier = pltpu.get_barrier_semaphore()
        around = [{"dp": ((self.z + step) % LINE) * 2 + self.x} for step in (1, 3)]
        for other in (*around, self.beside(), self.partner(), self.across()):
            pl.semaphore_signal(barrier, inc=1, device_id=other, device_id_type=MESH)
        pl.semaphore_wait(barrier, 5)

    def copy(self, index, src, dst, target):
        return pltpu.make_async_remote_copy(
            src_ref=src,
            dst_ref=dst,
            send_sem=self.send.at[index],
            recv_sem=self.recv.at[index],
            device_id=target,
            device_id_type=MESH,
        )

    def arrived(self, index, dst):
        self.copy(index, dst, dst, self.beside()).wait_recv()

    def sent(self, index, src):
        self.copy(index, src, src, self.beside()).wait_send()


class Gather:
    SEMS = 26

    def __init__(self, links, shard, full):
        self.links, self.shard, self.full = links, shard, full
        self.rows = shard.shape[0]
        self.bulk = self.rows * BULK // 16
        self.base = links.take(self.SEMS)
        self.own_sem = links.take_local()
        self.pending = []

    def at(self, z, x, rest):
        first = (z * 2 + x) * self.rows + (self.bulk if rest else 0)
        return self.full.at[pl.ds(first, self.rows - self.bulk if rest else self.bulk), :]

    def mine(self, rest):
        if rest:
            return self.shard.at[pl.ds(self.bulk, self.rows - self.bulk), :]
        return self.shard.at[pl.ds(0, self.bulk), :]

    def go(self, index, rest, src, dst, target, when=None):
        links = self.links

        def start():
            links.copy(self.base + index, src, dst, target).start()

        if when is None:
            start()
        else:
            pl.when(when())(start)
        self.pending.append((index, rest, when))

    def keep(self):
        links = self.links
        own = self.full.at[pl.ds((links.z * 2 + links.x) * self.rows, self.rows), :]
        return pltpu.make_async_copy(self.shard, own, links.local.at[self.own_sem])

    def there(self, side):
        place = self.links.z + side
        return place >= 0 if side < 0 else place <= LINE - 1

    def onward(self, side):
        z = self.links.z
        more = z < LINE - 1 if side <= 0 else z > 0
        return self.there(side) & more

    def start(self):
        links = self.links
        z, x = links.z, links.x
        self.keep().start()
        own, rest = self.mine(False), self.mine(True)
        self.go(0, False, own, self.at(z, x, False), links.up(), lambda: z < LINE - 1)
        self.go(3, False, own, self.at(z, x, False), links.down(), lambda: z > 0)
        self.go(13, True, rest, self.at(z, x, True), links.beside())
        self.go(6, False, own, self.at(z, x, False), links.beside())

    def bulk_step(self, k):
        links = self.links
        z, x = links.z, links.x
        for side, base, cross, target in ((-k, 0, 7, links.up()), (k, 3, 10, links.down())):
            piece = self.at(z + side, x, False)

            @pl.when(self.there(side))
            def _():
                links.arrived(self.base + base + k - 1, piece)

            if k < 3:
                self.go(base + k, False, piece, piece, target, lambda side=side: self.onward(side))
            self.go(
                cross + k - 1, False, piece, piece, links.beside(), lambda side=side: self.there(side)
            )

    def rest_start(self):
        links = self.links
        z, x = links.z, links.x
        other = self.at(z, 1 - x, True)
        links.arrived(self.base + 13, other)
        mine = self.mine(True)
        for index, src, dst in ((14, mine, self.at(z, x, True)), (15, other, other)):
            self.go(index, True, src, dst, links.up(), lambda: z < LINE - 1)
            self.go(index + 6, True, src, dst, links.down(), lambda: z > 0)

    def rest_step(self, k):
        links = self.links
        z, x = links.z, links.x
        for side, base, target in ((-k, 14, links.up()), (k, 20, links.down())):
            for which in range(2):
                piece = self.at(z + side, x if which == 0 else 1 - x, True)

                @pl.when(self.there(side))
                def _():
                    links.arrived(self.base + base + 2 * (k - 1) + which, piece)

                if k < 3:
                    self.go(
                        base + 2 * k + which, True, piece, piece, target,
                        lambda side=side: self.onward(side),
                    )

    def finish(self):
        self.landed()
        self.drain()

    def landed(self):
        links = self.links
        z, x = links.z, links.x
        links.arrived(self.base + 6, self.at(z, 1 - x, False))
        for k in (1, 2, 3):
            for side, cross in ((-k, 7), (k, 10)):
                there = z + side
                valid = there >= 0 if side < 0 else there <= 3

                @pl.when(valid)
                def _():
                    links.arrived(self.base + cross + k - 1, self.at(there, 1 - x, False))

        self.keep().wait()

    def drain(self):
        links = self.links
        for index, rest, when in self.pending:

            def done():
                links.sent(self.base + index, self.mine(rest))

            if when is None:
                done()
            else:
                pl.when(when())(done)


def add_rows(out, outs_at, terms, rows):
    def body(i, carry):
        tile = pl.ds(pl.multiple_of(i * 16, 16), 16)
        value = terms[0][tile, :].astype(f32)
        for term in terms[1:]:
            value = value + term[tile, :].astype(f32)
        out[pl.ds(pl.multiple_of(outs_at + i * 16, 16), 16), :] = value.astype(out.dtype)
        return carry

    lax.fori_loop(0, rows // 16, body, 0)


ORDER = ((3, 3, 0, 0), (2, 0, 3, 1), (1, 2, 1, 2), (0, 1, 2, 3))


def turn(order, k):
    return (
        (1 - k) * (2 - k) * (3 - k) // 6 * order[0]
        + k * (2 - k) * (3 - k) // 2 * order[1]
        + k * (k - 1) * (3 - k) // 2 * order[2]
        + k * (k - 1) * (k - 2) // 6 * order[3]
    )


class Scatter:
    SEMS = 15

    def __init__(self, links, total, own, buffers):
        self.links, self.total, self.own = links, total, own
        self.beside, self.kept, self.passed, self.kept2, self.passed2, self.last = buffers
        self.rows = total.shape[0] // (2 * LINE)
        self.bulk = self.rows * BULK // 16
        self.rest = self.rows - self.bulk
        self.base = links.take(self.SEMS)
        self.loads = links.take_local(12)
        low, high = links.z % 2, links.z // 2
        self.order = []
        for c in ORDER:
            self.order.append(
                c[0] + (c[1] - c[0]) * low + (c[2] - c[0]) * high
                + (c[3] - c[1] - c[2] + c[0]) * low * high
            )

    @staticmethod
    def scratch(rows, n):
        bulk = rows * BULK // 16
        rest = rows - bulk
        return [
            pltpu.VMEM((LINE, bulk, n), half),
            pltpu.VMEM((LINE, bulk, n), half),
            pltpu.VMEM((LINE + 1, bulk, n), half),
            pltpu.VMEM((LINE, 2 * rest, n), half),
            pltpu.VMEM((LINE + 1, 2 * rest, n), half),
            pltpu.VMEM((rest, n), half),
        ]

    def block(self, z, x, rest):
        first = (z * 2 + x) * self.rows + (self.bulk if rest else 0)
        return self.total.at[pl.ds(first, self.rest if rest else self.bulk), :]

    def turn(self, k):
        if isinstance(k, int):
            return self.order[k]
        return turn(self.order, k)

    def load(self, k, part):
        links = self.links
        d = self.turn(k)
        if part == 2:
            src, dst = self.block(d, links.x, False), self.kept.at[k]
        else:
            src = self.block(d, part, True)
            dst = self.kept2.at[k, pl.ds(part * self.rest, self.rest), :]
        return pltpu.make_async_copy(src, dst, links.local.at[self.loads + 3 * k + part])

    def start(self):
        for k in range(LINE):
            self.fetch(k)

    def fetch(self, k):
        for part in range(3):
            self.load(k, part).start()

    def aside(self, k):
        links = self.links
        src = self.block(self.turn(k), 1 - links.x, False)
        links.copy(self.base + k, src, self.beside.at[k], links.beside()).start()

    def step(self, k, rest):
        links = self.links
        z = links.z
        d = self.order[k]
        if rest:
            kept, passed, rows, first = self.kept2.at[k], self.passed2, 2 * self.rest, self.base + 9
            self.load(k, 0).wait()
            self.load(k, 1).wait()
            terms = [kept]
        else:
            kept, passed, rows, first = self.kept.at[k], self.passed, self.bulk, self.base + 4
            self.load(k, 2).wait()
            links.arrived(self.base + k, self.beside.at[k])
            terms = [kept, self.beside.at[k]]
        upward = d > z
        carried = (upward & (z > 0)) | ((d < z) & (z < 3))

        @pl.when(carried)
        def _():
            links.arrived(first + d, passed.at[d])
            add_rows(kept, 0, terms + [passed.at[d]], rows)

        if not rest:

            @pl.when(jnp.logical_not(carried))
            def _():
                add_rows(kept, 0, terms, rows)

        @pl.when(upward)
        def _():
            links.copy(first + d, kept, passed.at[d], links.up()).start()

        @pl.when((d < z) & (d < z - 1))
        def _():
            links.copy(first + d, kept, passed.at[d], links.down()).start()

        @pl.when((d < z) & (d == z - 1))
        def _():
            links.copy(first + LINE, kept, passed.at[LINE], links.down()).start()

    def close(self, rest):
        links = self.links
        z, x = links.z, links.x
        k = LINE - 1
        if rest:
            kept, passed, rows, first = self.kept2.at[k], self.passed2, 2 * self.rest, self.base + 9
            self.load(k, 0).wait()
            self.load(k, 1).wait()
            terms, out = [kept], kept
        else:
            kept, passed, rows, first = self.kept.at[k], self.passed, self.bulk, self.base + 4
            self.load(k, 2).wait()
            links.arrived(self.base + k, self.beside.at[k])
            terms, out = [kept, self.beside.at[k]], self.own

        @pl.when(z > 0)
        def _():
            links.arrived(first + z, passed.at[z])

        @pl.when(z < 3)
        def _():
            links.arrived(first + LINE, passed.at[LINE])

        @pl.when(z == 0)
        def _():
            add_rows(out, 0, terms + [passed.at[LINE]], rows)

        @pl.when(z == 3)
        def _():
            add_rows(out, 0, terms + [passed.at[z]], rows)

        @pl.when((z > 0) & (z < 3))
        def _():
            add_rows(out, 0, terms + [passed.at[z], passed.at[LINE]], rows)

        if rest:
            away = kept.at[pl.ds((1 - x) * self.rest, self.rest), :]
            links.copy(self.base + 14, away, self.last, links.beside()).start()

    def finish(self):
        links = self.links
        z, x = links.z, links.x
        links.arrived(self.base + 14, self.last)
        mine = self.kept2.at[LINE - 1, pl.ds(x * self.rest, self.rest), :]
        add_rows(self.own, self.bulk, [mine, self.last], self.rest)
        links.sent(self.base + 14, self.last)
        for k in range(LINE):
            links.sent(self.base + k, self.beside.at[k])
        for k in range(LINE - 1):
            d = self.order[k]
            for kept, first in ((self.kept.at[k], self.base + 4), (self.kept2.at[k], self.base + 9)):

                @pl.when((d > z) | (d < z - 1))
                def _():
                    links.sent(first + d, kept)

                @pl.when(d == z - 1)
                def _():
                    links.sent(first + LINE, kept)


class Total:
    def __init__(self, links, part, out, buffers, reverse=False):
        self.links, self.part, self.out, self.reverse = links, part, out, reverse
        self.mine, self.first, self.second = buffers
        self.pieces, self.rows = self.mine.shape[0], self.mine.shape[1]
        self.base = links.take(3 * self.pieces)
        self.loads = links.take_local(2 * self.pieces)

    @staticmethod
    def scratch(rows, n, pieces=PIECES):
        return [pltpu.VMEM((pieces, rows // 2 // pieces, n), half) for _ in range(3)]

    def at(self, ref, core, j):
        place = self.pieces - 1 - j if self.reverse else j
        first = (place * 2 + core) * self.rows
        return ref.at[pl.ds(pl.multiple_of(first, self.rows), self.rows), :]

    def load(self, j):
        src = self.at(self.part, self.links.core, j)
        return pltpu.make_async_copy(src, self.mine.at[j], self.links.local.at[self.loads + j])

    def store(self, j):
        dst = self.at(self.out, self.links.core, j)
        sem = self.links.local.at[self.loads + self.pieces + j]
        return pltpu.make_async_copy(self.first.at[j], dst, sem)

    def start(self):
        links = self.links
        for j in range(self.pieces):
            self.load(j).start()
            src = self.at(self.part, 1 - links.core, j)
            links.copy(self.base + j, src, self.first.at[j], links.partner()).start()

    def middle(self):
        links = self.links

        def body(j, state):
            self.load(j).wait()
            links.arrived(self.base + j, self.first.at[j])
            add_rows(self.mine.at[j], 0, [self.mine.at[j], self.first.at[j]], self.rows)
            index = self.base + self.pieces + j
            links.copy(index, self.mine.at[j], self.second.at[j], links.across()).start()
            return state

        lax.fori_loop(0, self.pieces, body, 0)

    def spread_piece(self, j):
        links = self.links
        links.arrived(self.base + self.pieces + j, self.second.at[j])
        add_rows(self.first.at[j], 0, [self.mine.at[j], self.second.at[j]], self.rows)
        index = self.base + 2 * self.pieces + j
        dst = self.at(self.out, links.core, j)
        links.copy(index, self.first.at[j], dst, links.partner()).start()
        self.store(j).start()

    def landed_piece(self, j):
        links = self.links
        links.arrived(self.base + 2 * self.pieces + j, self.at(self.out, 1 - links.core, j))
        self.store(j).wait()

    def spread(self):
        def body(j, state):
            self.spread_piece(j)
            return state

        lax.fori_loop(0, self.pieces, body, 0)

    def landed(self):
        for j in range(self.pieces):
            self.landed_piece(j)

    def finish(self):
        links = self.links
        for j in range(self.pieces):
            for stage in range(3):
                links.sent(self.base + stage * self.pieces + j, self.mine.at[j])


def exchange(number, shards=(), totals=(), parts=()):
    gathers, scatters, sums = len(shards), len(totals), len(parts)
    scratch = []
    for total in totals:
        scratch += Scatter.scratch(total.shape[0] // (2 * LINE), total.shape[1])
    for part in parts:
        scratch += Total.scratch(part.shape[0], part.shape[1])
    remote = Gather.SEMS * gathers + Scatter.SEMS * scatters + 3 * PIECES * sums
    near = gathers + 12 * scatters + 2 * PIECES * sums
    scratch += [
        pltpu.SemaphoreType.DMA((remote,)),
        pltpu.SemaphoreType.DMA((remote,)),
        pltpu.SemaphoreType.DMA((near,)),
    ]

    def kernel(*refs):
        refs = list(refs)

        def pop(count):
            taken, refs[:count] = refs[:count], []
            return taken

        shard_refs, total_refs, part_refs = pop(gathers), pop(scatters), pop(sums)
        full_refs, own_refs, sum_refs = pop(gathers), pop(scatters), pop(sums)
        buffers = [pop(6) for _ in range(scatters)]
        sum_buffers = [pop(3) for _ in range(sums)]
        links = Links(*refs)
        gather = [Gather(links, s, f) for s, f in zip(shard_refs, full_refs)]
        scatter = [Scatter(links, *a) for a in zip(total_refs, own_refs, buffers)]
        total = [Total(links, *a) for a in zip(part_refs, sum_refs, sum_buffers)]
        links.greet()
        for item in gather + scatter + total:
            item.start()
        for k in range(LINE):
            for item in scatter:
                item.aside(k)
        for item in total:
            item.middle()
        for k in range(LINE - 1):
            for item in scatter:
                item.step(k, True)
        for item in scatter:
            item.close(True)
        for item in gather:
            item.bulk_step(1)
        for item in gather:
            item.rest_start()
        for item in scatter:
            item.step(0, False)
        for item in gather:
            item.bulk_step(2)
        for item in gather:
            item.rest_step(1)
        for item in scatter:
            item.step(1, False)
        for item in gather:
            item.bulk_step(3)
        for item in scatter:
            item.step(2, False)
        for item in total:
            item.spread()
        for item in gather:
            item.rest_step(2)
        for item in scatter:
            item.close(False)
        for item in gather:
            item.rest_step(3)
        for item in total:
            item.landed()
        for item in gather + scatter + total:
            item.finish()

    whole = pl.BlockSpec(memory_space=pl.ANY)
    near_spec = pl.BlockSpec(memory_space=pltpu.VMEM)
    outs = pl.pallas_call(
        kernel,
        in_specs=[near_spec] * gathers + [whole] * (scatters + sums),
        out_specs=[whole] * gathers + [near_spec] * scatters + [whole] * sums,
        out_shape=[
            jax.ShapeDtypeStruct((s.shape[0] * 2 * LINE, s.shape[1]), half) for s in shards
        ]
        + [jax.ShapeDtypeStruct((t.shape[0] // (2 * LINE), t.shape[1]), f32) for t in totals]
        + [jax.ShapeDtypeStruct(p.shape, half) for p in parts],
        scratch_shapes=scratch,
        compiler_params=pltpu.CompilerParams(
            collective_id=number, has_side_effects=True, vmem_limit_bytes=60 * 2**20
        ),
        name=f"exchange_{number}",
    )(*shards, *totals, *parts)
    return outs[:gathers], outs[gathers : gathers + scatters], outs[gathers + scatters :]


class Stream:
    def __init__(self, sems, base, arrays, buffers, index):
        self.sems, self.base, self.arrays, self.buffers, self.index = (
            sems, base, arrays, buffers, index,
        )

    def copies(self, i, inward):
        slot = i % 2
        for n, (array, buffer) in enumerate(zip(self.arrays, self.buffers)):
            rows = buffer.shape[1]
            first = pl.multiple_of(self.index(i) * rows, rows)
            far, near = array.at[pl.ds(first, rows), :], buffer.at[slot]
            sem = self.sems.at[self.base + 2 * n + slot]
            src, dst = (far, near) if inward else (near, far)
            yield pltpu.make_async_copy(src, dst, sem)

    def start(self, i, inward):
        for copy in self.copies(i, inward):
            copy.start()

    def wait(self, i, inward):
        for copy in self.copies(i, inward):
            copy.wait()


class Maker:
    STEPS = 2 * LINE

    def __init__(self, links, sems, base, lefts, left_buffers, pairs):
        self.links, self.sems, self.base = links, sems, base
        self.lefts, self.left_buffers, self.pairs = lefts, left_buffers, pairs
        self.rows = left_buffers[0].shape[2]

    @staticmethod
    def sem_count(lefts, pairs):
        return 2 * (lefts + pairs)

    def place(self, j):
        order = self.pairs[0][4].order
        x = self.links.x
        column = 1 - x + (j % 2) * (2 * x - 1)
        return (turn(order, j // 2) * 2 + column) * self.rows

    def moves(self, j):
        first = pl.multiple_of(self.place(j), self.rows)
        slot = j % 2
        for n, (left, buffer) in enumerate(zip(self.lefts, self.left_buffers)):
            yield pltpu.make_async_copy(
                left.at[:, pl.ds(first, self.rows)], buffer.at[slot],
                self.sems.at[self.base + 2 * n + slot],
            )

    def stores(self, j):
        first = pl.multiple_of(self.place(j), self.rows)
        slot = j % 2
        base = self.base + 2 * len(self.lefts)
        for n, (_, _, buffer, total, _) in enumerate(self.pairs):
            yield pltpu.make_async_copy(
                buffer.at[slot], total.at[pl.ds(first, self.rows), :],
                self.sems.at[base + 2 * n + slot],
            )

    def start(self):
        for move in self.moves(0):
            move.start()

    def run(self, between):
        def body(j, state):
            @pl.when(j + 1 < self.STEPS)
            def _():
                for move in self.moves(j + 1):
                    move.start()

            for move in self.moves(j):
                move.wait()
            slot = j % 2
            for which, b, buffer, _, _ in self.pairs:
                left = self.left_buffers[which][slot]
                buffer[slot] = dot(left, b[...], TN).astype(half)
            for store in self.stores(j):
                store.start()

            @pl.when(j >= 1)
            def _():
                for store in self.stores(j - 1):
                    store.wait()

            @pl.when(j % 2 == 1)
            def _():
                for pair in self.pairs:
                    pair[4].aside(j // 2)

            @pl.when((j % 2 == 0) & (j >= 2))
            def _():
                for pair in self.pairs:
                    pair[4].fetch(j // 2 - 1)

            between(j)
            return state

        lax.fori_loop(0, self.STEPS, body, 0)
        for store in self.stores(self.STEPS - 1):
            store.wait()
        for pair in self.pairs:
            pair[4].fetch(LINE - 1)


def row_sum(values):
    return jnp.sum(values, axis=0, keepdims=True)


def attention_back(tile, weights, gains, sums, carry):
    (cot, middle, d_out, tokens, qkv, mixed, outgate, pre, scores, state) = tile
    (w_out, w_qkv, w_gate, w_small, w_decay, span) = weights
    gain_ffn, gain_head = gains
    sum_ffn, sum_head, sum_bias, sum_attn = sums
    unit, scale = rms_parts(middle[...].astype(f32))
    cot = cot[...].astype(f32)
    sum_ffn[...] += row_sum(cot * unit)
    weighted = cot * gain_ffn[...]
    inner = jnp.mean(weighted * unit, axis=-1, keepdims=True)
    d_attn = (d_out[...].astype(f32) + scale * (weighted - unit * inner)).astype(half)
    d_gated = dot(d_attn, w_out[...], NN)
    rows = mixed[...].astype(f32)
    gate = outgate[...].astype(f32)
    head_scale = lax.rsqrt(jnp.mean(rows * rows, axis=-1, keepdims=True) + head_eps)
    head_unit = rows * head_scale
    sig = jax.nn.sigmoid(gate)
    d_outgate = (
        d_gated * head_unit * gain_head[...] * sig * (1.0 + gate * (1.0 - sig))
    ).astype(half)
    d_normed_head = d_gated * gate * sig
    sum_head[...] += row_sum(d_normed_head * head_unit)
    weighted = d_normed_head * gain_head[...]
    inner = jnp.mean(weighted * head_unit, axis=-1, keepdims=True)
    d_mixed = (head_scale * (weighted - head_unit * inner)).astype(half)
    dk = w_decay.shape[1]
    d_qkv, d_pre = backward_math(
        pre[...], qkv[:, :dk], qkv[:, dk : 2 * dk], qkv[:, 2 * dk :], d_mixed,
        scores[...], state[...], span, carry,
    )
    sum_bias[...] += row_sum(d_pre)
    d_pre = d_pre.astype(half)
    d_rank = dot(d_pre, w_decay[...], NT).astype(half)
    d_normed = (
        dot(d_qkv, w_qkv[...], NT) + dot(d_outgate, w_gate[...], NT) + dot(d_rank, w_small[...], NT)
    )
    unit, _ = rms_parts(tokens[...].astype(f32))
    sum_attn[...] += row_sum(d_normed * unit)
    return d_attn, d_outgate, d_qkv, d_pre, d_rank, d_normed.astype(half)


def backward_exchange(number, part, rows_in, weights, gains, lefts, rights, w_down):
    scatters = len(lefts)
    length, width = part.shape
    count = length // CHUNK
    dk = weights[4].shape[1]
    dv = weights[0].shape[1]
    outs_wide = (width, dv, 2 * dk + dv, dk, 128, width)
    in_shapes = [(CHUNK, width)] + [(a.shape[0] // count, a.shape[1]) for a in rows_in]
    in_types = [half] + [a.dtype for a in rows_in]
    streams = len(in_shapes)
    sum_wide = (width, dv, dk, width)
    made = jax.ShapeDtypeStruct((lefts[0].shape[1], rights[0].shape[1]), half)
    rows = made.shape[0] // (2 * LINE)
    scratch = []
    for _ in range(scatters):
        scratch += Scatter.scratch(rows, made.shape[1])
    scratch += Total.scratch(length, width, count)
    scratch += [pltpu.VMEM((2,) + s, t) for s, t in zip(in_shapes, in_types)]
    scratch += [pltpu.VMEM((2, CHUNK, w), half) for w in outs_wide]
    scratch += [pltpu.VMEM(w.shape, half) for w in (*weights, rights[0], w_down)]
    scratch += [pltpu.VMEM((2, length, rows), half), pltpu.VMEM((2, rows, made.shape[1]), half)]
    scratch += [pltpu.VMEM((dk, dv), f32)]
    remote = Scatter.SEMS * scatters + 3 * count
    near = 12 * scatters + 2 * count
    ffn_base = 2 * streams + 2 * len(outs_wide) + len(weights) + 3
    maker_base = ffn_base + 2
    extra = maker_base + scatters * Maker.sem_count(1, 1)
    scratch += [
        pltpu.SemaphoreType.DMA((remote,)),
        pltpu.SemaphoreType.DMA((remote,)),
        pltpu.SemaphoreType.DMA((near,)),
        pltpu.SemaphoreType.DMA((extra,)),
    ]

    def kernel(*refs):
        refs = list(refs)

        def pop(count):
            taken, refs[:count] = refs[:count], []
            return taken

        (part_ref,), row_refs = pop(1), pop(streams - 1)
        weight_refs, left_refs, right_refs = pop(len(weights)), pop(scatters), pop(scatters)
        (down_ref,), gain_refs = pop(1), pop(2)
        own_refs, (sum_ref, ffn_ref), made_refs = pop(scatters), pop(2), pop(scatters)
        out_refs, gain_sums = pop(6), pop(4)
        buffers = [pop(6) for _ in range(scatters)]
        sum_buffers = pop(3)
        in_buffers, out_buffers, near_weights = pop(streams), pop(6), pop(len(weights))
        right_near, down_near, left_buffer, made_buffer, carry = pop(5)
        sems = refs.pop()
        links = Links(*refs)
        scatter = [Scatter(links, *a) for a in zip(made_refs, own_refs, buffers)]
        down, gate = scatter
        total = Total(links, part_ref, sum_ref, sum_buffers, True)
        inputs = Stream(sems, 0, [sum_ref] + row_refs, in_buffers, lambda i: count - 1 - i)
        outputs = Stream(sems, 2 * streams, out_refs, out_buffers, lambda i: count - 1 - i)
        ffn_out = Stream(sems, ffn_base, [ffn_ref], out_buffers[:1], lambda i: i)
        near_base = 2 * streams + 12
        loads = [
            pltpu.make_async_copy(far, close, sems.at[near_base + n])
            for n, (far, close) in enumerate(
                zip(
                    (right_refs[0], right_refs[1], down_ref, *weight_refs),
                    (right_near, right_near, down_near, *near_weights),
                )
            )
        ]
        makers = [
            Maker(
                links, sems, maker_base + n * Maker.sem_count(1, 1), [left_refs[n]], [left_buffer],
                [(0, right_near, made_buffer, made_refs[n], scatter[n])],
            )
            for n in range(scatters)
        ]
        loads[0].start()
        makers[0].start()
        for load in loads[2:]:
            load.start()
        links.greet()
        total.start()
        loads[0].wait()

        def between_first(j):
            @pl.when(j == 2)
            def _():
                total.middle()

        makers[0].run(between_first)
        makers[1].start()
        down.step(0, True)
        loads[2].wait()

        def ffn_body(i, state):
            tile = right_near[pl.ds(pl.multiple_of(2 * i * CHUNK, 2 * CHUNK), 2 * CHUNK), :]
            value = dot(tile, down_near[...], NT).astype(half)

            @pl.when(i >= 1)
            def _():
                ffn_out.wait(2 * i - 2, False)
                ffn_out.wait(2 * i - 1, False)

            for part in range(2):
                out_buffers[0][part] = value[part * CHUNK : (part + 1) * CHUNK]
                ffn_out.start(2 * i + part, False)

            @pl.when(i == 1)
            def _():
                down.step(1, True)
                down.step(0, False)

            return state

        lax.fori_loop(0, count // 2, ffn_body, 0)
        loads[1].start()
        down.step(2, True)
        ffn_out.wait(count - 2, False)
        ffn_out.wait(count - 1, False)
        loads[1].wait()

        def between_second(j):
            @pl.when(j == 2)
            def _():
                down.close(True)
                down.step(1, False)

            @pl.when(j == 7)
            def _():
                down.step(2, False)

        makers[1].run(between_second)
        for j in range(3):
            total.spread_piece(j)
        total.landed_piece(0)
        for load in loads[3:]:
            load.wait()
        for ref in (*gain_sums, carry):
            ref[...] = jnp.zeros_like(ref)
        inputs.start(0, True)

        def body(i, state):
            @pl.when(i + 1 < count)
            def _():
                total.landed_piece(i + 1)
                inputs.start(i + 1, True)

            @pl.when(i + 3 < count)
            def _():
                total.spread_piece(i + 3)

            inputs.wait(i, True)
            slot = i % 2
            results = attention_back(
                [b.at[slot] for b in in_buffers], near_weights, gain_refs, gain_sums, carry
            )

            @pl.when(i >= 2)
            def _():
                outputs.wait(i - 2, False)

            for buffer, value in zip(out_buffers, results):
                buffer[slot] = value
            outputs.start(i, False)

            @pl.when(i == 0)
            def _():
                gate.step(0, True)

            @pl.when(i == 1)
            def _():
                gate.step(1, True)
                down.close(False)

            @pl.when(i == 2)
            def _():
                gate.step(2, True)
                gate.step(0, False)

            @pl.when(i == 3)
            def _():
                gate.close(True)

            @pl.when(i == 4)
            def _():
                gate.step(1, False)

            @pl.when(i == 6)
            def _():
                gate.step(2, False)

            return state

        lax.fori_loop(0, count, body, 0)
        outputs.wait(count - 2, False)
        outputs.wait(count - 1, False)
        gate.close(False)
        for item in scatter:
            item.finish()
        total.finish()

    whole = pl.BlockSpec(memory_space=pl.ANY)
    near_spec = pl.BlockSpec(memory_space=pltpu.VMEM)
    outs = pl.pallas_call(
        kernel,
        in_specs=[whole] * (2 + len(rows_in) + len(weights) + 2 * scatters) + [near_spec] * 2,
        out_specs=[near_spec] * scatters + [whole] * (2 + scatters + 6) + [near_spec] * 4,
        out_shape=[jax.ShapeDtypeStruct((rows, made.shape[1]), f32)] * scatters
        + [jax.ShapeDtypeStruct(part.shape, half)] * 2
        + [made] * scatters
        + [jax.ShapeDtypeStruct((length, w), half) for w in outs_wide]
        + [jax.ShapeDtypeStruct((1, w), f32) for w in sum_wide],
        scratch_shapes=scratch,
        compiler_params=pltpu.CompilerParams(
            collective_id=number, has_side_effects=True, vmem_limit_bytes=VMEM_LIMIT
        ),
        name=f"backward_exchange_{number}",
    )(part, *rows_in, *weights, *lefts, *rights, w_down, *gains)
    rest = outs[2 * scatters + 2 :]
    return outs[:scatters], outs[scatters + 1], rest[:6], rest[6:]


def last_exchange(number, total, parts, left_up, right_up, left_norm, right_norms, left_out, right_out):
    ups = jax.ShapeDtypeStruct((left_up.shape[1], right_up.shape[1]), half)
    rest = [jax.ShapeDtypeStruct((left_out.shape[1], right_out.shape[1]), half)]
    rest += [jax.ShapeDtypeStruct((left_norm.shape[1], r.shape[1]), half) for r in right_norms]
    made = [ups, *rest]
    rights = [right_up, right_out, *right_norms]
    lefts = [left_up, left_out, left_norm]
    length = left_up.shape[0]
    rows = ups.shape[0] // (2 * LINE)
    scatters, sums = len(made) + 1, len(parts)
    scratch = []
    for item in (*made, total):
        scratch += Scatter.scratch(item.shape[0] // (2 * LINE), item.shape[1])
    for part in parts:
        scratch += Total.scratch(part.shape[0], part.shape[1])
    scratch += [pltpu.VMEM(r.shape, half) for r in rights]
    scratch += [pltpu.VMEM((2, length, rows), half)] * 2
    scratch += [pltpu.VMEM((2, rows, m.shape[1]), half) for m in made]
    remote = Scatter.SEMS * scatters + 3 * PIECES * sums
    near = 12 * scatters + 2 * PIECES * sums
    first_count, second_count = Maker.sem_count(1, 1), Maker.sem_count(2, len(rest))
    scratch += [
        pltpu.SemaphoreType.DMA((remote,)),
        pltpu.SemaphoreType.DMA((remote,)),
        pltpu.SemaphoreType.DMA((near,)),
        pltpu.SemaphoreType.DMA((first_count + second_count + len(rights),)),
    ]

    def kernel(*refs):
        refs = list(refs)

        def pop(count):
            taken, refs[:count] = refs[:count], []
            return taken

        (total_ref,), part_refs = pop(1), pop(sums)
        left_refs, right_refs = pop(3), pop(len(rights))
        own_refs, made_refs, sum_refs = pop(scatters), pop(len(made)), pop(sums)
        buffers = [pop(6) for _ in range(scatters)]
        sum_buffers = [pop(3) for _ in range(sums)]
        near_rights, left_buffers, made_buffers = pop(len(rights)), pop(2), pop(len(made))
        sems = refs.pop()
        links = Links(*refs)
        scatter = [Scatter(links, *a) for a in zip((*made_refs, total_ref), own_refs, buffers)]
        up, late, small = scatter[0], scatter[1:], scatter[-1]
        totals = [Total(links, *a) for a in zip(part_refs, sum_refs, sum_buffers)]
        loads = [
            pltpu.make_async_copy(far, close, sems.at[first_count + second_count + n])
            for n, (far, close) in enumerate(zip(right_refs, near_rights))
        ]
        first = Maker(
            links, sems, 0, left_refs[:1], left_buffers[:1],
            [(0, near_rights[0], made_buffers[0], made_refs[0], up)],
        )
        second = Maker(
            links, sems, first_count, left_refs[1:], left_buffers,
            [
                (min(n, 1), near_rights[n + 1], made_buffers[n + 1], made_refs[n + 1], scatter[n + 1])
                for n in range(len(rest))
            ],
        )
        links.greet()
        loads[0].start()
        first.start()
        for item in totals:
            item.start()
        for load in loads[1:]:
            load.start()
        small.start()
        loads[0].wait()

        def between_first(j):
            @pl.when(j == 5)
            def _():
                for item in totals:
                    item.middle()

        first.run(between_first)
        second.start()
        for k in range(LINE):
            small.aside(k)
        up.step(0, True)
        for load in loads[1:]:
            load.wait()

        def between_second(j):
            @pl.when(j == 1)
            def _():
                up.step(1, True)
                up.step(0, False)

            @pl.when(j == 3)
            def _():
                up.step(2, True)

            @pl.when(j == 5)
            def _():
                up.close(True)
                up.step(1, False)

        second.run(between_second)
        for item in late:
            item.step(0, True)
        up.step(2, False)
        for item in late:
            item.step(1, True)
        up.close(False)
        for item in late:
            item.step(2, True)
        for item in late:
            item.step(0, False)
        for item in late:
            item.close(True)
        for item in late:
            item.step(1, False)
        totals[0].spread()
        for item in late:
            item.step(2, False)
        for item in totals[1:]:
            item.spread()
        for item in late:
            item.close(False)
        for item in totals:
            item.landed()
        for item in scatter + totals:
            item.finish()

    whole = pl.BlockSpec(memory_space=pl.ANY)
    near_spec = pl.BlockSpec(memory_space=pltpu.VMEM)
    outs = pl.pallas_call(
        kernel,
        in_specs=[whole] * (1 + sums + 3 + len(rights)),
        out_specs=[near_spec] * scatters + [whole] * (len(made) + sums),
        out_shape=[
            jax.ShapeDtypeStruct((t.shape[0] // (2 * LINE), t.shape[1]), f32)
            for t in (*made, total)
        ]
        + made
        + [jax.ShapeDtypeStruct(p.shape, half) for p in parts],
        scratch_shapes=scratch,
        compiler_params=pltpu.CompilerParams(
            collective_id=number, has_side_effects=True, vmem_limit_bytes=VMEM_LIMIT
        ),
        name=f"last_exchange_{number}",
    )(total, *parts, *lefts, *rights)
    return outs[:scatters], outs[scatters + len(made) :]


def tile_loop(count, inputs, outputs, compute, between):
    inputs.start(0, True)

    def body(i, state):
        @pl.when(i + 1 < count)
        def _():
            inputs.start(i + 1, True)

        inputs.wait(i, True)
        slot = i % 2
        results = compute([b.at[slot] for b in inputs.buffers])

        @pl.when(i >= 2)
        def _():
            outputs.wait(i - 2, False)

        for buffer, value in zip(outputs.buffers, results):
            buffer[slot] = value
        outputs.start(i, False)
        between(i)
        return state

    lax.fori_loop(0, count, body, 0)
    outputs.wait(count - 2, False)
    outputs.wait(count - 1, False)


def front_exchange(number, tokens, nears, rows_near, shards, flips):
    length, width = tokens.shape
    count = length // CHUNK
    w_qkv, w_small, w_decay, span = nears
    dk = w_decay.shape[1]
    dv = w_qkv.shape[1] - 2 * dk
    shapes = [s.shape[::-1] if flip else s.shape for s, flip in zip(shards, flips)]
    ff = shapes[2][1]
    number_of = len(shards)
    first_out = [
        ((CHUNK, width), half), ((CHUNK, 2 * dk + dv), half), ((CHUNK, 128), f32),
        ((CHUNK, dk), f32), ((CHUNK, dv), half), ((CHUNK, CHUNK), half), ((dk, dv), half),
    ]
    second_in = [((CHUNK, width), half), ((CHUNK, dv), half)]
    second_out = [((CHUNK, dv), half), ((CHUNK, dv), half), ((CHUNK, width), half)]
    third_in = [((CHUNK, width), half), ((CHUNK, width), half)]
    third_out = [((CHUNK, width), half), ((CHUNK, width), half), ((CHUNK, ff), half), ((CHUNK, ff), half)]
    first_in = [((CHUNK, width), half)]
    groups = [first_in, first_out, second_in, second_out, third_in, third_out]
    fulls = [jax.ShapeDtypeStruct((s[0] * 2 * LINE, s[1]), half) for s in shapes]
    scratch = [pltpu.VMEM(s.shape, f32) for s in shards]
    scratch += [pltpu.VMEM(s, half) for s in shapes]
    scratch += Total.scratch(length, width)
    for group in groups:
        scratch += [pltpu.VMEM((2,) + s, t) for s, t in group]
    scratch += [pltpu.VMEM(w.shape, w.dtype) for w in nears]
    scratch += [pltpu.VMEM(f.shape, half) for f in fulls[:4]]
    scratch += [pltpu.VMEM((dk, dv), f32)]
    remote = Gather.SEMS * number_of + 3 * PIECES
    near = number_of + 2 * PIECES
    bases = [2 * sum(len(g) for g in groups[:n]) for n in range(len(groups) + 1)]
    extra = bases[-1] + number_of + len(nears) + 4
    scratch += [
        pltpu.SemaphoreType.DMA((remote,)),
        pltpu.SemaphoreType.DMA((remote,)),
        pltpu.SemaphoreType.DMA((near,)),
        pltpu.SemaphoreType.DMA((extra,)),
    ]
    outs_first = [((length // CHUNK) * s[0], s[1], t) for s, t in first_out]
    outs_second = [(length, s[1], t) for s, t in second_out]
    outs_third = [(length, s[1], t) for s, t in third_out]

    def kernel(*refs):
        refs = list(refs)

        def pop(count):
            taken, refs[:count] = refs[:count], []
            return taken

        (tokens_ref,), near_refs, shard_refs = pop(1), pop(len(nears)), pop(number_of)
        gain_attn, bias, gain_head, gain_ffn = pop(4)
        full_refs, (sum_ref,) = pop(number_of), pop(1)
        first_refs, second_refs, third_refs = pop(7), pop(3), pop(4)
        staged, cast = pop(number_of), pop(number_of)
        sum_buffers = pop(3)
        buffers = [pop(len(g)) for g in groups]
        close, full_near, (state,) = pop(len(nears)), pop(4), pop(1)
        sems = refs.pop()
        links = Links(*refs)
        gathers = [Gather(links, c, f) for c, f in zip(cast, full_refs)]
        early, (gate, up, down) = gathers[:2], gathers[2:]
        total = Total(links, second_refs[2], sum_ref, sum_buffers)
        sources = [
            [tokens_ref], first_refs, [first_refs[0], first_refs[4]], second_refs,
            [sum_ref, tokens_ref], third_refs,
        ]
        streams = [
            Stream(sems, b, arrays, near_by, lambda i: i)
            for b, arrays, near_by in zip(bases, sources, buffers)
        ]
        at = bases[-1]
        arrive = [
            pltpu.make_async_copy(far, by, sems.at[at + n])
            for n, (far, by) in enumerate(zip(shard_refs, staged))
        ]
        at += number_of
        loads = [
            pltpu.make_async_copy(far, by, sems.at[at + n])
            for n, (far, by) in enumerate(zip(near_refs, close))
        ]
        at += len(nears)
        weights = [
            pltpu.make_async_copy(far, by, sems.at[at + n])
            for n, (far, by) in enumerate(zip(full_refs, full_near))
        ]

        def prepare(n):
            arrive[n].wait()
            values = staged[n][...]
            cast[n][...] = (jnp.transpose(values) if flips[n] else values).astype(half)

        for copy in arrive:
            copy.start()
        for copy in loads:
            copy.start()
        links.greet()
        for n in range(3):
            prepare(n)
        for item in gathers[:3]:
            item.start()
        for n in range(3, number_of):
            prepare(n)
        for copy in loads:
            copy.wait()
        state[...] = jnp.zeros_like(state)

        def first(tile):
            unit, _ = rms_parts(tile[0][...].astype(f32))
            normed = (unit * gain_attn[...]).astype(half)
            qkv = dot(normed, close[0][...], NN).astype(half)
            rank = dot(normed, close[1][...], NN)
            pre = bias[...] + lax.dot_general(
                rank, close[2][...], (NN, ((), ())),
                precision=highest_precision, preferred_element_type=f32,
            )
            results = forward_math(
                pre, qkv[:, :dk], qkv[:, dk : 2 * dk], qkv[:, 2 * dk :], close[3], state
            )
            return normed, qkv, rank, pre, *results

        def first_between(i):
            @pl.when(i == 1)
            def _():
                for item in early:
                    item.bulk_step(1)
                for item in early:
                    item.rest_start()
                up.start()

            @pl.when(i == 4)
            def _():
                for item in early:
                    item.bulk_step(2)
                for item in early:
                    item.rest_step(1)

            @pl.when(i == 6)
            def _():
                gate.bulk_step(1)
                gate.rest_start()

        tile_loop(count, streams[0], streams[1], first, first_between)
        up.bulk_step(1)
        up.rest_start()
        for item in early:
            item.bulk_step(3)
        for k in (2, 3):
            for item in early:
                item.rest_step(k)
        for item in early:
            item.landed()
        for copy in weights[:2]:
            copy.start()
        for copy in weights[:2]:
            copy.wait()

        def second(tile):
            normed, mixed = tile
            outgate = dot(normed[...], full_near[0][...], NN).astype(half)
            gated = gated_rows(mixed[...].astype(f32), outgate.astype(f32), gain_head[...]).astype(half)
            return outgate, gated, dot(gated, full_near[1][...], NT).astype(half)

        def second_between(i):
            @pl.when(i == 3)
            def _():
                gate.bulk_step(2)
                gate.rest_step(1)

            @pl.when(i == 6)
            def _():
                up.bulk_step(2)
                up.rest_step(1)
                down.start()

        tile_loop(count, streams[2], streams[3], second, second_between)
        total.start()
        total.middle()
        gate.bulk_step(3)
        gate.rest_step(2)
        up.bulk_step(3)
        up.rest_step(2)
        down.bulk_step(1)
        down.rest_start()
        gate.rest_step(3)
        up.rest_step(3)
        total.spread()
        gate.landed()
        weights[2].start()
        up.landed()
        weights[3].start()
        total.landed()
        for copy in weights[2:]:
            copy.wait()

        def third(tile):
            middle = tile[1][...].astype(f32) + tile[0][...].astype(f32)
            unit, _ = rms_parts(middle)
            normed = (unit * gain_ffn[...]).astype(half)
            gate_rows = dot(normed, full_near[2][...], NN).astype(half)
            return middle.astype(half), normed, gate_rows, dot(normed, full_near[3][...], NN).astype(half)

        def third_between(i):
            @pl.when(i == 0)
            def _():
                down.bulk_step(2)
                down.rest_step(1)

            @pl.when(i == 3)
            def _():
                down.bulk_step(3)
                down.rest_step(2)

        tile_loop(count, streams[4], streams[5], third, third_between)
        down.rest_step(3)
        down.landed()
        for item in gathers:
            item.drain()
        total.finish()

    whole = pl.BlockSpec(memory_space=pl.ANY)
    near_spec = pl.BlockSpec(memory_space=pltpu.VMEM)
    outs = pl.pallas_call(
        kernel,
        in_specs=[whole] * (1 + len(nears) + number_of) + [near_spec] * 4,
        out_specs=[whole] * (number_of + 1 + 14),
        out_shape=fulls
        + [jax.ShapeDtypeStruct(tokens.shape, half)]
        + [
            jax.ShapeDtypeStruct((r, c), t) for r, c, t in (*outs_first, *outs_second, *outs_third)
        ],
        scratch_shapes=scratch,
        compiler_params=pltpu.CompilerParams(
            collective_id=number, has_side_effects=True, vmem_limit_bytes=VMEM_LIMIT
        ),
        name=f"front_exchange_{number}",
    )(tokens, *nears, *shards, *rows_near)
    return outs[2:number_of], outs[number_of + 1 :], outs[:2]


class Ring:
    def __init__(self, size):
        self.size = size
        self.wide = size // LINE
        place = lax.axis_index("dp")
        self.z = place // self.wide
        self.x = place % self.wide

    def z_pairs(self, step):
        wide = self.wide
        return [
            (z * wide + x, ((z + step) % LINE) * wide + x) for z in range(LINE) for x in range(wide)
        ]

    def x_pairs(self, step):
        wide = self.wide
        return [(z * wide + x, z * wide + (x + step) % wide) for z in range(LINE) for x in range(wide)]


def gather(ring, shard):
    rows = shard.shape[0]
    pieces = [(ring.z, shard)]
    for step in (1, 3, 2):
        pieces.append(((ring.z - step) % LINE, lax.ppermute(shard, "dp", ring.z_pairs(step))))
    out = jnp.zeros((ring.size * rows, shard.shape[1]), shard.dtype)
    for z, piece in pieces:
        for step in range(ring.wide):
            moved = lax.ppermute(piece, "dp", ring.x_pairs(step)) if step else piece
            place = z * ring.wide + (ring.x - step) % ring.wide
            out = lax.dynamic_update_slice(out, moved, (place * rows, 0))
    return out


def scatter(ring, total):
    rows = total.shape[0] // ring.size

    def block(z, x):
        place = (z % LINE) * ring.wide + x % ring.wide
        return lax.dynamic_slice(total, (place * rows, 0), (rows, total.shape[1]))

    result = None
    for step in (2, 1, 3, 0):
        z = ring.z + step
        kept = block(z, ring.x).astype(f32)
        for side in range(1, ring.wide):
            away = lax.ppermute(block(z, ring.x + side), "dp", ring.x_pairs(side))
            kept = kept + away.astype(f32)
        if step:
            kept = lax.ppermute(kept.astype(half), "dp", ring.z_pairs(step)).astype(f32)
        result = kept if result is None else result + kept
    return result


CORE = [(i, i ^ 1) for i in range(4)]
ACROSS = [(i, i ^ 2) for i in range(4)]


def tensor_sum(part):
    rows = part.shape[0] // 2
    second = (lax.axis_index("tensor") & 1) == 1
    upper, lower = part[:rows], part[rows:]
    mine = jnp.where(second, lower, upper)
    away = jnp.where(second, upper, lower)
    mine = (mine.astype(f32) + lax.ppermute(away, "tensor", CORE).astype(f32)).astype(half)
    mine = (mine.astype(f32) + lax.ppermute(mine, "tensor", ACROSS).astype(f32)).astype(half)
    theirs = lax.ppermute(mine, "tensor", CORE)
    return jnp.concatenate(
        [jnp.where(second, theirs, mine), jnp.where(second, mine, theirs)], axis=0
    )


def rms_parts(values):
    scale = lax.rsqrt(jnp.mean(values * values, axis=-1, keepdims=True) + norm_eps)
    return values * scale, scale


def rms_back(unit, scale, gain, cot):
    weighted = cot * gain
    inner = jnp.mean(weighted * unit, axis=-1, keepdims=True)
    return scale * (weighted - unit * inner), jnp.sum(cot * unit, axis=0)


def gated_rows(mixed, outgate, gain):
    scale = lax.rsqrt(jnp.mean(mixed * mixed, axis=-1, keepdims=True) + head_eps)
    return mixed * scale * gain * jax.nn.silu(outgate)


def local(
    tokens, lengths, norm_attn, query_proj, key_proj, value_proj, outgate_proj, rank_proj,
    decay_proj, decay_bias, head_gain, out_proj, norm_ffn, gate_proj, up_proj, down_proj, cotangent,
    *, size,
):
    ring = Ring(size)
    rows_total = tokens.shape[0]
    width = norm_attn.shape[0]
    rank = rank_proj.shape[1]
    dk = query_proj.shape[1]
    dv = value_proj.shape[1]
    ff = gate_proj.shape[1]
    bits = decay_proj.shape[2]
    gains = head_gain.shape[0]

    def as_column(values):
        flat = values.reshape(-1, 1)
        return jnp.pad(flat, ((0, width - flat.shape[0]), (0, 0)))

    decay_cols = rank * bits // width
    small = jnp.concatenate(
        [
            rank_proj,
            norm_attn[:, None],
            norm_ffn[:, None],
            as_column(head_gain),
            as_column(decay_bias),
            decay_proj.reshape(decay_cols, width).T,
        ],
        axis=1,
    )
    small = jnp.pad(small, ((0, 0), (0, 128 - small.shape[1]))).astype(half)
    qkv = jnp.concatenate([query_proj * 0.0625, key_proj, value_proj], axis=1).astype(half)
    fast = size == 2 * LINE

    def collect(number, shards, parts):
        if fast:
            fulls, _, sums = exchange(number, shards, (), parts)
            return fulls, sums
        return [gather(ring, s) for s in shards], [tensor_sum(p) for p in parts]

    def deliver(number, totals, parts):
        if fast:
            _, owns, sums = exchange(number, (), totals, parts)
            return owns, sums
        return [scatter(ring, t) for t in totals], [tensor_sum(p) for p in parts]

    if fast:
        (qkv_full, small_full), _ = collect(0, (qkv, small), ())
    else:
        late = (outgate_proj.astype(half), out_proj.T.astype(half))
        (qkv_full, small_full, outgate_full, out_full), _ = collect(0, (qkv, small, *late), ())
    rank_full = small_full[:, :rank]
    small32 = small_full.astype(f32)
    gain_attn = small32[:, rank]
    gain_ffn = small32[:, rank + 1]
    by_place = small32.reshape(size, width, 128)
    gain_head = by_place[:, :gains, rank + 2].reshape(-1)
    bias = by_place[:, :bits, rank + 3].reshape(-1)
    decay_weight = jnp.transpose(
        jnp.transpose(by_place[:, :, rank + 4 : rank + 4 + decay_cols], (0, 2, 1)).reshape(
            size, rank, bits
        ),
        (1, 0, 2),
    ).reshape(rank, -1)

    positions = jnp.arange(SEQ_LEN, dtype=jnp.int32)
    mask = (positions[None, :] < lengths[:, None]).astype(f32).reshape(rows_total, 1)
    tokens32 = tokens.astype(f32)
    unit, scale = rms_parts(tokens32)
    span = span_matrix()
    if fast:
        w_decay = jnp.pad(decay_weight, ((0, 128 - rank), (0, 0)))
        (gate_full, up_full, down_full), outs, (outgate_full, out_full) = front_exchange(
            1,
            tokens,
            (qkv_full, small_full, w_decay, span),
            (gain_attn[None, :], bias[None, :], gain_head[None, :], gain_ffn[None, :]),
            (outgate_proj, out_proj, gate_proj, up_proj, down_proj),
            (False, True, False, False, True),
        )
        (
            normed, qkv, rank_rows, pre, mixed, scores, states, outgate, gated, _,
            middle_half, normed_ffn, gate_rows, up_rows,
        ) = outs
        rank_rows = rank_rows[:, :rank]
        middle = middle_half.astype(f32)
        gate_rows = gate_rows.astype(f32)
        up_rows = up_rows.astype(f32)
    else:
        normed = (unit * gain_attn).astype(half)
        qkv = dot(normed, qkv_full, NN).astype(half)
        rank_rows = dot(normed, rank_full, NN)
        pre = (
            jnp.dot(
                rank_rows, decay_weight, precision=highest_precision, preferred_element_type=f32
            )
            + bias
        )
        mixed, scores, states = recur_forward(pre, qkv, span, dk, dv)
        outgate = dot(normed, outgate_full, NN).astype(half)
        gated, pull_gated = jax.vjp(gated_rows, mixed.astype(f32), outgate.astype(f32), gain_head)
        gated = gated.astype(half)
        second = (gate_proj.astype(half), up_proj.astype(half), down_proj.T.astype(half))
        (gate_full, up_full, down_full), (attn,) = collect(
            1, second, (dot(gated, out_full, NT).astype(half),)
        )
        middle = tokens32 + attn.astype(f32)
        unit_ffn, scale_ffn = rms_parts(middle)
        normed_ffn = (unit_ffn * gain_ffn).astype(half)
        gate_rows = dot(normed_ffn, gate_full, NN)
        up_rows = dot(normed_ffn, up_full, NN)
    hidden, pull_glu = jax.vjp(lambda g, u: jax.nn.silu(g) * u, gate_rows, up_rows)
    hidden = hidden.astype(half)
    d_out = cotangent.astype(f32) * mask
    d_out_half = d_out.astype(half)
    d_gate, d_up = pull_glu(dot(d_out_half, down_full, NN))
    d_gate = d_gate.astype(half)
    d_up = d_up.astype(half)
    d_normed_ffn = (dot(d_gate, gate_full, NT) + dot(d_up, up_full, NT)).astype(half)
    if fast:
        (down_own, gate_own), ffn, outs, sums = backward_exchange(
            2,
            d_normed_ffn,
            (
                middle_half, d_out_half, tokens, qkv, mixed, outgate, pre, scores, states,
            ),
            (out_full, qkv_full, outgate_full, small_full, w_decay.astype(half), span),
            (gain_ffn[None, :], gain_head[None, :]),
            (d_out_half, normed_ffn),
            (hidden, d_gate),
            down_full,
        )
        d_attn, d_outgate, d_qkv, d_pre_half, d_rank, d_normed = outs
        grad_gain_ffn, grad_head, grad_bias, grad_gain_attn = sums
        d_middle = d_attn.astype(f32)
        d_rank = d_rank[:, :rank]
    else:
        d_normed_ffn = tensor_sum(d_normed_ffn)
        d_back, grad_gain_ffn = rms_back(unit_ffn, scale_ffn, gain_ffn, d_normed_ffn.astype(f32))
        d_middle = d_out + d_back
        d_attn = d_middle.astype(half)
        d_mixed, d_outgate, grad_head = pull_gated(dot(d_attn, out_full, NN))
        d_outgate = d_outgate.astype(half)
        d_qkv, d_pre = recur_backward(pre, qkv, d_mixed.astype(half), scores, states, span, dk, dv)
        d_rank = dot(d_pre.astype(half), decay_weight.astype(half), NT).astype(half)
        d_normed = (
            dot(d_qkv, qkv_full, NT) + dot(d_outgate, outgate_full, NT) + dot(d_rank, rank_full, NT)
        )
        grad_gain_attn = jnp.sum(d_normed * unit, axis=0)
        d_normed = d_normed.astype(half)
        d_pre_half = d_pre.astype(half)
        grad_bias = jnp.sum(d_pre, axis=0)
    grad_rank = dot(normed, d_rank, TN)
    grad_decay = jnp.transpose(
        dot(rank_rows.astype(half), d_pre_half, TN).reshape(rank, size, bits), (1, 0, 2)
    ).reshape(size, decay_cols, width)

    def spread(values):
        blocks = values.reshape(size, -1, 1)
        return jnp.pad(blocks, ((0, 0), (0, width - blocks.shape[1]), (0, 0)))

    grad_small = jnp.concatenate(
        [
            grad_rank.reshape(size, width, rank),
            grad_gain_attn.reshape(size, width, 1),
            grad_gain_ffn.reshape(size, width, 1),
            spread(grad_head),
            spread(grad_bias),
            jnp.transpose(grad_decay, (0, 2, 1)),
        ],
        axis=2,
    )
    grad_small = jnp.pad(grad_small, ((0, 0), (0, 0), (0, 128 - grad_small.shape[2])))
    grad_small = grad_small.reshape(size * width, 128).astype(half)

    if fast:
        (up_own, out_own, outgate_own, qkv_own, small_own), (d_normed, ffn) = last_exchange(
            3, grad_small, (d_normed, ffn), normed_ffn, d_up, normed, (d_outgate, d_qkv), d_attn, gated
        )
    else:
        ffn = dot(hidden, down_full, NT).astype(half)
        waiting = (
            dot(d_out_half, hidden, TN).astype(half),
            dot(normed_ffn, d_gate, TN).astype(half),
            dot(normed_ffn, d_up, TN).astype(half),
            dot(d_attn, gated, TN).astype(half),
            dot(normed, d_outgate, TN).astype(half),
            dot(normed, d_qkv, TN).astype(half),
            grad_small,
        )
        (down_own, gate_own, up_own, out_own, outgate_own, qkv_own, small_own), (
            d_normed, ffn,
        ) = deliver(3, waiting, (d_normed, ffn))
    output = (mask * (middle + ffn.astype(f32))).astype(half)
    d_back, _ = rms_back(unit, scale, gain_attn, d_normed.astype(f32))
    grad_tokens = (d_middle + d_back).astype(half)
    heads_own = small_own.astype(half)
    heads_own = heads_own.astype(f32) + lax.ppermute(heads_own, "tensor", CORE).astype(f32)
    heads_own = heads_own.astype(half)
    heads_own = heads_own.astype(f32) + lax.ppermute(heads_own, "tensor", ACROSS).astype(f32)
    return (
        output,
        grad_tokens,
        heads_own[:, rank],
        qkv_own[:, :dk] * 0.0625,
        qkv_own[:, dk : 2 * dk],
        qkv_own[:, 2 * dk : 2 * dk + dv],
        outgate_own,
        heads_own[:, :rank],
        small_own[:, rank + 4 : rank + 4 + decay_cols].T.reshape(decay_proj.shape),
        small_own[:bits, rank + 3].reshape(decay_bias.shape),
        heads_own[:gains, rank + 2],
        out_own.T,
        heads_own[:, rank + 1] * 0.25,
        gate_own,
        up_own,
        down_own.T,
    )


def solution(mesh):
    size = mesh.shape["dp"]

    def run(*args):
        return local(*args, size=size)

    weight = P("dp", "tensor")
    cross = P("tensor", "dp")
    return jax.shard_map(
        run,
        mesh=mesh,
        in_specs=(
            P("dp", None), P("dp"), P("dp"), weight, weight, weight, weight, P("dp", None),
            P(None, "tensor", "dp"), cross, P("dp"), cross, P("dp"), weight, weight, cross,
            P("dp", None),
        ),
        out_specs=(
            P("dp", None), P("dp", None), P("dp"), weight, weight, weight, weight, P("dp", None),
            P(None, "tensor", "dp"), cross, P("dp"), cross, P("dp"), weight, weight, cross,
        ),
        check_vma=False,
    )
```

```python
import jax
import jax.numpy as jnp
from jax import lax
from jax.experimental import pallas as pl
from jax.experimental.pallas import tpu as pltpu
from jax.sharding import PartitionSpec as P

SEQ_LEN = 1024
LINE = 4

norm_eps = 1e-06
head_eps = 1.0
highest_precision = lax.Precision.HIGHEST
half = jnp.bfloat16
f32 = jnp.float32
CHUNK = 128


def level_count():
    return CHUNK.bit_length() - 1


def span_matrix():
    rows = lax.broadcasted_iota(jnp.int32, (CHUNK, CHUNK), 0)
    cols = lax.broadcasted_iota(jnp.int32, (CHUNK, CHUNK), 1)
    parts = []
    for level in range(level_count()):
        size = 1 << level
        middle = (rows // (2 * size)) * (2 * size) + size
        right = rows >= middle
        parts.append(
            jnp.where(right, (cols >= middle) & (cols <= rows), (cols > rows) & (cols < middle))
        )
    parts.append(cols <= rows)
    parts.append(cols > rows)
    stacked = jnp.concatenate(parts, axis=0).astype(half)
    return jnp.concatenate([stacked, stacked], axis=1)


def dot(left, right, dims):
    return lax.dot_general(left, right, (dims, ((), ())), preferred_element_type=f32)


NN = ((1,), (0,))
NT = ((1,), (1,))
TN = ((0,), (0,))


def log_decay(pre):
    return (jnp.minimum(pre, 0.0) - jnp.log1p(jnp.exp(-jnp.abs(pre)))) * (1.0 / 16.0)


def split_two(values):
    high = values.astype(half)
    low = (values - high.astype(f32)).astype(half)
    return jnp.concatenate([high, low], axis=0)


def level_parts(level):
    rows = lax.broadcasted_iota(jnp.int32, (CHUNK, CHUNK), 0)
    cols = lax.broadcasted_iota(jnp.int32, (CHUNK, CHUNK), 1)
    return rows, cols, (lax.shift_right_logical(rows ^ cols, level) == 1)


def forward_math(pre, q, k, v, span_ref, state):
    decay = log_decay(pre)
    sums = dot(span_ref[...], split_two(decay), NN)
    q32 = q.astype(f32)
    k32 = k.astype(f32)
    rows, cols, _ = level_parts(0)
    scores = jnp.where(rows == cols, dot(q, k, NT), 0.0)
    row_ids = lax.broadcasted_iota(jnp.int32, q.shape, 0)
    for level in range(level_count()):
        right = (lax.shift_right_logical(row_ids, level) & 1) == 1
        grow = jnp.exp(sums[level * CHUNK : (level + 1) * CHUNK])
        mixed_rows = (jnp.where(right, q32, k32) * grow).astype(half)
        pair = level_parts(level)[2] & (rows > cols)
        scores = jnp.where(pair, dot(mixed_rows, mixed_rows, NT), scores)
    levels = level_count()
    head_sum = sums[levels * CHUNK : (levels + 1) * CHUNK]
    tail_sum = sums[(levels + 1) * CHUNK :]
    q_in = (q32 * jnp.exp(head_sum)).astype(half)
    k_out = (k32 * jnp.exp(tail_sum)).astype(half)
    score_half = scores.astype(half)
    state_now = state[...]
    state_half = state_now.astype(half)
    mixed = dot(score_half, v, NN) + dot(q_in, state_half, NN)
    whole = jnp.exp(jnp.transpose(head_sum[CHUNK - 8 :, :]))[:, 7:8]
    state[...] = whole * state_now + dot(k_out, v, TN)
    return mixed.astype(half), score_half, state_half


def forward_body(pre_ref, q_ref, k_ref, v_ref, span_ref, mixed_ref, score_ref, state_ref, state):
    @pl.when(pl.program_id(0) == 0)
    def _():
        state[...] = jnp.zeros_like(state)

    mixed_ref[...], score_ref[...], state_ref[0] = forward_math(
        pre_ref[...], q_ref[...], k_ref[...], v_ref[...], span_ref, state
    )


def backward_math(pre, q, k, v, d_mixed, scores, state_half, span_ref, carry):
    levels = level_count()
    decay = log_decay(pre)
    sums = dot(span_ref[...], split_two(decay), NN)
    q32 = q.astype(f32)
    k32 = k.astype(f32)
    carry_now = carry[...]
    carry_half = carry_now.astype(half)
    rows, cols, _ = level_parts(0)
    row_ids = lax.broadcasted_iota(jnp.int32, q.shape, 0)
    d_scores = dot(d_mixed, v, NT)
    diagonal = jnp.where(rows == cols, d_scores, 0.0)
    sym = jnp.where(rows > cols, d_scores, jnp.transpose(d_scores))
    diag_col = jnp.sum(diagonal, axis=1, keepdims=True)
    dq = diag_col * k32
    dk = diag_col * q32
    pieces = []
    for level in range(levels):
        right = (lax.shift_right_logical(row_ids, level) & 1) == 1
        grow = jnp.exp(sums[level * CHUNK : (level + 1) * CHUNK])
        scaled = jnp.where(right, q32, k32) * grow
        block = jnp.where(level_parts(level)[2], sym, 0.0).astype(half)
        back = dot(block, scaled.astype(half), NN)
        pieces.append((scaled * back).astype(half))
        grown = grow * back
        dq = dq + jnp.where(right, grown, 0.0)
        dk = dk + jnp.where(right, 0.0, grown)
    head_sum = sums[levels * CHUNK : (levels + 1) * CHUNK]
    tail_sum = sums[(levels + 1) * CHUNK :]
    head_grow = jnp.exp(head_sum)
    tail_grow = jnp.exp(tail_sum)
    q_in = q32 * head_grow
    k_out = k32 * tail_grow
    k_out_half = k_out.astype(half)
    back_q = dot(d_mixed, state_half, NT)
    back_k = dot(v, carry_half, NT)
    pieces.append((q_in * back_q).astype(half))
    pieces.append((k_out * back_k).astype(half))
    dq = dq + head_grow * back_q
    dk = dk + tail_grow * back_k
    dv = dot(scores, d_mixed, TN) + dot(k_out_half, carry_half, NN)
    d_qkv = jnp.concatenate([dq.astype(half), dk.astype(half), dv.astype(half)], axis=1)
    whole = jnp.exp(jnp.transpose(head_sum[CHUNK - 8 :, :]))[:, 7:8]
    end_col = whole * jnp.sum(state_half.astype(f32) * carry_now, axis=1, keepdims=True)
    end_row = jnp.transpose(jnp.broadcast_to(end_col, (end_col.shape[0], 128)))[0:1, :]
    d_decay = dot(span_ref[:, :CHUNK], jnp.concatenate(pieces, axis=0), TN) + end_row
    carry[...] = whole * carry_now + dot(q_in.astype(half), d_mixed, TN)
    return d_qkv, d_decay * (jax.nn.sigmoid(-pre) * (1.0 / 16.0))


def backward_body(
    pre_ref, q_ref, k_ref, v_ref, d_ref, score_ref, state_ref, span_ref,
    dqkv_ref, dpre_ref, carry,
):
    @pl.when(pl.program_id(0) == 0)
    def _():
        carry[...] = jnp.zeros_like(carry)

    dqkv_ref[...], dpre_ref[...] = backward_math(
        pre_ref[...], q_ref[...], k_ref[...], v_ref[...], d_ref[...], score_ref[...],
        state_ref[0], span_ref, carry,
    )


def recur_forward(pre, qkv, span, dk, dv):
    length = qkv.shape[0]
    count = length // CHUNK

    def row(wide, place=0):
        return pl.BlockSpec((CHUNK, wide), lambda i: (i, place))

    return pl.pallas_call(
        forward_body,
        grid=(count,),
        in_specs=[
            row(dk), row(dk, 0), row(dk, 1), row(dv, 2 * dk // dv),
            pl.BlockSpec(span.shape, lambda i: (0, 0)),
        ],
        out_specs=[row(dv), row(CHUNK), pl.BlockSpec((1, dk, dv), lambda i: (i, 0, 0))],
        out_shape=[
            jax.ShapeDtypeStruct((length, dv), half),
            jax.ShapeDtypeStruct((length, CHUNK), half),
            jax.ShapeDtypeStruct((count, dk, dv), half),
        ],
        scratch_shapes=[pltpu.VMEM((dk, dv), f32)],
        compiler_params=pltpu.CompilerParams(dimension_semantics=("arbitrary",)),
        cost_estimate=pl.CostEstimate(
            flops=6 * 10**9, bytes_accessed=8 * 2**20, transcendentals=2 * 2**20
        ),
        name="recur_forward",
    )(pre, qkv, qkv, qkv, span)


def recur_backward(pre, qkv, d_mixed, scores, states, span, dk, dv):
    length = qkv.shape[0]
    count = length // CHUNK

    def row(wide, place=0):
        return pl.BlockSpec((CHUNK, wide), lambda i: (count - 1 - i, place))

    return pl.pallas_call(
        backward_body,
        grid=(count,),
        in_specs=[
            row(dk), row(dk, 0), row(dk, 1), row(dv, 2 * dk // dv), row(dv), row(CHUNK),
            pl.BlockSpec((1, dk, dv), lambda i: (count - 1 - i, 0, 0)),
            pl.BlockSpec(span.shape, lambda i: (0, 0)),
        ],
        out_specs=[row(2 * dk + dv), row(dk)],
        out_shape=[
            jax.ShapeDtypeStruct((length, 2 * dk + dv), half),
            jax.ShapeDtypeStruct((length, dk), f32),
        ],
        scratch_shapes=[pltpu.VMEM((dk, dv), f32)],
        compiler_params=pltpu.CompilerParams(dimension_semantics=("arbitrary",)),
        cost_estimate=pl.CostEstimate(
            flops=8 * 10**9, bytes_accessed=10 * 2**20, transcendentals=2 * 2**20
        ),
        name="recur_backward",
    )(pre, qkv, qkv, qkv, d_mixed, scores, states, span)

MESH = pl.DeviceIdType.MESH
BULK = 14
PIECES = 4
VMEM_LIMIT = 67043328


class Links:
    def __init__(self, send, recv, local):
        place = lax.axis_index("dp")
        self.z = place // 2
        self.x = place % 2
        self.t = lax.axis_index("tensor")
        self.core = self.t % 2
        self.send, self.recv, self.local = send, recv, local
        self.count = 0
        self.local_count = 0

    def take(self, number=1):
        first = self.count
        self.count += number
        return first

    def take_local(self, number=1):
        first = self.local_count
        self.local_count += number
        return first

    def beside(self):
        return {"dp": self.z * 2 + 1 - self.x}

    def up(self):
        return {"dp": self.z * 2 + 2 + self.x}

    def down(self):
        return {"dp": self.z * 2 - 2 + self.x}

    def partner(self):
        return {"tensor": self.t + 1 - 2 * self.core}

    def across(self):
        return {"tensor": (self.t + 2) % 4}

    def greet(self):
        barrier = pltpu.get_barrier_semaphore()
        around = [{"dp": ((self.z + step) % LINE) * 2 + self.x} for step in (1, 3)]
        for other in (*around, self.beside(), self.partner(), self.across()):
            pl.semaphore_signal(barrier, inc=1, device_id=other, device_id_type=MESH)
        pl.semaphore_wait(barrier, 5)

    def copy(self, index, src, dst, target):
        return pltpu.make_async_remote_copy(
            src_ref=src,
            dst_ref=dst,
            send_sem=self.send.at[index],
            recv_sem=self.recv.at[index],
            device_id=target,
            device_id_type=MESH,
        )

    def arrived(self, index, dst):
        self.copy(index, dst, dst, self.beside()).wait_recv()

    def sent(self, index, src):
        self.copy(index, src, src, self.beside()).wait_send()


class Gather:
    SEMS = 26

    def __init__(self, links, shard, full):
        self.links, self.shard, self.full = links, shard, full
        self.rows = shard.shape[0]
        self.bulk = self.rows * BULK // 16
        self.base = links.take(self.SEMS)
        self.own_sem = links.take_local()
        self.pending = []

    def at(self, z, x, rest):
        first = (z * 2 + x) * self.rows + (self.bulk if rest else 0)
        return self.full.at[pl.ds(first, self.rows - self.bulk if rest else self.bulk), :]

    def mine(self, rest):
        if rest:
            return self.shard.at[pl.ds(self.bulk, self.rows - self.bulk), :]
        return self.shard.at[pl.ds(0, self.bulk), :]

    def go(self, index, rest, src, dst, target, when=None):
        links = self.links

        def start():
            links.copy(self.base + index, src, dst, target).start()

        if when is None:
            start()
        else:
            pl.when(when())(start)
        self.pending.append((index, rest, when))

    def keep(self):
        links = self.links
        own = self.full.at[pl.ds((links.z * 2 + links.x) * self.rows, self.rows), :]
        return pltpu.make_async_copy(self.shard, own, links.local.at[self.own_sem])

    def there(self, side):
        place = self.links.z + side
        return place >= 0 if side < 0 else place <= LINE - 1

    def onward(self, side):
        z = self.links.z
        more = z < LINE - 1 if side <= 0 else z > 0
        return self.there(side) & more

    def start(self):
        links = self.links
        z, x = links.z, links.x
        self.keep().start()
        own, rest = self.mine(False), self.mine(True)
        self.go(0, False, own, self.at(z, x, False), links.up(), lambda: z < LINE - 1)
        self.go(3, False, own, self.at(z, x, False), links.down(), lambda: z > 0)
        self.go(13, True, rest, self.at(z, x, True), links.beside())
        self.go(6, False, own, self.at(z, x, False), links.beside())

    def bulk_step(self, k):
        links = self.links
        z, x = links.z, links.x
        for side, base, cross, target in ((-k, 0, 7, links.up()), (k, 3, 10, links.down())):
            piece = self.at(z + side, x, False)

            @pl.when(self.there(side))
            def _():
                links.arrived(self.base + base + k - 1, piece)

            if k < 3:
                self.go(base + k, False, piece, piece, target, lambda side=side: self.onward(side))
            self.go(
                cross + k - 1, False, piece, piece, links.beside(), lambda side=side: self.there(side)
            )

    def rest_start(self):
        links = self.links
        z, x = links.z, links.x
        other = self.at(z, 1 - x, True)
        links.arrived(self.base + 13, other)
        mine = self.mine(True)
        for index, src, dst in ((14, mine, self.at(z, x, True)), (15, other, other)):
            self.go(index, True, src, dst, links.up(), lambda: z < LINE - 1)
            self.go(index + 6, True, src, dst, links.down(), lambda: z > 0)

    def rest_step(self, k):
        links = self.links
        z, x = links.z, links.x
        for side, base, target in ((-k, 14, links.up()), (k, 20, links.down())):
            for which in range(2):
                piece = self.at(z + side, x if which == 0 else 1 - x, True)

                @pl.when(self.there(side))
                def _():
                    links.arrived(self.base + base + 2 * (k - 1) + which, piece)

                if k < 3:
                    self.go(
                        base + 2 * k + which, True, piece, piece, target,
                        lambda side=side: self.onward(side),
                    )

    def finish(self):
        self.landed()
        self.drain()

    def landed(self):
        links = self.links
        z, x = links.z, links.x
        links.arrived(self.base + 6, self.at(z, 1 - x, False))
        for k in (1, 2, 3):
            for side, cross in ((-k, 7), (k, 10)):
                there = z + side
                valid = there >= 0 if side < 0 else there <= 3

                @pl.when(valid)
                def _():
                    links.arrived(self.base + cross + k - 1, self.at(there, 1 - x, False))

        self.keep().wait()

    def drain(self):
        links = self.links
        for index, rest, when in self.pending:

            def done():
                links.sent(self.base + index, self.mine(rest))

            if when is None:
                done()
            else:
                pl.when(when())(done)


def add_rows(out, outs_at, terms, rows):
    def body(i, carry):
        tile = pl.ds(pl.multiple_of(i * 16, 16), 16)
        value = terms[0][tile, :].astype(f32)
        for term in terms[1:]:
            value = value + term[tile, :].astype(f32)
        out[pl.ds(pl.multiple_of(outs_at + i * 16, 16), 16), :] = value.astype(out.dtype)
        return carry

    lax.fori_loop(0, rows // 16, body, 0)


ORDER = ((3, 3, 0, 0), (2, 0, 3, 1), (1, 2, 1, 2), (0, 1, 2, 3))


def turn(order, k):
    return (
        (1 - k) * (2 - k) * (3 - k) // 6 * order[0]
        + k * (2 - k) * (3 - k) // 2 * order[1]
        + k * (k - 1) * (3 - k) // 2 * order[2]
        + k * (k - 1) * (k - 2) // 6 * order[3]
    )


class Scatter:
    SEMS = 15

    def __init__(self, links, total, own, buffers):
        self.links, self.total, self.own = links, total, own
        self.beside, self.kept, self.passed, self.kept2, self.passed2, self.last = buffers
        self.rows = total.shape[0] // (2 * LINE)
        self.bulk = self.rows * BULK // 16
        self.rest = self.rows - self.bulk
        self.base = links.take(self.SEMS)
        self.loads = links.take_local(12)
        low, high = links.z % 2, links.z // 2
        self.order = []
        for c in ORDER:
            self.order.append(
                c[0] + (c[1] - c[0]) * low + (c[2] - c[0]) * high
                + (c[3] - c[1] - c[2] + c[0]) * low * high
            )

    @staticmethod
    def scratch(rows, n):
        bulk = rows * BULK // 16
        rest = rows - bulk
        return [
            pltpu.VMEM((LINE, bulk, n), half),
            pltpu.VMEM((LINE, bulk, n), half),
            pltpu.VMEM((LINE + 1, bulk, n), half),
            pltpu.VMEM((LINE, 2 * rest, n), half),
            pltpu.VMEM((LINE + 1, 2 * rest, n), half),
            pltpu.VMEM((rest, n), half),
        ]

    def block(self, z, x, rest):
        first = (z * 2 + x) * self.rows + (self.bulk if rest else 0)
        return self.total.at[pl.ds(first, self.rest if rest else self.bulk), :]

    def turn(self, k):
        if isinstance(k, int):
            return self.order[k]
        return turn(self.order, k)

    def load(self, k, part):
        links = self.links
        d = self.turn(k)
        if part == 2:
            src, dst = self.block(d, links.x, False), self.kept.at[k]
        else:
            src = self.block(d, part, True)
            dst = self.kept2.at[k, pl.ds(part * self.rest, self.rest), :]
        return pltpu.make_async_copy(src, dst, links.local.at[self.loads + 3 * k + part])

    def start(self):
        for k in range(LINE):
            self.fetch(k)

    def fetch(self, k):
        for part in range(3):
            self.load(k, part).start()

    def aside(self, k):
        links = self.links
        src = self.block(self.turn(k), 1 - links.x, False)
        links.copy(self.base + k, src, self.beside.at[k], links.beside()).start()

    def step(self, k, rest):
        links = self.links
        z = links.z
        d = self.order[k]
        if rest:
            kept, passed, rows, first = self.kept2.at[k], self.passed2, 2 * self.rest, self.base + 9
            self.load(k, 0).wait()
            self.load(k, 1).wait()
            terms = [kept]
        else:
            kept, passed, rows, first = self.kept.at[k], self.passed, self.bulk, self.base + 4
            self.load(k, 2).wait()
            links.arrived(self.base + k, self.beside.at[k])
            terms = [kept, self.beside.at[k]]
        upward = d > z
        carried = (upward & (z > 0)) | ((d < z) & (z < 3))

        @pl.when(carried)
        def _():
            links.arrived(first + d, passed.at[d])
            add_rows(kept, 0, terms + [passed.at[d]], rows)

        if not rest:

            @pl.when(jnp.logical_not(carried))
            def _():
                add_rows(kept, 0, terms, rows)

        @pl.when(upward)
        def _():
            links.copy(first + d, kept, passed.at[d], links.up()).start()

        @pl.when((d < z) & (d < z - 1))
        def _():
            links.copy(first + d, kept, passed.at[d], links.down()).start()

        @pl.when((d < z) & (d == z - 1))
        def _():
            links.copy(first + LINE, kept, passed.at[LINE], links.down()).start()

    def close(self, rest):
        links = self.links
        z, x = links.z, links.x
        k = LINE - 1
        if rest:
            kept, passed, rows, first = self.kept2.at[k], self.passed2, 2 * self.rest, self.base + 9
            self.load(k, 0).wait()
            self.load(k, 1).wait()
            terms, out = [kept], kept
        else:
            kept, passed, rows, first = self.kept.at[k], self.passed, self.bulk, self.base + 4
            self.load(k, 2).wait()
            links.arrived(self.base + k, self.beside.at[k])
            terms, out = [kept, self.beside.at[k]], self.own

        @pl.when(z > 0)
        def _():
            links.arrived(first + z, passed.at[z])

        @pl.when(z < 3)
        def _():
            links.arrived(first + LINE, passed.at[LINE])

        @pl.when(z == 0)
        def _():
            add_rows(out, 0, terms + [passed.at[LINE]], rows)

        @pl.when(z == 3)
        def _():
            add_rows(out, 0, terms + [passed.at[z]], rows)

        @pl.when((z > 0) & (z < 3))
        def _():
            add_rows(out, 0, terms + [passed.at[z], passed.at[LINE]], rows)

        if rest:
            away = kept.at[pl.ds((1 - x) * self.rest, self.rest), :]
            links.copy(self.base + 14, away, self.last, links.beside()).start()

    def finish(self):
        links = self.links
        z, x = links.z, links.x
        links.arrived(self.base + 14, self.last)
        mine = self.kept2.at[LINE - 1, pl.ds(x * self.rest, self.rest), :]
        add_rows(self.own, self.bulk, [mine, self.last], self.rest)
        links.sent(self.base + 14, self.last)
        for k in range(LINE):
            links.sent(self.base + k, self.beside.at[k])
        for k in range(LINE - 1):
            d = self.order[k]
            for kept, first in ((self.kept.at[k], self.base + 4), (self.kept2.at[k], self.base + 9)):

                @pl.when((d > z) | (d < z - 1))
                def _():
                    links.sent(first + d, kept)

                @pl.when(d == z - 1)
                def _():
                    links.sent(first + LINE, kept)


class Total:
    def __init__(self, links, part, out, buffers, reverse=False):
        self.links, self.part, self.out, self.reverse = links, part, out, reverse
        self.mine, self.first, self.second = buffers
        self.pieces, self.rows = self.mine.shape[0], self.mine.shape[1]
        self.base = links.take(3 * self.pieces)
        self.loads = links.take_local(2 * self.pieces)

    @staticmethod
    def scratch(rows, n, pieces=PIECES):
        return [pltpu.VMEM((pieces, rows // 2 // pieces, n), half) for _ in range(3)]

    def at(self, ref, core, j):
        place = self.pieces - 1 - j if self.reverse else j
        first = (place * 2 + core) * self.rows
        return ref.at[pl.ds(pl.multiple_of(first, self.rows), self.rows), :]

    def load(self, j):
        src = self.at(self.part, self.links.core, j)
        return pltpu.make_async_copy(src, self.mine.at[j], self.links.local.at[self.loads + j])

    def store(self, j):
        dst = self.at(self.out, self.links.core, j)
        sem = self.links.local.at[self.loads + self.pieces + j]
        return pltpu.make_async_copy(self.first.at[j], dst, sem)

    def start(self):
        links = self.links
        for j in range(self.pieces):
            self.load(j).start()
            src = self.at(self.part, 1 - links.core, j)
            links.copy(self.base + j, src, self.first.at[j], links.partner()).start()

    def middle(self):
        links = self.links

        def body(j, state):
            self.load(j).wait()
            links.arrived(self.base + j, self.first.at[j])
            add_rows(self.mine.at[j], 0, [self.mine.at[j], self.first.at[j]], self.rows)
            index = self.base + self.pieces + j
            links.copy(index, self.mine.at[j], self.second.at[j], links.across()).start()
            return state

        lax.fori_loop(0, self.pieces, body, 0)

    def spread_piece(self, j):
        links = self.links
        links.arrived(self.base + self.pieces + j, self.second.at[j])
        add_rows(self.first.at[j], 0, [self.mine.at[j], self.second.at[j]], self.rows)
        index = self.base + 2 * self.pieces + j
        dst = self.at(self.out, links.core, j)
        links.copy(index, self.first.at[j], dst, links.partner()).start()
        self.store(j).start()

    def landed_piece(self, j):
        links = self.links
        links.arrived(self.base + 2 * self.pieces + j, self.at(self.out, 1 - links.core, j))
        self.store(j).wait()

    def spread(self):
        def body(j, state):
            self.spread_piece(j)
            return state

        lax.fori_loop(0, self.pieces, body, 0)

    def landed(self):
        for j in range(self.pieces):
            self.landed_piece(j)

    def finish(self):
        links = self.links
        for j in range(self.pieces):
            for stage in range(3):
                links.sent(self.base + stage * self.pieces + j, self.mine.at[j])


def exchange(number, shards=(), totals=(), parts=()):
    gathers, scatters, sums = len(shards), len(totals), len(parts)
    scratch = []
    for total in totals:
        scratch += Scatter.scratch(total.shape[0] // (2 * LINE), total.shape[1])
    for part in parts:
        scratch += Total.scratch(part.shape[0], part.shape[1])
    remote = Gather.SEMS * gathers + Scatter.SEMS * scatters + 3 * PIECES * sums
    near = gathers + 12 * scatters + 2 * PIECES * sums
    scratch += [
        pltpu.SemaphoreType.DMA((remote,)),
        pltpu.SemaphoreType.DMA((remote,)),
        pltpu.SemaphoreType.DMA((near,)),
    ]

    def kernel(*refs):
        refs = list(refs)

        def pop(count):
            taken, refs[:count] = refs[:count], []
            return taken

        shard_refs, total_refs, part_refs = pop(gathers), pop(scatters), pop(sums)
        full_refs, own_refs, sum_refs = pop(gathers), pop(scatters), pop(sums)
        buffers = [pop(6) for _ in range(scatters)]
        sum_buffers = [pop(3) for _ in range(sums)]
        links = Links(*refs)
        gather = [Gather(links, s, f) for s, f in zip(shard_refs, full_refs)]
        scatter = [Scatter(links, *a) for a in zip(total_refs, own_refs, buffers)]
        total = [Total(links, *a) for a in zip(part_refs, sum_refs, sum_buffers)]
        links.greet()
        for item in gather + scatter + total:
            item.start()
        for k in range(LINE):
            for item in scatter:
                item.aside(k)
        for item in total:
            item.middle()
        for k in range(LINE - 1):
            for item in scatter:
                item.step(k, True)
        for item in scatter:
            item.close(True)
        for item in gather:
            item.bulk_step(1)
        for item in gather:
            item.rest_start()
        for item in scatter:
            item.step(0, False)
        for item in gather:
            item.bulk_step(2)
        for item in gather:
            item.rest_step(1)
        for item in scatter:
            item.step(1, False)
        for item in gather:
            item.bulk_step(3)
        for item in scatter:
            item.step(2, False)
        for item in total:
            item.spread()
        for item in gather:
            item.rest_step(2)
        for item in scatter:
            item.close(False)
        for item in gather:
            item.rest_step(3)
        for item in total:
            item.landed()
        for item in gather + scatter + total:
            item.finish()

    whole = pl.BlockSpec(memory_space=pl.ANY)
    near_spec = pl.BlockSpec(memory_space=pltpu.VMEM)
    outs = pl.pallas_call(
        kernel,
        in_specs=[near_spec] * gathers + [whole] * (scatters + sums),
        out_specs=[whole] * gathers + [near_spec] * scatters + [whole] * sums,
        out_shape=[
            jax.ShapeDtypeStruct((s.shape[0] * 2 * LINE, s.shape[1]), half) for s in shards
        ]
        + [jax.ShapeDtypeStruct((t.shape[0] // (2 * LINE), t.shape[1]), f32) for t in totals]
        + [jax.ShapeDtypeStruct(p.shape, half) for p in parts],
        scratch_shapes=scratch,
        compiler_params=pltpu.CompilerParams(
            collective_id=number, has_side_effects=True, vmem_limit_bytes=60 * 2**20
        ),
        name=f"exchange_{number}",
    )(*shards, *totals, *parts)
    return outs[:gathers], outs[gathers : gathers + scatters], outs[gathers + scatters :]


class Stream:
    def __init__(self, sems, base, arrays, buffers, index):
        self.sems, self.base, self.arrays, self.buffers, self.index = (
            sems, base, arrays, buffers, index,
        )

    def copies(self, i, inward):
        slot = i % 2
        for n, (array, buffer) in enumerate(zip(self.arrays, self.buffers)):
            rows = buffer.shape[1]
            first = pl.multiple_of(self.index(i) * rows, rows)
            far, near = array.at[pl.ds(first, rows), :], buffer.at[slot]
            sem = self.sems.at[self.base + 2 * n + slot]
            src, dst = (far, near) if inward else (near, far)
            yield pltpu.make_async_copy(src, dst, sem)

    def start(self, i, inward):
        for copy in self.copies(i, inward):
            copy.start()

    def wait(self, i, inward):
        for copy in self.copies(i, inward):
            copy.wait()


class Maker:
    STEPS = 2 * LINE

    def __init__(self, links, sems, base, lefts, left_buffers, pairs):
        self.links, self.sems, self.base = links, sems, base
        self.lefts, self.left_buffers, self.pairs = lefts, left_buffers, pairs
        self.rows = left_buffers[0].shape[2]

    @staticmethod
    def sem_count(lefts, pairs):
        return 2 * (lefts + pairs)

    def place(self, j):
        order = self.pairs[0][4].order
        x = self.links.x
        column = 1 - x + (j % 2) * (2 * x - 1)
        return (turn(order, j // 2) * 2 + column) * self.rows

    def moves(self, j):
        first = pl.multiple_of(self.place(j), self.rows)
        slot = j % 2
        for n, (left, buffer) in enumerate(zip(self.lefts, self.left_buffers)):
            yield pltpu.make_async_copy(
                left.at[:, pl.ds(first, self.rows)], buffer.at[slot],
                self.sems.at[self.base + 2 * n + slot],
            )

    def stores(self, j):
        first = pl.multiple_of(self.place(j), self.rows)
        slot = j % 2
        base = self.base + 2 * len(self.lefts)
        for n, (_, _, buffer, total, _) in enumerate(self.pairs):
            yield pltpu.make_async_copy(
                buffer.at[slot], total.at[pl.ds(first, self.rows), :],
                self.sems.at[base + 2 * n + slot],
            )

    def start(self):
        for move in self.moves(0):
            move.start()

    def run(self, between):
        def body(j, state):
            @pl.when(j + 1 < self.STEPS)
            def _():
                for move in self.moves(j + 1):
                    move.start()

            for move in self.moves(j):
                move.wait()
            slot = j % 2
            for which, b, buffer, _, _ in self.pairs:
                left = self.left_buffers[which][slot]
                buffer[slot] = dot(left, b[...], TN).astype(half)
            for store in self.stores(j):
                store.start()

            @pl.when(j >= 1)
            def _():
                for store in self.stores(j - 1):
                    store.wait()

            @pl.when(j % 2 == 1)
            def _():
                for pair in self.pairs:
                    pair[4].aside(j // 2)

            @pl.when((j % 2 == 0) & (j >= 2))
            def _():
                for pair in self.pairs:
                    pair[4].fetch(j // 2 - 1)

            between(j)
            return state

        lax.fori_loop(0, self.STEPS, body, 0)
        for store in self.stores(self.STEPS - 1):
            store.wait()
        for pair in self.pairs:
            pair[4].fetch(LINE - 1)


def row_sum(values):
    return jnp.sum(values, axis=0, keepdims=True)


def attention_back(tile, weights, gains, sums, carry):
    (cot, middle, d_out, tokens, qkv, mixed, outgate, pre, scores, state) = tile
    (w_out, w_qkv, w_gate, w_small, w_decay, span) = weights
    gain_ffn, gain_head = gains
    sum_ffn, sum_head, sum_bias, sum_attn = sums
    unit, scale = rms_parts(middle[...].astype(f32))
    cot = cot[...].astype(f32)
    sum_ffn[...] += row_sum(cot * unit)
    weighted = cot * gain_ffn[...]
    inner = jnp.mean(weighted * unit, axis=-1, keepdims=True)
    d_attn = (d_out[...].astype(f32) + scale * (weighted - unit * inner)).astype(half)
    d_gated = dot(d_attn, w_out[...], NN)
    rows = mixed[...].astype(f32)
    gate = outgate[...].astype(f32)
    head_scale = lax.rsqrt(jnp.mean(rows * rows, axis=-1, keepdims=True) + head_eps)
    head_unit = rows * head_scale
    sig = jax.nn.sigmoid(gate)
    d_outgate = (
        d_gated * head_unit * gain_head[...] * sig * (1.0 + gate * (1.0 - sig))
    ).astype(half)
    d_normed_head = d_gated * gate * sig
    sum_head[...] += row_sum(d_normed_head * head_unit)
    weighted = d_normed_head * gain_head[...]
    inner = jnp.mean(weighted * head_unit, axis=-1, keepdims=True)
    d_mixed = (head_scale * (weighted - head_unit * inner)).astype(half)
    dk = w_decay.shape[1]
    d_qkv, d_pre = backward_math(
        pre[...], qkv[:, :dk], qkv[:, dk : 2 * dk], qkv[:, 2 * dk :], d_mixed,
        scores[...], state[...], span, carry,
    )
    sum_bias[...] += row_sum(d_pre)
    d_pre = d_pre.astype(half)
    d_rank = dot(d_pre, w_decay[...], NT).astype(half)
    d_normed = (
        dot(d_qkv, w_qkv[...], NT) + dot(d_outgate, w_gate[...], NT) + dot(d_rank, w_small[...], NT)
    )
    unit, _ = rms_parts(tokens[...].astype(f32))
    sum_attn[...] += row_sum(d_normed * unit)
    return d_attn, d_outgate, d_qkv, d_pre, d_rank, d_normed.astype(half)


def backward_exchange(number, part, rows_in, weights, gains, lefts, rights, w_down):
    scatters = len(lefts)
    length, width = part.shape
    count = length // CHUNK
    dk = weights[4].shape[1]
    dv = weights[0].shape[1]
    outs_wide = (width, dv, 2 * dk + dv, dk, 128, width)
    in_shapes = [(CHUNK, width)] + [(a.shape[0] // count, a.shape[1]) for a in rows_in]
    in_types = [half] + [a.dtype for a in rows_in]
    streams = len(in_shapes)
    sum_wide = (width, dv, dk, width)
    made = jax.ShapeDtypeStruct((lefts[0].shape[1], rights[0].shape[1]), half)
    rows = made.shape[0] // (2 * LINE)
    scratch = []
    for _ in range(scatters):
        scratch += Scatter.scratch(rows, made.shape[1])
    scratch += Total.scratch(length, width, count)
    scratch += [pltpu.VMEM((2,) + s, t) for s, t in zip(in_shapes, in_types)]
    scratch += [pltpu.VMEM((2, CHUNK, w), half) for w in outs_wide]
    scratch += [pltpu.VMEM(w.shape, half) for w in (*weights, rights[0], w_down)]
    scratch += [pltpu.VMEM((2, length, rows), half), pltpu.VMEM((2, rows, made.shape[1]), half)]
    scratch += [pltpu.VMEM((dk, dv), f32)]
    remote = Scatter.SEMS * scatters + 3 * count
    near = 12 * scatters + 2 * count
    ffn_base = 2 * streams + 2 * len(outs_wide) + len(weights) + 3
    maker_base = ffn_base + 2
    extra = maker_base + scatters * Maker.sem_count(1, 1)
    scratch += [
        pltpu.SemaphoreType.DMA((remote,)),
        pltpu.SemaphoreType.DMA((remote,)),
        pltpu.SemaphoreType.DMA((near,)),
        pltpu.SemaphoreType.DMA((extra,)),
    ]

    def kernel(*refs):
        refs = list(refs)

        def pop(count):
            taken, refs[:count] = refs[:count], []
            return taken

        (part_ref,), row_refs = pop(1), pop(streams - 1)
        weight_refs, left_refs, right_refs = pop(len(weights)), pop(scatters), pop(scatters)
        (down_ref,), gain_refs = pop(1), pop(2)
        own_refs, (sum_ref, ffn_ref), made_refs = pop(scatters), pop(2), pop(scatters)
        out_refs, gain_sums = pop(6), pop(4)
        buffers = [pop(6) for _ in range(scatters)]
        sum_buffers = pop(3)
        in_buffers, out_buffers, near_weights = pop(streams), pop(6), pop(len(weights))
        right_near, down_near, left_buffer, made_buffer, carry = pop(5)
        sems = refs.pop()
        links = Links(*refs)
        scatter = [Scatter(links, *a) for a in zip(made_refs, own_refs, buffers)]
        down, gate = scatter
        total = Total(links, part_ref, sum_ref, sum_buffers, True)
        inputs = Stream(sems, 0, [sum_ref] + row_refs, in_buffers, lambda i: count - 1 - i)
        outputs = Stream(sems, 2 * streams, out_refs, out_buffers, lambda i: count - 1 - i)
        ffn_out = Stream(sems, ffn_base, [ffn_ref], out_buffers[:1], lambda i: i)
        near_base = 2 * streams + 12
        loads = [
            pltpu.make_async_copy(far, close, sems.at[near_base + n])
            for n, (far, close) in enumerate(
                zip(
                    (right_refs[0], right_refs[1], down_ref, *weight_refs),
                    (right_near, right_near, down_near, *near_weights),
                )
            )
        ]
        makers = [
            Maker(
                links, sems, maker_base + n * Maker.sem_count(1, 1), [left_refs[n]], [left_buffer],
                [(0, right_near, made_buffer, made_refs[n], scatter[n])],
            )
            for n in range(scatters)
        ]
        loads[0].start()
        makers[0].start()
        for load in loads[2:]:
            load.start()
        links.greet()
        total.start()
        loads[0].wait()

        def between_first(j):
            @pl.when(j == 2)
            def _():
                total.middle()

        makers[0].run(between_first)
        makers[1].start()
        down.step(0, True)
        loads[2].wait()

        def ffn_body(i, state):
            tile = right_near[pl.ds(pl.multiple_of(2 * i * CHUNK, 2 * CHUNK), 2 * CHUNK), :]
            value = dot(tile, down_near[...], NT).astype(half)

            @pl.when(i >= 1)
            def _():
                ffn_out.wait(2 * i - 2, False)
                ffn_out.wait(2 * i - 1, False)

            for part in range(2):
                out_buffers[0][part] = value[part * CHUNK : (part + 1) * CHUNK]
                ffn_out.start(2 * i + part, False)

            @pl.when(i == 1)
            def _():
                down.step(1, True)
                down.step(0, False)

            return state

        lax.fori_loop(0, count // 2, ffn_body, 0)
        loads[1].start()
        down.step(2, True)
        ffn_out.wait(count - 2, False)
        ffn_out.wait(count - 1, False)
        loads[1].wait()

        def between_second(j):
            @pl.when(j == 2)
            def _():
                down.close(True)
                down.step(1, False)

            @pl.when(j == 7)
            def _():
                down.step(2, False)

        makers[1].run(between_second)
        for j in range(3):
            total.spread_piece(j)
        total.landed_piece(0)
        for load in loads[3:]:
            load.wait()
        for ref in (*gain_sums, carry):
            ref[...] = jnp.zeros_like(ref)
        inputs.start(0, True)

        def body(i, state):
            @pl.when(i + 1 < count)
            def _():
                total.landed_piece(i + 1)
                inputs.start(i + 1, True)

            @pl.when(i + 3 < count)
            def _():
                total.spread_piece(i + 3)

            inputs.wait(i, True)
            slot = i % 2
            results = attention_back(
                [b.at[slot] for b in in_buffers], near_weights, gain_refs, gain_sums, carry
            )

            @pl.when(i >= 2)
            def _():
                outputs.wait(i - 2, False)

            for buffer, value in zip(out_buffers, results):
                buffer[slot] = value
            outputs.start(i, False)

            @pl.when(i == 0)
            def _():
                gate.step(0, True)

            @pl.when(i == 1)
            def _():
                gate.step(1, True)
                down.close(False)

            @pl.when(i == 2)
            def _():
                gate.step(2, True)
                gate.step(0, False)

            @pl.when(i == 3)
            def _():
                gate.close(True)

            @pl.when(i == 4)
            def _():
                gate.step(1, False)

            @pl.when(i == 6)
            def _():
                gate.step(2, False)

            return state

        lax.fori_loop(0, count, body, 0)
        outputs.wait(count - 2, False)
        outputs.wait(count - 1, False)
        gate.close(False)
        for item in scatter:
            item.finish()
        total.finish()

    whole = pl.BlockSpec(memory_space=pl.ANY)
    near_spec = pl.BlockSpec(memory_space=pltpu.VMEM)
    outs = pl.pallas_call(
        kernel,
        in_specs=[whole] * (2 + len(rows_in) + len(weights) + 2 * scatters) + [near_spec] * 2,
        out_specs=[near_spec] * scatters + [whole] * (2 + scatters + 6) + [near_spec] * 4,
        out_shape=[jax.ShapeDtypeStruct((rows, made.shape[1]), f32)] * scatters
        + [jax.ShapeDtypeStruct(part.shape, half)] * 2
        + [made] * scatters
        + [jax.ShapeDtypeStruct((length, w), half) for w in outs_wide]
        + [jax.ShapeDtypeStruct((1, w), f32) for w in sum_wide],
        scratch_shapes=scratch,
        compiler_params=pltpu.CompilerParams(
            collective_id=number, has_side_effects=True, vmem_limit_bytes=VMEM_LIMIT
        ),
        name=f"backward_exchange_{number}",
    )(part, *rows_in, *weights, *lefts, *rights, w_down, *gains)
    rest = outs[2 * scatters + 2 :]
    return outs[:scatters], outs[scatters + 1], rest[:6], rest[6:]


def last_exchange(number, total, parts, left_up, right_up, left_norm, right_norms, left_out, right_out):
    ups = jax.ShapeDtypeStruct((left_up.shape[1], right_up.shape[1]), half)
    rest = [jax.ShapeDtypeStruct((left_out.shape[1], right_out.shape[1]), half)]
    rest += [jax.ShapeDtypeStruct((left_norm.shape[1], r.shape[1]), half) for r in right_norms]
    made = [ups, *rest]
    rights = [right_up, right_out, *right_norms]
    lefts = [left_up, left_out, left_norm]
    length = left_up.shape[0]
    rows = ups.shape[0] // (2 * LINE)
    scatters, sums = len(made) + 1, len(parts)
    scratch = []
    for item in (*made, total):
        scratch += Scatter.scratch(item.shape[0] // (2 * LINE), item.shape[1])
    for part in parts:
        scratch += Total.scratch(part.shape[0], part.shape[1])
    scratch += [pltpu.VMEM(r.shape, half) for r in rights]
    scratch += [pltpu.VMEM((2, length, rows), half)] * 2
    scratch += [pltpu.VMEM((2, rows, m.shape[1]), half) for m in made]
    remote = Scatter.SEMS * scatters + 3 * PIECES * sums
    near = 12 * scatters + 2 * PIECES * sums
    first_count, second_count = Maker.sem_count(1, 1), Maker.sem_count(2, len(rest))
    scratch += [
        pltpu.SemaphoreType.DMA((remote,)),
        pltpu.SemaphoreType.DMA((remote,)),
        pltpu.SemaphoreType.DMA((near,)),
        pltpu.SemaphoreType.DMA((first_count + second_count + len(rights),)),
    ]

    def kernel(*refs):
        refs = list(refs)

        def pop(count):
            taken, refs[:count] = refs[:count], []
            return taken

        (total_ref,), part_refs = pop(1), pop(sums)
        left_refs, right_refs = pop(3), pop(len(rights))
        own_refs, made_refs, sum_refs = pop(scatters), pop(len(made)), pop(sums)
        buffers = [pop(6) for _ in range(scatters)]
        sum_buffers = [pop(3) for _ in range(sums)]
        near_rights, left_buffers, made_buffers = pop(len(rights)), pop(2), pop(len(made))
        sems = refs.pop()
        links = Links(*refs)
        scatter = [Scatter(links, *a) for a in zip((*made_refs, total_ref), own_refs, buffers)]
        up, late, small = scatter[0], scatter[1:], scatter[-1]
        totals = [Total(links, *a) for a in zip(part_refs, sum_refs, sum_buffers)]
        loads = [
            pltpu.make_async_copy(far, close, sems.at[first_count + second_count + n])
            for n, (far, close) in enumerate(zip(right_refs, near_rights))
        ]
        first = Maker(
            links, sems, 0, left_refs[:1], left_buffers[:1],
            [(0, near_rights[0], made_buffers[0], made_refs[0], up)],
        )
        second = Maker(
            links, sems, first_count, left_refs[1:], left_buffers,
            [
                (min(n, 1), near_rights[n + 1], made_buffers[n + 1], made_refs[n + 1], scatter[n + 1])
                for n in range(len(rest))
            ],
        )
        links.greet()
        loads[0].start()
        first.start()
        for item in totals:
            item.start()
        for load in loads[1:]:
            load.start()
        small.start()
        loads[0].wait()

        def between_first(j):
            @pl.when(j == 5)
            def _():
                for item in totals:
                    item.middle()

        first.run(between_first)
        second.start()
        for k in range(LINE):
            small.aside(k)
        up.step(0, True)
        for load in loads[1:]:
            load.wait()

        def between_second(j):
            @pl.when(j == 1)
            def _():
                up.step(1, True)
                up.step(0, False)

            @pl.when(j == 3)
            def _():
                up.step(2, True)

            @pl.when(j == 5)
            def _():
                up.close(True)
                up.step(1, False)

        second.run(between_second)
        for item in late:
            item.step(0, True)
        up.step(2, False)
        for item in late:
            item.step(1, True)
        up.close(False)
        for item in late:
            item.step(2, True)
        for item in late:
            item.step(0, False)
        for item in late:
            item.close(True)
        for item in late:
            item.step(1, False)
        totals[0].spread()
        for item in late:
            item.step(2, False)
        for item in totals[1:]:
            item.spread()
        for item in late:
            item.close(False)
        for item in totals:
            item.landed()
        for item in scatter + totals:
            item.finish()

    whole = pl.BlockSpec(memory_space=pl.ANY)
    near_spec = pl.BlockSpec(memory_space=pltpu.VMEM)
    outs = pl.pallas_call(
        kernel,
        in_specs=[whole] * (1 + sums + 3 + len(rights)),
        out_specs=[near_spec] * scatters + [whole] * (len(made) + sums),
        out_shape=[
            jax.ShapeDtypeStruct((t.shape[0] // (2 * LINE), t.shape[1]), f32)
            for t in (*made, total)
        ]
        + made
        + [jax.ShapeDtypeStruct(p.shape, half) for p in parts],
        scratch_shapes=scratch,
        compiler_params=pltpu.CompilerParams(
            collective_id=number, has_side_effects=True, vmem_limit_bytes=VMEM_LIMIT
        ),
        name=f"last_exchange_{number}",
    )(total, *parts, *lefts, *rights)
    return outs[:scatters], outs[scatters + len(made) :]


def tile_loop(count, inputs, outputs, compute, between):
    inputs.start(0, True)

    def body(i, state):
        @pl.when(i + 1 < count)
        def _():
            inputs.start(i + 1, True)

        inputs.wait(i, True)
        slot = i % 2
        results = compute([b.at[slot] for b in inputs.buffers])

        @pl.when(i >= 2)
        def _():
            outputs.wait(i - 2, False)

        for buffer, value in zip(outputs.buffers, results):
            buffer[slot] = value
        outputs.start(i, False)
        between(i)
        return state

    lax.fori_loop(0, count, body, 0)
    outputs.wait(count - 2, False)
    outputs.wait(count - 1, False)


def front_exchange(number, tokens, nears, rows_near, shards, flips):
    length, width = tokens.shape
    count = length // CHUNK
    w_qkv, w_small, w_decay, span = nears
    dk = w_decay.shape[1]
    dv = w_qkv.shape[1] - 2 * dk
    shapes = [s.shape[::-1] if flip else s.shape for s, flip in zip(shards, flips)]
    ff = shapes[2][1]
    number_of = len(shards)
    first_out = [
        ((CHUNK, width), half), ((CHUNK, 2 * dk + dv), half), ((CHUNK, 128), f32),
        ((CHUNK, dk), f32), ((CHUNK, dv), half), ((CHUNK, CHUNK), half), ((dk, dv), half),
    ]
    second_in = [((CHUNK, width), half), ((CHUNK, dv), half)]
    second_out = [((CHUNK, dv), half), ((CHUNK, dv), half), ((CHUNK, width), half)]
    third_in = [((CHUNK, width), half), ((CHUNK, width), half)]
    third_out = [((CHUNK, width), half), ((CHUNK, width), half), ((CHUNK, ff), half), ((CHUNK, ff), half)]
    first_in = [((CHUNK, width), half)]
    groups = [first_in, first_out, second_in, second_out, third_in, third_out]
    fulls = [jax.ShapeDtypeStruct((s[0] * 2 * LINE, s[1]), half) for s in shapes]
    scratch = [pltpu.VMEM(s.shape, f32) for s in shards]
    scratch += [pltpu.VMEM(s, half) for s in shapes]
    scratch += Total.scratch(length, width)
    for group in groups:
        scratch += [pltpu.VMEM((2,) + s, t) for s, t in group]
    scratch += [pltpu.VMEM(w.shape, w.dtype) for w in nears]
    scratch += [pltpu.VMEM(f.shape, half) for f in fulls[:4]]
    scratch += [pltpu.VMEM((dk, dv), f32)]
    remote = Gather.SEMS * number_of + 3 * PIECES
    near = number_of + 2 * PIECES
    bases = [2 * sum(len(g) for g in groups[:n]) for n in range(len(groups) + 1)]
    extra = bases[-1] + number_of + len(nears) + 4
    scratch += [
        pltpu.SemaphoreType.DMA((remote,)),
        pltpu.SemaphoreType.DMA((remote,)),
        pltpu.SemaphoreType.DMA((near,)),
        pltpu.SemaphoreType.DMA((extra,)),
    ]
    outs_first = [((length // CHUNK) * s[0], s[1], t) for s, t in first_out]
    outs_second = [(length, s[1], t) for s, t in second_out]
    outs_third = [(length, s[1], t) for s, t in third_out]

    def kernel(*refs):
        refs = list(refs)

        def pop(count):
            taken, refs[:count] = refs[:count], []
            return taken

        (tokens_ref,), near_refs, shard_refs = pop(1), pop(len(nears)), pop(number_of)
        gain_attn, bias, gain_head, gain_ffn = pop(4)
        full_refs, (sum_ref,) = pop(number_of), pop(1)
        first_refs, second_refs, third_refs = pop(7), pop(3), pop(4)
        staged, cast = pop(number_of), pop(number_of)
        sum_buffers = pop(3)
        buffers = [pop(len(g)) for g in groups]
        close, full_near, (state,) = pop(len(nears)), pop(4), pop(1)
        sems = refs.pop()
        links = Links(*refs)
        gathers = [Gather(links, c, f) for c, f in zip(cast, full_refs)]
        early, (gate, up, down) = gathers[:2], gathers[2:]
        total = Total(links, second_refs[2], sum_ref, sum_buffers)
        sources = [
            [tokens_ref], first_refs, [first_refs[0], first_refs[4]], second_refs,
            [sum_ref, tokens_ref], third_refs,
        ]
        streams = [
            Stream(sems, b, arrays, near_by, lambda i: i)
            for b, arrays, near_by in zip(bases, sources, buffers)
        ]
        at = bases[-1]
        arrive = [
            pltpu.make_async_copy(far, by, sems.at[at + n])
            for n, (far, by) in enumerate(zip(shard_refs, staged))
        ]
        at += number_of
        loads = [
            pltpu.make_async_copy(far, by, sems.at[at + n])
            for n, (far, by) in enumerate(zip(near_refs, close))
        ]
        at += len(nears)
        weights = [
            pltpu.make_async_copy(far, by, sems.at[at + n])
            for n, (far, by) in enumerate(zip(full_refs, full_near))
        ]

        def prepare(n):
            arrive[n].wait()
            values = staged[n][...]
            cast[n][...] = (jnp.transpose(values) if flips[n] else values).astype(half)

        for copy in arrive:
            copy.start()
        for copy in loads:
            copy.start()
        links.greet()
        for n in range(3):
            prepare(n)
        for item in gathers[:3]:
            item.start()
        for n in range(3, number_of):
            prepare(n)
        for copy in loads:
            copy.wait()
        state[...] = jnp.zeros_like(state)

        def first(tile):
            unit, _ = rms_parts(tile[0][...].astype(f32))
            normed = (unit * gain_attn[...]).astype(half)
            qkv = dot(normed, close[0][...], NN).astype(half)
            rank = dot(normed, close[1][...], NN)
            pre = bias[...] + lax.dot_general(
                rank, close[2][...], (NN, ((), ())),
                precision=highest_precision, preferred_element_type=f32,
            )
            results = forward_math(
                pre, qkv[:, :dk], qkv[:, dk : 2 * dk], qkv[:, 2 * dk :], close[3], state
            )
            return normed, qkv, rank, pre, *results

        def first_between(i):
            @pl.when(i == 1)
            def _():
                for item in early:
                    item.bulk_step(1)
                for item in early:
                    item.rest_start()
                up.start()

            @pl.when(i == 4)
            def _():
                for item in early:
                    item.bulk_step(2)
                for item in early:
                    item.rest_step(1)

            @pl.when(i == 6)
            def _():
                gate.bulk_step(1)
                gate.rest_start()

        tile_loop(count, streams[0], streams[1], first, first_between)
        up.bulk_step(1)
        up.rest_start()
        for item in early:
            item.bulk_step(3)
        for k in (2, 3):
            for item in early:
                item.rest_step(k)
        for item in early:
            item.landed()
        for copy in weights[:2]:
            copy.start()
        for copy in weights[:2]:
            copy.wait()

        def second(tile):
            normed, mixed = tile
            outgate = dot(normed[...], full_near[0][...], NN).astype(half)
            gated = gated_rows(mixed[...].astype(f32), outgate.astype(f32), gain_head[...]).astype(half)
            return outgate, gated, dot(gated, full_near[1][...], NT).astype(half)

        def second_between(i):
            @pl.when(i == 3)
            def _():
                gate.bulk_step(2)
                gate.rest_step(1)

            @pl.when(i == 6)
            def _():
                up.bulk_step(2)
                up.rest_step(1)
                down.start()

        tile_loop(count, streams[2], streams[3], second, second_between)
        total.start()
        total.middle()
        gate.bulk_step(3)
        gate.rest_step(2)
        up.bulk_step(3)
        up.rest_step(2)
        down.bulk_step(1)
        down.rest_start()
        gate.rest_step(3)
        up.rest_step(3)
        total.spread()
        gate.landed()
        weights[2].start()
        up.landed()
        weights[3].start()
        total.landed()
        for copy in weights[2:]:
            copy.wait()

        def third(tile):
            middle = tile[1][...].astype(f32) + tile[0][...].astype(f32)
            unit, _ = rms_parts(middle)
            normed = (unit * gain_ffn[...]).astype(half)
            gate_rows = dot(normed, full_near[2][...], NN).astype(half)
            return middle.astype(half), normed, gate_rows, dot(normed, full_near[3][...], NN).astype(half)

        def third_between(i):
            @pl.when(i == 0)
            def _():
                down.bulk_step(2)
                down.rest_step(1)

            @pl.when(i == 3)
            def _():
                down.bulk_step(3)
                down.rest_step(2)

        tile_loop(count, streams[4], streams[5], third, third_between)
        down.rest_step(3)
        down.landed()
        for item in gathers:
            item.drain()
        total.finish()

    whole = pl.BlockSpec(memory_space=pl.ANY)
    near_spec = pl.BlockSpec(memory_space=pltpu.VMEM)
    outs = pl.pallas_call(
        kernel,
        in_specs=[whole] * (1 + len(nears) + number_of) + [near_spec] * 4,
        out_specs=[whole] * (number_of + 1 + 14),
        out_shape=fulls
        + [jax.ShapeDtypeStruct(tokens.shape, half)]
        + [
            jax.ShapeDtypeStruct((r, c), t) for r, c, t in (*outs_first, *outs_second, *outs_third)
        ],
        scratch_shapes=scratch,
        compiler_params=pltpu.CompilerParams(
            collective_id=number, has_side_effects=True, vmem_limit_bytes=VMEM_LIMIT
        ),
        name=f"front_exchange_{number}",
    )(tokens, *nears, *shards, *rows_near)
    return outs[2:number_of], outs[number_of + 1 :], outs[:2]


class Ring:
    def __init__(self, size):
        self.size = size
        self.wide = size // LINE
        place = lax.axis_index("dp")
        self.z = place // self.wide
        self.x = place % self.wide

    def z_pairs(self, step):
        wide = self.wide
        return [
            (z * wide + x, ((z + step) % LINE) * wide + x) for z in range(LINE) for x in range(wide)
        ]

    def x_pairs(self, step):
        wide = self.wide
        return [(z * wide + x, z * wide + (x + step) % wide) for z in range(LINE) for x in range(wide)]


def gather(ring, shard):
    rows = shard.shape[0]
    pieces = [(ring.z, shard)]
    for step in (1, 3, 2):
        pieces.append(((ring.z - step) % LINE, lax.ppermute(shard, "dp", ring.z_pairs(step))))
    out = jnp.zeros((ring.size * rows, shard.shape[1]), shard.dtype)
    for z, piece in pieces:
        for step in range(ring.wide):
            moved = lax.ppermute(piece, "dp", ring.x_pairs(step)) if step else piece
            place = z * ring.wide + (ring.x - step) % ring.wide
            out = lax.dynamic_update_slice(out, moved, (place * rows, 0))
    return out


def scatter(ring, total):
    rows = total.shape[0] // ring.size

    def block(z, x):
        place = (z % LINE) * ring.wide + x % ring.wide
        return lax.dynamic_slice(total, (place * rows, 0), (rows, total.shape[1]))

    result = None
    for step in (2, 1, 3, 0):
        z = ring.z + step
        kept = block(z, ring.x).astype(f32)
        for side in range(1, ring.wide):
            away = lax.ppermute(block(z, ring.x + side), "dp", ring.x_pairs(side))
            kept = kept + away.astype(f32)
        if step:
            kept = lax.ppermute(kept.astype(half), "dp", ring.z_pairs(step)).astype(f32)
        result = kept if result is None else result + kept
    return result


CORE = [(i, i ^ 1) for i in range(4)]
ACROSS = [(i, i ^ 2) for i in range(4)]


def tensor_sum(part):
    rows = part.shape[0] // 2
    second = (lax.axis_index("tensor") & 1) == 1
    upper, lower = part[:rows], part[rows:]
    mine = jnp.where(second, lower, upper)
    away = jnp.where(second, upper, lower)
    mine = (mine.astype(f32) + lax.ppermute(away, "tensor", CORE).astype(f32)).astype(half)
    mine = (mine.astype(f32) + lax.ppermute(mine, "tensor", ACROSS).astype(f32)).astype(half)
    theirs = lax.ppermute(mine, "tensor", CORE)
    return jnp.concatenate(
        [jnp.where(second, theirs, mine), jnp.where(second, mine, theirs)], axis=0
    )


def rms_parts(values):
    scale = lax.rsqrt(jnp.mean(values * values, axis=-1, keepdims=True) + norm_eps)
    return values * scale, scale


def rms_back(unit, scale, gain, cot):
    weighted = cot * gain
    inner = jnp.mean(weighted * unit, axis=-1, keepdims=True)
    return scale * (weighted - unit * inner), jnp.sum(cot * unit, axis=0)


def gated_rows(mixed, outgate, gain):
    scale = lax.rsqrt(jnp.mean(mixed * mixed, axis=-1, keepdims=True) + head_eps)
    return mixed * scale * gain * jax.nn.silu(outgate)


def local(
    tokens, lengths, norm_attn, query_proj, key_proj, value_proj, outgate_proj, rank_proj,
    decay_proj, decay_bias, head_gain, out_proj, norm_ffn, gate_proj, up_proj, down_proj, cotangent,
    *, size,
):
    ring = Ring(size)
    rows_total = tokens.shape[0]
    width = norm_attn.shape[0]
    rank = rank_proj.shape[1]
    dk = query_proj.shape[1]
    dv = value_proj.shape[1]
    ff = gate_proj.shape[1]
    bits = decay_proj.shape[2]
    gains = head_gain.shape[0]

    def as_column(values):
        flat = values.reshape(-1, 1)
        return jnp.pad(flat, ((0, width - flat.shape[0]), (0, 0)))

    decay_cols = rank * bits // width
    small = jnp.concatenate(
        [
            rank_proj,
            norm_attn[:, None],
            norm_ffn[:, None],
            as_column(head_gain),
            as_column(decay_bias),
            decay_proj.reshape(decay_cols, width).T,
        ],
        axis=1,
    )
    small = jnp.pad(small, ((0, 0), (0, 128 - small.shape[1]))).astype(half)
    qkv = jnp.concatenate([query_proj * 0.0625, key_proj, value_proj], axis=1).astype(half)
    fast = size == 2 * LINE

    def collect(number, shards, parts):
        if fast:
            fulls, _, sums = exchange(number, shards, (), parts)
            return fulls, sums
        return [gather(ring, s) for s in shards], [tensor_sum(p) for p in parts]

    def deliver(number, totals, parts):
        if fast:
            _, owns, sums = exchange(number, (), totals, parts)
            return owns, sums
        return [scatter(ring, t) for t in totals], [tensor_sum(p) for p in parts]

    if fast:
        (qkv_full, small_full), _ = collect(0, (qkv, small), ())
    else:
        late = (outgate_proj.astype(half), out_proj.T.astype(half))
        (qkv_full, small_full, outgate_full, out_full), _ = collect(0, (qkv, small, *late), ())
    rank_full = small_full[:, :rank]
    small32 = small_full.astype(f32)
    gain_attn = small32[:, rank]
    gain_ffn = small32[:, rank + 1]
    by_place = small32.reshape(size, width, 128)
    gain_head = by_place[:, :gains, rank + 2].reshape(-1)
    bias = by_place[:, :bits, rank + 3].reshape(-1)
    decay_weight = jnp.transpose(
        jnp.transpose(by_place[:, :, rank + 4 : rank + 4 + decay_cols], (0, 2, 1)).reshape(
            size, rank, bits
        ),
        (1, 0, 2),
    ).reshape(rank, -1)

    positions = jnp.arange(SEQ_LEN, dtype=jnp.int32)
    mask = (positions[None, :] < lengths[:, None]).astype(f32).reshape(rows_total, 1)
    tokens32 = tokens.astype(f32)
    unit, scale = rms_parts(tokens32)
    span = span_matrix()
    if fast:
        w_decay = jnp.pad(decay_weight, ((0, 128 - rank), (0, 0)))
        (gate_full, up_full, down_full), outs, (outgate_full, out_full) = front_exchange(
            1,
            tokens,
            (qkv_full, small_full, w_decay, span),
            (gain_attn[None, :], bias[None, :], gain_head[None, :], gain_ffn[None, :]),
            (outgate_proj, out_proj, gate_proj, up_proj, down_proj),
            (False, True, False, False, True),
        )
        (
            normed, qkv, rank_rows, pre, mixed, scores, states, outgate, gated, _,
            middle_half, normed_ffn, gate_rows, up_rows,
        ) = outs
        rank_rows = rank_rows[:, :rank]
        middle = middle_half.astype(f32)
        gate_rows = gate_rows.astype(f32)
        up_rows = up_rows.astype(f32)
    else:
        normed = (unit * gain_attn).astype(half)
        qkv = dot(normed, qkv_full, NN).astype(half)
        rank_rows = dot(normed, rank_full, NN)
        pre = (
            jnp.dot(
                rank_rows, decay_weight, precision=highest_precision, preferred_element_type=f32
            )
            + bias
        )
        mixed, scores, states = recur_forward(pre, qkv, span, dk, dv)
        outgate = dot(normed, outgate_full, NN).astype(half)
        gated, pull_gated = jax.vjp(gated_rows, mixed.astype(f32), outgate.astype(f32), gain_head)
        gated = gated.astype(half)
        second = (gate_proj.astype(half), up_proj.astype(half), down_proj.T.astype(half))
        (gate_full, up_full, down_full), (attn,) = collect(
            1, second, (dot(gated, out_full, NT).astype(half),)
        )
        middle = tokens32 + attn.astype(f32)
        unit_ffn, scale_ffn = rms_parts(middle)
        normed_ffn = (unit_ffn * gain_ffn).astype(half)
        gate_rows = dot(normed_ffn, gate_full, NN)
        up_rows = dot(normed_ffn, up_full, NN)
    hidden, pull_glu = jax.vjp(lambda g, u: jax.nn.silu(g) * u, gate_rows, up_rows)
    hidden = hidden.astype(half)
    d_out = cotangent.astype(f32) * mask
    d_out_half = d_out.astype(half)
    d_gate, d_up = pull_glu(dot(d_out_half, down_full, NN))
    d_gate = d_gate.astype(half)
    d_up = d_up.astype(half)
    d_normed_ffn = (dot(d_gate, gate_full, NT) + dot(d_up, up_full, NT)).astype(half)
    if fast:
        (down_own, gate_own), ffn, outs, sums = backward_exchange(
            2,
            d_normed_ffn,
            (
                middle_half, d_out_half, tokens, qkv, mixed, outgate, pre, scores, states,
            ),
            (out_full, qkv_full, outgate_full, small_full, w_decay.astype(half), span),
            (gain_ffn[None, :], gain_head[None, :]),
            (d_out_half, normed_ffn),
            (hidden, d_gate),
            down_full,
        )
        d_attn, d_outgate, d_qkv, d_pre_half, d_rank, d_normed = outs
        grad_gain_ffn, grad_head, grad_bias, grad_gain_attn = sums
        d_middle = d_attn.astype(f32)
        d_rank = d_rank[:, :rank]
    else:
        d_normed_ffn = tensor_sum(d_normed_ffn)
        d_back, grad_gain_ffn = rms_back(unit_ffn, scale_ffn, gain_ffn, d_normed_ffn.astype(f32))
        d_middle = d_out + d_back
        d_attn = d_middle.astype(half)
        d_mixed, d_outgate, grad_head = pull_gated(dot(d_attn, out_full, NN))
        d_outgate = d_outgate.astype(half)
        d_qkv, d_pre = recur_backward(pre, qkv, d_mixed.astype(half), scores, states, span, dk, dv)
        d_rank = dot(d_pre.astype(half), decay_weight.astype(half), NT).astype(half)
        d_normed = (
            dot(d_qkv, qkv_full, NT) + dot(d_outgate, outgate_full, NT) + dot(d_rank, rank_full, NT)
        )
        grad_gain_attn = jnp.sum(d_normed * unit, axis=0)
        d_normed = d_normed.astype(half)
        d_pre_half = d_pre.astype(half)
        grad_bias = jnp.sum(d_pre, axis=0)
    grad_rank = dot(normed, d_rank, TN)
    grad_decay = jnp.transpose(
        dot(rank_rows.astype(half), d_pre_half, TN).reshape(rank, size, bits), (1, 0, 2)
    ).reshape(size, decay_cols, width)

    def spread(values):
        blocks = values.reshape(size, -1, 1)
        return jnp.pad(blocks, ((0, 0), (0, width - blocks.shape[1]), (0, 0)))

    grad_small = jnp.concatenate(
        [
            grad_rank.reshape(size, width, rank),
            grad_gain_attn.reshape(size, width, 1),
            grad_gain_ffn.reshape(size, width, 1),
            spread(grad_head),
            spread(grad_bias),
            jnp.transpose(grad_decay, (0, 2, 1)),
        ],
        axis=2,
    )
    grad_small = jnp.pad(grad_small, ((0, 0), (0, 0), (0, 128 - grad_small.shape[2])))
    grad_small = grad_small.reshape(size * width, 128).astype(half)

    if fast:
        (up_own, out_own, outgate_own, qkv_own, small_own), (d_normed, ffn) = last_exchange(
            3, grad_small, (d_normed, ffn), normed_ffn, d_up, normed, (d_outgate, d_qkv), d_attn, gated
        )
    else:
        ffn = dot(hidden, down_full, NT).astype(half)
        waiting = (
            dot(d_out_half, hidden, TN).astype(half),
            dot(normed_ffn, d_gate, TN).astype(half),
            dot(normed_ffn, d_up, TN).astype(half),
            dot(d_attn, gated, TN).astype(half),
            dot(normed, d_outgate, TN).astype(half),
            dot(normed, d_qkv, TN).astype(half),
            grad_small,
        )
        (down_own, gate_own, up_own, out_own, outgate_own, qkv_own, small_own), (
            d_normed, ffn,
        ) = deliver(3, waiting, (d_normed, ffn))
    output = (mask * (middle + ffn.astype(f32))).astype(half)
    d_back, _ = rms_back(unit, scale, gain_attn, d_normed.astype(f32))
    grad_tokens = (d_middle + d_back).astype(half)
    heads_own = small_own.astype(half)
    heads_own = heads_own.astype(f32) + lax.ppermute(heads_own, "tensor", CORE).astype(f32)
    heads_own = heads_own.astype(half)
    heads_own = heads_own.astype(f32) + lax.ppermute(heads_own, "tensor", ACROSS).astype(f32)
    return (
        output,
        grad_tokens,
        heads_own[:, rank],
        qkv_own[:, :dk] * 0.0625,
        qkv_own[:, dk : 2 * dk],
        qkv_own[:, 2 * dk : 2 * dk + dv],
        outgate_own,
        heads_own[:, :rank],
        small_own[:, rank + 4 : rank + 4 + decay_cols].T.reshape(decay_proj.shape),
        small_own[:bits, rank + 3].reshape(decay_bias.shape),
        heads_own[:gains, rank + 2],
        out_own.T,
        heads_own[:, rank + 1] * 0.25,
        gate_own,
        up_own,
        down_own.T,
    )


def solution(mesh):
    size = mesh.shape["dp"]

    def run(*args):
        return local(*args, size=size)

    weight = P("dp", "tensor")
    cross = P("tensor", "dp")
    return jax.shard_map(
        run,
        mesh=mesh,
        in_specs=(
            P("dp", None), P("dp"), P("dp"), weight, weight, weight, weight, P("dp", None),
            P(None, "tensor", "dp"), cross, P("dp"), cross, P("dp"), weight, weight, cross,
            P("dp", None),
        ),
        out_specs=(
            P("dp", None), P("dp", None), P("dp"), weight, weight, weight, weight, P("dp", None),
            P(None, "tensor", "dp"), cross, P("dp"), cross, P("dp"), weight, weight, cross,
        ),
        check_vma=False,
    )
```
